32 devices in a mesh: dp: 32 (over z, y, x, core).
Axes of the slice: x: 2, y: 2, z: 4, core: 2. Of those that a mesh axis runs over, the one named last changes fastest.
Arguments:
- questions: bfloat16 [160, 64, 256], P('dp'), may hold values from -6 to 6
- passages: bfloat16 [160, 256, 256], P('dp'), may hold values from -6 to 6
- cot_questions: bfloat16 [160, 64, 256], P('dp'), may hold values from -6 to 6
- cot_passages: bfloat16 [160, 256, 256], P('dp'), may hold values from -6 to 6
- len_questions: int32 [160], P('dp'), may hold values from 8 to 64, as said below
- len_passages: int32 [160], P('dp'), may hold values from 40 to 256, as said below
- positive: int32 [160], replicated, may hold values from 0 to 159
- query_key_value_weight: bfloat16 [2, 256, 768], replicated, may hold values from -0.375 to 0.375
- query_bias: bfloat16 [2, 256], replicated, may hold values from -0.59765625 to 0.59765625
- value_bias: bfloat16 [2, 256], replicated, may hold values from -0.59765625 to 0.59765625
- attention_out_weight: bfloat16 [2, 256, 256], replicated, may hold values from -1.5 to 1.5
- attention_out_bias: bfloat16 [2, 256], replicated, may hold values from -0.59765625 to 0.59765625
- attn_gain: bfloat16 [2, 256], replicated, may hold values from 0.5 to 1.5
- attn_shift: bfloat16 [2, 256], replicated, may hold values from -0.59765625 to 0.59765625
- feedforward_in_weight: bfloat16 [2, 256, 1024], replicated, may hold values from -0.375 to 0.375
- feedforward_hidden_bias: bfloat16 [2, 1024], replicated, may hold values from -0.59765625 to 0.59765625
- feedforward_out_weight: bfloat16 [2, 1024, 256], replicated, may hold values from -0.1875 to 0.1875
- feedforward_out_bias: bfloat16 [2, 256], replicated, may hold values from -0.59765625 to 0.59765625
- ffn_gain: bfloat16 [2, 256], replicated, may hold values from 0.5 to 1.5
- ffn_shift: bfloat16 [2, 256], replicated, may hold values from -0.59765625 to 0.59765625
Outputs:
- loss_rows: float32 [160], P('dp')
- out_questions: bfloat16 [160, 64, 256], P('dp')
- out_passages: bfloat16 [160, 256, 256], P('dp')
- grad_questions: bfloat16 [160, 64, 256], P('dp')
- grad_passages: bfloat16 [160, 256, 256], P('dp')
- qkv_weight_grad: float32 [2, 256, 768], replicated
- query_bias_grad: float32 [2, 256], replicated
- value_bias_grad: float32 [2, 256], replicated
- proj_weight_grad: float32 [2, 256, 256], replicated
- proj_bias_grad: float32 [2, 256], replicated
- attn_gain_grad: float32 [2, 256], replicated
- attn_shift_grad: float32 [2, 256], replicated
- up_weight_grad: float32 [2, 256, 1024], replicated
- up_bias_grad: float32 [2, 1024], replicated
- down_weight_grad: float32 [2, 1024, 256], replicated
- down_bias_grad: float32 [2, 256], replicated
- ffn_gain_grad: float32 [2, 256], replicated
- ffn_shift_grad: float32 [2, 256], replicated
The draws below stay inside these ranges and needn't reach their ends.
Inputs may be any that keep to these rules, and one draw needn't show every extreme that they name: `len_questions`: some question has exactly 64 tokens. `len_passages`: some passage has exactly 256 tokens.
All inputs are finite; a program needn't handle non-finite values.
Results may differ from the reference program's by a relative error of at most 0.008.
The reference program's roundings to bfloat16 on the way count: a program that leaves them out, or rounds other values in their place, can miss the bound.
Values may be sent and summed in bfloat16 or wider, within the bound.
No kernel may reach another device: no remote copies, remote signals or barrier semaphores. Data moves between devices by JAX's collectives and lax.ppermute only.
A program may use at most 128 MiB of HBM per device.

```python
import math
import jax
import jax.numpy as jnp
from jax import lax

D = 256
HEAD_DIM = 64
FF = 1024
LQ = 64
LP = 256
MINQ = 8
MINP = 40
QUESTIONS = 160
PASSAGES = 160


def ragged_lengths(key, salt, entries, shortest, longest):
    base_key = jax.random.fold_in(key, salt)
    draw_key, spot_key = jax.random.split(base_key)
    values = jax.random.randint(draw_key, (entries,), shortest, longest + 1, dtype=jnp.int32)
    spot_index = jax.random.randint(spot_key, (), 0, entries, dtype=jnp.int32)
    return values.at[spot_index].set(longest)


def draw_len_questions(key, part):
    return ragged_lengths(key, 17, QUESTIONS, MINQ, LQ)


def draw_len_passages(key, part):
    return ragged_lengths(key, 29, PASSAGES, MINP, LP)


def with_ends(array, key, least, high):
    longest = array.shape.index(max(array.shape))
    spots = []
    for shift in (0, 1):
        where = [jax.random.randint(jax.random.fold_in(key, axis), (), 0, length) for axis, length in enumerate(array.shape)]
        where[longest] = (where[longest] + shift) % array.shape[longest]
        spots.append(tuple(where))
    return array.at[spots[0]].set(least).at[spots[1]].set(high)


def steps_of(own_key, dims, shards, low, largest):
    loudness = 1.0
    for position, parts in shards:
        steps = jax.random.uniform(jax.random.fold_in(jax.random.fold_in(own_key, 6), position), (parts,), jnp.float32, low / len(shards), largest / len(shards))
        loudness = loudness * jnp.repeat(jnp.exp(steps), dims[position] // parts).reshape((-1,) + (1,) * (len(dims) - 1 - position))
    return loudness


def bell_draw(rng, dims, scale, reach, cuts=(), kind=jnp.bfloat16):
    values = jax.random.normal(rng, dims, jnp.float32) * scale
    if len(cuts) > 0:
        values = steps_of(rng, dims, cuts, -0.22, 0.18) * values
    return jnp.clip(values, min=-reach, max=reach).astype(kind)


def setup_inputs(seed: int = 0) -> dict:
    key_list = jax.random.split(jax.random.key(seed), 21)
    return {
        "questions": bell_draw(key_list[0], (QUESTIONS, LQ, D), 1.0, 6.0, ((0, 32),)),
        "passages": bell_draw(key_list[1], (PASSAGES, LP, D), 1.0, 6.0, ((0, 32),)),
        "cot_questions": bell_draw(key_list[2], (QUESTIONS, LQ, D), 1.0, 6.0, ((0, 32),)),
        "cot_passages": bell_draw(key_list[3], (PASSAGES, LP, D), 1.0, 6.0, ((0, 32),)),
        "len_questions": draw_len_questions(jax.random.fold_in(key_list[20], 71), 0),
        "len_passages": draw_len_passages(jax.random.fold_in(key_list[20], 71), 0),
        "positive": with_ends(jax.random.randint(key_list[6], (QUESTIONS,), 0, PASSAGES), jax.random.fold_in(key_list[6], 1), 0, PASSAGES - 1).astype(jnp.int32),
        "query_key_value_weight": bell_draw(key_list[7], (2, D, 3 * D), D ** -0.5, 0.375),
        "query_bias": bell_draw(key_list[8], (2, D), 0.1, 0.59765625),
        "value_bias": bell_draw(key_list[9], (2, D), 0.1, 0.59765625),
        "attention_out_weight": bell_draw(key_list[10], (2, D, D), (D // 16) ** -0.5, 1.5),
        "attention_out_bias": bell_draw(key_list[11], (2, D), 0.1, 0.59765625),
        "attn_gain": jnp.clip(1.0 + 0.1 * jax.random.normal(key_list[12], (2, D), jnp.float32), 0.5, 1.5).astype(jnp.bfloat16),
        "attn_shift": bell_draw(key_list[13], (2, D), 0.1, 0.59765625),
        "feedforward_in_weight": bell_draw(key_list[14], (2, D, FF), D ** -0.5, 0.375),
        "feedforward_hidden_bias": bell_draw(key_list[15], (2, FF), 0.1, 0.59765625),
        "feedforward_out_weight": bell_draw(key_list[16], (2, FF, D), FF ** -0.5, 0.1875),
        "feedforward_out_bias": bell_draw(key_list[17], (2, D), 0.1, 0.59765625),
        "ffn_gain": jnp.clip(1.0 + 0.1 * jax.random.normal(key_list[18], (2, D), jnp.float32), 0.5, 1.5).astype(jnp.bfloat16),
        "ffn_shift": bell_draw(key_list[19], (2, D), 0.1, 0.59765625),
    }


ln_eps = 1e-06
score_scale = 0.125
masked_score = -1e+30
highest_precision = lax.Precision.HIGHEST

@jax.custom_vjp
def low(v):
    return lax.optimization_barrier(v.astype(jnp.bfloat16)).astype(jnp.float32)

@jax.custom_vjp
def low_back(v):
    return v

def low_keep(v):
    return (low(v), None)

def low_pass(kept, grad):
    return (grad,)

def back_keep(v):
    return (v, None)

def back_low(kept, grad):
    return (low(grad),)
low.defvjp(low_keep, low_pass)
low_back.defvjp(back_keep, back_low)

def layer_norm(values, gain_row, shift_row):
    average = lax.optimization_barrier(jnp.mean(values, axis=-1, keepdims=True))
    centered = values - average
    variance = lax.optimization_barrier(jnp.mean(centered * centered, axis=-1, keepdims=True))
    return centered * lax.rsqrt(variance + ln_eps) * gain_row + shift_row

def gelu_exact(values):
    return 0.5 * values * (1.0 + lax.erf(values * 0.7071067811865476))

def encode_group(params, input_rows, lengths):
    query_key_value_weight, query_bias, value_bias, attention_out_weight, attention_out_bias, attn_gain, attn_shift, feedforward_in_weight, feedforward_hidden_bias, feedforward_out_weight, feedforward_out_bias, ffn_gain, ffn_shift = params
    seq_count, seq_len, model_width = input_rows.shape
    head_count = model_width // HEAD_DIM
    positions = jnp.arange(seq_len, dtype=jnp.int32)
    valid_key = positions[None, :] < lengths[:, None]
    query_key_value_bias = jnp.concatenate([query_bias, jnp.zeros_like(query_bias), value_bias])
    query_key_value_rows = jnp.einsum('gvp,pj->gvj', low(input_rows), query_key_value_weight, precision=highest_precision) + query_key_value_bias
    query_key_value_rows = low(low_back(query_key_value_rows)).reshape(seq_count, seq_len, 3, head_count, HEAD_DIM)
    raw_scores = jnp.einsum('sqhd,skhd->shqk', query_key_value_rows[:, :, 0], query_key_value_rows[:, :, 1], precision=highest_precision)
    raw_scores = low_back(raw_scores * score_scale)
    raw_scores = jnp.where(valid_key[:, None, None, :], raw_scores, masked_score)
    row_top = lax.optimization_barrier(jnp.max(raw_scores, axis=-1, keepdims=True))
    exp_scores = jnp.exp(raw_scores - row_top)
    attn_prob = exp_scores / lax.optimization_barrier(jnp.sum(exp_scores, axis=-1, keepdims=True))
    context_rows = jnp.einsum('shqk,skhd->sqhd', low(attn_prob), query_key_value_rows[:, :, 2], precision=highest_precision)
    context_rows = low(low_back(context_rows.reshape(seq_count, seq_len, model_width)))
    attended_rows = low_back(jnp.einsum('jgu,uq->jgq', context_rows, attention_out_weight, precision=highest_precision) + attention_out_bias)
    normalized_rows = layer_norm(input_rows + attended_rows, attn_gain, attn_shift)
    hidden_preactivation = low_back(jnp.einsum('pct,ti->pci', low(normalized_rows), feedforward_in_weight, precision=highest_precision) + feedforward_hidden_bias)
    gelu_activated_rows = low(gelu_exact(hidden_preactivation))
    feedforward_output = low_back(jnp.einsum('wkh,hi->wki', gelu_activated_rows, feedforward_out_weight, precision=highest_precision) + feedforward_out_bias)
    result = layer_norm(normalized_rows + feedforward_output, ffn_gain, ffn_shift)
    return result * valid_key[:, :, None].astype(result.dtype)

def encode_all(params, input_rows, lengths):
    count_all, seq_len, model_width = input_rows.shape
    group_size = math.gcd(count_all, max(1, 4096 // seq_len))
    grouped = input_rows.reshape(count_all // group_size, group_size, seq_len, model_width)
    grouped_len = lengths.reshape(count_all // group_size, group_size)

    def one_group(group_args):
        return encode_group(params, group_args[0], group_args[1])
    outputs = lax.map(jax.checkpoint(one_group), (grouped, grouped_len))
    return outputs.reshape(count_all, seq_len, model_width)

def forward(params_all, question_in, passage_in, len_questions, len_passages, positive):
    question_params = tuple((member[0] for member in params_all))
    passage_params = tuple((member[1] for member in params_all))
    question_out = encode_all(question_params, question_in, len_questions)
    passage_out = encode_all(passage_params, passage_in, len_passages)
    question_cls = low(question_out[:, 0])
    passage_cls = low(passage_out[:, 0])
    logits = low_back(jnp.dot(question_cls, passage_cls.T, precision=highest_precision) * score_scale)
    row_top = lax.optimization_barrier(jnp.max(logits, axis=1, keepdims=True))
    log_total = row_top[:, 0] + jnp.log(lax.optimization_barrier(jnp.sum(jnp.exp(logits - row_top), axis=1)))
    picked = jnp.take_along_axis(logits, positive[:, None].astype(jnp.int32), axis=1)[:, 0]
    loss_rows = log_total - picked
    return (question_out, passage_out, loss_rows)

def reference(questions, passages, cot_questions, cot_passages, len_questions, len_passages, positive, query_key_value_weight, query_bias, value_bias, attention_out_weight, attention_out_bias, attn_gain, attn_shift, feedforward_in_weight, feedforward_hidden_bias, feedforward_out_weight, feedforward_out_bias, ffn_gain, ffn_shift):
    params_all = tuple((member.astype(jnp.float32) for member in (query_key_value_weight, query_bias, value_bias, attention_out_weight, attention_out_bias, attn_gain, attn_shift, feedforward_in_weight, feedforward_hidden_bias, feedforward_out_weight, feedforward_out_bias, ffn_gain, ffn_shift)))
    question_in = questions.astype(jnp.float32)
    passage_in = passages.astype(jnp.float32)

    def objective(params_now, question_now, passage_now):
        return forward(params_now, question_now, passage_now, len_questions, len_passages, positive)
    (question_out, passage_out, loss_rows), pullback = jax.vjp(objective, params_all, question_in, passage_in)
    param_grads, question_grad, passage_grad = pullback((cot_questions.astype(jnp.float32), cot_passages.astype(jnp.float32), jnp.ones(loss_rows.shape, jnp.float32)))
    return (loss_rows, question_out.astype(jnp.bfloat16), passage_out.astype(jnp.bfloat16), question_grad.astype(jnp.bfloat16), passage_grad.astype(jnp.bfloat16), param_grads[0], param_grads[1], param_grads[2], param_grads[3], param_grads[4], param_grads[5], param_grads[6], param_grads[7], param_grads[8], param_grads[9], param_grads[10], param_grads[11], param_grads[12])
```

```python
import jax
import jax.numpy as jnp
from jax import lax
from jax.sharding import PartitionSpec as P

HEAD_DIM = 64


ln_eps = 1e-06
score_scale = 0.125
masked_score = -1e30


def layer_norm(values, gain_row, shift_row):
    average = jnp.mean(values, axis=-1, keepdims=True)
    centered = values - average
    variance = jnp.mean(centered * centered, axis=-1, keepdims=True)
    return centered * lax.rsqrt(variance + ln_eps) * gain_row + shift_row


def gelu_exact(values):
    return 0.5 * values * (1.0 + lax.erf(values * 0.7071067811865476))


def norm_pullback(values, gain_row, shift_row, grad_rows):
    _, pullback = jax.vjp(layer_norm, values, gain_row, shift_row)
    return pullback(grad_rows)


def layer_forward(params, input_rows, lengths):
    (
        query_key_value_weight,
        query_bias,
        value_bias,
        attention_out_weight,
        attention_out_bias,
        attn_gain,
        attn_shift,
        feedforward_in_weight,
        feedforward_hidden_bias,
        feedforward_out_weight,
        feedforward_out_bias,
        ffn_gain,
        ffn_shift,
    ) = params
    seq_count, seq_len, model_width = input_rows.shape
    head_count = model_width // HEAD_DIM
    positions = jnp.arange(seq_len, dtype=jnp.int32)
    valid_key = positions[None, :] < lengths[:, None]
    query_key_value_bias = jnp.concatenate(
        [query_bias, jnp.zeros_like(query_bias), value_bias]
    ).astype(jnp.float32)
    query_key_value_rows = (
        jnp.einsum(
            "gvp,pj->gvj", input_rows, query_key_value_weight, preferred_element_type=jnp.float32
        )
        + query_key_value_bias
    )
    qkv_heads = query_key_value_rows.astype(jnp.bfloat16).reshape(
        seq_count, seq_len, 3, head_count, HEAD_DIM
    )
    raw_scores = (
        jnp.einsum(
            "sqhd,skhd->shqk",
            qkv_heads[:, :, 0],
            qkv_heads[:, :, 1],
            preferred_element_type=jnp.float32,
        )
        * score_scale
    )
    raw_scores = jnp.where(valid_key[:, None, None, :], raw_scores, masked_score)
    row_top = jnp.max(raw_scores, axis=-1, keepdims=True)
    exp_scores = jnp.exp(raw_scores - row_top)
    attn_prob = exp_scores / jnp.sum(exp_scores, axis=-1, keepdims=True)
    context_rows = jnp.einsum(
        "shqk,skhd->sqhd",
        attn_prob.astype(jnp.bfloat16),
        qkv_heads[:, :, 2],
        preferred_element_type=jnp.float32,
    )
    context_rows = context_rows.reshape(seq_count, seq_len, model_width).astype(jnp.bfloat16)
    attended_rows = jnp.einsum(
        "jgu,uq->jgq", context_rows, attention_out_weight, preferred_element_type=jnp.float32
    ) + attention_out_bias.astype(jnp.float32)
    residual_one = input_rows.astype(jnp.float32) + attended_rows
    normalized_rows = layer_norm(
        residual_one, attn_gain.astype(jnp.float32), attn_shift.astype(jnp.float32)
    )
    normalized_reduced_rows = normalized_rows.astype(jnp.bfloat16)
    hidden_preactivation = jnp.einsum(
        "pct,ti->pci",
        normalized_reduced_rows,
        feedforward_in_weight,
        preferred_element_type=jnp.float32,
    ) + feedforward_hidden_bias.astype(jnp.float32)
    gelu_activated_rows = gelu_exact(hidden_preactivation).astype(jnp.bfloat16)
    feedforward_output = jnp.einsum(
        "wkh,hi->wki",
        gelu_activated_rows,
        feedforward_out_weight,
        preferred_element_type=jnp.float32,
    ) + feedforward_out_bias.astype(jnp.float32)
    residual_two = normalized_rows + feedforward_output
    valid_rows = valid_key.astype(jnp.float32)[:, :, None]
    result = (
        layer_norm(residual_two, ffn_gain.astype(jnp.float32), ffn_shift.astype(jnp.float32))
        * valid_rows
    )
    saved_rows = (
        qkv_heads,
        attn_prob,
        context_rows,
        residual_one,
        normalized_reduced_rows,
        hidden_preactivation,
        gelu_activated_rows,
        residual_two,
        valid_rows,
    )
    return (result, saved_rows)


def layer_backward(params, input_rows, lengths, grad_out):
    (
        query_key_value_weight,
        query_bias,
        value_bias,
        attention_out_weight,
        attention_out_bias,
        attn_gain,
        attn_shift,
        feedforward_in_weight,
        feedforward_hidden_bias,
        feedforward_out_weight,
        feedforward_out_bias,
        ffn_gain,
        ffn_shift,
    ) = params
    _, saved_rows = layer_forward(params, input_rows, lengths)
    (
        qkv_heads,
        attn_prob,
        context_rows,
        residual_one,
        normalized_reduced_rows,
        hidden_preactivation,
        gelu_activated_rows,
        residual_two,
        valid_rows,
    ) = saved_rows
    seq_count, seq_len, model_width = input_rows.shape
    head_count = model_width // HEAD_DIM
    grad_result = grad_out * valid_rows
    grad_two, ffn_gain_grad, ffn_shift_grad = norm_pullback(
        residual_two, ffn_gain.astype(jnp.float32), ffn_shift.astype(jnp.float32), grad_result
    )
    feedforward_gradient = grad_two.astype(jnp.bfloat16)
    down_weight_grad = jnp.einsum(
        "inu,inm->um", gelu_activated_rows, feedforward_gradient, preferred_element_type=jnp.float32
    )
    down_bias_grad = jnp.sum(feedforward_gradient.astype(jnp.float32), axis=(0, 1))
    activation_gradient = jnp.einsum(
        "tjx,ux->tju",
        feedforward_gradient,
        feedforward_out_weight,
        preferred_element_type=jnp.float32,
    )
    _, gelu_pull = jax.vjp(gelu_exact, hidden_preactivation)
    preactivation_gradient = gelu_pull(activation_gradient)[0].astype(jnp.bfloat16)
    up_weight_grad = jnp.einsum(
        "hir,him->rm",
        normalized_reduced_rows,
        preactivation_gradient,
        preferred_element_type=jnp.float32,
    )
    up_bias_grad = jnp.sum(preactivation_gradient.astype(jnp.float32), axis=(0, 1))
    grad_normed = grad_two + jnp.einsum(
        "hzn,rn->hzr",
        preactivation_gradient,
        feedforward_in_weight,
        preferred_element_type=jnp.float32,
    )
    grad_one, attn_gain_grad, attn_shift_grad = norm_pullback(
        residual_one, attn_gain.astype(jnp.float32), attn_shift.astype(jnp.float32), grad_normed
    )
    attention_gradient = grad_one.astype(jnp.bfloat16)
    proj_weight_grad = jnp.einsum(
        "upb,uph->bh", context_rows, attention_gradient, preferred_element_type=jnp.float32
    )
    proj_bias_grad = jnp.sum(attention_gradient.astype(jnp.float32), axis=(0, 1))
    grad_context = jnp.einsum(
        "rbv,av->rba", attention_gradient, attention_out_weight, preferred_element_type=jnp.float32
    )
    grad_context = grad_context.astype(jnp.bfloat16).reshape(
        seq_count, seq_len, head_count, HEAD_DIM
    )
    query_rows = qkv_heads[:, :, 0]
    key_rows = qkv_heads[:, :, 1]
    value_rows = qkv_heads[:, :, 2]
    grad_prob = jnp.einsum(
        "sqhd,skhd->shqk", grad_context, value_rows, preferred_element_type=jnp.float32
    )
    grad_values = jnp.einsum(
        "shqk,sqhd->skhd",
        attn_prob.astype(jnp.bfloat16),
        grad_context,
        preferred_element_type=jnp.float32,
    )
    prob_dot = jnp.sum(attn_prob * grad_prob, axis=-1, keepdims=True)
    grad_raw = (attn_prob * (grad_prob - prob_dot)).astype(jnp.bfloat16)
    grad_queries = (
        jnp.einsum("shqk,skhd->sqhd", grad_raw, key_rows, preferred_element_type=jnp.float32)
        * score_scale
    )
    grad_keys = (
        jnp.einsum("shqk,sqhd->skhd", grad_raw, query_rows, preferred_element_type=jnp.float32)
        * score_scale
    )
    projected_gradient = jnp.stack([grad_queries, grad_keys, grad_values], axis=2)
    projected_gradient = projected_gradient.reshape(seq_count, seq_len, 3 * model_width).astype(
        jnp.bfloat16
    )
    qkv_weight_grad = jnp.einsum(
        "qjb,qjc->bc", input_rows, projected_gradient, preferred_element_type=jnp.float32
    )
    bias_sums = jnp.sum(projected_gradient.astype(jnp.float32), axis=(0, 1))
    query_bias_grad = bias_sums[:model_width]
    value_bias_grad = bias_sums[2 * model_width :]
    grad_inputs = grad_one + jnp.einsum(
        "ncf,yf->ncy",
        projected_gradient,
        query_key_value_weight,
        preferred_element_type=jnp.float32,
    )
    weight_grads = (
        qkv_weight_grad,
        query_bias_grad,
        value_bias_grad,
        proj_weight_grad,
        proj_bias_grad,
        attn_gain_grad,
        attn_shift_grad,
        up_weight_grad,
        up_bias_grad,
        down_weight_grad,
        down_bias_grad,
        ffn_gain_grad,
        ffn_shift_grad,
    )
    return (grad_inputs.astype(jnp.bfloat16), weight_grads)


def stages(count):
    masks = []
    bit = 1
    while bit < count:
        masks.append(bit)
        bit = bit * 2
    groups = [masks[:1]]
    rest = masks[1:]
    while rest:
        groups.append(rest[:2])
        rest = rest[2:]
    return [group for group in groups if group]


def partner_send(values, mask, count):
    return lax.ppermute(values, "dp", [(i, i ^ mask) for i in range(count)])


def combos(group):
    low = group[0]
    return [index * low for index in range(1, 2 ** len(group))]


def reduce_scatter(buffer, count, me):
    for group in stages(count):
        radix = 2 ** len(group)
        digit = (me // group[0]) % radix
        split = buffer.reshape((radix, buffer.shape[0] // radix) + buffer.shape[1:])
        received = []
        for step, mask in enumerate(combos(group), start=1):
            outgoing = lax.dynamic_index_in_dim(split, digit ^ step, 0, keepdims=False)
            received.append(partner_send(outgoing, mask, count))
        total = lax.dynamic_index_in_dim(split, digit, 0, keepdims=False).astype(jnp.float32)
        for piece in received:
            total = total + piece.astype(jnp.float32)
        buffer = total.astype(jnp.bfloat16)
    return buffer


def gather_back(chunk, count, me):
    buffer = chunk
    for group in reversed(stages(count)):
        radix = 2 ** len(group)
        digit = (me // group[0]) % radix
        whole = jnp.zeros((radix,) + buffer.shape, buffer.dtype)
        pieces = [buffer]
        for mask in combos(group):
            pieces.append(partner_send(buffer, mask, count))
        for step, piece in enumerate(pieces):
            whole = lax.dynamic_update_index_in_dim(whole, piece, digit ^ step, 0)
        buffer = whole.reshape((radix * buffer.shape[0],) + buffer.shape[1:])
    return buffer


TAIL = 8
MATRICES = (0, 3, 7, 9)
VECTORS = (1, 2, 4, 5, 6, 8, 10, 11, 12)


def to_blocks(matrix):
    rows, columns = matrix.shape
    if columns == 256:
        return matrix
    return matrix.reshape(rows, columns // 256, 256).transpose(1, 0, 2).reshape(-1, 256)


def from_blocks(blocks, shape):
    rows, columns = shape
    if columns == 256:
        return blocks
    return blocks.reshape(columns // 256, rows, 256).transpose(1, 0, 2).reshape(rows, columns)


def pack_group(grads, count):
    main = jnp.concatenate([to_blocks(grads[i]).astype(jnp.bfloat16) for i in MATRICES])
    small = jnp.concatenate([grads[i].reshape(-1, 256).astype(jnp.bfloat16) for i in VECTORS])
    small = jnp.pad(small, ((0, count * TAIL - small.shape[0]), (0, 0)))
    return jnp.concatenate(
        [main.reshape(count, -1, 256), small.reshape(count, TAIL, 256)], axis=1
    )


def unpack_group(buffer, grads):
    count, chunk, _ = buffer.shape
    main = buffer[:, : chunk - TAIL].reshape(-1, 256)
    small = buffer[:, chunk - TAIL :].reshape(-1, 256)
    summed = [None] * len(grads)
    row = 0
    for i in MATRICES:
        rows = grads[i].size // 256
        summed[i] = from_blocks(main[row : row + rows], grads[i].shape).astype(jnp.float32)
        row += rows
    row = 0
    for i in VECTORS:
        rows = grads[i].size // 256
        summed[i] = small[row : row + rows].reshape(-1).astype(jnp.float32)
        row += rows
    return summed


def body(
    questions,
    passages,
    cot_questions,
    cot_passages,
    len_questions,
    len_passages,
    positive,
    query_key_value_weight,
    query_bias,
    value_bias,
    attention_out_weight,
    attention_out_bias,
    attn_gain,
    attn_shift,
    feedforward_in_weight,
    feedforward_hidden_bias,
    feedforward_out_weight,
    feedforward_out_bias,
    ffn_gain,
    ffn_shift,
):
    weights = (
        query_key_value_weight,
        query_bias,
        value_bias,
        attention_out_weight,
        attention_out_bias,
        attn_gain,
        attn_shift,
        feedforward_in_weight,
        feedforward_hidden_bias,
        feedforward_out_weight,
        feedforward_out_bias,
        ffn_gain,
        ffn_shift,
    )
    question_params = tuple((member[0] for member in weights))
    passage_params = tuple((member[1] for member in weights))
    local_count = questions.shape[0]
    question_out, _ = layer_forward(question_params, questions, len_questions)
    passage_out, _ = layer_forward(passage_params, passages, len_passages)
    question_low = question_out.astype(jnp.bfloat16)
    passage_low = passage_out.astype(jnp.bfloat16)
    question_cls = question_low[:, 0]
    passage_cls = passage_low[:, 0]
    count = positive.shape[0] // local_count
    me = lax.axis_index("dp")
    both_cls = jnp.concatenate([question_cls, passage_cls])
    all_cls = lax.all_to_all(
        jnp.broadcast_to(both_cls[None], (count,) + both_cls.shape), "dp", 0, 0, tiled=True
    )
    all_question_cls = all_cls[:, :local_count].reshape(-1, both_cls.shape[1])
    all_passage_cls = all_cls[:, local_count:].reshape(-1, both_cls.shape[1])
    first_row = me * local_count
    all_logits = (
        jnp.einsum(
            "qd,pd->qp", all_question_cls, all_passage_cls, preferred_element_type=jnp.float32
        )
        * score_scale
    )
    row_top = jnp.max(all_logits, axis=1, keepdims=True)
    log_total = row_top + jnp.log(jnp.sum(jnp.exp(all_logits - row_top), axis=1, keepdims=True))
    columns = jnp.arange(all_logits.shape[1], dtype=jnp.int32)
    positive_hot = (columns[None, :] == positive[:, None]).astype(jnp.float32)
    grad_logits = (jnp.exp(all_logits - log_total) - positive_hot).astype(jnp.bfloat16)
    all_loss = log_total[:, 0] - jnp.sum(all_logits * positive_hot, axis=1)
    loss_rows = lax.dynamic_slice_in_dim(all_loss, first_row, local_count)
    own_rows = lax.dynamic_slice_in_dim(grad_logits, first_row, local_count, axis=0)
    own_columns = lax.dynamic_slice_in_dim(grad_logits, first_row, local_count, axis=1)
    grad_cls_q = (
        jnp.einsum("qp,pd->qd", own_rows, all_passage_cls, preferred_element_type=jnp.float32)
        * score_scale
    )
    grad_cls_p = (
        jnp.einsum("qp,qd->pd", own_columns, all_question_cls, preferred_element_type=jnp.float32)
        * score_scale
    )
    grad_out_q = cot_questions.astype(jnp.float32).at[:, 0].add(grad_cls_q)
    grad_out_p = cot_passages.astype(jnp.float32).at[:, 0].add(grad_cls_p)
    grad_in_q, question_grads = layer_backward(
        question_params, questions, len_questions, grad_out_q
    )
    question_sum = gather_back(
        reduce_scatter(pack_group(question_grads, count), count, me), count, me
    )
    grad_in_p, passage_grads = layer_backward(passage_params, passages, len_passages, grad_out_p)
    passage_sum = gather_back(
        reduce_scatter(pack_group(passage_grads, count), count, me), count, me
    )
    summed = tuple(
        jnp.stack([question_part, passage_part])
        for question_part, passage_part in zip(
            unpack_group(question_sum, question_grads), unpack_group(passage_sum, passage_grads)
        )
    )
    return (loss_rows, question_low, passage_low, grad_in_q, grad_in_p) + summed


def solution(mesh):
    return jax.shard_map(
        body,
        mesh=mesh,
        in_specs=(
            P("dp", None, None),
            P("dp", None, None),
            P("dp", None, None),
            P("dp", None, None),
            P("dp"),
            P("dp"),
            P(),
            P(),
            P(),
            P(),
            P(),
            P(),
            P(),
            P(),
            P(),
            P(),
            P(),
            P(),
            P(),
            P(),
        ),
        out_specs=(
            P("dp"),
            P("dp", None, None),
            P("dp", None, None),
            P("dp", None, None),
            P("dp", None, None),
            P(),
            P(),
            P(),
            P(),
            P(),
            P(),
            P(),
            P(),
            P(),
            P(),
            P(),
            P(),
            P(),
        ),
        check_vma=False,
    )
```

```python
import functools

import jax
import jax.numpy as jnp
from jax import lax
from jax.experimental import pallas as pl
from jax.experimental.pallas import tpu as pltpu
from jax.sharding import PartitionSpec as P

HEAD_DIM = 64
WIDTH = 256
HEADS = WIDTH // HEAD_DIM
HIDDEN = 1024
BLOCKS = HIDDEN // WIDTH
PAD = 8
VECTOR_ROWS = 16
GROUP_ROWS = 13 * WIDTH
ln_eps = 1e-06
score_scale = 0.125
masked_score = -1e30
f32 = jnp.float32
bf16 = jnp.bfloat16

QUERY_BIAS, VALUE_BIAS, PROJ_BIAS, ATTN_GAIN, ATTN_SHIFT, DOWN_BIAS, FFN_GAIN, FFN_SHIFT = range(8)
UP_BIAS = 8


def dot(a, b):
    return lax.dot_general(a, b, (((1,), (0,)), ((), ())), preferred_element_type=f32)


def dot_nt(a, b):
    return lax.dot_general(a, b, (((1,), (1,)), ((), ())), preferred_element_type=f32)


def dot_tn(a, b):
    return lax.dot_general(a, b, (((0,), (0,)), ((), ())), preferred_element_type=f32)


def row_loop(rows, chunk, step):
    def body(index, carry):
        step(pl.multiple_of(index * chunk, chunk))
        return carry

    lax.fori_loop(0, rows // chunk, body, 0)


def vector(ref, which):
    return ref[...].astype(f32)[which : which + 1]


def lane_head(rows):
    return lax.broadcasted_iota(jnp.int32, (rows, WIDTH), 1) // HEAD_DIM


def stack_heads(values):
    head = lane_head(values.shape[0])
    wide = values.astype(f32)
    return jnp.concatenate(
        [jnp.where(head == h, wide, 0.0).astype(bf16) for h in range(HEADS)], axis=0
    )


def pick_heads(stacked, rows):
    head = lane_head(rows)
    result = stacked[:rows]
    for h in range(1, HEADS):
        result = jnp.where(head == h, stacked[h * rows : (h + 1) * rows], result)
    return result


def forward_kernel(
    which, seqs, length,
    len_ref, x_ref, wqkv_ref, qb_ref, vb_ref, wo_ref, ob_ref, g1_ref, b1_ref,
    w1_ref, hb_ref, w2_ref, fb_ref, g2_ref, b2_ref,
    out_ref, cls_ref, qkv_ref, p_ref, ctx_ref, n1_ref, r1_ref, nb_ref, gp_ref, act_ref, n2_ref, r2_ref,
    wide_ref, score_ref, prob_ref,
):
    rows = seqs * length
    step = pl.program_id(0)
    x = x_ref[...]
    qkv_ref[:, :WIDTH] = (dot(x, wqkv_ref[:, :WIDTH]) + vector(qb_ref, which)).astype(bf16)
    qkv_ref[:, WIDTH : 2 * WIDTH] = dot(x, wqkv_ref[:, WIDTH : 2 * WIDTH]).astype(bf16)
    qkv_ref[:, 2 * WIDTH :] = (dot(x, wqkv_ref[:, 2 * WIDTH :]) + vector(vb_ref, which)).astype(bf16)
    stack_rows = HEADS * length
    for s in range(seqs):
        span = slice(s * length, (s + 1) * length)
        size = len_ref[step * seqs + s]
        queries = stack_heads(qkv_ref[span, :WIDTH])
        score_ref[...] = dot_nt(queries, qkv_ref[span, WIDTH : 2 * WIDTH])

        def softmax(row):
            part = score_ref[pl.ds(row, 32), :] * score_scale
            key = lax.broadcasted_iota(jnp.int32, part.shape, 1)
            part = jnp.where(key < size, part, masked_score)
            part = jnp.exp(part - jnp.max(part, axis=1, keepdims=True))
            prob = part * (1.0 / jnp.sum(part, axis=1, keepdims=True))
            p_ref[pl.ds(s * stack_rows + row, 32), :] = prob
            prob_ref[pl.ds(row, 32), :] = prob.astype(bf16)

        row_loop(stack_rows, 32, softmax)
        context = dot(prob_ref[...], qkv_ref[span, 2 * WIDTH :])
        ctx_ref[span, :] = pick_heads(context, length).astype(bf16)
    n2_ref[...] = dot(ctx_ref[...], wo_ref[...])
    ob, g1, b1 = vector(ob_ref, which), vector(g1_ref, which), vector(b1_ref, which)

    def first_norm(row):
        here = pl.ds(row, 32)
        value = x_ref[here, :].astype(f32) + (n2_ref[here, :] + ob)
        centered = value - jnp.mean(value, axis=1, keepdims=True)
        inverse = lax.rsqrt(jnp.mean(centered * centered, axis=1, keepdims=True) + ln_eps)
        unit = centered * inverse
        n1_ref[here, :] = unit
        r1_ref[here, :] = inverse
        nb_ref[here, :] = (unit * g1 + b1).astype(bf16)

    row_loop(rows, 32, first_norm)
    wide_ref[...] = dot(nb_ref[...], w1_ref[...])
    hb = vector(hb_ref, which)

    def gelu(row):
        here = pl.ds(row, 16)
        for j in range(BLOCKS):
            lanes = slice(j * WIDTH, (j + 1) * WIDTH)
            value = wide_ref[here, lanes] + hb[:, lanes]
            cumulative = 0.5 + 0.5 * lax.erf(value * 0.7071067811865476)
            density = jnp.exp(value * value * -0.5) * 0.3989422804014327
            act_ref[here, lanes] = (value * cumulative).astype(bf16)
            gp_ref[here, lanes] = cumulative + value * density

    row_loop(rows, 16, gelu)
    n2_ref[...] = dot(act_ref[...], w2_ref[...])
    fb, g2, b2 = vector(fb_ref, which), vector(g2_ref, which), vector(b2_ref, which)

    for s in range(seqs):
        size = len_ref[step * seqs + s]

        def second_norm(row):
            here = pl.ds(s * length + row, 32)
            value = (n1_ref[here, :] * g1 + b1) + (n2_ref[here, :] + fb)
            centered = value - jnp.mean(value, axis=1, keepdims=True)
            inverse = lax.rsqrt(jnp.mean(centered * centered, axis=1, keepdims=True) + ln_eps)
            unit = centered * inverse
            n2_ref[here, :] = unit
            r2_ref[here, :] = inverse
            position = row + lax.broadcasted_iota(jnp.int32, (32, WIDTH), 0)
            out_ref[here, :] = jnp.where(position < size, unit * g2 + b2, 0.0).astype(bf16)

        row_loop(length, 32, second_norm)
        cls_ref[pl.ds(step * seqs + s, 1), :] = out_ref[s * length : s * length + 16, :].astype(f32)[:1]


def add_row(vec_ref, row, values):
    vec_ref[row : row + 1, :] = vec_ref[row : row + 1, :] + jnp.sum(values, axis=0, keepdims=True)


def ffn_phase(which, seqs, length, first, len_ref, cls_ref, cot_ref, n2_ref, r2_ref, gp_ref, w2_ref, g2_ref, two_ref, gffn_ref, gpre_ref, vec_ref, wide_ref):
    g2 = vector(g2_ref, which)
    for s in range(seqs):
        size = len_ref[first + s]
        cls_row = cls_ref[pl.ds(first + s, 1), :]

        def norm_back(row):
            here = pl.ds(s * length + row, 32)
            position = row + lax.broadcasted_iota(jnp.int32, (32, WIDTH), 0)
            grad = cot_ref[here, :].astype(f32) + jnp.where(position == 0, cls_row, 0.0)
            grad = jnp.where(position < size, grad, 0.0)
            unit = n2_ref[here, :]
            scaled = grad * g2
            first_mean = jnp.mean(scaled, axis=1, keepdims=True)
            second_mean = jnp.mean(scaled * unit, axis=1, keepdims=True)
            two = r2_ref[here, :] * (scaled - first_mean - unit * second_mean)
            low = two.astype(bf16)
            two_ref[here, :] = two
            gffn_ref[here, :] = low
            add_row(vec_ref, FFN_GAIN, grad * unit)
            add_row(vec_ref, FFN_SHIFT, grad)
            add_row(vec_ref, DOWN_BIAS, low.astype(f32))

        row_loop(length, 32, norm_back)
    wide_ref[...] = dot_nt(gffn_ref[...], w2_ref[...])

    def gelu_back(row):
        here = pl.ds(row, 16)
        for j in range(BLOCKS):
            lanes = slice(j * WIDTH, (j + 1) * WIDTH)
            low = (wide_ref[here, lanes] * gp_ref[here, lanes]).astype(bf16)
            gpre_ref[here, lanes] = low
            add_row(vec_ref, UP_BIAS + j, low.astype(f32))

    row_loop(seqs * length, 16, gelu_back)


def attn_norm_phase(which, rows, gpre_ref, w1_ref, two_ref, n1_ref, r1_ref, g1_ref, wo_ref, one_ref, gatt_ref, dctx_ref, vec_ref):
    one_ref[...] = dot_nt(gpre_ref[...], w1_ref[...])
    g1 = vector(g1_ref, which)

    def norm_back(row):
        here = pl.ds(row, 32)
        grad = two_ref[here, :] + one_ref[here, :]
        unit = n1_ref[here, :]
        scaled = grad * g1
        first_mean = jnp.mean(scaled, axis=1, keepdims=True)
        second_mean = jnp.mean(scaled * unit, axis=1, keepdims=True)
        one = r1_ref[here, :] * (scaled - first_mean - unit * second_mean)
        low = one.astype(bf16)
        one_ref[here, :] = one
        gatt_ref[here, :] = low
        add_row(vec_ref, ATTN_GAIN, grad * unit)
        add_row(vec_ref, ATTN_SHIFT, grad)
        add_row(vec_ref, PROJ_BIAS, low.astype(f32))

    row_loop(rows, 32, norm_back)
    dctx_ref[...] = dot_nt(gatt_ref[...], wo_ref[...]).astype(bf16)


def attn_core_phase(seqs, length, dctx_ref, qkv_ref, p_ref, gqkv_ref, vec_ref, dp_ref, ds_ref, pb_ref):
    stack_rows = HEADS * length
    for s in range(seqs):
        span = slice(s * length, (s + 1) * length)
        context = stack_heads(dctx_ref[span, :])
        dp_ref[...] = dot_nt(context, qkv_ref[span, 2 * WIDTH :])

        def softmax_back(row):
            prob = p_ref[pl.ds(s * stack_rows + row, 32), :]
            grad = dp_ref[pl.ds(row, 32), :]
            inner = jnp.sum(prob * grad, axis=1, keepdims=True)
            ds_ref[pl.ds(row, 32), :] = (prob * (grad - inner)).astype(bf16)
            pb_ref[pl.ds(row, 32), :] = prob.astype(bf16)

        row_loop(stack_rows, 32, softmax_back)
        queries = stack_heads(qkv_ref[span, :WIDTH])
        grad_q = (pick_heads(dot(ds_ref[...], qkv_ref[span, WIDTH : 2 * WIDTH]), length) * score_scale).astype(bf16)
        gqkv_ref[span, :WIDTH] = grad_q
        add_row(vec_ref, QUERY_BIAS, grad_q.astype(f32))
        gqkv_ref[span, WIDTH : 2 * WIDTH] = (dot_tn(ds_ref[...], queries) * score_scale).astype(bf16)
        grad_v = dot_tn(pb_ref[...], context).astype(bf16)
        gqkv_ref[span, 2 * WIDTH :] = grad_v
        add_row(vec_ref, VALUE_BIAS, grad_v.astype(f32))


def first_step(vec_ref):
    @pl.when(pl.program_id(0) == 0)
    def _():
        vec_ref[...] = jnp.zeros_like(vec_ref)


def ffn_kernel(which, length, len_ref, cls_ref, cot_ref, n2_ref, r2_ref, gp_ref, w2_ref, g2_ref, two_ref, gffn_ref, gpre_ref, vec_ref, wide_ref):
    first_step(vec_ref)
    ffn_phase(which, 1, length, pl.program_id(0), len_ref, cls_ref, cot_ref, n2_ref, r2_ref, gp_ref, w2_ref, g2_ref, two_ref, gffn_ref, gpre_ref, vec_ref, wide_ref)


def ffn_weight_kernel(act_ref, gffn_ref, nb_ref, gpre_ref, up_ref, down_ref):
    down_ref[...] = dot_tn(act_ref[...], gffn_ref[...]).astype(bf16)
    up_ref[...] = dot_tn(nb_ref[...], gpre_ref[...]).astype(bf16)


def attn_norm_kernel(which, length, gpre_ref, w1_ref, two_ref, n1_ref, r1_ref, g1_ref, wo_ref, ctx_ref, one_ref, dctx_ref, vec_ref, proj_ref, gatt_ref, acc_ref):
    first_step(vec_ref)
    first_step(acc_ref)
    attn_norm_phase(which, length, gpre_ref, w1_ref, two_ref, n1_ref, r1_ref, g1_ref, wo_ref, one_ref, gatt_ref, dctx_ref, vec_ref)
    acc_ref[...] += dot_tn(ctx_ref[...], gatt_ref[...])

    @pl.when(pl.program_id(0) == pl.num_programs(0) - 1)
    def _():
        proj_ref[...] = acc_ref[...].astype(bf16)


def attn_core_kernel(length, dctx_ref, qkv_ref, p_ref, x_ref, wqkv_ref, one_ref, gx_ref, vec_ref, dw_ref, gqkv_ref, dp_ref, ds_ref, pb_ref, acc_ref):
    first_step(vec_ref)
    first_step(acc_ref)
    attn_core_phase(1, length, dctx_ref, qkv_ref, p_ref, gqkv_ref, vec_ref, dp_ref, ds_ref, pb_ref)
    gx_ref[...] = (one_ref[...] + dot_nt(gqkv_ref[...], wqkv_ref[...])).astype(bf16)
    for j in range(3):
        acc_ref[j * WIDTH : (j + 1) * WIDTH, :] += dot_tn(x_ref[...], gqkv_ref[:, j * WIDTH : (j + 1) * WIDTH])

    @pl.when(pl.program_id(0) == pl.num_programs(0) - 1)
    def _():
        dw_ref[...] = acc_ref[...].astype(bf16)


def question_back_kernel(
    which, seqs, length,
    len_ref, cls_ref, cot_ref, x_ref, qkv_ref, p_ref, ctx_ref, n1_ref, r1_ref, nb_ref, gp_ref, act_ref, n2_ref, r2_ref,
    wqkv_ref, wo_ref, g1_ref, w1_ref, w2_ref, g2_ref,
    gx_ref, pack_ref,
    two_ref, gffn_ref, gpre_ref, vec_ref, wide_ref, one_ref, gatt_ref, dctx_ref, gqkv_ref, dp_ref, ds_ref, pb_ref,
):
    rows = seqs * length
    vec_ref[...] = jnp.zeros_like(vec_ref)
    ffn_phase(which, seqs, length, 0, len_ref, cls_ref, cot_ref, n2_ref, r2_ref, gp_ref, w2_ref, g2_ref, two_ref, gffn_ref, gpre_ref, vec_ref, wide_ref)
    for j in range(BLOCKS):
        lanes = slice(j * WIDTH, (j + 1) * WIDTH)
        pack_ref[(4 + j) * WIDTH : (5 + j) * WIDTH, :] = dot_tn(nb_ref[...], gpre_ref[:, lanes]).astype(bf16)
        pack_ref[(8 + j) * WIDTH : (9 + j) * WIDTH, :] = dot_tn(act_ref[:, lanes], gffn_ref[...]).astype(bf16)
    attn_norm_phase(which, rows, gpre_ref, w1_ref, two_ref, n1_ref, r1_ref, g1_ref, wo_ref, one_ref, gatt_ref, dctx_ref, vec_ref)
    pack_ref[3 * WIDTH : 4 * WIDTH, :] = dot_tn(ctx_ref[...], gatt_ref[...]).astype(bf16)
    attn_core_phase(seqs, length, dctx_ref, qkv_ref, p_ref, gqkv_ref, vec_ref, dp_ref, ds_ref, pb_ref)
    for j in range(3):
        lanes = slice(j * WIDTH, (j + 1) * WIDTH)
        pack_ref[j * WIDTH : (j + 1) * WIDTH, :] = dot_tn(x_ref[...], gqkv_ref[:, lanes]).astype(bf16)
    gx_ref[...] = (one_ref[...] + dot_nt(gqkv_ref[...], wqkv_ref[...])).astype(bf16)
    pack_ref[12 * WIDTH :, :] = jnp.zeros((WIDTH, WIDTH), bf16)
    pack_ref[12 * WIDTH : 12 * WIDTH + VECTOR_ROWS, :] = vec_ref[...].astype(bf16)


def loss_kernel(local, me_ref, all_ref, hot_ref, own_hot_ref, loss_ref, gq_ref, gp_ref, q_ref, p_ref):
    count = all_ref.shape[0]
    me = me_ref[0]
    wide = all_ref[...].astype(f32)
    q_ref[...] = wide[:, :PAD].reshape(count * PAD, WIDTH).astype(bf16)
    p_ref[...] = wide[:, PAD:].reshape(count * PAD, WIDTH).astype(bf16)
    own_q = all_ref[me][:PAD]
    own_p = all_ref[me][PAD:]
    logits = dot_nt(own_q, p_ref[...]) * score_scale
    column = lax.broadcasted_iota(jnp.int32, logits.shape, 1)
    logits = jnp.where(column % PAD < local, logits, masked_score)
    top = jnp.max(logits, axis=1, keepdims=True)
    total = top + jnp.log(jnp.sum(jnp.exp(logits - top), axis=1, keepdims=True))
    hot = (column == own_hot_ref[...]).astype(f32)
    loss_ref[...] = jnp.broadcast_to(total - jnp.sum(logits * hot, axis=1, keepdims=True), loss_ref.shape)
    grad = (jnp.exp(logits - total) - hot).astype(bf16)
    gq_ref[...] = dot(grad, p_ref[...]) * score_scale
    gp_ref[...] = jnp.zeros_like(gp_ref)
    block = 256 if count * PAD % 256 == 0 else count * PAD

    def part(index, carry):
        start = pl.multiple_of(index * block, block)
        queries = q_ref[pl.ds(start, block), :]
        scores = dot_nt(p_ref[...], queries) * score_scale
        row = lax.broadcasted_iota(jnp.int32, scores.shape, 0)
        scores = jnp.where(row % PAD < local, scores, masked_score)
        peak = jnp.max(scores, axis=0, keepdims=True)
        sums = peak + jnp.log(jnp.sum(jnp.exp(scores - peak), axis=0, keepdims=True))
        own = dot_nt(own_p, queries) * score_scale
        own_row = lax.broadcasted_iota(jnp.int32, own.shape, 0)
        own_lane = lax.broadcasted_iota(jnp.int32, own.shape, 1)
        own_hits = (own_row + me * PAD == hot_ref[:, pl.ds(start, block)]).astype(f32)
        own_grad = jnp.where(own_lane % PAD < local, jnp.exp(own - sums) - own_hits, 0.0)
        gp_ref[...] += dot(own_grad.astype(bf16), queries) * score_scale
        return carry

    lax.fori_loop(0, count * PAD // block, part, 0)


def unpack_kernel(q_ref, p_ref, qkv_ref, proj_ref, up_ref, down_ref, vec_ref):
    for which, ref in enumerate((q_ref, p_ref)):
        for j in range(3):
            qkv_ref[which, :, j * WIDTH : (j + 1) * WIDTH] = ref[j * WIDTH : (j + 1) * WIDTH, :].astype(f32)
        proj_ref[which] = ref[3 * WIDTH : 4 * WIDTH, :].astype(f32)
        for j in range(BLOCKS):
            up_ref[which, :, j * WIDTH : (j + 1) * WIDTH] = ref[(4 + j) * WIDTH : (5 + j) * WIDTH, :].astype(f32)
        down_ref[which] = ref[8 * WIDTH : 12 * WIDTH, :].astype(f32)
        vec_ref[which] = ref[12 * WIDTH : 12 * WIDTH + VECTOR_ROWS, :].astype(f32)


def smem():
    return pl.BlockSpec(memory_space=pltpu.SMEM)


def whole(shape):
    return pl.BlockSpec(shape, lambda i: (0,) * len(shape))


def rows_of(rows, columns):
    return pl.BlockSpec((rows, columns), lambda i: (i, 0))


def part_of(which, shape):
    return pl.BlockSpec((None,) + shape, lambda i: (which, 0, 0))


def params():
    return pltpu.CompilerParams(vmem_limit_bytes=56 * 1024 * 1024)


def shape(dims, kind):
    return jax.ShapeDtypeStruct(dims, kind)


def cost(flops, moved):
    return pl.CostEstimate(flops=flops, bytes_accessed=moved, transcendentals=0)


def pair(columns):
    return whole((2, columns))


def forward(which, steps, seqs, length, lengths, x, weights):
    wqkv, qb, vb, wo, ob, g1, b1, w1, hb, w2, fb, g2, b2 = weights
    rows = seqs * length
    total = steps * rows
    stack = HEADS * length
    kinds = [
        (WIDTH, bf16), (3 * WIDTH, bf16), (WIDTH, bf16), (WIDTH, f32), (1, f32), (WIDTH, bf16),
        (HIDDEN, f32), (HIDDEN, bf16), (WIDTH, f32), (1, f32),
    ]
    out_shape = [shape((total, c), k) for c, k in kinds]
    out_specs = [rows_of(rows, c) for c, _ in kinds]
    out_shape[1:1] = [shape((PAD, WIDTH), f32)]
    out_specs[1:1] = [whole((PAD, WIDTH))]
    out_shape[3:3] = [shape((steps * seqs * stack, length), f32)]
    out_specs[3:3] = [rows_of(seqs * stack, length)]
    return pl.pallas_call(
        functools.partial(forward_kernel, which, seqs, length),
        out_shape=out_shape,
        grid=(steps,),
        in_specs=[
            smem(), rows_of(rows, WIDTH), part_of(which, (WIDTH, 3 * WIDTH)), pair(WIDTH), pair(WIDTH),
            part_of(which, (WIDTH, WIDTH)), pair(WIDTH), pair(WIDTH), pair(WIDTH),
            part_of(which, (WIDTH, HIDDEN)), pair(HIDDEN), part_of(which, (HIDDEN, WIDTH)),
            pair(WIDTH), pair(WIDTH), pair(WIDTH),
        ],
        out_specs=out_specs,
        scratch_shapes=[
            pltpu.VMEM((rows, HIDDEN), f32),
            pltpu.VMEM((stack, length), f32),
            pltpu.VMEM((stack, length), bf16),
        ],
        compiler_params=params(),
        cost_estimate=cost(total * 2 * 800000, total * 12000),
        name="forward",
    )(lengths, x, wqkv, qb, vb, wo, ob, g1, b1, w1, hb, w2, fb, g2, b2)


def question_backward(which, seqs, length, lengths, cls_grad, cot, x, saved, weights):
    wqkv, qb, vb, wo, ob, g1, b1, w1, hb, w2, fb, g2, b2 = weights
    _, _, qkv, p, ctx, n1, r1, nb, gp, act, n2, r2 = saved
    rows = seqs * length
    stack = HEADS * length
    return pl.pallas_call(
        functools.partial(question_back_kernel, which, seqs, length),
        out_shape=[shape((rows, WIDTH), bf16), shape((GROUP_ROWS, WIDTH), bf16)],
        grid=(1,),
        in_specs=[
            smem(), whole((PAD, WIDTH)), rows_of(rows, WIDTH), rows_of(rows, WIDTH), rows_of(rows, 3 * WIDTH),
            rows_of(seqs * stack, length), rows_of(rows, WIDTH), rows_of(rows, WIDTH), rows_of(rows, 1),
            rows_of(rows, WIDTH), rows_of(rows, HIDDEN), rows_of(rows, HIDDEN), rows_of(rows, WIDTH), rows_of(rows, 1),
            part_of(which, (WIDTH, 3 * WIDTH)), part_of(which, (WIDTH, WIDTH)), pair(WIDTH),
            part_of(which, (WIDTH, HIDDEN)), part_of(which, (HIDDEN, WIDTH)), pair(WIDTH),
        ],
        out_specs=[rows_of(rows, WIDTH), rows_of(GROUP_ROWS, WIDTH)],
        scratch_shapes=[
            pltpu.VMEM((rows, WIDTH), f32), pltpu.VMEM((rows, WIDTH), bf16), pltpu.VMEM((rows, HIDDEN), bf16),
            pltpu.VMEM((VECTOR_ROWS, WIDTH), f32), pltpu.VMEM((rows, HIDDEN), f32), pltpu.VMEM((rows, WIDTH), f32),
            pltpu.VMEM((rows, WIDTH), bf16), pltpu.VMEM((rows, WIDTH), bf16), pltpu.VMEM((rows, 3 * WIDTH), bf16),
            pltpu.VMEM((stack, length), f32), pltpu.VMEM((stack, length), bf16), pltpu.VMEM((stack, length), bf16),
        ],
        compiler_params=params(),
        cost_estimate=cost(rows * 4 * 800000, rows * 12000),
        name="question_back",
    )(lengths, cls_grad, cot, x, qkv, p, ctx, n1, r1, nb, gp, act, n2, r2, wqkv, wo, g1, w1, w2, g2)


def passage_backward(which, steps, length, lengths, cls_grad, cot, x, saved, weights):
    wqkv, qb, vb, wo, ob, g1, b1, w1, hb, w2, fb, g2, b2 = weights
    _, _, qkv, p, ctx, n1, r1, nb, gp, act, n2, r2 = saved
    rows = length
    total = steps * rows
    stack = HEADS * length
    vec = shape((VECTOR_ROWS, WIDTH), f32)
    vec_spec = whole((VECTOR_ROWS, WIDTH))
    two, gffn, gpre, vec_a = pl.pallas_call(
        functools.partial(ffn_kernel, which, length),
        out_shape=[shape((total, WIDTH), f32), shape((total, WIDTH), bf16), shape((total, HIDDEN), bf16), vec],
        grid=(steps,),
        in_specs=[
            smem(), whole((PAD, WIDTH)), rows_of(rows, WIDTH), rows_of(rows, WIDTH), rows_of(rows, 1),
            rows_of(rows, HIDDEN), part_of(which, (HIDDEN, WIDTH)), pair(WIDTH),
        ],
        out_specs=[rows_of(rows, WIDTH), rows_of(rows, WIDTH), rows_of(rows, HIDDEN), vec_spec],
        scratch_shapes=[pltpu.VMEM((rows, HIDDEN), f32)],
        compiler_params=params(),
        cost_estimate=cost(total * 2 * 600000, total * 8000),
        name="ffn_back",
    )(lengths, cls_grad, cot, n2, r2, gp, w2, g2)
    up, down = pl.pallas_call(
        ffn_weight_kernel,
        out_shape=[shape((HIDDEN, WIDTH), bf16), shape((HIDDEN, WIDTH), bf16)],
        grid=(BLOCKS,),
        in_specs=[
            pl.BlockSpec((total, WIDTH), lambda i: (0, i)), whole((total, WIDTH)), whole((total, WIDTH)),
            pl.BlockSpec((total, WIDTH), lambda i: (0, i)),
        ],
        out_specs=[rows_of(WIDTH, WIDTH), rows_of(WIDTH, WIDTH)],
        compiler_params=params(),
        cost_estimate=cost(total * 2 * 600000, total * 6000),
        name="ffn_weights",
    )(act, gffn, nb, gpre)
    one, dctx, vec_b, proj = pl.pallas_call(
        functools.partial(attn_norm_kernel, which, length),
        out_shape=[shape((total, WIDTH), f32), shape((total, WIDTH), bf16), vec, shape((WIDTH, WIDTH), bf16)],
        grid=(steps,),
        in_specs=[
            rows_of(rows, HIDDEN), part_of(which, (WIDTH, HIDDEN)), rows_of(rows, WIDTH), rows_of(rows, WIDTH),
            rows_of(rows, 1), pair(WIDTH), part_of(which, (WIDTH, WIDTH)), rows_of(rows, WIDTH),
        ],
        out_specs=[rows_of(rows, WIDTH), rows_of(rows, WIDTH), vec_spec, whole((WIDTH, WIDTH))],
        scratch_shapes=[pltpu.VMEM((rows, WIDTH), bf16), pltpu.VMEM((WIDTH, WIDTH), f32)],
        compiler_params=params(),
        cost_estimate=cost(total * 2 * 600000, total * 8000),
        name="attn_norm_back",
    )(gpre, w1, two, n1, r1, g1, wo, ctx)
    gx, vec_c, dqkv = pl.pallas_call(
        functools.partial(attn_core_kernel, length),
        out_shape=[shape((total, WIDTH), bf16), vec, shape((3 * WIDTH, WIDTH), bf16)],
        grid=(steps,),
        in_specs=[
            rows_of(rows, WIDTH), rows_of(rows, 3 * WIDTH), rows_of(stack, length), rows_of(rows, WIDTH),
            part_of(which, (WIDTH, 3 * WIDTH)), rows_of(rows, WIDTH),
        ],
        out_specs=[rows_of(rows, WIDTH), vec_spec, whole((3 * WIDTH, WIDTH))],
        scratch_shapes=[
            pltpu.VMEM((rows, 3 * WIDTH), bf16), pltpu.VMEM((stack, length), f32), pltpu.VMEM((stack, length), bf16),
            pltpu.VMEM((stack, length), bf16), pltpu.VMEM((3 * WIDTH, WIDTH), f32),
        ],
        compiler_params=params(),
        cost_estimate=cost(total * 2 * 1000000, total * 10000),
        name="attn_core_back",
    )(dctx, qkv, p, x, wqkv, one)
    vecs = jnp.pad((vec_a + vec_b + vec_c).astype(bf16), ((0, WIDTH - VECTOR_ROWS), (0, 0)))
    return gx, jnp.concatenate([dqkv, proj, up, down, vecs])


def stages(count):
    masks = []
    bit = 1
    while bit < count:
        masks.append(bit)
        bit = bit * 2
    groups = [masks[:1]]
    rest = masks[1:]
    while rest:
        groups.append(rest[:2])
        rest = rest[2:]
    return [group for group in groups if group]


def partner_send(values, mask, count):
    return lax.ppermute(values, "dp", [(i, i ^ mask) for i in range(count)])


def combos(group):
    return [index * group[0] for index in range(1, 2 ** len(group))]


def reduce_scatter(buffer, count, me):
    for group in stages(count):
        radix = 2 ** len(group)
        digit = (me // group[0]) % radix
        split = buffer.reshape((radix, buffer.shape[0] // radix) + buffer.shape[1:])
        received = []
        for step, mask in enumerate(combos(group), start=1):
            outgoing = lax.dynamic_index_in_dim(split, digit ^ step, 0, keepdims=False)
            received.append(partner_send(outgoing, mask, count))
        total = lax.dynamic_index_in_dim(split, digit, 0, keepdims=False).astype(f32)
        for piece in received:
            total = total + piece.astype(f32)
        buffer = total.astype(bf16)
    return buffer


def gather_back(buffer, count, me):
    for group in reversed(stages(count)):
        radix = 2 ** len(group)
        digit = (me // group[0]) % radix
        joined = jnp.zeros((radix,) + buffer.shape, buffer.dtype)
        pieces = [buffer]
        for mask in combos(group):
            pieces.append(partner_send(buffer, mask, count))
        for step, piece in enumerate(pieces):
            joined = lax.dynamic_update_index_in_dim(joined, piece, digit ^ step, 0)
        buffer = joined.reshape((radix * buffer.shape[0],) + buffer.shape[1:])
    return buffer


def body(questions, passages, cot_questions, cot_passages, len_questions, len_passages, positive, *weights):
    local = questions.shape[0]
    question_length = questions.shape[1]
    passage_length = passages.shape[1]
    count = positive.shape[0] // local
    me = lax.axis_index("dp")
    x_q = questions.reshape(-1, WIDTH)
    x_p = passages.reshape(-1, WIDTH)
    saved_p = forward(1, local, 1, passage_length, len_passages, x_p, weights)
    saved_q = forward(0, 1, local, question_length, len_questions, x_q, weights)
    own_cls = jnp.concatenate([saved_q[1], saved_p[1]]).astype(bf16)
    all_cls = lax.all_to_all(
        jnp.broadcast_to(own_cls[None], (count,) + own_cls.shape), "dp", 0, 0, tiled=True
    )
    slots = positive // local * PAD + positive % local
    slots = jnp.pad(slots.reshape(count, local), ((0, 0), (0, PAD - local)), constant_values=-1)
    own_slots = lax.dynamic_slice_in_dim(slots, me, 1, axis=0).reshape(PAD, 1)
    loss, grad_cls_q, grad_cls_p = pl.pallas_call(
        functools.partial(loss_kernel, local),
        out_shape=[shape((PAD, 128), f32), shape((PAD, WIDTH), f32), shape((PAD, WIDTH), f32)],
        grid=(1,),
        in_specs=[smem(), whole((count, 2 * PAD, WIDTH)), whole((1, count * PAD)), whole((PAD, 1))],
        out_specs=[whole((PAD, 128)), whole((PAD, WIDTH)), whole((PAD, WIDTH))],
        scratch_shapes=[pltpu.VMEM((count * PAD, WIDTH), bf16), pltpu.VMEM((count * PAD, WIDTH), bf16)],
        compiler_params=params(),
        name="loss",
    )(me.reshape(1), all_cls, slots.reshape(1, -1), own_slots)
    loss_rows = loss[:local, 0]
    grad_q, pack_q = question_backward(
        0, local, question_length, len_questions, grad_cls_q, cot_questions.reshape(-1, WIDTH), x_q, saved_q, weights
    )
    sum_q = gather_back(reduce_scatter(pack_q, count, me), count, me)
    grad_p, pack_p = passage_backward(
        1, local, passage_length, len_passages, grad_cls_p, cot_passages.reshape(-1, WIDTH), x_p, saved_p, weights
    )
    sum_p = gather_back(reduce_scatter(pack_p, count, me), count, me)
    d_qkv, d_proj, d_up, d_down, vecs = pl.pallas_call(
        unpack_kernel,
        out_shape=[
            shape((2, WIDTH, 3 * WIDTH), f32), shape((2, WIDTH, WIDTH), f32), shape((2, WIDTH, HIDDEN), f32),
            shape((2, HIDDEN, WIDTH), f32), shape((2, VECTOR_ROWS, WIDTH), f32),
        ],
        grid=(1,),
        in_specs=[whole((GROUP_ROWS, WIDTH)), whole((GROUP_ROWS, WIDTH))],
        out_specs=[
            whole((2, WIDTH, 3 * WIDTH)), whole((2, WIDTH, WIDTH)), whole((2, WIDTH, HIDDEN)),
            whole((2, HIDDEN, WIDTH)), whole((2, VECTOR_ROWS, WIDTH)),
        ],
        compiler_params=params(),
        name="unpack",
    )(sum_q, sum_p)
    return (
        loss_rows, saved_q[0].reshape(questions.shape), saved_p[0].reshape(passages.shape),
        grad_q.reshape(questions.shape), grad_p.reshape(passages.shape),
        d_qkv, vecs[:, QUERY_BIAS], vecs[:, VALUE_BIAS], d_proj, vecs[:, PROJ_BIAS], vecs[:, ATTN_GAIN],
        vecs[:, ATTN_SHIFT], d_up, vecs[:, UP_BIAS : UP_BIAS + BLOCKS].reshape(2, HIDDEN), d_down,
        vecs[:, DOWN_BIAS], vecs[:, FFN_GAIN], vecs[:, FFN_SHIFT],
    )


def solution(mesh):
    split = P("dp", None, None)
    return jax.shard_map(
        body,
        mesh=mesh,
        in_specs=(split, split, split, split, P("dp"), P("dp")) + (P(),) * 14,
        out_specs=(P("dp"), split, split, split, split) + (P(),) * 13,
        check_vma=False,
    )
```

```python
import functools

import jax
import jax.numpy as jnp
from jax import lax
from jax.experimental import pallas as pl
from jax.experimental.pallas import tpu as pltpu
from jax.sharding import PartitionSpec as P

HEAD_DIM = 64
WIDTH = 256
HEADS = WIDTH // HEAD_DIM
HIDDEN = 1024
BLOCKS = HIDDEN // WIDTH
PAD = 8
VECTOR_ROWS = 16
GROUP_ROWS = 13 * WIDTH
SOFT = 128
NORM = 64
GELU = 32
ln_eps = 1e-06
score_scale = 0.125
masked_score = -1e30
f32 = jnp.float32
bf16 = jnp.bfloat16

QUERY_BIAS, VALUE_BIAS, PROJ_BIAS, ATTN_GAIN, ATTN_SHIFT, DOWN_BIAS, FFN_GAIN, FFN_SHIFT = range(8)
UP_BIAS = 8


def dot(a, b):
    return lax.dot_general(a, b, (((1,), (0,)), ((), ())), preferred_element_type=f32)


def dot_nt(a, b):
    return lax.dot_general(a, b, (((1,), (1,)), ((), ())), preferred_element_type=f32)


def dot_tn(a, b):
    return lax.dot_general(a, b, (((0,), (0,)), ((), ())), preferred_element_type=f32)


def row_loop(rows, chunk, step):
    def body(index, carry):
        step(pl.multiple_of(index * chunk, chunk))
        return carry

    lax.fori_loop(0, rows // chunk, body, 0, unroll=rows // chunk)


def vector(ref, which):
    return ref[...].astype(f32)[which : which + 1]


def lane_head(rows):
    return lax.broadcasted_iota(jnp.int32, (rows, WIDTH), 1) // HEAD_DIM


def stack_heads(values):
    head = lane_head(values.shape[0])
    wide = values.astype(f32)
    return jnp.concatenate(
        [jnp.where(head == h, wide, 0.0).astype(bf16) for h in range(HEADS)], axis=0
    )


def pick_heads(stacked, rows):
    head = lane_head(rows)
    result = stacked[:rows]
    for h in range(1, HEADS):
        result = jnp.where(head == h, stacked[h * rows : (h + 1) * rows], result)
    return result


def forward_kernel(
    which, seqs, length,
    len_ref, x_ref, wqkv_ref, qb_ref, vb_ref, wo_ref, ob_ref, g1_ref, b1_ref,
    w1_ref, hb_ref, w2_ref, fb_ref, g2_ref, b2_ref,
    out_ref, cls_ref, qkv_ref, p_ref, ctx_ref, n1_ref, r1_ref, nb_ref, gp_ref, act_ref, n2_ref, r2_ref,
    wide_ref, score_ref, prob_ref,
):
    rows = seqs * length
    step = pl.program_id(0)
    x = x_ref[...]
    qkv_ref[:, :WIDTH] = (dot(x, wqkv_ref[:, :WIDTH]) + vector(qb_ref, which)).astype(bf16)
    qkv_ref[:, WIDTH : 2 * WIDTH] = dot(x, wqkv_ref[:, WIDTH : 2 * WIDTH]).astype(bf16)
    qkv_ref[:, 2 * WIDTH :] = (dot(x, wqkv_ref[:, 2 * WIDTH :]) + vector(vb_ref, which)).astype(bf16)
    stack_rows = HEADS * length
    for s in range(seqs):
        span = slice(s * length, (s + 1) * length)
        size = len_ref[step * seqs + s]
        queries = stack_heads(qkv_ref[span, :WIDTH])
        score_ref[...] = dot_nt(queries, qkv_ref[span, WIDTH : 2 * WIDTH])

        def softmax(row):
            part = score_ref[pl.ds(row, SOFT), :] * score_scale
            key = lax.broadcasted_iota(jnp.int32, part.shape, 1)
            part = jnp.where(key < size, part, masked_score)
            part = jnp.exp(part - jnp.max(part, axis=1, keepdims=True))
            prob = part * (1.0 / jnp.sum(part, axis=1, keepdims=True))
            p_ref[pl.ds(s * stack_rows + row, SOFT), :] = prob
            prob_ref[pl.ds(row, SOFT), :] = prob.astype(bf16)

        row_loop(stack_rows, SOFT, softmax)
        context = dot(prob_ref[...], qkv_ref[span, 2 * WIDTH :])
        ctx_ref[span, :] = pick_heads(context, length).astype(bf16)
    n2_ref[...] = dot(ctx_ref[...], wo_ref[...])
    ob, g1, b1 = vector(ob_ref, which), vector(g1_ref, which), vector(b1_ref, which)

    def first_norm(row):
        here = pl.ds(row, NORM)
        value = x_ref[here, :].astype(f32) + (n2_ref[here, :] + ob)
        centered = value - jnp.mean(value, axis=1, keepdims=True)
        inverse = lax.rsqrt(jnp.mean(centered * centered, axis=1, keepdims=True) + ln_eps)
        unit = centered * inverse
        n1_ref[here, :] = unit
        r1_ref[here, :] = inverse
        nb_ref[here, :] = (unit * g1 + b1).astype(bf16)

    row_loop(rows, NORM, first_norm)
    wide_ref[...] = dot(nb_ref[...], w1_ref[...])
    hb = vector(hb_ref, which)

    def gelu(row):
        here = pl.ds(row, GELU)
        for j in range(BLOCKS):
            lanes = slice(j * WIDTH, (j + 1) * WIDTH)
            value = wide_ref[here, lanes] + hb[:, lanes]
            cumulative = 0.5 + 0.5 * lax.erf(value * 0.7071067811865476)
            density = jnp.exp(value * value * -0.5) * 0.3989422804014327
            act_ref[here, lanes] = (value * cumulative).astype(bf16)
            gp_ref[here, lanes] = cumulative + value * density

    row_loop(rows, GELU, gelu)
    n2_ref[...] = dot(act_ref[...], w2_ref[...])
    fb, g2, b2 = vector(fb_ref, which), vector(g2_ref, which), vector(b2_ref, which)

    for s in range(seqs):
        size = len_ref[step * seqs + s]

        def second_norm(row):
            here = pl.ds(s * length + row, NORM)
            value = (n1_ref[here, :] * g1 + b1) + (n2_ref[here, :] + fb)
            centered = value - jnp.mean(value, axis=1, keepdims=True)
            inverse = lax.rsqrt(jnp.mean(centered * centered, axis=1, keepdims=True) + ln_eps)
            unit = centered * inverse
            n2_ref[here, :] = unit
            r2_ref[here, :] = inverse
            position = row + lax.broadcasted_iota(jnp.int32, (NORM, WIDTH), 0)
            out_ref[here, :] = jnp.where(position < size, unit * g2 + b2, 0.0).astype(bf16)

        row_loop(length, NORM, second_norm)
        cls_ref[pl.ds(step * seqs + s, 1), :] = out_ref[s * length : s * length + 16, :].astype(f32)[:1]


def add_row(vec_ref, row, values):
    vec_ref[row : row + 1, :] = vec_ref[row : row + 1, :] + jnp.sum(values, axis=0, keepdims=True)


def ffn_phase(which, seqs, length, first, len_ref, cls_ref, cot_ref, n2_ref, r2_ref, gp_ref, w2_ref, g2_ref, two_ref, gffn_ref, gpre_ref, vec_ref, wide_ref):
    g2 = vector(g2_ref, which)
    for s in range(seqs):
        size = len_ref[first + s]
        cls_row = cls_ref[pl.ds(first + s, 1), :]

        def norm_back(row):
            here = pl.ds(s * length + row, NORM)
            position = row + lax.broadcasted_iota(jnp.int32, (NORM, WIDTH), 0)
            grad = cot_ref[here, :].astype(f32) + jnp.where(position == 0, cls_row, 0.0)
            grad = jnp.where(position < size, grad, 0.0)
            unit = n2_ref[here, :]
            scaled = grad * g2
            first_mean = jnp.mean(scaled, axis=1, keepdims=True)
            second_mean = jnp.mean(scaled * unit, axis=1, keepdims=True)
            two = r2_ref[here, :] * (scaled - first_mean - unit * second_mean)
            low = two.astype(bf16)
            two_ref[here, :] = two
            gffn_ref[here, :] = low
            add_row(vec_ref, FFN_GAIN, grad * unit)
            add_row(vec_ref, FFN_SHIFT, grad)
            add_row(vec_ref, DOWN_BIAS, low.astype(f32))

        row_loop(length, NORM, norm_back)
    wide_ref[...] = dot_nt(gffn_ref[...], w2_ref[...])

    def gelu_back(row):
        here = pl.ds(row, GELU)
        for j in range(BLOCKS):
            lanes = slice(j * WIDTH, (j + 1) * WIDTH)
            low = (wide_ref[here, lanes] * gp_ref[here, lanes]).astype(bf16)
            gpre_ref[here, lanes] = low
            add_row(vec_ref, UP_BIAS + j, low.astype(f32))

    row_loop(seqs * length, GELU, gelu_back)


def attn_norm_phase(which, rows, gpre_ref, w1_ref, two_ref, n1_ref, r1_ref, g1_ref, wo_ref, one_ref, gatt_ref, dctx_ref, vec_ref):
    one_ref[...] = dot_nt(gpre_ref[...], w1_ref[...])
    g1 = vector(g1_ref, which)

    def norm_back(row):
        here = pl.ds(row, NORM)
        grad = two_ref[here, :] + one_ref[here, :]
        unit = n1_ref[here, :]
        scaled = grad * g1
        first_mean = jnp.mean(scaled, axis=1, keepdims=True)
        second_mean = jnp.mean(scaled * unit, axis=1, keepdims=True)
        one = r1_ref[here, :] * (scaled - first_mean - unit * second_mean)
        low = one.astype(bf16)
        one_ref[here, :] = one
        gatt_ref[here, :] = low
        add_row(vec_ref, ATTN_GAIN, grad * unit)
        add_row(vec_ref, ATTN_SHIFT, grad)
        add_row(vec_ref, PROJ_BIAS, low.astype(f32))

    row_loop(rows, NORM, norm_back)
    dctx_ref[...] = dot_nt(gatt_ref[...], wo_ref[...]).astype(bf16)


def attn_core_phase(seqs, length, dctx_ref, qkv_ref, p_ref, gqkv_ref, vec_ref, dp_ref, ds_ref, pb_ref):
    stack_rows = HEADS * length
    for s in range(seqs):
        span = slice(s * length, (s + 1) * length)
        context = stack_heads(dctx_ref[span, :])
        dp_ref[...] = dot_nt(context, qkv_ref[span, 2 * WIDTH :])

        def softmax_back(row):
            prob = p_ref[pl.ds(s * stack_rows + row, SOFT), :]
            grad = dp_ref[pl.ds(row, SOFT), :]
            inner = jnp.sum(prob * grad, axis=1, keepdims=True)
            ds_ref[pl.ds(row, SOFT), :] = (prob * (grad - inner)).astype(bf16)
            pb_ref[pl.ds(row, SOFT), :] = prob.astype(bf16)

        row_loop(stack_rows, SOFT, softmax_back)
        queries = stack_heads(qkv_ref[span, :WIDTH])
        grad_q = (pick_heads(dot(ds_ref[...], qkv_ref[span, WIDTH : 2 * WIDTH]), length) * score_scale).astype(bf16)
        gqkv_ref[span, :WIDTH] = grad_q
        add_row(vec_ref, QUERY_BIAS, grad_q.astype(f32))
        gqkv_ref[span, WIDTH : 2 * WIDTH] = (dot_tn(ds_ref[...], queries) * score_scale).astype(bf16)
        grad_v = dot_tn(pb_ref[...], context).astype(bf16)
        gqkv_ref[span, 2 * WIDTH :] = grad_v
        add_row(vec_ref, VALUE_BIAS, grad_v.astype(f32))


def first_step(vec_ref):
    @pl.when(pl.program_id(0) == 0)
    def _():
        vec_ref[...] = jnp.zeros_like(vec_ref)


def ffn_kernel(which, length, len_ref, cls_ref, cot_ref, n2_ref, r2_ref, gp_ref, w2_ref, g2_ref, two_ref, gffn_ref, gpre_ref, vec_ref, wide_ref):
    first_step(vec_ref)
    ffn_phase(which, 1, length, pl.program_id(0), len_ref, cls_ref, cot_ref, n2_ref, r2_ref, gp_ref, w2_ref, g2_ref, two_ref, gffn_ref, gpre_ref, vec_ref, wide_ref)


def pack_kernel(act_ref, gffn_ref, nb_ref, gpre_ref, dqkv_ref, proj_ref, va_ref, vb_ref, vc_ref, pack_ref):
    j = pl.program_id(0)
    up_rows = pl.ds(pl.multiple_of((4 + j) * WIDTH, WIDTH), WIDTH)
    down_rows = pl.ds(pl.multiple_of((8 + j) * WIDTH, WIDTH), WIDTH)
    pack_ref[down_rows, :] = dot_tn(act_ref[...], gffn_ref[...]).astype(bf16)
    pack_ref[up_rows, :] = dot_tn(nb_ref[...], gpre_ref[...]).astype(bf16)

    @pl.when(j == 0)
    def _():
        pack_ref[: 3 * WIDTH, :] = dqkv_ref[...]
        pack_ref[3 * WIDTH : 4 * WIDTH, :] = proj_ref[...]
        pack_ref[12 * WIDTH :, :] = jnp.zeros((WIDTH, WIDTH), bf16)
        pack_ref[12 * WIDTH : 12 * WIDTH + VECTOR_ROWS, :] = (va_ref[...] + vb_ref[...] + vc_ref[...]).astype(bf16)


def attn_norm_kernel(which, length, gpre_ref, w1_ref, two_ref, n1_ref, r1_ref, g1_ref, wo_ref, ctx_ref, one_ref, dctx_ref, vec_ref, proj_ref, gatt_ref, acc_ref):
    first_step(vec_ref)
    first_step(acc_ref)
    attn_norm_phase(which, length, gpre_ref, w1_ref, two_ref, n1_ref, r1_ref, g1_ref, wo_ref, one_ref, gatt_ref, dctx_ref, vec_ref)
    acc_ref[...] += dot_tn(ctx_ref[...], gatt_ref[...])

    @pl.when(pl.program_id(0) == pl.num_programs(0) - 1)
    def _():
        proj_ref[...] = acc_ref[...].astype(bf16)


def attn_core_kernel(length, dctx_ref, qkv_ref, p_ref, x_ref, wqkv_ref, one_ref, gx_ref, vec_ref, dw_ref, gqkv_ref, dp_ref, ds_ref, pb_ref, acc_ref):
    first_step(vec_ref)
    first_step(acc_ref)
    attn_core_phase(1, length, dctx_ref, qkv_ref, p_ref, gqkv_ref, vec_ref, dp_ref, ds_ref, pb_ref)
    gx_ref[...] = (one_ref[...] + dot_nt(gqkv_ref[...], wqkv_ref[...])).astype(bf16)
    for j in range(3):
        acc_ref[j * WIDTH : (j + 1) * WIDTH, :] += dot_tn(x_ref[...], gqkv_ref[:, j * WIDTH : (j + 1) * WIDTH])

    @pl.when(pl.program_id(0) == pl.num_programs(0) - 1)
    def _():
        dw_ref[...] = acc_ref[...].astype(bf16)


def question_back_kernel(
    which, seqs, length,
    len_ref, cls_ref, cot_ref, x_ref, qkv_ref, p_ref, ctx_ref, n1_ref, r1_ref, nb_ref, gp_ref, act_ref, n2_ref, r2_ref,
    wqkv_ref, wo_ref, g1_ref, w1_ref, w2_ref, g2_ref,
    gx_ref, pack_ref,
    two_ref, gffn_ref, gpre_ref, vec_ref, wide_ref, one_ref, gatt_ref, dctx_ref, gqkv_ref, dp_ref, ds_ref, pb_ref,
):
    rows = seqs * length
    vec_ref[...] = jnp.zeros_like(vec_ref)
    ffn_phase(which, seqs, length, 0, len_ref, cls_ref, cot_ref, n2_ref, r2_ref, gp_ref, w2_ref, g2_ref, two_ref, gffn_ref, gpre_ref, vec_ref, wide_ref)
    for j in range(BLOCKS):
        lanes = slice(j * WIDTH, (j + 1) * WIDTH)
        pack_ref[(4 + j) * WIDTH : (5 + j) * WIDTH, :] = dot_tn(nb_ref[...], gpre_ref[:, lanes]).astype(bf16)
        pack_ref[(8 + j) * WIDTH : (9 + j) * WIDTH, :] = dot_tn(act_ref[:, lanes], gffn_ref[...]).astype(bf16)
    attn_norm_phase(which, rows, gpre_ref, w1_ref, two_ref, n1_ref, r1_ref, g1_ref, wo_ref, one_ref, gatt_ref, dctx_ref, vec_ref)
    pack_ref[3 * WIDTH : 4 * WIDTH, :] = dot_tn(ctx_ref[...], gatt_ref[...]).astype(bf16)
    attn_core_phase(seqs, length, dctx_ref, qkv_ref, p_ref, gqkv_ref, vec_ref, dp_ref, ds_ref, pb_ref)
    for j in range(3):
        lanes = slice(j * WIDTH, (j + 1) * WIDTH)
        pack_ref[j * WIDTH : (j + 1) * WIDTH, :] = dot_tn(x_ref[...], gqkv_ref[:, lanes]).astype(bf16)
    gx_ref[...] = (one_ref[...] + dot_nt(gqkv_ref[...], wqkv_ref[...])).astype(bf16)
    pack_ref[12 * WIDTH :, :] = jnp.zeros((WIDTH, WIDTH), bf16)
    pack_ref[12 * WIDTH : 12 * WIDTH + VECTOR_ROWS, :] = vec_ref[...].astype(bf16)


def loss_kernel(local, me_ref, all_ref, hot_ref, own_hot_ref, loss_ref, gq_ref, gp_ref, q_ref, p_ref):
    count = all_ref.shape[0]
    me = me_ref[0]
    wide = all_ref[...].astype(f32)
    q_ref[...] = wide[:, :PAD].reshape(count * PAD, WIDTH).astype(bf16)
    p_ref[...] = wide[:, PAD:].reshape(count * PAD, WIDTH).astype(bf16)
    own_q = all_ref[me][:PAD]
    own_p = all_ref[me][PAD:]
    logits = dot_nt(own_q, p_ref[...]) * score_scale
    column = lax.broadcasted_iota(jnp.int32, logits.shape, 1)
    logits = jnp.where(column % PAD < local, logits, masked_score)
    top = jnp.max(logits, axis=1, keepdims=True)
    total = top + jnp.log(jnp.sum(jnp.exp(logits - top), axis=1, keepdims=True))
    hot = (column == own_hot_ref[...]).astype(f32)
    loss_ref[...] = jnp.broadcast_to(total - jnp.sum(logits * hot, axis=1, keepdims=True), loss_ref.shape)
    grad = (jnp.exp(logits - total) - hot).astype(bf16)
    gq_ref[...] = dot(grad, p_ref[...]) * score_scale
    gp_ref[...] = jnp.zeros_like(gp_ref)
    block = 256 if count * PAD % 256 == 0 else count * PAD

    def part(index, carry):
        start = pl.multiple_of(index * block, block)
        queries = q_ref[pl.ds(start, block), :]
        scores = dot_nt(p_ref[...], queries) * score_scale
        row = lax.broadcasted_iota(jnp.int32, scores.shape, 0)
        scores = jnp.where(row % PAD < local, scores, masked_score)
        peak = jnp.max(scores, axis=0, keepdims=True)
        sums = peak + jnp.log(jnp.sum(jnp.exp(scores - peak), axis=0, keepdims=True))
        own = dot_nt(own_p, queries) * score_scale
        own_row = lax.broadcasted_iota(jnp.int32, own.shape, 0)
        own_lane = lax.broadcasted_iota(jnp.int32, own.shape, 1)
        own_hits = (own_row + me * PAD == hot_ref[:, pl.ds(start, block)]).astype(f32)
        own_grad = jnp.where(own_lane % PAD < local, jnp.exp(own - sums) - own_hits, 0.0)
        gp_ref[...] += dot(own_grad.astype(bf16), queries) * score_scale
        return carry

    lax.fori_loop(0, count * PAD // block, part, 0)


VECTOR_OUTS = (QUERY_BIAS, VALUE_BIAS, PROJ_BIAS, ATTN_GAIN, ATTN_SHIFT, DOWN_BIAS, FFN_GAIN, FFN_SHIFT)


def unpack_kernel(q_ref, p_ref, qkv_ref, proj_ref, up_ref, down_ref, up_bias_ref, *vector_refs):
    tails = []
    for which, ref in enumerate((q_ref, p_ref)):
        for j in range(3):
            qkv_ref[which, :, j * WIDTH : (j + 1) * WIDTH] = ref[j * WIDTH : (j + 1) * WIDTH, :].astype(f32)
        proj_ref[which] = ref[3 * WIDTH : 4 * WIDTH, :].astype(f32)
        for j in range(BLOCKS):
            up_ref[which, :, j * WIDTH : (j + 1) * WIDTH] = ref[(4 + j) * WIDTH : (5 + j) * WIDTH, :].astype(f32)
        down_ref[which] = ref[8 * WIDTH : 12 * WIDTH, :].astype(f32)
        tails.append(ref[12 * WIDTH : 12 * WIDTH + VECTOR_ROWS, :].astype(f32))
    for row, ref in zip(VECTOR_OUTS, vector_refs):
        for which in range(2):
            ref[which : which + 1, :] = tails[which][row : row + 1]
    for j in range(BLOCKS):
        for which in range(2):
            up_bias_ref[which : which + 1, j * WIDTH : (j + 1) * WIDTH] = tails[which][UP_BIAS + j : UP_BIAS + j + 1]


def smem():
    return pl.BlockSpec(memory_space=pltpu.SMEM)


def whole(shape):
    return pl.BlockSpec(shape, lambda i: (0,) * len(shape))


def rows_of(rows, columns):
    return pl.BlockSpec((rows, columns), lambda i: (i, 0))


def part_of(which, shape):
    return pl.BlockSpec((None,) + shape, lambda i: (which, 0, 0))


def params():
    return pltpu.CompilerParams(vmem_limit_bytes=24 * 1024 * 1024)


def shape(dims, kind):
    return jax.ShapeDtypeStruct(dims, kind)


def cost(flops, moved):
    return pl.CostEstimate(flops=flops, bytes_accessed=moved, transcendentals=0)


def pair(columns):
    return whole((2, columns))


def forward(which, steps, seqs, length, lengths, x, weights):
    wqkv, qb, vb, wo, ob, g1, b1, w1, hb, w2, fb, g2, b2 = weights
    rows = seqs * length
    total = steps * rows
    stack = HEADS * length
    kinds = [
        (WIDTH, bf16), (3 * WIDTH, bf16), (WIDTH, bf16), (WIDTH, f32), (1, f32), (WIDTH, bf16),
        (HIDDEN, f32), (HIDDEN, bf16), (WIDTH, f32), (1, f32),
    ]
    out_shape = [shape((total, c), k) for c, k in kinds]
    out_specs = [rows_of(rows, c) for c, _ in kinds]
    out_shape[1:1] = [shape((PAD, WIDTH), f32)]
    out_specs[1:1] = [whole((PAD, WIDTH))]
    out_shape[3:3] = [shape((steps * seqs * stack, length), f32)]
    out_specs[3:3] = [rows_of(seqs * stack, length)]
    return pl.pallas_call(
        functools.partial(forward_kernel, which, seqs, length),
        out_shape=out_shape,
        grid=(steps,),
        in_specs=[
            smem(), rows_of(rows, WIDTH), part_of(which, (WIDTH, 3 * WIDTH)), pair(WIDTH), pair(WIDTH),
            part_of(which, (WIDTH, WIDTH)), pair(WIDTH), pair(WIDTH), pair(WIDTH),
            part_of(which, (WIDTH, HIDDEN)), pair(HIDDEN), part_of(which, (HIDDEN, WIDTH)),
            pair(WIDTH), pair(WIDTH), pair(WIDTH),
        ],
        out_specs=out_specs,
        scratch_shapes=[
            pltpu.VMEM((rows, HIDDEN), f32),
            pltpu.VMEM((stack, length), f32),
            pltpu.VMEM((stack, length), bf16),
        ],
        compiler_params=params(),
        cost_estimate=cost(total * 2 * 800000, total * 12000),
        name="forward",
    )(lengths, x, wqkv, qb, vb, wo, ob, g1, b1, w1, hb, w2, fb, g2, b2)


def question_backward(which, seqs, length, lengths, cls_grad, cot, x, saved, weights):
    wqkv, qb, vb, wo, ob, g1, b1, w1, hb, w2, fb, g2, b2 = weights
    _, _, qkv, p, ctx, n1, r1, nb, gp, act, n2, r2 = saved
    rows = seqs * length
    stack = HEADS * length
    return pl.pallas_call(
        functools.partial(question_back_kernel, which, seqs, length),
        out_shape=[shape((rows, WIDTH), bf16), shape((GROUP_ROWS, WIDTH), bf16)],
        grid=(1,),
        in_specs=[
            smem(), whole((PAD, WIDTH)), rows_of(rows, WIDTH), rows_of(rows, WIDTH), rows_of(rows, 3 * WIDTH),
            rows_of(seqs * stack, length), rows_of(rows, WIDTH), rows_of(rows, WIDTH), rows_of(rows, 1),
            rows_of(rows, WIDTH), rows_of(rows, HIDDEN), rows_of(rows, HIDDEN), rows_of(rows, WIDTH), rows_of(rows, 1),
            part_of(which, (WIDTH, 3 * WIDTH)), part_of(which, (WIDTH, WIDTH)), pair(WIDTH),
            part_of(which, (WIDTH, HIDDEN)), part_of(which, (HIDDEN, WIDTH)), pair(WIDTH),
        ],
        out_specs=[rows_of(rows, WIDTH), rows_of(GROUP_ROWS, WIDTH)],
        scratch_shapes=[
            pltpu.VMEM((rows, WIDTH), f32), pltpu.VMEM((rows, WIDTH), bf16), pltpu.VMEM((rows, HIDDEN), bf16),
            pltpu.VMEM((VECTOR_ROWS, WIDTH), f32), pltpu.VMEM((rows, HIDDEN), f32), pltpu.VMEM((rows, WIDTH), f32),
            pltpu.VMEM((rows, WIDTH), bf16), pltpu.VMEM((rows, WIDTH), bf16), pltpu.VMEM((rows, 3 * WIDTH), bf16),
            pltpu.VMEM((stack, length), f32), pltpu.VMEM((stack, length), bf16), pltpu.VMEM((stack, length), bf16),
        ],
        compiler_params=params(),
        cost_estimate=cost(rows * 4 * 800000, rows * 12000),
        name="question_back",
    )(lengths, cls_grad, cot, x, qkv, p, ctx, n1, r1, nb, gp, act, n2, r2, wqkv, wo, g1, w1, w2, g2)


def passage_backward(which, steps, length, lengths, cls_grad, cot, x, saved, weights):
    wqkv, qb, vb, wo, ob, g1, b1, w1, hb, w2, fb, g2, b2 = weights
    _, _, qkv, p, ctx, n1, r1, nb, gp, act, n2, r2 = saved
    rows = length
    total = steps * rows
    stack = HEADS * length
    vec = shape((VECTOR_ROWS, WIDTH), f32)
    vec_spec = whole((VECTOR_ROWS, WIDTH))
    two, gffn, gpre, vec_a = pl.pallas_call(
        functools.partial(ffn_kernel, which, length),
        out_shape=[shape((total, WIDTH), f32), shape((total, WIDTH), bf16), shape((total, HIDDEN), bf16), vec],
        grid=(steps,),
        in_specs=[
            smem(), whole((PAD, WIDTH)), rows_of(rows, WIDTH), rows_of(rows, WIDTH), rows_of(rows, 1),
            rows_of(rows, HIDDEN), part_of(which, (HIDDEN, WIDTH)), pair(WIDTH),
        ],
        out_specs=[rows_of(rows, WIDTH), rows_of(rows, WIDTH), rows_of(rows, HIDDEN), vec_spec],
        scratch_shapes=[pltpu.VMEM((rows, HIDDEN), f32)],
        compiler_params=params(),
        cost_estimate=cost(total * 2 * 600000, total * 8000),
        name="ffn_back",
    )(lengths, cls_grad, cot, n2, r2, gp, w2, g2)
    one, dctx, vec_b, proj = pl.pallas_call(
        functools.partial(attn_norm_kernel, which, length),
        out_shape=[shape((total, WIDTH), f32), shape((total, WIDTH), bf16), vec, shape((WIDTH, WIDTH), bf16)],
        grid=(steps,),
        in_specs=[
            rows_of(rows, HIDDEN), part_of(which, (WIDTH, HIDDEN)), rows_of(rows, WIDTH), rows_of(rows, WIDTH),
            rows_of(rows, 1), pair(WIDTH), part_of(which, (WIDTH, WIDTH)), rows_of(rows, WIDTH),
        ],
        out_specs=[rows_of(rows, WIDTH), rows_of(rows, WIDTH), vec_spec, whole((WIDTH, WIDTH))],
        scratch_shapes=[pltpu.VMEM((rows, WIDTH), bf16), pltpu.VMEM((WIDTH, WIDTH), f32)],
        compiler_params=params(),
        cost_estimate=cost(total * 2 * 600000, total * 8000),
        name="attn_norm_back",
    )(gpre, w1, two, n1, r1, g1, wo, ctx)
    gx, vec_c, dqkv = pl.pallas_call(
        functools.partial(attn_core_kernel, length),
        out_shape=[shape((total, WIDTH), bf16), vec, shape((3 * WIDTH, WIDTH), bf16)],
        grid=(steps,),
        in_specs=[
            rows_of(rows, WIDTH), rows_of(rows, 3 * WIDTH), rows_of(stack, length), rows_of(rows, WIDTH),
            part_of(which, (WIDTH, 3 * WIDTH)), rows_of(rows, WIDTH),
        ],
        out_specs=[rows_of(rows, WIDTH), vec_spec, whole((3 * WIDTH, WIDTH))],
        scratch_shapes=[
            pltpu.VMEM((rows, 3 * WIDTH), bf16), pltpu.VMEM((stack, length), f32), pltpu.VMEM((stack, length), bf16),
            pltpu.VMEM((stack, length), bf16), pltpu.VMEM((3 * WIDTH, WIDTH), f32),
        ],
        compiler_params=params(),
        cost_estimate=cost(total * 2 * 1000000, total * 10000),
        name="attn_core_back",
    )(dctx, qkv, p, x, wqkv, one)
    pack = pl.pallas_call(
        pack_kernel,
        out_shape=shape((GROUP_ROWS, WIDTH), bf16),
        grid=(BLOCKS,),
        in_specs=[
            pl.BlockSpec((total, WIDTH), lambda i: (0, i)), whole((total, WIDTH)), whole((total, WIDTH)),
            pl.BlockSpec((total, WIDTH), lambda i: (0, i)), whole((3 * WIDTH, WIDTH)), whole((WIDTH, WIDTH)),
            vec_spec, vec_spec, vec_spec,
        ],
        out_specs=whole((GROUP_ROWS, WIDTH)),
        compiler_params=params(),
        cost_estimate=cost(total * 2 * 600000, total * 6000),
        name="ffn_weights",
    )(act, gffn, nb, gpre, dqkv, proj, vec_a, vec_b, vec_c)
    return gx, pack


def stages(count):
    masks = []
    bit = 1
    while bit < count:
        masks.append(bit)
        bit = bit * 2
    groups = [masks[:1]]
    rest = masks[1:]
    while rest:
        groups.append(rest[:2])
        rest = rest[2:]
    return [group for group in groups if group]


def partner_send(values, mask, count):
    return lax.ppermute(values, "dp", [(i, i ^ mask) for i in range(count)])


def combos(group):
    return [index * group[0] for index in range(1, 2 ** len(group))]


def reduce_scatter(buffer, count, me):
    for group in stages(count):
        radix = 2 ** len(group)
        digit = (me // group[0]) % radix
        split = buffer.reshape((radix, buffer.shape[0] // radix) + buffer.shape[1:])
        received = []
        for step, mask in enumerate(combos(group), start=1):
            outgoing = lax.dynamic_index_in_dim(split, digit ^ step, 0, keepdims=False)
            received.append(partner_send(outgoing, mask, count))
        total = lax.dynamic_index_in_dim(split, digit, 0, keepdims=False).astype(f32)
        for piece in received:
            total = total + piece.astype(f32)
        buffer = total.astype(bf16)
    return buffer


def gather_back(buffer, count, me):
    for group in reversed(stages(count)):
        radix = 2 ** len(group)
        digit = (me // group[0]) % radix
        joined = jnp.zeros((radix,) + buffer.shape, buffer.dtype)
        pieces = [buffer]
        for mask in combos(group):
            pieces.append(partner_send(buffer, mask, count))
        for step, piece in enumerate(pieces):
            joined = lax.dynamic_update_index_in_dim(joined, piece, digit ^ step, 0)
        buffer = joined.reshape((radix * buffer.shape[0],) + buffer.shape[1:])
    return buffer


def body(questions, passages, cot_questions, cot_passages, len_questions, len_passages, positive, *weights):
    local = questions.shape[0]
    question_length = questions.shape[1]
    passage_length = passages.shape[1]
    count = positive.shape[0] // local
    me = lax.axis_index("dp")
    x_q = questions.reshape(-1, WIDTH)
    x_p = passages.reshape(-1, WIDTH)
    saved_p = forward(1, local, 1, passage_length, len_passages, x_p, weights)
    saved_q = forward(0, 1, local, question_length, len_questions, x_q, weights)
    own_cls = jnp.concatenate([saved_q[1], saved_p[1]]).astype(bf16)
    all_cls = lax.all_to_all(
        jnp.broadcast_to(own_cls[None], (count,) + own_cls.shape), "dp", 0, 0, tiled=True
    )
    slots = positive // local * PAD + positive % local
    slots = jnp.pad(slots.reshape(count, local), ((0, 0), (0, PAD - local)), constant_values=-1)
    own_slots = lax.dynamic_slice_in_dim(slots, me, 1, axis=0).reshape(PAD, 1)
    loss, grad_cls_q, grad_cls_p = pl.pallas_call(
        functools.partial(loss_kernel, local),
        out_shape=[shape((PAD, 128), f32), shape((PAD, WIDTH), f32), shape((PAD, WIDTH), f32)],
        grid=(1,),
        in_specs=[smem(), whole((count, 2 * PAD, WIDTH)), whole((1, count * PAD)), whole((PAD, 1))],
        out_specs=[whole((PAD, 128)), whole((PAD, WIDTH)), whole((PAD, WIDTH))],
        scratch_shapes=[pltpu.VMEM((count * PAD, WIDTH), bf16), pltpu.VMEM((count * PAD, WIDTH), bf16)],
        compiler_params=params(),
        name="loss",
    )(me.reshape(1), all_cls, slots.reshape(1, -1), own_slots)
    loss_rows = loss[:local, 0]
    grad_q, pack_q = question_backward(
        0, local, question_length, len_questions, grad_cls_q, cot_questions.reshape(-1, WIDTH), x_q, saved_q, weights
    )
    sum_q = gather_back(reduce_scatter(pack_q, count, me), count, me)
    grad_p, pack_p = passage_backward(
        1, local, passage_length, len_passages, grad_cls_p, cot_passages.reshape(-1, WIDTH), x_p, saved_p, weights
    )
    sum_p = gather_back(reduce_scatter(pack_p, count, me), count, me)
    dims = [(2, WIDTH, 3 * WIDTH), (2, WIDTH, WIDTH), (2, WIDTH, HIDDEN), (2, HIDDEN, WIDTH), (2, HIDDEN)]
    dims += [(2, WIDTH)] * len(VECTOR_OUTS)
    d_qkv, d_proj, d_up, d_down, up_bias, query_bias, value_bias, proj_bias, gain_a, shift_a, down_bias, gain_f, shift_f = pl.pallas_call(
        unpack_kernel,
        out_shape=[shape(d, f32) for d in dims],
        grid=(1,),
        in_specs=[whole((GROUP_ROWS, WIDTH)), whole((GROUP_ROWS, WIDTH))],
        out_specs=[whole(d) for d in dims],
        compiler_params=params(),
        name="unpack",
    )(sum_q, sum_p)
    return (
        loss_rows, saved_q[0].reshape(questions.shape), saved_p[0].reshape(passages.shape),
        grad_q.reshape(questions.shape), grad_p.reshape(passages.shape),
        d_qkv, query_bias, value_bias, d_proj, proj_bias, gain_a, shift_a, d_up, up_bias, d_down,
        down_bias, gain_f, shift_f,
    )


def solution(mesh):
    split = P("dp", None, None)
    return jax.shard_map(
        body,
        mesh=mesh,
        in_specs=(split, split, split, split, P("dp"), P("dp")) + (P(),) * 14,
        out_specs=(P("dp"), split, split, split, split) + (P(),) * 13,
        check_vma=False,
    )
```

```python
import functools

import jax
import jax.numpy as jnp
from jax import lax
from jax.experimental import pallas as pl
from jax.experimental.pallas import tpu as pltpu
from jax.sharding import PartitionSpec as P

HEAD_DIM = 64
WIDTH = 256
HEADS = WIDTH // HEAD_DIM
HIDDEN = 1024
BLOCKS = HIDDEN // WIDTH
PAD = 8
VECTOR_ROWS = 16
GROUP_ROWS = 13 * WIDTH
SOFT = 128
NORM = 64
GELU = 32
ln_eps = 1e-06
score_scale = 0.125
masked_score = -1e30
f32 = jnp.float32
bf16 = jnp.bfloat16

QUERY_BIAS, VALUE_BIAS, PROJ_BIAS, ATTN_GAIN, ATTN_SHIFT, DOWN_BIAS, FFN_GAIN, FFN_SHIFT = range(8)
UP_BIAS = 8


def dot(a, b):
    return lax.dot_general(a, b, (((1,), (0,)), ((), ())), preferred_element_type=f32)


def dot_nt(a, b):
    return lax.dot_general(a, b, (((1,), (1,)), ((), ())), preferred_element_type=f32)


def dot_tn(a, b):
    return lax.dot_general(a, b, (((0,), (0,)), ((), ())), preferred_element_type=f32)


def row_loop(rows, chunk, step):
    def body(index, carry):
        step(pl.multiple_of(index * chunk, chunk))
        return carry

    lax.fori_loop(0, rows // chunk, body, 0, unroll=rows // chunk)


def vector(ref, which):
    return ref[...].astype(f32)[which : which + 1]


def lane_head(rows):
    return lax.broadcasted_iota(jnp.int32, (rows, WIDTH), 1) // HEAD_DIM


def stack_heads(values):
    head = lane_head(values.shape[0])
    wide = values.astype(f32)
    return jnp.concatenate(
        [jnp.where(head == h, wide, 0.0).astype(bf16) for h in range(HEADS)], axis=0
    )


def pick_heads(stacked, rows):
    head = lane_head(rows)
    result = stacked[:rows]
    for h in range(1, HEADS):
        result = jnp.where(head == h, stacked[h * rows : (h + 1) * rows], result)
    return result


def forward_kernel(
    which, seqs, length,
    len_ref, x_ref, wqkv_ref, qb_ref, vb_ref, wo_ref, ob_ref, g1_ref, b1_ref,
    w1_ref, hb_ref, w2_ref, fb_ref, g2_ref, b2_ref,
    out_ref, cls_ref, qkv_ref, p_ref, ctx_ref, n1_ref, r1_ref, nb_ref, gp_ref, act_ref, n2_ref, r2_ref,
    wide_ref, score_ref, prob_ref,
):
    rows = seqs * length
    step = pl.program_id(0)
    x = x_ref[...]
    qkv_ref[:, :WIDTH] = (dot(x, wqkv_ref[:, :WIDTH]) + vector(qb_ref, which)).astype(bf16)
    qkv_ref[:, WIDTH : 2 * WIDTH] = dot(x, wqkv_ref[:, WIDTH : 2 * WIDTH]).astype(bf16)
    qkv_ref[:, 2 * WIDTH :] = (dot(x, wqkv_ref[:, 2 * WIDTH :]) + vector(vb_ref, which)).astype(bf16)
    stack_rows = HEADS * length
    for s in range(seqs):
        span = slice(s * length, (s + 1) * length)
        size = len_ref[step * seqs + s]
        queries = stack_heads(qkv_ref[span, :WIDTH])
        score_ref[...] = dot_nt(queries, qkv_ref[span, WIDTH : 2 * WIDTH])

        def softmax(row):
            part = score_ref[pl.ds(row, SOFT), :] * score_scale
            key = lax.broadcasted_iota(jnp.int32, part.shape, 1)
            part = jnp.where(key < size, part, masked_score)
            part = jnp.exp(part - jnp.max(part, axis=1, keepdims=True))
            prob = part * (1.0 / jnp.sum(part, axis=1, keepdims=True))
            p_ref[pl.ds(s * stack_rows + row, SOFT), :] = prob
            prob_ref[pl.ds(row, SOFT), :] = prob.astype(bf16)

        row_loop(stack_rows, SOFT, softmax)
        context = dot(prob_ref[...], qkv_ref[span, 2 * WIDTH :])
        ctx_ref[span, :] = pick_heads(context, length).astype(bf16)
    n2_ref[...] = dot(ctx_ref[...], wo_ref[...])
    ob, g1, b1 = vector(ob_ref, which), vector(g1_ref, which), vector(b1_ref, which)

    def first_norm(row):
        here = pl.ds(row, NORM)
        value = x_ref[here, :].astype(f32) + (n2_ref[here, :] + ob)
        centered = value - jnp.mean(value, axis=1, keepdims=True)
        inverse = lax.rsqrt(jnp.mean(centered * centered, axis=1, keepdims=True) + ln_eps)
        unit = centered * inverse
        n1_ref[here, :] = unit
        r1_ref[here, :] = inverse
        nb_ref[here, :] = (unit * g1 + b1).astype(bf16)

    row_loop(rows, NORM, first_norm)
    wide_ref[...] = dot(nb_ref[...], w1_ref[...])
    hb = vector(hb_ref, which)

    def gelu(row):
        here = pl.ds(row, GELU)
        for j in range(BLOCKS):
            lanes = slice(j * WIDTH, (j + 1) * WIDTH)
            value = wide_ref[here, lanes] + hb[:, lanes]
            cumulative = 0.5 + 0.5 * lax.erf(value * 0.7071067811865476)
            density = jnp.exp(value * value * -0.5) * 0.3989422804014327
            act_ref[here, lanes] = (value * cumulative).astype(bf16)
            gp_ref[here, lanes] = cumulative + value * density

    row_loop(rows, GELU, gelu)
    n2_ref[...] = dot(act_ref[...], w2_ref[...])
    fb, g2, b2 = vector(fb_ref, which), vector(g2_ref, which), vector(b2_ref, which)

    for s in range(seqs):
        size = len_ref[step * seqs + s]

        def second_norm(row):
            here = pl.ds(s * length + row, NORM)
            value = (n1_ref[here, :] * g1 + b1) + (n2_ref[here, :] + fb)
            centered = value - jnp.mean(value, axis=1, keepdims=True)
            inverse = lax.rsqrt(jnp.mean(centered * centered, axis=1, keepdims=True) + ln_eps)
            unit = centered * inverse
            n2_ref[here, :] = unit
            r2_ref[here, :] = inverse
            position = row + lax.broadcasted_iota(jnp.int32, (NORM, WIDTH), 0)
            out_ref[here, :] = jnp.where(position < size, unit * g2 + b2, 0.0).astype(bf16)

        row_loop(length, NORM, second_norm)
        cls_ref[pl.ds(step * seqs + s, 1), :] = out_ref[s * length : s * length + 16, :].astype(f32)[:1]


def add_row(vec_ref, row, values):
    vec_ref[row : row + 1, :] = vec_ref[row : row + 1, :] + jnp.sum(values, axis=0, keepdims=True)


def ffn_phase(which, seqs, length, first, len_ref, cls_ref, cot_ref, n2_ref, r2_ref, gp_ref, w2_ref, g2_ref, two_ref, gffn_ref, gpre_ref, vec_ref, wide_ref):
    g2 = vector(g2_ref, which)
    for s in range(seqs):
        size = len_ref[first + s]
        cls_row = cls_ref[pl.ds(first + s, 1), :]

        def norm_back(row):
            here = pl.ds(s * length + row, NORM)
            position = row + lax.broadcasted_iota(jnp.int32, (NORM, WIDTH), 0)
            grad = cot_ref[here, :].astype(f32) + jnp.where(position == 0, cls_row, 0.0)
            grad = jnp.where(position < size, grad, 0.0)
            unit = n2_ref[here, :]
            scaled = grad * g2
            first_mean = jnp.mean(scaled, axis=1, keepdims=True)
            second_mean = jnp.mean(scaled * unit, axis=1, keepdims=True)
            two = r2_ref[here, :] * (scaled - first_mean - unit * second_mean)
            low = two.astype(bf16)
            two_ref[here, :] = two
            gffn_ref[here, :] = low
            add_row(vec_ref, FFN_GAIN, grad * unit)
            add_row(vec_ref, FFN_SHIFT, grad)
            add_row(vec_ref, DOWN_BIAS, low.astype(f32))

        row_loop(length, NORM, norm_back)
    wide_ref[...] = dot_nt(gffn_ref[...], w2_ref[...])

    def gelu_back(row):
        here = pl.ds(row, GELU)
        for j in range(BLOCKS):
            lanes = slice(j * WIDTH, (j + 1) * WIDTH)
            low = (wide_ref[here, lanes] * gp_ref[here, lanes]).astype(bf16)
            gpre_ref[here, lanes] = low
            add_row(vec_ref, UP_BIAS + j, low.astype(f32))

    row_loop(seqs * length, GELU, gelu_back)


def attn_norm_phase(which, rows, gpre_ref, w1_ref, two_ref, n1_ref, r1_ref, g1_ref, wo_ref, one_ref, gatt_ref, dctx_ref, vec_ref):
    one_ref[...] = dot_nt(gpre_ref[...], w1_ref[...])
    g1 = vector(g1_ref, which)

    def norm_back(row):
        here = pl.ds(row, NORM)
        grad = two_ref[here, :] + one_ref[here, :]
        unit = n1_ref[here, :]
        scaled = grad * g1
        first_mean = jnp.mean(scaled, axis=1, keepdims=True)
        second_mean = jnp.mean(scaled * unit, axis=1, keepdims=True)
        one = r1_ref[here, :] * (scaled - first_mean - unit * second_mean)
        low = one.astype(bf16)
        one_ref[here, :] = one
        gatt_ref[here, :] = low
        add_row(vec_ref, ATTN_GAIN, grad * unit)
        add_row(vec_ref, ATTN_SHIFT, grad)
        add_row(vec_ref, PROJ_BIAS, low.astype(f32))

    row_loop(rows, NORM, norm_back)
    dctx_ref[...] = dot_nt(gatt_ref[...], wo_ref[...]).astype(bf16)


def attn_core_phase(seqs, length, dctx_ref, qkv_ref, p_ref, gqkv_ref, vec_ref, dp_ref, ds_ref, pb_ref):
    stack_rows = HEADS * length
    for s in range(seqs):
        span = slice(s * length, (s + 1) * length)
        context = stack_heads(dctx_ref[span, :])
        dp_ref[...] = dot_nt(context, qkv_ref[span, 2 * WIDTH :])

        def softmax_back(row):
            prob = p_ref[pl.ds(s * stack_rows + row, SOFT), :]
            grad = dp_ref[pl.ds(row, SOFT), :]
            inner = jnp.sum(prob * grad, axis=1, keepdims=True)
            ds_ref[pl.ds(row, SOFT), :] = (prob * (grad - inner)).astype(bf16)
            pb_ref[pl.ds(row, SOFT), :] = prob.astype(bf16)

        row_loop(stack_rows, SOFT, softmax_back)
        queries = stack_heads(qkv_ref[span, :WIDTH])
        grad_q = (pick_heads(dot(ds_ref[...], qkv_ref[span, WIDTH : 2 * WIDTH]), length) * score_scale).astype(bf16)
        gqkv_ref[span, :WIDTH] = grad_q
        add_row(vec_ref, QUERY_BIAS, grad_q.astype(f32))
        gqkv_ref[span, WIDTH : 2 * WIDTH] = (dot_tn(ds_ref[...], queries) * score_scale).astype(bf16)
        grad_v = dot_tn(pb_ref[...], context).astype(bf16)
        gqkv_ref[span, 2 * WIDTH :] = grad_v
        add_row(vec_ref, VALUE_BIAS, grad_v.astype(f32))


def first_step(vec_ref):
    @pl.when(pl.program_id(0) == 0)
    def _():
        vec_ref[...] = jnp.zeros_like(vec_ref)


def ffn_kernel(which, length, len_ref, cls_ref, cot_ref, n2_ref, r2_ref, gp_ref, w2_ref, g2_ref, two_ref, gffn_ref, gpre_ref, vec_ref, wide_ref):
    first_step(vec_ref)
    ffn_phase(which, 1, length, pl.program_id(0), len_ref, cls_ref, cot_ref, n2_ref, r2_ref, gp_ref, w2_ref, g2_ref, two_ref, gffn_ref, gpre_ref, vec_ref, wide_ref)


def pack_kernel(act_ref, gffn_ref, nb_ref, gpre_ref, dqkv_ref, proj_ref, va_ref, vb_ref, vc_ref, pack_ref):
    j = pl.program_id(0)
    up_rows = pl.ds(pl.multiple_of((4 + j) * WIDTH, WIDTH), WIDTH)
    down_rows = pl.ds(pl.multiple_of((8 + j) * WIDTH, WIDTH), WIDTH)
    pack_ref[down_rows, :] = dot_tn(act_ref[...], gffn_ref[...]).astype(bf16)
    pack_ref[up_rows, :] = dot_tn(nb_ref[...], gpre_ref[...]).astype(bf16)

    @pl.when(j == 0)
    def _():
        pack_ref[: 3 * WIDTH, :] = dqkv_ref[...]
        pack_ref[3 * WIDTH : 4 * WIDTH, :] = proj_ref[...]
        pack_ref[12 * WIDTH :, :] = jnp.zeros((WIDTH, WIDTH), bf16)
        pack_ref[12 * WIDTH : 12 * WIDTH + VECTOR_ROWS, :] = (va_ref[...] + vb_ref[...] + vc_ref[...]).astype(bf16)


def attn_norm_kernel(which, length, gpre_ref, w1_ref, two_ref, n1_ref, r1_ref, g1_ref, wo_ref, ctx_ref, one_ref, dctx_ref, vec_ref, proj_ref, gatt_ref, acc_ref):
    first_step(vec_ref)
    first_step(acc_ref)
    attn_norm_phase(which, length, gpre_ref, w1_ref, two_ref, n1_ref, r1_ref, g1_ref, wo_ref, one_ref, gatt_ref, dctx_ref, vec_ref)
    acc_ref[...] += dot_tn(ctx_ref[...], gatt_ref[...])

    @pl.when(pl.program_id(0) == pl.num_programs(0) - 1)
    def _():
        proj_ref[...] = acc_ref[...].astype(bf16)


def attn_core_kernel(length, dctx_ref, qkv_ref, p_ref, x_ref, wqkv_ref, one_ref, gx_ref, vec_ref, dw_ref, gqkv_ref, dp_ref, ds_ref, pb_ref, acc_ref):
    first_step(vec_ref)
    first_step(acc_ref)
    attn_core_phase(1, length, dctx_ref, qkv_ref, p_ref, gqkv_ref, vec_ref, dp_ref, ds_ref, pb_ref)
    gx_ref[...] = (one_ref[...] + dot_nt(gqkv_ref[...], wqkv_ref[...])).astype(bf16)
    for j in range(3):
        acc_ref[j * WIDTH : (j + 1) * WIDTH, :] += dot_tn(x_ref[...], gqkv_ref[:, j * WIDTH : (j + 1) * WIDTH])

    @pl.when(pl.program_id(0) == pl.num_programs(0) - 1)
    def _():
        dw_ref[...] = acc_ref[...].astype(bf16)


def question_back_kernel(
    which, seqs, length,
    len_ref, cls_ref, cot_ref, x_ref, qkv_ref, p_ref, ctx_ref, n1_ref, r1_ref, nb_ref, gp_ref, act_ref, n2_ref, r2_ref,
    wqkv_ref, wo_ref, g1_ref, w1_ref, w2_ref, g2_ref,
    gx_ref, pack_ref,
    two_ref, gffn_ref, gpre_ref, vec_ref, wide_ref, one_ref, gatt_ref, dctx_ref, gqkv_ref, dp_ref, ds_ref, pb_ref,
):
    rows = seqs * length
    vec_ref[...] = jnp.zeros_like(vec_ref)
    ffn_phase(which, seqs, length, 0, len_ref, cls_ref, cot_ref, n2_ref, r2_ref, gp_ref, w2_ref, g2_ref, two_ref, gffn_ref, gpre_ref, vec_ref, wide_ref)
    for j in range(BLOCKS):
        lanes = slice(j * WIDTH, (j + 1) * WIDTH)
        pack_ref[(4 + j) * WIDTH : (5 + j) * WIDTH, :] = dot_tn(nb_ref[...], gpre_ref[:, lanes]).astype(bf16)
        pack_ref[(8 + j) * WIDTH : (9 + j) * WIDTH, :] = dot_tn(act_ref[:, lanes], gffn_ref[...]).astype(bf16)
    attn_norm_phase(which, rows, gpre_ref, w1_ref, two_ref, n1_ref, r1_ref, g1_ref, wo_ref, one_ref, gatt_ref, dctx_ref, vec_ref)
    pack_ref[3 * WIDTH : 4 * WIDTH, :] = dot_tn(ctx_ref[...], gatt_ref[...]).astype(bf16)
    attn_core_phase(seqs, length, dctx_ref, qkv_ref, p_ref, gqkv_ref, vec_ref, dp_ref, ds_ref, pb_ref)
    for j in range(3):
        lanes = slice(j * WIDTH, (j + 1) * WIDTH)
        pack_ref[j * WIDTH : (j + 1) * WIDTH, :] = dot_tn(x_ref[...], gqkv_ref[:, lanes]).astype(bf16)
    gx_ref[...] = (one_ref[...] + dot_nt(gqkv_ref[...], wqkv_ref[...])).astype(bf16)
    pack_ref[12 * WIDTH :, :] = jnp.zeros((WIDTH, WIDTH), bf16)
    pack_ref[12 * WIDTH : 12 * WIDTH + VECTOR_ROWS, :] = vec_ref[...].astype(bf16)


def loss_kernel(local, me_ref, all_ref, hot_ref, own_hot_ref, loss_ref, gq_ref, gp_ref, q_ref, p_ref):
    count = all_ref.shape[0]
    me = me_ref[0]
    wide = all_ref[...].astype(f32)
    q_ref[...] = wide[:, :PAD].reshape(count * PAD, WIDTH).astype(bf16)
    p_ref[...] = wide[:, PAD:].reshape(count * PAD, WIDTH).astype(bf16)
    own_q = all_ref[me][:PAD]
    own_p = all_ref[me][PAD:]
    logits = dot_nt(own_q, p_ref[...]) * score_scale
    column = lax.broadcasted_iota(jnp.int32, logits.shape, 1)
    logits = jnp.where(column % PAD < local, logits, masked_score)
    top = jnp.max(logits, axis=1, keepdims=True)
    total = top + jnp.log(jnp.sum(jnp.exp(logits - top), axis=1, keepdims=True))
    hot = (column == own_hot_ref[...]).astype(f32)
    loss_ref[...] = jnp.broadcast_to(total - jnp.sum(logits * hot, axis=1, keepdims=True), loss_ref.shape)
    grad = (jnp.exp(logits - total) - hot).astype(bf16)
    gq_ref[...] = dot(grad, p_ref[...]) * score_scale
    gp_ref[...] = jnp.zeros_like(gp_ref)
    block = 256 if count * PAD % 256 == 0 else count * PAD

    def part(index, carry):
        start = pl.multiple_of(index * block, block)
        queries = q_ref[pl.ds(start, block), :]
        scores = dot_nt(p_ref[...], queries) * score_scale
        row = lax.broadcasted_iota(jnp.int32, scores.shape, 0)
        scores = jnp.where(row % PAD < local, scores, masked_score)
        peak = jnp.max(scores, axis=0, keepdims=True)
        sums = peak + jnp.log(jnp.sum(jnp.exp(scores - peak), axis=0, keepdims=True))
        own = dot_nt(own_p, queries) * score_scale
        own_row = lax.broadcasted_iota(jnp.int32, own.shape, 0)
        own_lane = lax.broadcasted_iota(jnp.int32, own.shape, 1)
        own_hits = (own_row + me * PAD == hot_ref[:, pl.ds(start, block)]).astype(f32)
        own_grad = jnp.where(own_lane % PAD < local, jnp.exp(own - sums) - own_hits, 0.0)
        gp_ref[...] += dot(own_grad.astype(bf16), queries) * score_scale
        return carry

    lax.fori_loop(0, count * PAD // block, part, 0)


VECTOR_OUTS = (QUERY_BIAS, VALUE_BIAS, PROJ_BIAS, ATTN_GAIN, ATTN_SHIFT, DOWN_BIAS, FFN_GAIN, FFN_SHIFT)


def unpack_kernel(q_ref, p_ref, qkv_ref, proj_ref, up_ref, down_ref, up_bias_ref, *vector_refs):
    tails = []
    for which, ref in enumerate((q_ref, p_ref)):
        for j in range(3):
            qkv_ref[which, :, j * WIDTH : (j + 1) * WIDTH] = ref[j * WIDTH : (j + 1) * WIDTH, :].astype(f32)
        proj_ref[which] = ref[3 * WIDTH : 4 * WIDTH, :].astype(f32)
        for j in range(BLOCKS):
            up_ref[which, :, j * WIDTH : (j + 1) * WIDTH] = ref[(4 + j) * WIDTH : (5 + j) * WIDTH, :].astype(f32)
        down_ref[which] = ref[8 * WIDTH : 12 * WIDTH, :].astype(f32)
        tails.append(ref[12 * WIDTH : 12 * WIDTH + VECTOR_ROWS, :].astype(f32))
    for row, ref in zip(VECTOR_OUTS, vector_refs):
        for which in range(2):
            ref[which : which + 1, :] = tails[which][row : row + 1]
    for j in range(BLOCKS):
        for which in range(2):
            up_bias_ref[which : which + 1, j * WIDTH : (j + 1) * WIDTH] = tails[which][UP_BIAS + j : UP_BIAS + j + 1]


def smem():
    return pl.BlockSpec(memory_space=pltpu.SMEM)


def whole(shape):
    return pl.BlockSpec(shape, lambda i: (0,) * len(shape))


def rows_of(rows, columns):
    return pl.BlockSpec((rows, columns), lambda i: (i, 0))


def part_of(which, shape):
    return pl.BlockSpec((None,) + shape, lambda i: (which, 0, 0))


def params():
    return pltpu.CompilerParams(vmem_limit_bytes=24 * 1024 * 1024)


def shape(dims, kind):
    return jax.ShapeDtypeStruct(dims, kind)


def cost(flops, moved):
    return pl.CostEstimate(flops=flops, bytes_accessed=moved, transcendentals=0)


def pair(columns):
    return whole((2, columns))


def in_hbm(values):
    return pltpu.with_memory_space_constraint(values, pltpu.HBM)


def in_vmem(values):
    return pltpu.with_memory_space_constraint(values, pltpu.VMEM)


def forward(which, steps, seqs, length, lengths, x, weights):
    x = in_hbm(x)
    wqkv, qb, vb, wo, ob, g1, b1, w1, hb, w2, fb, g2, b2 = [in_hbm(member) for member in weights]
    rows = seqs * length
    total = steps * rows
    stack = HEADS * length
    kinds = [
        (WIDTH, bf16), (3 * WIDTH, bf16), (WIDTH, bf16), (WIDTH, f32), (1, f32), (WIDTH, bf16),
        (HIDDEN, f32), (HIDDEN, bf16), (WIDTH, f32), (1, f32),
    ]
    out_shape = [shape((total, c), k) for c, k in kinds]
    out_specs = [rows_of(rows, c) for c, _ in kinds]
    out_shape[1:1] = [shape((PAD, WIDTH), f32)]
    out_specs[1:1] = [whole((PAD, WIDTH))]
    out_shape[3:3] = [shape((steps * seqs * stack, length), f32)]
    out_specs[3:3] = [rows_of(seqs * stack, length)]
    out_shape[1:] = [pltpu.VMEM(o.shape, o.dtype) for o in out_shape[1:]]
    return pl.pallas_call(
        functools.partial(forward_kernel, which, seqs, length),
        out_shape=out_shape,
        grid=(steps,),
        in_specs=[
            smem(), rows_of(rows, WIDTH), part_of(which, (WIDTH, 3 * WIDTH)), pair(WIDTH), pair(WIDTH),
            part_of(which, (WIDTH, WIDTH)), pair(WIDTH), pair(WIDTH), pair(WIDTH),
            part_of(which, (WIDTH, HIDDEN)), pair(HIDDEN), part_of(which, (HIDDEN, WIDTH)),
            pair(WIDTH), pair(WIDTH), pair(WIDTH),
        ],
        out_specs=out_specs,
        scratch_shapes=[
            pltpu.VMEM((rows, HIDDEN), f32),
            pltpu.VMEM((stack, length), f32),
            pltpu.VMEM((stack, length), bf16),
        ],
        compiler_params=params(),
        cost_estimate=cost(total * 2 * 800000, total * 12000),
        name="forward",
    )(lengths, x, wqkv, qb, vb, wo, ob, g1, b1, w1, hb, w2, fb, g2, b2)


def question_backward(which, seqs, length, lengths, cls_grad, cot, x, saved, weights):
    wqkv, qb, vb, wo, ob, g1, b1, w1, hb, w2, fb, g2, b2 = weights
    qkv, p, ctx, n1, r1, nb, gp, act, n2, r2 = [in_vmem(member) for member in saved[2:]]
    rows = seqs * length
    stack = HEADS * length
    return pl.pallas_call(
        functools.partial(question_back_kernel, which, seqs, length),
        out_shape=[shape((rows, WIDTH), bf16), shape((GROUP_ROWS, WIDTH), bf16)],
        grid=(1,),
        in_specs=[
            smem(), whole((PAD, WIDTH)), rows_of(rows, WIDTH), rows_of(rows, WIDTH), rows_of(rows, 3 * WIDTH),
            rows_of(seqs * stack, length), rows_of(rows, WIDTH), rows_of(rows, WIDTH), rows_of(rows, 1),
            rows_of(rows, WIDTH), rows_of(rows, HIDDEN), rows_of(rows, HIDDEN), rows_of(rows, WIDTH), rows_of(rows, 1),
            part_of(which, (WIDTH, 3 * WIDTH)), part_of(which, (WIDTH, WIDTH)), pair(WIDTH),
            part_of(which, (WIDTH, HIDDEN)), part_of(which, (HIDDEN, WIDTH)), pair(WIDTH),
        ],
        out_specs=[rows_of(rows, WIDTH), rows_of(GROUP_ROWS, WIDTH)],
        scratch_shapes=[
            pltpu.VMEM((rows, WIDTH), f32), pltpu.VMEM((rows, WIDTH), bf16), pltpu.VMEM((rows, HIDDEN), bf16),
            pltpu.VMEM((VECTOR_ROWS, WIDTH), f32), pltpu.VMEM((rows, HIDDEN), f32), pltpu.VMEM((rows, WIDTH), f32),
            pltpu.VMEM((rows, WIDTH), bf16), pltpu.VMEM((rows, WIDTH), bf16), pltpu.VMEM((rows, 3 * WIDTH), bf16),
            pltpu.VMEM((stack, length), f32), pltpu.VMEM((stack, length), bf16), pltpu.VMEM((stack, length), bf16),
        ],
        compiler_params=params(),
        cost_estimate=cost(rows * 4 * 800000, rows * 12000),
        name="question_back",
    )(lengths, cls_grad, cot, x, qkv, p, ctx, n1, r1, nb, gp, act, n2, r2, wqkv, wo, g1, w1, w2, g2)


def passage_backward(which, steps, length, lengths, cls_grad, cot, x, saved, weights):
    wqkv, qb, vb, wo, ob, g1, b1, w1, hb, w2, fb, g2, b2 = weights
    qkv, p, ctx, n1, r1, nb, gp, act, n2, r2 = [in_vmem(member) for member in saved[2:]]
    rows = length
    total = steps * rows
    stack = HEADS * length
    vec = shape((VECTOR_ROWS, WIDTH), f32)
    vec_spec = whole((VECTOR_ROWS, WIDTH))
    two, gffn, gpre, vec_a = pl.pallas_call(
        functools.partial(ffn_kernel, which, length),
        out_shape=[shape((total, WIDTH), f32), shape((total, WIDTH), bf16), shape((total, HIDDEN), bf16), vec],
        grid=(steps,),
        in_specs=[
            smem(), whole((PAD, WIDTH)), rows_of(rows, WIDTH), rows_of(rows, WIDTH), rows_of(rows, 1),
            rows_of(rows, HIDDEN), part_of(which, (HIDDEN, WIDTH)), pair(WIDTH),
        ],
        out_specs=[rows_of(rows, WIDTH), rows_of(rows, WIDTH), rows_of(rows, HIDDEN), vec_spec],
        scratch_shapes=[pltpu.VMEM((rows, HIDDEN), f32)],
        compiler_params=params(),
        cost_estimate=cost(total * 2 * 600000, total * 8000),
        name="ffn_back",
    )(lengths, cls_grad, cot, n2, r2, gp, w2, g2)
    one, dctx, vec_b, proj = pl.pallas_call(
        functools.partial(attn_norm_kernel, which, length),
        out_shape=[shape((total, WIDTH), f32), shape((total, WIDTH), bf16), vec, shape((WIDTH, WIDTH), bf16)],
        grid=(steps,),
        in_specs=[
            rows_of(rows, HIDDEN), part_of(which, (WIDTH, HIDDEN)), rows_of(rows, WIDTH), rows_of(rows, WIDTH),
            rows_of(rows, 1), pair(WIDTH), part_of(which, (WIDTH, WIDTH)), rows_of(rows, WIDTH),
        ],
        out_specs=[rows_of(rows, WIDTH), rows_of(rows, WIDTH), vec_spec, whole((WIDTH, WIDTH))],
        scratch_shapes=[pltpu.VMEM((rows, WIDTH), bf16), pltpu.VMEM((WIDTH, WIDTH), f32)],
        compiler_params=params(),
        cost_estimate=cost(total * 2 * 600000, total * 8000),
        name="attn_norm_back",
    )(gpre, w1, two, n1, r1, g1, wo, ctx)
    gx, vec_c, dqkv = pl.pallas_call(
        functools.partial(attn_core_kernel, length),
        out_shape=[shape((total, WIDTH), bf16), vec, shape((3 * WIDTH, WIDTH), bf16)],
        grid=(steps,),
        in_specs=[
            rows_of(rows, WIDTH), rows_of(rows, 3 * WIDTH), rows_of(stack, length), rows_of(rows, WIDTH),
            part_of(which, (WIDTH, 3 * WIDTH)), rows_of(rows, WIDTH),
        ],
        out_specs=[rows_of(rows, WIDTH), vec_spec, whole((3 * WIDTH, WIDTH))],
        scratch_shapes=[
            pltpu.VMEM((rows, 3 * WIDTH), bf16), pltpu.VMEM((stack, length), f32), pltpu.VMEM((stack, length), bf16),
            pltpu.VMEM((stack, length), bf16), pltpu.VMEM((3 * WIDTH, WIDTH), f32),
        ],
        compiler_params=params(),
        cost_estimate=cost(total * 2 * 1000000, total * 10000),
        name="attn_core_back",
    )(dctx, qkv, p, x, wqkv, one)
    pack = pl.pallas_call(
        pack_kernel,
        out_shape=shape((GROUP_ROWS, WIDTH), bf16),
        grid=(BLOCKS,),
        in_specs=[
            pl.BlockSpec((total, WIDTH), lambda i: (0, i)), whole((total, WIDTH)), whole((total, WIDTH)),
            pl.BlockSpec((total, WIDTH), lambda i: (0, i)), whole((3 * WIDTH, WIDTH)), whole((WIDTH, WIDTH)),
            vec_spec, vec_spec, vec_spec,
        ],
        out_specs=whole((GROUP_ROWS, WIDTH)),
        compiler_params=params(),
        cost_estimate=cost(total * 2 * 600000, total * 6000),
        name="ffn_weights",
    )(act, gffn, nb, gpre, dqkv, proj, vec_a, vec_b, vec_c)
    return gx, pack


def stages(count):
    masks = []
    bit = 1
    while bit < count:
        masks.append(bit)
        bit = bit * 2
    groups = [masks[:1]]
    rest = masks[1:]
    while rest:
        groups.append(rest[:2])
        rest = rest[2:]
    return [group for group in groups if group]


def partner_send(values, mask, count):
    return lax.ppermute(values, "dp", [(i, i ^ mask) for i in range(count)])


def combos(group):
    return [index * group[0] for index in range(1, 2 ** len(group))]


def reduce_scatter(buffer, count, me):
    for group in stages(count):
        radix = 2 ** len(group)
        digit = (me // group[0]) % radix
        split = buffer.reshape((radix, buffer.shape[0] // radix) + buffer.shape[1:])
        received = []
        for step, mask in enumerate(combos(group), start=1):
            outgoing = lax.dynamic_index_in_dim(split, digit ^ step, 0, keepdims=False)
            received.append(partner_send(outgoing, mask, count))
        total = lax.dynamic_index_in_dim(split, digit, 0, keepdims=False).astype(f32)
        for piece in received:
            total = total + piece.astype(f32)
        buffer = total.astype(bf16)
    return buffer


def gather_back(buffer, count, me):
    for group in reversed(stages(count)):
        radix = 2 ** len(group)
        digit = (me // group[0]) % radix
        joined = jnp.zeros((radix,) + buffer.shape, buffer.dtype)
        pieces = [buffer]
        for mask in combos(group):
            pieces.append(partner_send(buffer, mask, count))
        for step, piece in enumerate(pieces):
            joined = lax.dynamic_update_index_in_dim(joined, piece, digit ^ step, 0)
        buffer = joined.reshape((radix * buffer.shape[0],) + buffer.shape[1:])
    return buffer


def body(questions, passages, cot_questions, cot_passages, len_questions, len_passages, positive, *weights):
    local = questions.shape[0]
    question_length = questions.shape[1]
    passage_length = passages.shape[1]
    count = positive.shape[0] // local
    me = lax.axis_index("dp")
    x_q = questions.reshape(-1, WIDTH)
    x_p = passages.reshape(-1, WIDTH)
    saved_p = forward(1, local, 1, passage_length, len_passages, x_p, weights)
    saved_q = forward(0, 1, local, question_length, len_questions, x_q, weights)
    own_cls = jnp.concatenate([saved_q[1], saved_p[1]]).astype(bf16)
    all_cls = lax.all_to_all(
        jnp.broadcast_to(own_cls[None], (count,) + own_cls.shape), "dp", 0, 0, tiled=True
    )
    slots = positive // local * PAD + positive % local
    slots = jnp.pad(slots.reshape(count, local), ((0, 0), (0, PAD - local)), constant_values=-1)
    own_slots = lax.dynamic_slice_in_dim(slots, me, 1, axis=0).reshape(PAD, 1)
    loss, grad_cls_q, grad_cls_p = pl.pallas_call(
        functools.partial(loss_kernel, local),
        out_shape=[shape((PAD, 128), f32), shape((PAD, WIDTH), f32), shape((PAD, WIDTH), f32)],
        grid=(1,),
        in_specs=[smem(), whole((count, 2 * PAD, WIDTH)), whole((1, count * PAD)), whole((PAD, 1))],
        out_specs=[whole((PAD, 128)), whole((PAD, WIDTH)), whole((PAD, WIDTH))],
        scratch_shapes=[pltpu.VMEM((count * PAD, WIDTH), bf16), pltpu.VMEM((count * PAD, WIDTH), bf16)],
        compiler_params=params(),
        name="loss",
    )(me.reshape(1), all_cls, slots.reshape(1, -1), own_slots)
    loss_rows = loss[:local, 0]
    grad_q, pack_q = question_backward(
        0, local, question_length, len_questions, grad_cls_q, cot_questions.reshape(-1, WIDTH), x_q, saved_q, weights
    )
    sum_q = gather_back(reduce_scatter(pack_q, count, me), count, me)
    grad_p, pack_p = passage_backward(
        1, local, passage_length, len_passages, grad_cls_p, cot_passages.reshape(-1, WIDTH), x_p, saved_p, weights
    )
    sum_p = gather_back(reduce_scatter(pack_p, count, me), count, me)
    dims = [(2, WIDTH, 3 * WIDTH), (2, WIDTH, WIDTH), (2, WIDTH, HIDDEN), (2, HIDDEN, WIDTH), (2, HIDDEN)]
    dims += [(2, WIDTH)] * len(VECTOR_OUTS)
    d_qkv, d_proj, d_up, d_down, up_bias, query_bias, value_bias, proj_bias, gain_a, shift_a, down_bias, gain_f, shift_f = pl.pallas_call(
        unpack_kernel,
        out_shape=[shape(d, f32) for d in dims],
        grid=(1,),
        in_specs=[whole((GROUP_ROWS, WIDTH)), whole((GROUP_ROWS, WIDTH))],
        out_specs=[whole(d) for d in dims],
        compiler_params=params(),
        name="unpack",
    )(sum_q, sum_p)
    return (
        loss_rows, saved_q[0].reshape(questions.shape), saved_p[0].reshape(passages.shape),
        grad_q.reshape(questions.shape), grad_p.reshape(passages.shape),
        d_qkv, query_bias, value_bias, d_proj, proj_bias, gain_a, shift_a, d_up, up_bias, d_down,
        down_bias, gain_f, shift_f,
    )


def solution(mesh):
    split = P("dp", None, None)
    return jax.shard_map(
        body,
        mesh=mesh,
        in_specs=(split, split, split, split, P("dp"), P("dp")) + (P(),) * 14,
        out_specs=(P("dp"), split, split, split, split) + (P(),) * 13,
        check_vma=False,
    )
```

```python
import functools

import jax
import jax.numpy as jnp
from jax import lax
from jax.experimental import pallas as pl
from jax.experimental.pallas import tpu as pltpu
from jax.sharding import PartitionSpec as P

HEAD_DIM = 64
WIDTH = 256
HEADS = WIDTH // HEAD_DIM
HIDDEN = 1024
BLOCKS = HIDDEN // WIDTH
PAD = 8
VECTOR_ROWS = 16
HALF = 6 * WIDTH + 128
GROUP_ROWS = 2 * HALF
SOFT = 128
NORM = 64
GELU = 32
ln_eps = 1e-06
score_scale = 0.125
masked_score = -1e30
f32 = jnp.float32
bf16 = jnp.bfloat16

QUERY_BIAS, VALUE_BIAS, PROJ_BIAS, ATTN_GAIN, ATTN_SHIFT, DOWN_BIAS, FFN_GAIN, FFN_SHIFT = range(8)
UP_BIAS = 8


def dot(a, b):
    return lax.dot_general(a, b, (((1,), (0,)), ((), ())), preferred_element_type=f32)


def dot_nt(a, b):
    return lax.dot_general(a, b, (((1,), (1,)), ((), ())), preferred_element_type=f32)


def dot_tn(a, b):
    return lax.dot_general(a, b, (((0,), (0,)), ((), ())), preferred_element_type=f32)


def row_loop(rows, chunk, step):
    def body(index, carry):
        step(pl.multiple_of(index * chunk, chunk))
        return carry

    lax.fori_loop(0, rows // chunk, body, 0, unroll=rows // chunk)


def vector(ref, which):
    return ref[...].astype(f32)[which : which + 1]


def lane_head(rows):
    return lax.broadcasted_iota(jnp.int32, (rows, WIDTH), 1) // HEAD_DIM


def stack_heads(values):
    head = lane_head(values.shape[0])
    wide = values.astype(f32)
    return jnp.concatenate(
        [jnp.where(head == h, wide, 0.0).astype(bf16) for h in range(HEADS)], axis=0
    )


def pick_heads(stacked, rows):
    head = lane_head(rows)
    result = stacked[:rows]
    for h in range(1, HEADS):
        result = jnp.where(head == h, stacked[h * rows : (h + 1) * rows], result)
    return result


def block_rows(block):
    start = block * WIDTH if block < 6 else HALF + (block - 6) * WIDTH
    return slice(start, start + WIDTH)


VECTOR_START = 6 * WIDTH
QKV_BLOCK, PROJ_BLOCK, UP_BLOCK, DOWN_BLOCK = 0, 3, 4, 8


def normalize(value):
    centered = value - jnp.mean(value, axis=1, keepdims=True)
    inverse = lax.rsqrt(jnp.mean(centered * centered, axis=1, keepdims=True) + ln_eps)
    return centered * inverse, inverse


def masked_softmax(scores, size):
    part = scores * score_scale
    key = lax.broadcasted_iota(jnp.int32, part.shape, 1)
    part = jnp.where(key < size, part, masked_score)
    part = jnp.exp(part - jnp.max(part, axis=1, keepdims=True))
    return part * (1.0 / jnp.sum(part, axis=1, keepdims=True))


def gelu_parts(value):
    cumulative = 0.5 + 0.5 * lax.erf(value * 0.7071067811865476)
    density = jnp.exp(value * value * -0.5) * 0.3989422804014327
    return (value * cumulative).astype(bf16), cumulative + value * density


def first_rows(which, seqs, length, len_ref, x_ref, k_ref, v_ref, wqkv_ref, qb_ref, vb_ref, wo_ref, ob_ref, g1_ref, b1_ref, w1_ref, hb_ref, w2_ref, fb_ref, g2_ref, b2_ref):
    weights = wqkv_ref[which]
    x = x_ref[...]
    k_ref[...] = dot(x, weights[:, WIDTH : 2 * WIDTH]).astype(bf16)
    v_ref[...] = (dot(x, weights[:, 2 * WIDTH :]) + vector(vb_ref, which)).astype(bf16)
    contexts, inputs = [], []
    for s in range(seqs):
        first = x_ref[s * length : s * length + 16, :]
        query = (dot(first, weights[:, :WIDTH]) + vector(qb_ref, which)).astype(bf16)
        span = slice(s * length, (s + 1) * length)
        prob = masked_softmax(dot_nt(stack_heads(query), k_ref[span, :]), len_ref[s])
        contexts.append(pick_heads(dot(prob.astype(bf16), v_ref[span, :]), 16)[:1])
        inputs.append(first.astype(f32)[:1])
    filler = jnp.zeros((PAD - seqs, WIDTH), f32)
    context = jnp.concatenate(contexts + [filler], axis=0).astype(bf16)
    value = jnp.concatenate(inputs + [filler], axis=0)
    value = value + (dot(context, wo_ref[which]) + vector(ob_ref, which))
    unit, _ = normalize(value)
    normed = unit * vector(g1_ref, which) + vector(b1_ref, which)
    hidden = dot(normed.astype(bf16), w1_ref[which]) + vector(hb_ref, which)
    active, _ = gelu_parts(hidden)
    value = normed + (dot(active, w2_ref[which]) + vector(fb_ref, which))
    unit, _ = normalize(value)
    result = unit * vector(g2_ref, which) + vector(b2_ref, which)
    row = lax.broadcasted_iota(jnp.int32, result.shape, 0)
    return jnp.where(row < seqs, result, 0.0)


def first_kernel(seqs, lq_ref, lp_ref, xq_ref, xp_ref, *refs):
    weights, (cls_ref, kq_ref, vq_ref, kp_ref, vp_ref) = refs[:13], refs[13:]
    count = cls_ref.shape[0]
    question = first_rows(0, seqs, xq_ref.shape[0] // seqs, lq_ref, xq_ref, kq_ref, vq_ref, *weights)
    passage = first_rows(1, seqs, xp_ref.shape[0] // seqs, lp_ref, xp_ref, kp_ref, vp_ref, *weights)
    both = jnp.concatenate([question, passage], axis=0).astype(bf16)
    for i in range(count) if count <= 32 else ():
        cls_ref[i] = both
    if count > 32:

        def store(i, carry):
            cls_ref[i] = both
            return carry

        lax.fori_loop(0, count, store, 0)


def forward_phase(
    which, seqs, length, first,
    len_ref, x_ref, wqkv_ref, qb_ref, vb_ref, wo_ref, ob_ref, g1_ref, b1_ref,
    w1_ref, hb_ref, w2_ref, fb_ref, g2_ref, b2_ref,
    out_ref, qkv_ref, p_ref, ctx_ref, n1_ref, r1_ref, nb_ref, gp_ref, act_ref, n2_ref, r2_ref,
    wide_ref, score_ref, prob_ref,
):
    rows = seqs * length
    x = x_ref[...]
    qkv_ref[:, :WIDTH] = (dot(x, wqkv_ref[:, :WIDTH]) + vector(qb_ref, which)).astype(bf16)
    qkv_ref[:, WIDTH : 2 * WIDTH] = dot(x, wqkv_ref[:, WIDTH : 2 * WIDTH]).astype(bf16)
    qkv_ref[:, 2 * WIDTH :] = (dot(x, wqkv_ref[:, 2 * WIDTH :]) + vector(vb_ref, which)).astype(bf16)
    stack_rows = HEADS * length
    for s in range(seqs):
        span = slice(s * length, (s + 1) * length)
        stack = slice(s * stack_rows, (s + 1) * stack_rows)
        size = len_ref[first + s]
        score_ref[stack, :] = dot_nt(stack_heads(qkv_ref[span, :WIDTH]), qkv_ref[span, WIDTH : 2 * WIDTH])

        def softmax(row):
            here = pl.ds(s * stack_rows + row, SOFT)
            prob = masked_softmax(score_ref[here, :], size)
            p_ref[here, :] = prob
            prob_ref[here, :] = prob.astype(bf16)

        row_loop(stack_rows, SOFT, softmax)
        ctx_ref[span, :] = pick_heads(dot(prob_ref[stack, :], qkv_ref[span, 2 * WIDTH :]), length).astype(bf16)
    n2_ref[...] = dot(ctx_ref[...], wo_ref[...])
    ob, g1, b1 = vector(ob_ref, which), vector(g1_ref, which), vector(b1_ref, which)

    def first_norm(row):
        here = pl.ds(row, NORM)
        unit, inverse = normalize(x_ref[here, :].astype(f32) + (n2_ref[here, :] + ob))
        n1_ref[here, :] = unit
        r1_ref[here, :] = inverse
        nb_ref[here, :] = (unit * g1 + b1).astype(bf16)

    row_loop(rows, NORM, first_norm)
    wide_ref[...] = dot(nb_ref[...], w1_ref[...])
    hb = vector(hb_ref, which)

    def gelu(row):
        here = pl.ds(row, GELU)
        for j in range(BLOCKS):
            lanes = slice(j * WIDTH, (j + 1) * WIDTH)
            active, slope = gelu_parts(wide_ref[here, lanes] + hb[:, lanes])
            act_ref[here, lanes] = active
            gp_ref[here, lanes] = slope

    row_loop(rows, GELU, gelu)
    n2_ref[...] = dot(act_ref[...], w2_ref[...])
    fb, g2, b2 = vector(fb_ref, which), vector(g2_ref, which), vector(b2_ref, which)
    for s in range(seqs):
        size = len_ref[first + s]

        def second_norm(row):
            here = pl.ds(s * length + row, NORM)
            unit, inverse = normalize((n1_ref[here, :] * g1 + b1) + (n2_ref[here, :] + fb))
            n2_ref[here, :] = unit
            r2_ref[here, :] = inverse
            position = row + lax.broadcasted_iota(jnp.int32, (NORM, WIDTH), 0)
            out_ref[here, :] = jnp.where(position < size, unit * g2 + b2, 0.0).astype(bf16)

        row_loop(length, NORM, second_norm)


def add_row(vec_ref, row, values):
    vec_ref[row : row + 1, :] = vec_ref[row : row + 1, :] + jnp.sum(values, axis=0, keepdims=True)


def ffn_phase(which, seqs, length, first, len_ref, cls_ref, cot_ref, n2_ref, r2_ref, gp_ref, w2_ref, g2_ref, two_ref, gffn_ref, gpre_ref, vec_ref, wide_ref):
    g2 = vector(g2_ref, which)
    for s in range(seqs):
        size = len_ref[first + s]
        cls_row = cls_ref[pl.ds(first + s, 1), :]

        def norm_back(row):
            here = pl.ds(s * length + row, NORM)
            position = row + lax.broadcasted_iota(jnp.int32, (NORM, WIDTH), 0)
            grad = cot_ref[here, :].astype(f32) + jnp.where(position == 0, cls_row, 0.0)
            grad = jnp.where(position < size, grad, 0.0)
            unit = n2_ref[here, :]
            scaled = grad * g2
            first_mean = jnp.mean(scaled, axis=1, keepdims=True)
            second_mean = jnp.mean(scaled * unit, axis=1, keepdims=True)
            two = r2_ref[here, :] * (scaled - first_mean - unit * second_mean)
            low = two.astype(bf16)
            two_ref[here, :] = two
            gffn_ref[here, :] = low
            add_row(vec_ref, FFN_GAIN, grad * unit)
            add_row(vec_ref, FFN_SHIFT, grad)
            add_row(vec_ref, DOWN_BIAS, low.astype(f32))

        row_loop(length, NORM, norm_back)
    wide_ref[...] = dot_nt(gffn_ref[...], w2_ref[...])

    def gelu_back(row):
        here = pl.ds(row, GELU)
        for j in range(BLOCKS):
            lanes = slice(j * WIDTH, (j + 1) * WIDTH)
            low = (wide_ref[here, lanes] * gp_ref[here, lanes]).astype(bf16)
            gpre_ref[here, lanes] = low
            add_row(vec_ref, UP_BIAS + j, low.astype(f32))

    row_loop(seqs * length, GELU, gelu_back)


def attn_norm_phase(which, rows, gpre_ref, w1_ref, two_ref, n1_ref, r1_ref, g1_ref, wo_ref, one_ref, gatt_ref, dctx_ref, vec_ref):
    one_ref[...] = dot_nt(gpre_ref[...], w1_ref[...])
    g1 = vector(g1_ref, which)

    def norm_back(row):
        here = pl.ds(row, NORM)
        grad = two_ref[here, :] + one_ref[here, :]
        unit = n1_ref[here, :]
        scaled = grad * g1
        first_mean = jnp.mean(scaled, axis=1, keepdims=True)
        second_mean = jnp.mean(scaled * unit, axis=1, keepdims=True)
        one = r1_ref[here, :] * (scaled - first_mean - unit * second_mean)
        low = one.astype(bf16)
        one_ref[here, :] = one
        gatt_ref[here, :] = low
        add_row(vec_ref, ATTN_GAIN, grad * unit)
        add_row(vec_ref, ATTN_SHIFT, grad)
        add_row(vec_ref, PROJ_BIAS, low.astype(f32))

    row_loop(rows, NORM, norm_back)
    dctx_ref[...] = dot_nt(gatt_ref[...], wo_ref[...]).astype(bf16)


def attn_core_phase(seqs, length, dctx_ref, qkv_ref, p_ref, gqkv_ref, vec_ref, dp_ref, ds_ref, pb_ref):
    stack_rows = HEADS * length
    for s in range(seqs):
        span = slice(s * length, (s + 1) * length)
        context = stack_heads(dctx_ref[span, :])
        stack = slice(s * stack_rows, (s + 1) * stack_rows)
        dp_ref[stack, :] = dot_nt(context, qkv_ref[span, 2 * WIDTH :])

        def softmax_back(row):
            here = pl.ds(s * stack_rows + row, SOFT)
            prob = p_ref[here, :]
            grad = dp_ref[here, :]
            inner = jnp.sum(prob * grad, axis=1, keepdims=True)
            ds_ref[here, :] = (prob * (grad - inner)).astype(bf16)

        row_loop(stack_rows, SOFT, softmax_back)
        queries = stack_heads(qkv_ref[span, :WIDTH])
        grad_q = (pick_heads(dot(ds_ref[stack, :], qkv_ref[span, WIDTH : 2 * WIDTH]), length) * score_scale).astype(bf16)
        gqkv_ref[span, :WIDTH] = grad_q
        add_row(vec_ref, QUERY_BIAS, grad_q.astype(f32))
        gqkv_ref[span, WIDTH : 2 * WIDTH] = (dot_tn(ds_ref[stack, :], queries) * score_scale).astype(bf16)
        grad_v = dot_tn(pb_ref[stack, :], context).astype(bf16)
        gqkv_ref[span, 2 * WIDTH :] = grad_v
        add_row(vec_ref, VALUE_BIAS, grad_v.astype(f32))


def layer_kernel(
    which, steps, seqs, length,
    bit_ref, len_ref, cls_ref, x_ref, cot_ref,
    wqkv_ref, qb_ref, vb_ref, wo_ref, ob_ref, g1_ref, b1_ref, w1_ref, hb_ref, w2_ref, fb_ref, g2_ref, b2_ref,
    out_ref, gx_ref, keep_ref, send_ref,
    acc_ref, vec_ref, qkv_ref, p_ref, ctx_ref, n1_ref, r1_ref, nb_ref, gp_ref, act_ref, n2_ref, r2_ref,
    wide_ref, score_ref, prob_ref, two_ref, gffn_ref, gpre_ref, one_ref, gatt_ref, dctx_ref, gqkv_ref, ds_ref,
):
    rows = seqs * length
    step = pl.program_id(0)

    def start():
        vec_ref[...] = jnp.zeros_like(vec_ref)
        if steps > 1:
            acc_ref[...] = jnp.zeros_like(acc_ref)

    if steps > 1:
        pl.when(step == 0)(start)
    else:
        start()

    def add_block(block, value):
        if steps > 1:
            acc_ref[block_rows(block), :] += value
        else:
            acc_ref[block_rows(block), :] = value

    forward_phase(
        which, seqs, length, step * seqs,
        len_ref, x_ref, wqkv_ref, qb_ref, vb_ref, wo_ref, ob_ref, g1_ref, b1_ref,
        w1_ref, hb_ref, w2_ref, fb_ref, g2_ref, b2_ref,
        out_ref, qkv_ref, p_ref, ctx_ref, n1_ref, r1_ref, nb_ref, gp_ref, act_ref, n2_ref, r2_ref,
        wide_ref, score_ref, prob_ref,
    )
    ffn_phase(which, seqs, length, step * seqs, len_ref, cls_ref, cot_ref, n2_ref, r2_ref, gp_ref, w2_ref, g2_ref, two_ref, gffn_ref, gpre_ref, vec_ref, wide_ref)
    for j in range(BLOCKS):
        lanes = slice(j * WIDTH, (j + 1) * WIDTH)
        add_block(DOWN_BLOCK + j, dot_tn(act_ref[:, lanes], gffn_ref[...]))
        add_block(UP_BLOCK + j, dot_tn(nb_ref[...], gpre_ref[:, lanes]))
    attn_norm_phase(which, rows, gpre_ref, w1_ref, two_ref, n1_ref, r1_ref, g1_ref, wo_ref, one_ref, gatt_ref, dctx_ref, vec_ref)
    add_block(PROJ_BLOCK, dot_tn(ctx_ref[...], gatt_ref[...]))
    attn_core_phase(seqs, length, dctx_ref, qkv_ref, p_ref, gqkv_ref, vec_ref, score_ref, ds_ref, prob_ref)
    for j in range(3):
        add_block(QKV_BLOCK + j, dot_tn(x_ref[...], gqkv_ref[:, j * WIDTH : (j + 1) * WIDTH]))
    gx_ref[...] = (one_ref[...] + dot_nt(gqkv_ref[...], wqkv_ref[...])).astype(bf16)

    def finish():
        acc_ref[VECTOR_START : VECTOR_START + VECTOR_ROWS, :] = vec_ref[...]
        if steps == 1:
            acc_ref[VECTOR_START + VECTOR_ROWS : HALF, :] = jnp.zeros((HALF - VECTOR_START - VECTOR_ROWS, WIDTH), f32)
            acc_ref[HALF + 6 * WIDTH :, :] = jnp.zeros((HALF - 6 * WIDTH, WIDTH), f32)
        keep = pl.multiple_of(bit_ref[0] * HALF, HALF)
        send = pl.multiple_of((1 - bit_ref[0]) * HALF, HALF)
        keep_ref[...] = acc_ref[pl.ds(keep, HALF), :].astype(bf16)
        send_ref[...] = acc_ref[pl.ds(send, HALF), :].astype(bf16)

    if steps > 1:
        pl.when(step == steps - 1)(finish)
    else:
        finish()


def loss_kernel(local, me_ref, all_ref, hot_ref, own_hot_ref, loss_ref, gq_ref, gp_ref, q_ref, p_ref):
    count = all_ref.shape[0]
    me = me_ref[0]
    wide = all_ref[...].astype(f32)
    q_ref[...] = wide[:, :PAD].reshape(count * PAD, WIDTH).astype(bf16)
    p_ref[...] = wide[:, PAD:].reshape(count * PAD, WIDTH).astype(bf16)
    own_q = all_ref[me][:PAD]
    own_p = all_ref[me][PAD:]
    logits = dot_nt(own_q, p_ref[...]) * score_scale
    column = lax.broadcasted_iota(jnp.int32, logits.shape, 1)
    logits = jnp.where(column % PAD < local, logits, masked_score)
    top = jnp.max(logits, axis=1, keepdims=True)
    total = top + jnp.log(jnp.sum(jnp.exp(logits - top), axis=1, keepdims=True))
    hot = (column == own_hot_ref[...]).astype(f32)
    loss_ref[...] = jnp.broadcast_to(total - jnp.sum(logits * hot, axis=1, keepdims=True), loss_ref.shape)
    grad = (jnp.exp(logits - total) - hot).astype(bf16)
    gq_ref[...] = dot(grad, p_ref[...]) * score_scale
    gp_ref[...] = jnp.zeros_like(gp_ref)
    block = 256 if count * PAD % 256 == 0 else count * PAD

    def part(index, carry):
        start = pl.multiple_of(index * block, block)
        queries = q_ref[pl.ds(start, block), :]
        scores = dot_nt(p_ref[...], queries) * score_scale
        row = lax.broadcasted_iota(jnp.int32, scores.shape, 0)
        scores = jnp.where(row % PAD < local, scores, masked_score)
        peak = jnp.max(scores, axis=0, keepdims=True)
        sums = peak + jnp.log(jnp.sum(jnp.exp(scores - peak), axis=0, keepdims=True))
        own = dot_nt(own_p, queries) * score_scale
        own_row = lax.broadcasted_iota(jnp.int32, own.shape, 0)
        own_lane = lax.broadcasted_iota(jnp.int32, own.shape, 1)
        own_hits = (own_row + me * PAD == hot_ref[:, pl.ds(start, block)]).astype(f32)
        own_grad = jnp.where(own_lane % PAD < local, jnp.exp(own - sums) - own_hits, 0.0)
        gp_ref[...] += dot(own_grad.astype(bf16), queries) * score_scale
        return carry

    lax.fori_loop(0, count * PAD // block, part, 0)


def combine_kernel(radix, digit_ref, *refs):
    total_ref = refs[-1]
    sends = refs[-1 - (radix - 1) : -1]
    keep_ref = refs[-1 - radix]
    pieces = refs[: -1 - radix]
    total = pieces[0][...].astype(f32)
    for piece in pieces[1:]:
        total = total + piece[...].astype(f32)
    total_ref[...] = total
    part = total_ref.shape[0] // radix
    digit = digit_ref[0]

    def section(which):
        return total_ref[pl.ds(pl.multiple_of(which * part, part), part), :].astype(bf16)

    keep_ref[...] = section(digit)
    for step, ref in enumerate(sends, start=1):
        ref[...] = section(digit ^ step)


VECTOR_OUTS = (QUERY_BIAS, VALUE_BIAS, PROJ_BIAS, ATTN_GAIN, ATTN_SHIFT, DOWN_BIAS, FFN_GAIN, FFN_SHIFT)


def unpack_kernel(bit_ref, q_own_ref, q_ref, p_own_ref, p_ref, qkv_ref, proj_ref, up_ref, down_ref, up_bias_ref, *refs):
    vector_refs, whole_ref = refs[:-1], refs[-1]
    own = pl.multiple_of(bit_ref[0] * HALF, HALF)
    other = pl.multiple_of((1 - bit_ref[0]) * HALF, HALF)
    tails = []
    for which, (own_ref, other_ref) in enumerate(((q_own_ref, q_ref), (p_own_ref, p_ref))):
        ref = whole_ref.at[which]
        ref[pl.ds(own, HALF), :] = own_ref[...]
        ref[pl.ds(other, HALF), :] = other_ref[...]
        for j in range(3):
            qkv_ref[which, :, j * WIDTH : (j + 1) * WIDTH] = ref[block_rows(QKV_BLOCK + j), :].astype(f32)
        proj_ref[which] = ref[block_rows(PROJ_BLOCK), :].astype(f32)
        for j in range(BLOCKS):
            up_ref[which, :, j * WIDTH : (j + 1) * WIDTH] = ref[block_rows(UP_BLOCK + j), :].astype(f32)
            down_ref[which, j * WIDTH : (j + 1) * WIDTH, :] = ref[block_rows(DOWN_BLOCK + j), :].astype(f32)
        tails.append(ref[VECTOR_START : VECTOR_START + VECTOR_ROWS, :].astype(f32))
    for row, ref in zip(VECTOR_OUTS, vector_refs):
        for which in range(2):
            ref[which : which + 1, :] = tails[which][row : row + 1]
    for j in range(BLOCKS):
        for which in range(2):
            up_bias_ref[which : which + 1, j * WIDTH : (j + 1) * WIDTH] = tails[which][UP_BIAS + j : UP_BIAS + j + 1]


def smem():
    return pl.BlockSpec(memory_space=pltpu.SMEM)


def whole(shape):
    return pl.BlockSpec(shape, lambda i: (0,) * len(shape))


def rows_of(rows, columns):
    return pl.BlockSpec((rows, columns), lambda i: (i, 0))


def part_of(which, shape):
    return pl.BlockSpec((None,) + shape, lambda i: (which, 0, 0))


def params():
    return pltpu.CompilerParams(vmem_limit_bytes=24 * 1024 * 1024)


def shape(dims, kind):
    return jax.ShapeDtypeStruct(dims, kind)


def cost(flops, moved):
    return pl.CostEstimate(flops=flops, bytes_accessed=moved, transcendentals=0)


def pair(columns):
    return whole((2, columns))


def in_hbm(values):
    return pltpu.with_memory_space_constraint(values, pltpu.HBM)


def weight_specs(which):
    return [
        part_of(which, (WIDTH, 3 * WIDTH)), pair(WIDTH), pair(WIDTH), part_of(which, (WIDTH, WIDTH)),
        pair(WIDTH), pair(WIDTH), pair(WIDTH), part_of(which, (WIDTH, HIDDEN)), pair(HIDDEN),
        part_of(which, (HIDDEN, WIDTH)), pair(WIDTH), pair(WIDTH), pair(WIDTH),
    ]


def layer(which, steps, seqs, length, bit, lengths, cls_grad, x, cot, weights):
    rows = seqs * length
    total = steps * rows
    stack = seqs * HEADS * length
    return pl.pallas_call(
        functools.partial(layer_kernel, which, steps, seqs, length),
        out_shape=[shape((total, WIDTH), bf16), shape((total, WIDTH), bf16), shape((HALF, WIDTH), bf16), shape((HALF, WIDTH), bf16)],
        grid=(steps,),
        in_specs=[smem(), smem(), whole((PAD, WIDTH)), rows_of(rows, WIDTH), rows_of(rows, WIDTH)] + weight_specs(which),
        out_specs=[rows_of(rows, WIDTH), rows_of(rows, WIDTH), whole((HALF, WIDTH)), whole((HALF, WIDTH))],
        scratch_shapes=[
            pltpu.VMEM((GROUP_ROWS, WIDTH), f32), pltpu.VMEM((VECTOR_ROWS, WIDTH), f32),
            pltpu.VMEM((rows, 3 * WIDTH), bf16), pltpu.VMEM((stack, length), f32), pltpu.VMEM((rows, WIDTH), bf16),
            pltpu.VMEM((rows, WIDTH), f32), pltpu.VMEM((rows, 1), f32), pltpu.VMEM((rows, WIDTH), bf16),
            pltpu.VMEM((rows, HIDDEN), f32), pltpu.VMEM((rows, HIDDEN), bf16), pltpu.VMEM((rows, WIDTH), f32),
            pltpu.VMEM((rows, 1), f32), pltpu.VMEM((rows, HIDDEN), f32), pltpu.VMEM((stack, length), f32),
            pltpu.VMEM((stack, length), bf16), pltpu.VMEM((rows, WIDTH), f32), pltpu.VMEM((rows, WIDTH), bf16),
            pltpu.VMEM((rows, HIDDEN), bf16), pltpu.VMEM((rows, WIDTH), f32), pltpu.VMEM((rows, WIDTH), bf16),
            pltpu.VMEM((rows, WIDTH), bf16), pltpu.VMEM((rows, 3 * WIDTH), bf16), pltpu.VMEM((stack, length), bf16),
        ],
        compiler_params=params(),
        cost_estimate=cost(total * 6 * 800000, total * 4000),
        name="layer",
    )(bit, lengths, cls_grad, in_hbm(x), in_hbm(cot), *[in_hbm(member) for member in weights])


def stages(count):
    masks = []
    bit = 1
    while bit < count:
        masks.append(bit)
        bit = bit * 2
    groups = [masks[:1]]
    rest = masks[1:]
    while rest:
        groups.append(rest[:2])
        rest = rest[2:]
    return [group for group in groups if group]


def partner_send(values, mask, count):
    return lax.ppermute(values, "dp", [(i, i ^ mask) for i in range(count)])


def combos(group):
    return [index * group[0] for index in range(1, 2 ** len(group))]


def combine(pieces, group, me):
    radix = 2 ** len(group)
    digit = (me // group[0]) % radix
    rows = pieces[0].shape[0]
    part = rows // radix
    if part % 8 == 0:
        return pl.pallas_call(
            functools.partial(combine_kernel, radix),
            out_shape=[shape((part, WIDTH), bf16)] * radix,
            grid=(1,),
            in_specs=[smem()] + [whole((rows, WIDTH))] * len(pieces),
            out_specs=[whole((part, WIDTH))] * radix,
            scratch_shapes=[pltpu.VMEM((rows, WIDTH), f32)],
            compiler_params=params(),
            name="combine",
        )(digit.reshape(1), *pieces)
    total = pieces[0].astype(f32)
    for piece in pieces[1:]:
        total = total + piece.astype(f32)
    split = total.astype(bf16).reshape(radix, part, WIDTH)
    return [lax.dynamic_index_in_dim(split, digit ^ step, 0, keepdims=False) for step in range(radix)]


def reduce_scatter(keep, send, count, me):
    groups = stages(count)
    pieces = [keep, partner_send(send, groups[0][0], count)]
    for group in groups[1:]:
        own, *sends = combine(pieces, group, me)
        pieces = [own] + [partner_send(part, mask, count) for part, mask in zip(sends, combos(group))]
    total = pieces[0].astype(f32)
    for piece in pieces[1:]:
        total = total + piece.astype(f32)
    return total.astype(bf16)


def gather_back(buffer, count, me):
    groups = stages(count)
    for group in reversed(groups[1:]):
        radix = 2 ** len(group)
        digit = (me // group[0]) % radix
        joined = jnp.zeros((radix,) + buffer.shape, buffer.dtype)
        pieces = [buffer] + [partner_send(buffer, mask, count) for mask in combos(group)]
        for step, piece in enumerate(pieces):
            joined = lax.dynamic_update_index_in_dim(joined, piece, digit ^ step, 0)
        buffer = joined.reshape((radix * buffer.shape[0],) + buffer.shape[1:])
    return buffer, partner_send(buffer, groups[0][0], count)


def body(questions, passages, cot_questions, cot_passages, len_questions, len_passages, positive, *weights):
    local = questions.shape[0]
    question_length = questions.shape[1]
    passage_length = passages.shape[1]
    count = positive.shape[0] // local
    me = lax.axis_index("dp")
    bit = (me % 2).reshape(1)
    x_q = questions.reshape(-1, WIDTH)
    x_p = passages.reshape(-1, WIDTH)
    own_cls = pl.pallas_call(
        functools.partial(first_kernel, local),
        out_shape=shape((count, 2 * PAD, WIDTH), bf16),
        grid=(1,),
        in_specs=[smem(), smem(), whole(x_q.shape), whole(x_p.shape)] + [whole(member.shape) for member in weights],
        out_specs=whole((count, 2 * PAD, WIDTH)),
        scratch_shapes=[pltpu.VMEM(x_q.shape, bf16)] * 2 + [pltpu.VMEM(x_p.shape, bf16)] * 2,
        compiler_params=params(),
        name="first",
    )(len_questions, len_passages, in_hbm(x_q), in_hbm(x_p), *[in_hbm(member) for member in weights])
    all_cls = lax.all_to_all(own_cls, "dp", 0, 0, tiled=True)
    slots = positive // local * PAD + positive % local
    slots = jnp.pad(slots.reshape(count, local), ((0, 0), (0, PAD - local)), constant_values=-1)
    own_slots = lax.dynamic_slice_in_dim(slots, me, 1, axis=0).reshape(PAD, 1)
    loss, grad_cls_q, grad_cls_p = pl.pallas_call(
        functools.partial(loss_kernel, local),
        out_shape=[shape((PAD, 128), f32), shape((PAD, WIDTH), f32), shape((PAD, WIDTH), f32)],
        grid=(1,),
        in_specs=[smem(), whole((count, 2 * PAD, WIDTH)), whole((1, count * PAD)), whole((PAD, 1))],
        out_specs=[whole((PAD, 128)), whole((PAD, WIDTH)), whole((PAD, WIDTH))],
        scratch_shapes=[pltpu.VMEM((count * PAD, WIDTH), bf16), pltpu.VMEM((count * PAD, WIDTH), bf16)],
        compiler_params=params(),
        name="loss",
    )(me.reshape(1), all_cls, slots.reshape(1, -1), own_slots)
    loss_rows = loss[:local, 0]
    out_q, grad_q, keep_q, send_q = layer(
        0, 1, local, question_length, bit, len_questions, grad_cls_q, x_q, cot_questions.reshape(-1, WIDTH), weights
    )
    own_q, other_q = gather_back(reduce_scatter(keep_q, send_q, count, me), count, me)
    out_p, grad_p, keep_p, send_p = layer(
        1, local, 1, passage_length, bit, len_passages, grad_cls_p, x_p, cot_passages.reshape(-1, WIDTH), weights
    )
    own_p, other_p = gather_back(reduce_scatter(keep_p, send_p, count, me), count, me)
    dims = [(2, WIDTH, 3 * WIDTH), (2, WIDTH, WIDTH), (2, WIDTH, HIDDEN), (2, HIDDEN, WIDTH), (2, HIDDEN)]
    dims += [(2, WIDTH)] * len(VECTOR_OUTS)
    d_qkv, d_proj, d_up, d_down, up_bias, query_bias, value_bias, proj_bias, gain_a, shift_a, down_bias, gain_f, shift_f = pl.pallas_call(
        unpack_kernel,
        out_shape=[shape(d, f32) for d in dims],
        grid=(1,),
        in_specs=[smem()] + [whole((HALF, WIDTH))] * 4,
        out_specs=[whole(d) for d in dims],
        scratch_shapes=[pltpu.VMEM((2, GROUP_ROWS, WIDTH), bf16)],
        compiler_params=params(),
        name="unpack",
    )(bit, own_q, other_q, own_p, other_p)
    return (
        loss_rows, out_q.reshape(questions.shape), out_p.reshape(passages.shape),
        grad_q.reshape(questions.shape), grad_p.reshape(passages.shape),
        d_qkv, query_bias, value_bias, d_proj, proj_bias, gain_a, shift_a, d_up, up_bias, d_down,
        down_bias, gain_f, shift_f,
    )


def solution(mesh):
    split = P("dp", None, None)
    return jax.shard_map(
        body,
        mesh=mesh,
        in_specs=(split, split, split, split, P("dp"), P("dp")) + (P(),) * 14,
        out_specs=(P("dp"), split, split, split, split) + (P(),) * 13,
        check_vma=False,
    )
```

```python
import functools

import jax
import jax.numpy as jnp
from jax import lax
from jax.experimental import pallas as pl
from jax.experimental.pallas import tpu as pltpu
from jax.sharding import PartitionSpec as P

HEAD_DIM = 64
WIDTH = 256
HEADS = WIDTH // HEAD_DIM
HIDDEN = 1024
BLOCKS = HIDDEN // WIDTH
PAD = 8
VECTOR_ROWS = 16
HALF = 6 * WIDTH + 128
GROUP_ROWS = 2 * HALF
ORDERED = True
SOFT = 128
NORM = 64
GELU = 32
ln_eps = 1e-06
score_scale = 0.125
masked_score = -1e30
f32 = jnp.float32
bf16 = jnp.bfloat16

QUERY_BIAS, VALUE_BIAS, PROJ_BIAS, ATTN_GAIN, ATTN_SHIFT, DOWN_BIAS, FFN_GAIN, FFN_SHIFT = range(8)
UP_BIAS = 8


def dot(a, b):
    return lax.dot_general(a, b, (((1,), (0,)), ((), ())), preferred_element_type=f32)


def dot_nt(a, b):
    return lax.dot_general(a, b, (((1,), (1,)), ((), ())), preferred_element_type=f32)


def dot_tn(a, b):
    return lax.dot_general(a, b, (((0,), (0,)), ((), ())), preferred_element_type=f32)


def row_loop(rows, chunk, step):
    def body(index, carry):
        step(pl.multiple_of(index * chunk, chunk))
        return carry

    lax.fori_loop(0, rows // chunk, body, 0, unroll=rows // chunk)


def vector(ref, which):
    return ref[...].astype(f32)[which : which + 1]


def lane_head(rows):
    return lax.broadcasted_iota(jnp.int32, (rows, WIDTH), 1) // HEAD_DIM


def stack_heads(values):
    head = lane_head(values.shape[0])
    wide = values.astype(f32)
    return jnp.concatenate(
        [jnp.where(head == h, wide, 0.0).astype(bf16) for h in range(HEADS)], axis=0
    )


def one_head(values, h):
    return jnp.where(lane_head(values.shape[0]) == h, values.astype(f32), 0.0).astype(bf16)


def pick_heads(stacked, rows):
    head = lane_head(rows)
    result = stacked[:rows]
    for h in range(1, HEADS):
        result = jnp.where(head == h, stacked[h * rows : (h + 1) * rows], result)
    return result


def block_rows(block):
    start = block * WIDTH if block < 6 else HALF + (block - 6) * WIDTH
    return slice(start, start + WIDTH)


VECTOR_START = 6 * WIDTH
QKV_BLOCK, PROJ_BLOCK, UP_BLOCK, DOWN_BLOCK = 0, 3, 4, 8


def normalize(value):
    centered = value - jnp.mean(value, axis=1, keepdims=True)
    inverse = lax.rsqrt(jnp.mean(centered * centered, axis=1, keepdims=True) + ln_eps)
    return centered * inverse, inverse


def masked_softmax(scores, size):
    part = scores * score_scale
    key = lax.broadcasted_iota(jnp.int32, part.shape, 1)
    part = jnp.where(key < size, part, masked_score)
    part = jnp.exp(part - jnp.max(part, axis=1, keepdims=True))
    return part * (1.0 / jnp.sum(part, axis=1, keepdims=True))


def gelu_parts(value):
    cumulative = 0.5 + 0.5 * lax.erf(value * 0.7071067811865476)
    density = jnp.exp(value * value * -0.5) * 0.3989422804014327
    return (value * cumulative).astype(bf16), cumulative + value * density


def first_rows(which, seqs, length, len_ref, x_ref, k_ref, v_ref, wqkv_ref, qb_ref, vb_ref, wo_ref, ob_ref, g1_ref, b1_ref, w1_ref, hb_ref, w2_ref, fb_ref, g2_ref, b2_ref):
    weights = wqkv_ref[which]
    x = x_ref[...]
    k_ref[...] = dot(x, weights[:, WIDTH : 2 * WIDTH]).astype(bf16)
    v_ref[...] = (dot(x, weights[:, 2 * WIDTH :]) + vector(vb_ref, which)).astype(bf16)
    contexts, inputs = [], []
    for s in range(seqs):
        first = x_ref[s * length : s * length + 16, :]
        query = (dot(first, weights[:, :WIDTH]) + vector(qb_ref, which)).astype(bf16)
        span = slice(s * length, (s + 1) * length)
        prob = masked_softmax(dot_nt(stack_heads(query), k_ref[span, :]), len_ref[s])
        contexts.append(pick_heads(dot(prob.astype(bf16), v_ref[span, :]), 16)[:1])
        inputs.append(first.astype(f32)[:1])
    filler = jnp.zeros((PAD - seqs, WIDTH), f32)
    context = jnp.concatenate(contexts + [filler], axis=0).astype(bf16)
    value = jnp.concatenate(inputs + [filler], axis=0)
    value = value + (dot(context, wo_ref[which]) + vector(ob_ref, which))
    unit, _ = normalize(value)
    normed = unit * vector(g1_ref, which) + vector(b1_ref, which)
    hidden = dot(normed.astype(bf16), w1_ref[which]) + vector(hb_ref, which)
    active, _ = gelu_parts(hidden)
    value = normed + (dot(active, w2_ref[which]) + vector(fb_ref, which))
    unit, _ = normalize(value)
    result = unit * vector(g2_ref, which) + vector(b2_ref, which)
    row = lax.broadcasted_iota(jnp.int32, result.shape, 0)
    return jnp.where(row < seqs, result, 0.0)


def first_kernel(seqs, lq_ref, lp_ref, xq_ref, xp_ref, *refs):
    weights, (cls_ref, kq_ref, vq_ref, kp_ref, vp_ref) = refs[:13], refs[13:]
    count = cls_ref.shape[0]
    question = first_rows(0, seqs, xq_ref.shape[0] // seqs, lq_ref, xq_ref, kq_ref, vq_ref, *weights)
    passage = first_rows(1, seqs, xp_ref.shape[0] // seqs, lp_ref, xp_ref, kp_ref, vp_ref, *weights)
    both = jnp.concatenate([question, passage], axis=0).astype(bf16)
    for i in range(count) if count <= 32 else ():
        cls_ref[i] = both
    if count > 32:

        def store(i, carry):
            cls_ref[i] = both
            return carry

        lax.fori_loop(0, count, store, 0)


def attend_kernel(which, seqs, length, len_ref, x_ref, wqkv_ref, qb_ref, vb_ref, qkv_ref, p_ref, ctx_ref, score_ref, prob_ref):
    step = pl.program_id(0)
    x = x_ref[...]
    qkv_ref[:, :WIDTH] = (dot(x, wqkv_ref[:, :WIDTH]) + vector(qb_ref, which)).astype(bf16)
    qkv_ref[:, WIDTH : 2 * WIDTH] = dot(x, wqkv_ref[:, WIDTH : 2 * WIDTH]).astype(bf16)
    qkv_ref[:, 2 * WIDTH :] = (dot(x, wqkv_ref[:, 2 * WIDTH :]) + vector(vb_ref, which)).astype(bf16)
    stack_rows = HEADS * length
    for s in range(seqs):
        span = slice(s * length, (s + 1) * length)
        stack = slice(s * stack_rows, (s + 1) * stack_rows)
        size = len_ref[step * seqs + s]
        queries = qkv_ref[span, :WIDTH]
        for h in range(HEADS):
            start = s * stack_rows + h * length
            score_ref[start : start + length, :] = dot_nt(one_head(queries, h), qkv_ref[span, WIDTH : 2 * WIDTH])

            def softmax(row):
                here = pl.ds(start + row, min(SOFT, length))
                prob = masked_softmax(score_ref[here, :], size)
                p_ref[here, :] = prob
                prob_ref[here, :] = prob.astype(bf16)

            row_loop(length, min(SOFT, length), softmax)
        ctx_ref[span, :] = pick_heads(dot(prob_ref[stack, :], qkv_ref[span, 2 * WIDTH :]), length).astype(bf16)


def forward_phase(
    which, seqs, length, first,
    len_ref, x_ref, wo_ref, ob_ref, g1_ref, b1_ref, w1_ref, hb_ref, w2_ref, fb_ref, g2_ref, b2_ref,
    out_ref, ctx_ref, n1_ref, r1_ref, nb_ref, gp_ref, act_ref, n2_ref, r2_ref, wide_ref,
):
    rows = seqs * length
    n2_ref[...] = dot(ctx_ref[...], wo_ref[...])
    ob, g1, b1 = vector(ob_ref, which), vector(g1_ref, which), vector(b1_ref, which)

    def first_norm(row):
        here = pl.ds(row, NORM)
        unit, inverse = normalize(x_ref[here, :].astype(f32) + (n2_ref[here, :] + ob))
        n1_ref[here, :] = unit
        r1_ref[here, :] = inverse
        nb_ref[here, :] = (unit * g1 + b1).astype(bf16)

    row_loop(rows, NORM, first_norm)
    hb = vector(hb_ref, which)
    for j in range(BLOCKS):
        lanes = slice(j * WIDTH, (j + 1) * WIDTH)
        wide_ref[:, lanes] = dot(nb_ref[...], w1_ref[:, lanes])

        def gelu(row):
            here = pl.ds(row, GELU)
            active, slope = gelu_parts(wide_ref[here, lanes] + hb[:, lanes])
            act_ref[here, lanes] = active
            gp_ref[here, lanes] = slope

        row_loop(rows, GELU, gelu)
    n2_ref[...] = dot(act_ref[...], w2_ref[...])
    fb, g2, b2 = vector(fb_ref, which), vector(g2_ref, which), vector(b2_ref, which)
    for s in range(seqs):
        size = len_ref[first + s]

        def second_norm(row):
            here = pl.ds(s * length + row, NORM)
            unit, inverse = normalize((n1_ref[here, :] * g1 + b1) + (n2_ref[here, :] + fb))
            n2_ref[here, :] = unit
            r2_ref[here, :] = inverse
            position = row + lax.broadcasted_iota(jnp.int32, (NORM, WIDTH), 0)
            out_ref[here, :] = jnp.where(position < size, unit * g2 + b2, 0.0).astype(bf16)

        row_loop(length, NORM, second_norm)


def add_row(vec_ref, row, values):
    vec_ref[row : row + 1, :] = vec_ref[row : row + 1, :] + jnp.sum(values, axis=0, keepdims=True)


def ffn_phase(which, seqs, length, first, len_ref, cls_ref, cot_ref, n2_ref, r2_ref, gp_ref, w2_ref, g2_ref, two_ref, gffn_ref, gpre_ref, vec_ref, wide_ref):
    g2 = vector(g2_ref, which)
    for s in range(seqs):
        size = len_ref[first + s]
        cls_row = cls_ref[pl.ds(first + s, 1), :]

        def norm_back(row):
            here = pl.ds(s * length + row, NORM)
            position = row + lax.broadcasted_iota(jnp.int32, (NORM, WIDTH), 0)
            grad = cot_ref[here, :].astype(f32) + jnp.where(position == 0, cls_row, 0.0)
            grad = jnp.where(position < size, grad, 0.0)
            unit = n2_ref[here, :]
            scaled = grad * g2
            first_mean = jnp.mean(scaled, axis=1, keepdims=True)
            second_mean = jnp.mean(scaled * unit, axis=1, keepdims=True)
            two = r2_ref[here, :] * (scaled - first_mean - unit * second_mean)
            low = two.astype(bf16)
            two_ref[here, :] = two
            gffn_ref[here, :] = low
            add_row(vec_ref, FFN_GAIN, grad * unit)
            add_row(vec_ref, FFN_SHIFT, grad)
            add_row(vec_ref, DOWN_BIAS, low.astype(f32))

        row_loop(length, NORM, norm_back)
    for j in range(BLOCKS):
        lanes = slice(j * WIDTH, (j + 1) * WIDTH)
        wide_ref[:, lanes] = dot_nt(gffn_ref[...], w2_ref[lanes, :])

        def gelu_back(row):
            here = pl.ds(row, GELU)
            low = (wide_ref[here, lanes] * gp_ref[here, lanes]).astype(bf16)
            gpre_ref[here, lanes] = low
            add_row(vec_ref, UP_BIAS + j, low.astype(f32))

        row_loop(seqs * length, GELU, gelu_back)


def attn_norm_phase(which, rows, gpre_ref, w1_ref, two_ref, n1_ref, r1_ref, g1_ref, wo_ref, one_ref, gatt_ref, dctx_ref, vec_ref):
    one_ref[...] = dot_nt(gpre_ref[...], w1_ref[...])
    g1 = vector(g1_ref, which)

    def norm_back(row):
        here = pl.ds(row, NORM)
        grad = two_ref[here, :] + one_ref[here, :]
        unit = n1_ref[here, :]
        scaled = grad * g1
        first_mean = jnp.mean(scaled, axis=1, keepdims=True)
        second_mean = jnp.mean(scaled * unit, axis=1, keepdims=True)
        one = r1_ref[here, :] * (scaled - first_mean - unit * second_mean)
        low = one.astype(bf16)
        one_ref[here, :] = one
        gatt_ref[here, :] = low
        add_row(vec_ref, ATTN_GAIN, grad * unit)
        add_row(vec_ref, ATTN_SHIFT, grad)
        add_row(vec_ref, PROJ_BIAS, low.astype(f32))

    row_loop(rows, NORM, norm_back)
    dctx_ref[...] = dot_nt(gatt_ref[...], wo_ref[...]).astype(bf16)


def attn_core_phase(seqs, length, dctx_ref, qkv_ref, p_ref, gqkv_ref, vec_ref, dp_ref, ds_ref, pb_ref):
    stack_rows = HEADS * length
    for s in range(seqs):
        span = slice(s * length, (s + 1) * length)
        stack = slice(s * stack_rows, (s + 1) * stack_rows)
        contexts = [one_head(dctx_ref[span, :], h) for h in range(HEADS)]
        for h in range(HEADS):
            start = s * stack_rows + h * length
            dp_ref[start : start + length, :] = dot_nt(contexts[h], qkv_ref[span, 2 * WIDTH :])

            def softmax_back(row):
                here = pl.ds(start + row, min(SOFT, length))
                prob = p_ref[here, :]
                grad = dp_ref[here, :]
                inner = jnp.sum(prob * grad, axis=1, keepdims=True)
                ds_ref[here, :] = (prob * (grad - inner)).astype(bf16)
                pb_ref[here, :] = prob.astype(bf16)

            row_loop(length, min(SOFT, length), softmax_back)
        context = jnp.concatenate(contexts, axis=0)
        queries = stack_heads(qkv_ref[span, :WIDTH])
        grad_q = (pick_heads(dot(ds_ref[stack, :], qkv_ref[span, WIDTH : 2 * WIDTH]), length) * score_scale).astype(bf16)
        gqkv_ref[span, :WIDTH] = grad_q
        add_row(vec_ref, QUERY_BIAS, grad_q.astype(f32))
        gqkv_ref[span, WIDTH : 2 * WIDTH] = (dot_tn(ds_ref[stack, :], queries) * score_scale).astype(bf16)
        grad_v = dot_tn(pb_ref[stack, :], context).astype(bf16)
        gqkv_ref[span, 2 * WIDTH :] = grad_v
        add_row(vec_ref, VALUE_BIAS, grad_v.astype(f32))


def layer_kernel(
    which, steps, seqs, length,
    bit_ref, len_ref, cls_ref, x_ref, cot_ref, qkv_ref, p_ref, ctx_ref,
    wqkv_ref, wo_ref, ob_ref, g1_ref, b1_ref, w1_ref, hb_ref, w2_ref, fb_ref, g2_ref, b2_ref,
    out_ref, gx_ref, keep_ref, send_ref,
    acc_ref, vec_ref, n1_ref, r1_ref, nb_ref, gp_ref, act_ref, n2_ref, r2_ref,
    wide_ref, score_ref, prob_ref, two_ref, gffn_ref, gpre_ref, one_ref, gatt_ref, dctx_ref, gqkv_ref, ds_ref,
):
    rows = seqs * length
    step = pl.program_id(0)

    def start():
        vec_ref[...] = jnp.zeros_like(vec_ref)
        if steps > 1:
            acc_ref[...] = jnp.zeros_like(acc_ref)

    if steps > 1:
        pl.when(step == 0)(start)
    else:
        start()

    def add_block(block, value):
        if steps > 1:
            acc_ref[block_rows(block), :] += value
        else:
            acc_ref[block_rows(block), :] = value

    forward_phase(
        which, seqs, length, step * seqs,
        len_ref, x_ref, wo_ref, ob_ref, g1_ref, b1_ref, w1_ref, hb_ref, w2_ref, fb_ref, g2_ref, b2_ref,
        out_ref, ctx_ref, n1_ref, r1_ref, nb_ref, gp_ref, act_ref, n2_ref, r2_ref, wide_ref,
    )
    ffn_phase(which, seqs, length, step * seqs, len_ref, cls_ref, cot_ref, n2_ref, r2_ref, gp_ref, w2_ref, g2_ref, two_ref, gffn_ref, gpre_ref, vec_ref, wide_ref)
    for j in range(BLOCKS):
        lanes = slice(j * WIDTH, (j + 1) * WIDTH)
        add_block(DOWN_BLOCK + j, dot_tn(act_ref[:, lanes], gffn_ref[...]))
        add_block(UP_BLOCK + j, dot_tn(nb_ref[...], gpre_ref[:, lanes]))
    attn_norm_phase(which, rows, gpre_ref, w1_ref, two_ref, n1_ref, r1_ref, g1_ref, wo_ref, one_ref, gatt_ref, dctx_ref, vec_ref)
    add_block(PROJ_BLOCK, dot_tn(ctx_ref[...], gatt_ref[...]))
    attn_core_phase(seqs, length, dctx_ref, qkv_ref, p_ref, gqkv_ref, vec_ref, score_ref, ds_ref, prob_ref)
    for j in range(3):
        add_block(QKV_BLOCK + j, dot_tn(x_ref[...], gqkv_ref[:, j * WIDTH : (j + 1) * WIDTH]))
    gx_ref[...] = (one_ref[...] + dot_nt(gqkv_ref[...], wqkv_ref[...])).astype(bf16)

    def finish():
        acc_ref[VECTOR_START : VECTOR_START + VECTOR_ROWS, :] = vec_ref[...]
        if steps == 1:
            acc_ref[VECTOR_START + VECTOR_ROWS : HALF, :] = jnp.zeros((HALF - VECTOR_START - VECTOR_ROWS, WIDTH), f32)
            acc_ref[HALF + 6 * WIDTH :, :] = jnp.zeros((HALF - 6 * WIDTH, WIDTH), f32)
        keep = pl.multiple_of(bit_ref[0] * HALF, HALF)
        send = pl.multiple_of((1 - bit_ref[0]) * HALF, HALF)
        keep_ref[...] = acc_ref[pl.ds(keep, HALF), :].astype(bf16)
        send_ref[...] = acc_ref[pl.ds(send, HALF), :].astype(bf16)

    if steps > 1:
        pl.when(step == steps - 1)(finish)
    else:
        finish()


def loss_kernel(local, me_ref, all_ref, hot_ref, own_hot_ref, loss_ref, gq_ref, gp_ref, q_ref, p_ref):
    count = all_ref.shape[0]
    me = me_ref[0]
    wide = all_ref[...].astype(f32)
    q_ref[...] = wide[:, :PAD].reshape(count * PAD, WIDTH).astype(bf16)
    p_ref[...] = wide[:, PAD:].reshape(count * PAD, WIDTH).astype(bf16)
    own_q = all_ref[me][:PAD]
    own_p = all_ref[me][PAD:]
    logits = dot_nt(own_q, p_ref[...]) * score_scale
    column = lax.broadcasted_iota(jnp.int32, logits.shape, 1)
    logits = jnp.where(column % PAD < local, logits, masked_score)
    top = jnp.max(logits, axis=1, keepdims=True)
    total = top + jnp.log(jnp.sum(jnp.exp(logits - top), axis=1, keepdims=True))
    hot = (column == own_hot_ref[...]).astype(f32)
    loss_ref[...] = jnp.broadcast_to(total - jnp.sum(logits * hot, axis=1, keepdims=True), loss_ref.shape)
    grad = (jnp.exp(logits - total) - hot).astype(bf16)
    gq_ref[...] = dot(grad, p_ref[...]) * score_scale
    gp_ref[...] = jnp.zeros_like(gp_ref)
    block = 256 if count * PAD % 256 == 0 else count * PAD

    def part(index, carry):
        start = pl.multiple_of(index * block, block)
        queries = q_ref[pl.ds(start, block), :]
        scores = dot_nt(p_ref[...], queries) * score_scale
        row = lax.broadcasted_iota(jnp.int32, scores.shape, 0)
        scores = jnp.where(row % PAD < local, scores, masked_score)
        peak = jnp.max(scores, axis=0, keepdims=True)
        sums = peak + jnp.log(jnp.sum(jnp.exp(scores - peak), axis=0, keepdims=True))
        own = dot_nt(own_p, queries) * score_scale
        own_row = lax.broadcasted_iota(jnp.int32, own.shape, 0)
        own_lane = lax.broadcasted_iota(jnp.int32, own.shape, 1)
        own_hits = (own_row + me * PAD == hot_ref[:, pl.ds(start, block)]).astype(f32)
        own_grad = jnp.where(own_lane % PAD < local, jnp.exp(own - sums) - own_hits, 0.0)
        gp_ref[...] += dot(own_grad.astype(bf16), queries) * score_scale
        return carry

    lax.fori_loop(0, count * PAD // block, part, 0)


def combine_kernel(radix, digit_ref, *refs):
    total_ref = refs[-1]
    sends = refs[-1 - (radix - 1) : -1]
    keep_ref = refs[-1 - radix]
    pieces = refs[: -1 - radix]
    total = pieces[0][...].astype(f32)
    for piece in pieces[1:]:
        total = total + piece[...].astype(f32)
    total_ref[...] = total
    part = total_ref.shape[0] // radix
    digit = digit_ref[0]

    def section(which):
        return total_ref[pl.ds(pl.multiple_of(which * part, part), part), :].astype(bf16)

    keep_ref[...] = section(digit)
    for step, ref in enumerate(sends, start=1):
        ref[...] = section(digit ^ step)


VECTOR_OUTS = (QUERY_BIAS, VALUE_BIAS, PROJ_BIAS, ATTN_GAIN, ATTN_SHIFT, DOWN_BIAS, FFN_GAIN, FFN_SHIFT)


def unpack_kernel(bit_ref, q_own_ref, q_ref, p_own_ref, p_ref, qkv_ref, proj_ref, up_ref, down_ref, up_bias_ref, *refs):
    vector_refs, whole_ref = refs[:-1], refs[-1]
    own = pl.multiple_of(bit_ref[0] * HALF, HALF)
    other = pl.multiple_of((1 - bit_ref[0]) * HALF, HALF)
    tails = []
    for which, (own_ref, other_ref) in enumerate(((q_own_ref, q_ref), (p_own_ref, p_ref))):
        ref = whole_ref.at[which]
        ref[pl.ds(own, HALF), :] = own_ref[...]
        ref[pl.ds(other, HALF), :] = other_ref[...]
        for j in range(3):
            qkv_ref[which, :, j * WIDTH : (j + 1) * WIDTH] = ref[block_rows(QKV_BLOCK + j), :].astype(f32)
        proj_ref[which] = ref[block_rows(PROJ_BLOCK), :].astype(f32)
        for j in range(BLOCKS):
            up_ref[which, :, j * WIDTH : (j + 1) * WIDTH] = ref[block_rows(UP_BLOCK + j), :].astype(f32)
            down_ref[which, j * WIDTH : (j + 1) * WIDTH, :] = ref[block_rows(DOWN_BLOCK + j), :].astype(f32)
        tails.append(ref[VECTOR_START : VECTOR_START + VECTOR_ROWS, :].astype(f32))
    for row, ref in zip(VECTOR_OUTS, vector_refs):
        for which in range(2):
            ref[which : which + 1, :] = tails[which][row : row + 1]
    for j in range(BLOCKS):
        for which in range(2):
            up_bias_ref[which : which + 1, j * WIDTH : (j + 1) * WIDTH] = tails[which][UP_BIAS + j : UP_BIAS + j + 1]


def smem():
    return pl.BlockSpec(memory_space=pltpu.SMEM)


def whole(shape):
    return pl.BlockSpec(shape, lambda i: (0,) * len(shape))


def rows_of(rows, columns):
    return pl.BlockSpec((rows, columns), lambda i: (i, 0))


def part_of(which, shape):
    return pl.BlockSpec((None,) + shape, lambda i: (which, 0, 0))


def params():
    return pltpu.CompilerParams(vmem_limit_bytes=24 * 1024 * 1024)


def shape(dims, kind):
    return jax.ShapeDtypeStruct(dims, kind)


def cost(flops, moved):
    return pl.CostEstimate(flops=flops, bytes_accessed=moved, transcendentals=0)


def pair(columns):
    return whole((2, columns))


def in_hbm(values):
    return pltpu.with_memory_space_constraint(values, pltpu.HBM)


def attend(which, steps, seqs, length, lengths, x, weights):
    wqkv, qb, vb, *_ = weights
    rows = seqs * length
    total = steps * rows
    stack = seqs * HEADS * length
    return pl.pallas_call(
        functools.partial(attend_kernel, which, seqs, length),
        out_shape=[
            pltpu.HBM((total, 3 * WIDTH), bf16), pltpu.HBM((steps * stack, length), f32), pltpu.HBM((total, WIDTH), bf16),
        ],
        grid=(steps,),
        in_specs=[smem(), rows_of(rows, WIDTH), part_of(which, (WIDTH, 3 * WIDTH)), pair(WIDTH), pair(WIDTH)],
        out_specs=[rows_of(rows, 3 * WIDTH), rows_of(stack, length), rows_of(rows, WIDTH)],
        scratch_shapes=[pltpu.VMEM((stack, length), f32), pltpu.VMEM((stack, length), bf16)],
        compiler_params=params(),
        cost_estimate=cost(total * 2 * 400000, total * 6000),
        name="attend",
    )(lengths, in_hbm(x), in_hbm(wqkv), in_hbm(qb), in_hbm(vb))


def layer(which, steps, seqs, length, bit, lengths, cls_grad, x, cot, attended, weights):
    rows = seqs * length
    total = steps * rows
    stack = seqs * HEADS * length
    wqkv, _, _, *rest = weights
    return pl.pallas_call(
        functools.partial(layer_kernel, which, steps, seqs, length),
        out_shape=[shape((total, WIDTH), bf16), shape((total, WIDTH), bf16), shape((HALF, WIDTH), bf16), shape((HALF, WIDTH), bf16)],
        grid=(steps,),
        in_specs=[
            smem(), smem(), whole((PAD, WIDTH)), rows_of(rows, WIDTH), rows_of(rows, WIDTH),
            rows_of(rows, 3 * WIDTH), rows_of(stack, length), rows_of(rows, WIDTH),
            part_of(which, (WIDTH, 3 * WIDTH)), part_of(which, (WIDTH, WIDTH)),
            pair(WIDTH), pair(WIDTH), pair(WIDTH), part_of(which, (WIDTH, HIDDEN)), pair(HIDDEN),
            part_of(which, (HIDDEN, WIDTH)), pair(WIDTH), pair(WIDTH), pair(WIDTH),
        ],
        out_specs=[rows_of(rows, WIDTH), rows_of(rows, WIDTH), whole((HALF, WIDTH)), whole((HALF, WIDTH))],
        scratch_shapes=[
            pltpu.VMEM((GROUP_ROWS, WIDTH), f32), pltpu.VMEM((VECTOR_ROWS, WIDTH), f32),
            pltpu.VMEM((rows, WIDTH), f32), pltpu.VMEM((rows, 1), f32), pltpu.VMEM((rows, WIDTH), bf16),
            pltpu.VMEM((rows, HIDDEN), f32), pltpu.VMEM((rows, HIDDEN), bf16), pltpu.VMEM((rows, WIDTH), f32),
            pltpu.VMEM((rows, 1), f32), pltpu.VMEM((rows, HIDDEN), f32), pltpu.VMEM((stack, length), f32),
            pltpu.VMEM((stack, length), bf16), pltpu.VMEM((rows, WIDTH), f32), pltpu.VMEM((rows, WIDTH), bf16),
            pltpu.VMEM((rows, HIDDEN), bf16), pltpu.VMEM((rows, WIDTH), f32), pltpu.VMEM((rows, WIDTH), bf16),
            pltpu.VMEM((rows, WIDTH), bf16), pltpu.VMEM((rows, 3 * WIDTH), bf16), pltpu.VMEM((stack, length), bf16),
        ],
        compiler_params=params(),
        cost_estimate=cost(total * 6 * 800000, total * 4000),
        name="layer",
    )(bit, lengths, cls_grad, in_hbm(x), in_hbm(cot), *[in_hbm(member) for member in attended], in_hbm(wqkv), *[in_hbm(member) for member in rest])


def stages(count):
    masks = []
    bit = 1
    while bit < count:
        masks.append(bit)
        bit = bit * 2
    groups = [masks[:1]]
    rest = masks[1:]
    while rest:
        groups.append(rest[:2])
        rest = rest[2:]
    return [group for group in groups if group]


def partner_send(values, mask, count):
    return lax.ppermute(values, "dp", [(i, i ^ mask) for i in range(count)])


def combos(group):
    return [index * group[0] for index in range(1, 2 ** len(group))]


def combine(pieces, group, me):
    radix = 2 ** len(group)
    digit = (me // group[0]) % radix
    rows = pieces[0].shape[0]
    part = rows // radix
    if part % 8 == 0:
        return pl.pallas_call(
            functools.partial(combine_kernel, radix),
            out_shape=[shape((part, WIDTH), bf16)] * radix,
            grid=(1,),
            in_specs=[smem()] + [whole((rows, WIDTH))] * len(pieces),
            out_specs=[whole((part, WIDTH))] * radix,
            scratch_shapes=[pltpu.VMEM((rows, WIDTH), f32)],
            compiler_params=params(),
            name="combine",
        )(digit.reshape(1), *pieces)
    total = pieces[0].astype(f32)
    for piece in pieces[1:]:
        total = total + piece.astype(f32)
    split = total.astype(bf16).reshape(radix, part, WIDTH)
    return [lax.dynamic_index_in_dim(split, digit ^ step, 0, keepdims=False) for step in range(radix)]


def send_parts(cut, group, count):
    own, *sends = cut
    return [own] + [partner_send(part, mask, count) for part, mask in zip(sends, combos(group))]


def send_whole(buffer, group, count):
    return [buffer] + [partner_send(buffer, mask, count) for mask in combos(group)]


def add_up(pieces):
    total = pieces[0].astype(f32)
    for piece in pieces[1:]:
        total = total + piece.astype(f32)
    return total.astype(bf16)


def join(pieces, group, me):
    radix = 2 ** len(group)
    digit = (me // group[0]) % radix
    joined = jnp.zeros((radix,) + pieces[0].shape, pieces[0].dtype)
    for step, piece in enumerate(pieces):
        joined = lax.dynamic_update_index_in_dim(joined, piece, digit ^ step, 0)
    return joined.reshape((radix * pieces[0].shape[0],) + pieces[0].shape[1:])


def prepare(pieces, done, following, me):
    reduce_done, group_done = done
    reduce_next, group_next = following
    if not reduce_done:
        return [join(pieces, group_done, me)]
    if reduce_next:
        return combine(pieces, group_next, me)
    return [add_up(pieces)]


def launch(operands, stage, count):
    reduce, group = stage
    return send_parts(operands, group, count) if reduce else send_whole(operands[0], group, count)


def after(values, *others):
    return list(lax.optimization_barrier((tuple(values), others))[0])


def body(questions, passages, cot_questions, cot_passages, len_questions, len_passages, positive, *weights):
    local = questions.shape[0]
    question_length = questions.shape[1]
    passage_length = passages.shape[1]
    count = positive.shape[0] // local
    me = lax.axis_index("dp")
    bit = (me % 2).reshape(1)
    x_q = questions.reshape(-1, WIDTH)
    x_p = passages.reshape(-1, WIDTH)
    own_cls = pl.pallas_call(
        functools.partial(first_kernel, local),
        out_shape=shape((count, 2 * PAD, WIDTH), bf16),
        grid=(1,),
        in_specs=[smem(), smem(), whole(x_q.shape), whole(x_p.shape)] + [whole(member.shape) for member in weights],
        out_specs=whole((count, 2 * PAD, WIDTH)),
        scratch_shapes=[pltpu.VMEM(x_q.shape, bf16)] * 2 + [pltpu.VMEM(x_p.shape, bf16)] * 2,
        compiler_params=params(),
        name="first",
    )(len_questions, len_passages, in_hbm(x_q), in_hbm(x_p), *[in_hbm(member) for member in weights])
    own_cls, x_q, x_p = lax.optimization_barrier((own_cls, x_q, x_p))
    all_cls = lax.all_to_all(own_cls, "dp", 0, 0, tiled=True)
    attended_p = attend(1, local, 1, passage_length, len_passages, x_p, weights)
    attended_q = attend(0, 1, local, question_length, len_questions, x_q, weights)
    (all_cls,) = after([all_cls], attended_p[2], attended_q[2])
    slots = positive // local * PAD + positive % local
    slots = jnp.pad(slots.reshape(count, local), ((0, 0), (0, PAD - local)), constant_values=-1)
    own_slots = lax.dynamic_slice_in_dim(slots, me, 1, axis=0).reshape(PAD, 1)
    loss, grad_cls_q, grad_cls_p = pl.pallas_call(
        functools.partial(loss_kernel, local),
        out_shape=[shape((PAD, 128), f32), shape((PAD, WIDTH), f32), shape((PAD, WIDTH), f32)],
        grid=(1,),
        in_specs=[smem(), whole((count, 2 * PAD, WIDTH)), whole((1, count * PAD)), whole((PAD, 1))],
        out_specs=[whole((PAD, 128)), whole((PAD, WIDTH)), whole((PAD, WIDTH))],
        scratch_shapes=[pltpu.VMEM((count * PAD, WIDTH), bf16), pltpu.VMEM((count * PAD, WIDTH), bf16)],
        compiler_params=params(),
        name="loss",
    )(me.reshape(1), all_cls, slots.reshape(1, -1), own_slots)
    loss_rows = loss[:local, 0]
    out_q, grad_q, keep_q, send_q = layer(
        0, 1, local, question_length, bit, len_questions, grad_cls_q, x_q, cot_questions.reshape(-1, WIDTH),
        attended_q, weights,
    )
    groups = stages(count)
    steps = [(True, group) for group in groups] + [(False, group) for group in groups[::-1]]
    operands_q = prepare([keep_q, partner_send(send_q, groups[0][0], count)], steps[0], steps[1], me)
    (grad_cls_p,) = after([grad_cls_p], *operands_q)
    pieces_q = launch(operands_q, steps[1], count)
    out_p, grad_p, keep_p, send_p = layer(
        1, local, 1, passage_length, bit, len_passages, grad_cls_p, x_p, cot_passages.reshape(-1, WIDTH),
        attended_p, weights,
    )
    (send_p,) = after([send_p], *pieces_q)
    pieces_p = [keep_p, partner_send(send_p, groups[0][0], count)]
    for place in range(len(steps)):
        if place > 0:
            pieces_p = after(pieces_p, *operands_q)
            operands_p = prepare(pieces_p, steps[place - 1], steps[place], me)
            pieces_p = launch(operands_p, steps[place], count)
            pieces_q = after(pieces_q, *operands_p)
        if place + 2 < len(steps):
            operands_q = prepare(pieces_q, steps[place + 1], steps[place + 2], me)
            pieces_q = launch(operands_q, steps[place + 2], count)
    (own_q, other_q), (own_p, other_p) = pieces_q, pieces_p
    dims = [(2, WIDTH, 3 * WIDTH), (2, WIDTH, WIDTH), (2, WIDTH, HIDDEN), (2, HIDDEN, WIDTH), (2, HIDDEN)]
    dims += [(2, WIDTH)] * len(VECTOR_OUTS)
    d_qkv, d_proj, d_up, d_down, up_bias, query_bias, value_bias, proj_bias, gain_a, shift_a, down_bias, gain_f, shift_f = pl.pallas_call(
        unpack_kernel,
        out_shape=[shape(d, f32) for d in dims],
        grid=(1,),
        in_specs=[smem()] + [whole((HALF, WIDTH))] * 4,
        out_specs=[whole(d) for d in dims],
        scratch_shapes=[pltpu.VMEM((2, GROUP_ROWS, WIDTH), bf16)],
        compiler_params=params(),
        name="unpack",
    )(bit, own_q, other_q, own_p, other_p)
    return (
        loss_rows, out_q.reshape(questions.shape), out_p.reshape(passages.shape),
        grad_q.reshape(questions.shape), grad_p.reshape(passages.shape),
        d_qkv, query_bias, value_bias, d_proj, proj_bias, gain_a, shift_a, d_up, up_bias, d_down,
        down_bias, gain_f, shift_f,
    )


def solution(mesh):
    split = P("dp", None, None)
    return jax.shard_map(
        body,
        mesh=mesh,
        in_specs=(split, split, split, split, P("dp"), P("dp")) + (P(),) * 14,
        out_specs=(P("dp"), split, split, split, split) + (P(),) * 13,
        check_vma=False,
    )
```

```python
import functools

import jax
import jax.numpy as jnp
from jax import lax
from jax.experimental import pallas as pl
from jax.experimental.pallas import tpu as pltpu
from jax.sharding import PartitionSpec as P

HEAD_DIM = 64
WIDTH = 256
HEADS = WIDTH // HEAD_DIM
HIDDEN = 1024
BLOCKS = HIDDEN // WIDTH
PAD = 8
VECTOR_ROWS = 16
HALF = 6 * WIDTH + 128
GROUP_ROWS = 2 * HALF
SOFT = 128
NORM = 64
GELU = 32
ln_eps = 1e-06
score_scale = 0.125
masked_score = -1e30
f32 = jnp.float32
bf16 = jnp.bfloat16

QUERY_BIAS, VALUE_BIAS, PROJ_BIAS, ATTN_GAIN, ATTN_SHIFT, DOWN_BIAS, FFN_GAIN, FFN_SHIFT = range(8)
UP_BIAS = 8


def dot(a, b):
    return lax.dot_general(a, b, (((1,), (0,)), ((), ())), preferred_element_type=f32)


def dot_nt(a, b):
    return lax.dot_general(a, b, (((1,), (1,)), ((), ())), preferred_element_type=f32)


def dot_tn(a, b):
    return lax.dot_general(a, b, (((0,), (0,)), ((), ())), preferred_element_type=f32)


def row_loop(rows, chunk, step):
    def body(index, carry):
        step(pl.multiple_of(index * chunk, chunk))
        return carry

    lax.fori_loop(0, rows // chunk, body, 0, unroll=rows // chunk)


def vector(ref, which):
    return ref[...].astype(f32)[which : which + 1]


def lane_head(rows):
    return lax.broadcasted_iota(jnp.int32, (rows, WIDTH), 1) // HEAD_DIM


def stack_heads(values):
    head = lane_head(values.shape[0])
    wide = values.astype(f32)
    return jnp.concatenate(
        [jnp.where(head == h, wide, 0.0).astype(bf16) for h in range(HEADS)], axis=0
    )


def one_head(values, h):
    return jnp.where(lane_head(values.shape[0]) == h, values.astype(f32), 0.0).astype(bf16)


def pick_heads(stacked, rows):
    head = lane_head(rows)
    result = stacked[:rows]
    for h in range(1, HEADS):
        result = jnp.where(head == h, stacked[h * rows : (h + 1) * rows], result)
    return result


def block_rows(block):
    start = block * WIDTH if block < 6 else HALF + (block - 6) * WIDTH
    return slice(start, start + WIDTH)


VECTOR_START = 6 * WIDTH
QKV_BLOCK, PROJ_BLOCK, UP_BLOCK, DOWN_BLOCK = 0, 3, 4, 8


def normalize(value):
    centered = value - jnp.mean(value, axis=1, keepdims=True)
    inverse = lax.rsqrt(jnp.mean(centered * centered, axis=1, keepdims=True) + ln_eps)
    return centered * inverse, inverse


def masked_softmax(scores, size):
    part = scores * score_scale
    key = lax.broadcasted_iota(jnp.int32, part.shape, 1)
    part = jnp.where(key < size, part, masked_score)
    part = jnp.exp(part - jnp.max(part, axis=1, keepdims=True))
    return part * (1.0 / jnp.sum(part, axis=1, keepdims=True))


def gelu_parts(value):
    cumulative = 0.5 + 0.5 * lax.erf(value * 0.7071067811865476)
    density = jnp.exp(value * value * -0.5) * 0.3989422804014327
    return (value * cumulative).astype(bf16), cumulative + value * density


def first_rows(which, seqs, length, len_ref, x_ref, k_ref, v_ref, wqkv_ref, qb_ref, vb_ref, wo_ref, ob_ref, g1_ref, b1_ref, w1_ref, hb_ref, w2_ref, fb_ref, g2_ref, b2_ref):
    rows = seqs * length
    firsts = [x_ref[s * length : s * length + 16, :].astype(f32)[:1] for s in range(seqs)]
    filler = jnp.zeros((PAD - seqs, WIDTH), f32)
    inputs = jnp.concatenate(firsts + [filler], axis=0)
    queries = (dot(inputs.astype(bf16), wqkv_ref[:, :WIDTH]) + vector(qb_ref, which)).astype(bf16).astype(f32)
    x = x_ref[...]
    k_ref[:rows, :] = dot(x, wqkv_ref[:, WIDTH : 2 * WIDTH]).astype(bf16)
    v_ref[:rows, :] = (dot(x, wqkv_ref[:, 2 * WIDTH :]) + vector(vb_ref, which)).astype(bf16)
    own_lanes = lane_head(PAD) == lax.broadcasted_iota(jnp.int32, (PAD, WIDTH), 0)
    contexts = []
    for s in range(seqs):
        span = slice(s * length, (s + 1) * length)
        heads = jnp.where(own_lanes, queries[s : s + 1], 0.0).astype(bf16)
        prob = masked_softmax(dot_nt(heads, k_ref[span, :]), len_ref[s])
        context = dot(prob.astype(bf16), v_ref[span, :])
        contexts.append(jnp.sum(jnp.where(own_lanes, context, 0.0), axis=0, keepdims=True))
    context = jnp.concatenate(contexts + [filler], axis=0).astype(bf16)
    value = inputs + (dot(context, wo_ref[...]) + vector(ob_ref, which))
    unit, _ = normalize(value)
    normed = unit * vector(g1_ref, which) + vector(b1_ref, which)
    hidden = dot(normed.astype(bf16), w1_ref[...]) + vector(hb_ref, which)
    active, _ = gelu_parts(hidden)
    value = normed + (dot(active, w2_ref[...]) + vector(fb_ref, which))
    unit, _ = normalize(value)
    result = unit * vector(g2_ref, which) + vector(b2_ref, which)
    row = lax.broadcasted_iota(jnp.int32, result.shape, 0)
    return jnp.where(row < seqs, result, 0.0)


def first_kernel(seqs, lq_ref, lp_ref, xq_ref, xp_ref, *refs):
    weights, (cls_ref, k_ref, v_ref, passage_ref) = refs[:13], refs[13:]

    @pl.when(pl.program_id(0) == 0)
    def _():
        passage_ref[...] = first_rows(1, seqs, xp_ref.shape[0] // seqs, lp_ref, xp_ref, k_ref, v_ref, *weights)

    @pl.when(pl.program_id(0) == 1)
    def _():
        question = first_rows(0, seqs, xq_ref.shape[0] // seqs, lq_ref, xq_ref, k_ref, v_ref, *weights)
        both = jnp.concatenate([question, passage_ref[...]], axis=0).astype(bf16)

        def store(i, carry):
            cls_ref[i] = both
            return carry

        lax.fori_loop(0, cls_ref.shape[0], store, 0)


def attend_kernel(which, seqs, length, len_ref, x_ref, wqkv_ref, qb_ref, vb_ref, qkv_ref, p_ref, ctx_ref, score_ref, prob_ref):
    step = pl.program_id(0)
    x = x_ref[...]
    qkv_ref[:, :WIDTH] = (dot(x, wqkv_ref[:, :WIDTH]) + vector(qb_ref, which)).astype(bf16)
    qkv_ref[:, WIDTH : 2 * WIDTH] = dot(x, wqkv_ref[:, WIDTH : 2 * WIDTH]).astype(bf16)
    qkv_ref[:, 2 * WIDTH :] = (dot(x, wqkv_ref[:, 2 * WIDTH :]) + vector(vb_ref, which)).astype(bf16)
    stack_rows = HEADS * length
    for s in range(seqs):
        span = slice(s * length, (s + 1) * length)
        stack = slice(s * stack_rows, (s + 1) * stack_rows)
        size = len_ref[step * seqs + s]
        queries = qkv_ref[span, :WIDTH]
        for h in range(HEADS):
            start = s * stack_rows + h * length
            score_ref[start : start + length, :] = dot_nt(one_head(queries, h), qkv_ref[span, WIDTH : 2 * WIDTH])

            def softmax(row):
                here = pl.ds(start + row, min(SOFT, length))
                prob = masked_softmax(score_ref[here, :], size)
                p_ref[here, :] = prob
                prob_ref[here, :] = prob.astype(bf16)

            row_loop(length, min(SOFT, length), softmax)
        ctx_ref[span, :] = pick_heads(dot(prob_ref[stack, :], qkv_ref[span, 2 * WIDTH :]), length).astype(bf16)


def forward_phase(
    which, seqs, length, first,
    len_ref, x_ref, wo_ref, ob_ref, g1_ref, b1_ref, w1_ref, hb_ref, w2_ref, fb_ref, g2_ref, b2_ref,
    out_ref, ctx_ref, n1_ref, r1_ref, nb_ref, gp_ref, act_ref, n2_ref, r2_ref, wide_ref,
):
    rows = seqs * length
    n2_ref[...] = dot(ctx_ref[...], wo_ref[...])
    ob, g1, b1 = vector(ob_ref, which), vector(g1_ref, which), vector(b1_ref, which)

    def first_norm(row):
        here = pl.ds(row, NORM)
        unit, inverse = normalize(x_ref[here, :].astype(f32) + (n2_ref[here, :] + ob))
        n1_ref[here, :] = unit
        r1_ref[here, :] = inverse
        nb_ref[here, :] = (unit * g1 + b1).astype(bf16)

    row_loop(rows, NORM, first_norm)
    hb = vector(hb_ref, which)
    for j in range(BLOCKS):
        lanes = slice(j * WIDTH, (j + 1) * WIDTH)
        wide_ref[:, lanes] = dot(nb_ref[...], w1_ref[:, lanes])

        def gelu(row):
            here = pl.ds(row, GELU)
            active, slope = gelu_parts(wide_ref[here, lanes] + hb[:, lanes])
            act_ref[here, lanes] = active
            gp_ref[here, lanes] = slope

        row_loop(rows, GELU, gelu)
    n2_ref[...] = dot(act_ref[...], w2_ref[...])
    fb, g2, b2 = vector(fb_ref, which), vector(g2_ref, which), vector(b2_ref, which)
    for s in range(seqs):
        size = len_ref[first + s]

        def second_norm(row):
            here = pl.ds(s * length + row, NORM)
            unit, inverse = normalize((n1_ref[here, :] * g1 + b1) + (n2_ref[here, :] + fb))
            n2_ref[here, :] = unit
            r2_ref[here, :] = inverse
            position = row + lax.broadcasted_iota(jnp.int32, (NORM, WIDTH), 0)
            out_ref[here, :] = jnp.where(position < size, unit * g2 + b2, 0.0).astype(bf16)

        row_loop(length, NORM, second_norm)


def add_row(vec_ref, row, values):
    vec_ref[row : row + 1, :] = vec_ref[row : row + 1, :] + jnp.sum(values, axis=0, keepdims=True)


def ffn_phase(which, seqs, length, first, len_ref, cls_ref, cot_ref, n2_ref, r2_ref, gp_ref, w2_ref, g2_ref, two_ref, gffn_ref, gpre_ref, vec_ref, wide_ref):
    g2 = vector(g2_ref, which)
    for s in range(seqs):
        size = len_ref[first + s]
        cls_row = cls_ref[pl.ds(first + s, 1), :]

        def norm_back(row):
            here = pl.ds(s * length + row, NORM)
            position = row + lax.broadcasted_iota(jnp.int32, (NORM, WIDTH), 0)
            grad = cot_ref[here, :].astype(f32) + jnp.where(position == 0, cls_row, 0.0)
            grad = jnp.where(position < size, grad, 0.0)
            unit = n2_ref[here, :]
            scaled = grad * g2
            first_mean = jnp.mean(scaled, axis=1, keepdims=True)
            second_mean = jnp.mean(scaled * unit, axis=1, keepdims=True)
            two = r2_ref[here, :] * (scaled - first_mean - unit * second_mean)
            low = two.astype(bf16)
            two_ref[here, :] = two
            gffn_ref[here, :] = low
            add_row(vec_ref, FFN_GAIN, grad * unit)
            add_row(vec_ref, FFN_SHIFT, grad)
            add_row(vec_ref, DOWN_BIAS, low.astype(f32))

        row_loop(length, NORM, norm_back)
    for j in range(BLOCKS):
        lanes = slice(j * WIDTH, (j + 1) * WIDTH)
        wide_ref[:, lanes] = dot_nt(gffn_ref[...], w2_ref[lanes, :])

        def gelu_back(row):
            here = pl.ds(row, GELU)
            low = (wide_ref[here, lanes] * gp_ref[here, lanes]).astype(bf16)
            gpre_ref[here, lanes] = low
            add_row(vec_ref, UP_BIAS + j, low.astype(f32))

        row_loop(seqs * length, GELU, gelu_back)


def attn_norm_phase(which, rows, gpre_ref, w1_ref, two_ref, n1_ref, r1_ref, g1_ref, wo_ref, one_ref, gatt_ref, dctx_ref, vec_ref):
    one_ref[...] = dot_nt(gpre_ref[...], w1_ref[...])
    g1 = vector(g1_ref, which)

    def norm_back(row):
        here = pl.ds(row, NORM)
        grad = two_ref[here, :] + one_ref[here, :]
        unit = n1_ref[here, :]
        scaled = grad * g1
        first_mean = jnp.mean(scaled, axis=1, keepdims=True)
        second_mean = jnp.mean(scaled * unit, axis=1, keepdims=True)
        one = r1_ref[here, :] * (scaled - first_mean - unit * second_mean)
        low = one.astype(bf16)
        one_ref[here, :] = one
        gatt_ref[here, :] = low
        add_row(vec_ref, ATTN_GAIN, grad * unit)
        add_row(vec_ref, ATTN_SHIFT, grad)
        add_row(vec_ref, PROJ_BIAS, low.astype(f32))

    row_loop(rows, NORM, norm_back)
    dctx_ref[...] = dot_nt(gatt_ref[...], wo_ref[...]).astype(bf16)


def attn_core_phase(seqs, length, dctx_ref, qkv_ref, p_ref, gqkv_ref, vec_ref, dp_ref, ds_ref, pb_ref):
    stack_rows = HEADS * length
    for s in range(seqs):
        span = slice(s * length, (s + 1) * length)
        stack = slice(s * stack_rows, (s + 1) * stack_rows)
        contexts = [one_head(dctx_ref[span, :], h) for h in range(HEADS)]
        for h in range(HEADS):
            start = s * stack_rows + h * length
            dp_ref[start : start + length, :] = dot_nt(contexts[h], qkv_ref[span, 2 * WIDTH :])

            def softmax_back(row):
                here = pl.ds(start + row, min(SOFT, length))
                prob = p_ref[here, :]
                grad = dp_ref[here, :]
                inner = jnp.sum(prob * grad, axis=1, keepdims=True)
                ds_ref[here, :] = (prob * (grad - inner)).astype(bf16)
                pb_ref[here, :] = prob.astype(bf16)

            row_loop(length, min(SOFT, length), softmax_back)
        context = jnp.concatenate(contexts, axis=0)
        queries = stack_heads(qkv_ref[span, :WIDTH])
        grad_q = (pick_heads(dot(ds_ref[stack, :], qkv_ref[span, WIDTH : 2 * WIDTH]), length) * score_scale).astype(bf16)
        gqkv_ref[span, :WIDTH] = grad_q
        add_row(vec_ref, QUERY_BIAS, grad_q.astype(f32))
        gqkv_ref[span, WIDTH : 2 * WIDTH] = (dot_tn(ds_ref[stack, :], queries) * score_scale).astype(bf16)
        grad_v = dot_tn(pb_ref[stack, :], context).astype(bf16)
        gqkv_ref[span, 2 * WIDTH :] = grad_v
        add_row(vec_ref, VALUE_BIAS, grad_v.astype(f32))


def layer_kernel(
    which, steps, seqs, length,
    bit_ref, len_ref, cls_ref, x_ref, cot_ref, qkv_ref, p_ref, ctx_ref,
    wqkv_ref, wo_ref, ob_ref, g1_ref, b1_ref, w1_ref, hb_ref, w2_ref, fb_ref, g2_ref, b2_ref,
    out_ref, gx_ref, keep_ref, send_ref,
    acc_ref, vec_ref, n1_ref, r1_ref, nb_ref, gp_ref, act_ref, n2_ref, r2_ref,
    wide_ref, score_ref, prob_ref, two_ref, gffn_ref, gpre_ref, one_ref, gatt_ref, dctx_ref, gqkv_ref, ds_ref,
):
    rows = seqs * length
    step = pl.program_id(0)

    def start():
        vec_ref[...] = jnp.zeros_like(vec_ref)
        if steps > 1:
            acc_ref[...] = jnp.zeros_like(acc_ref)

    if steps > 1:
        pl.when(step == 0)(start)
    else:
        start()

    def add_block(block, value):
        if steps > 1:
            acc_ref[block_rows(block), :] += value
        else:
            acc_ref[block_rows(block), :] = value

    forward_phase(
        which, seqs, length, step * seqs,
        len_ref, x_ref, wo_ref, ob_ref, g1_ref, b1_ref, w1_ref, hb_ref, w2_ref, fb_ref, g2_ref, b2_ref,
        out_ref, ctx_ref, n1_ref, r1_ref, nb_ref, gp_ref, act_ref, n2_ref, r2_ref, wide_ref,
    )
    ffn_phase(which, seqs, length, step * seqs, len_ref, cls_ref, cot_ref, n2_ref, r2_ref, gp_ref, w2_ref, g2_ref, two_ref, gffn_ref, gpre_ref, vec_ref, wide_ref)
    for j in range(BLOCKS):
        lanes = slice(j * WIDTH, (j + 1) * WIDTH)
        add_block(DOWN_BLOCK + j, dot_tn(act_ref[:, lanes], gffn_ref[...]))
        add_block(UP_BLOCK + j, dot_tn(nb_ref[...], gpre_ref[:, lanes]))
    attn_norm_phase(which, rows, gpre_ref, w1_ref, two_ref, n1_ref, r1_ref, g1_ref, wo_ref, one_ref, gatt_ref, dctx_ref, vec_ref)
    add_block(PROJ_BLOCK, dot_tn(ctx_ref[...], gatt_ref[...]))
    attn_core_phase(seqs, length, dctx_ref, qkv_ref, p_ref, gqkv_ref, vec_ref, score_ref, ds_ref, prob_ref)
    for j in range(3):
        add_block(QKV_BLOCK + j, dot_tn(x_ref[...], gqkv_ref[:, j * WIDTH : (j + 1) * WIDTH]))
    gx_ref[...] = (one_ref[...] + dot_nt(gqkv_ref[...], wqkv_ref[...])).astype(bf16)

    def finish():
        acc_ref[VECTOR_START : VECTOR_START + VECTOR_ROWS, :] = vec_ref[...]
        if steps == 1:
            acc_ref[VECTOR_START + VECTOR_ROWS : HALF, :] = jnp.zeros((HALF - VECTOR_START - VECTOR_ROWS, WIDTH), f32)
            acc_ref[HALF + 6 * WIDTH :, :] = jnp.zeros((HALF - 6 * WIDTH, WIDTH), f32)
        keep = pl.multiple_of(bit_ref[0] * HALF, HALF)
        send = pl.multiple_of((1 - bit_ref[0]) * HALF, HALF)
        keep_ref[...] = acc_ref[pl.ds(keep, HALF), :].astype(bf16)
        send_ref[...] = acc_ref[pl.ds(send, HALF), :].astype(bf16)

    if steps > 1:
        pl.when(step == steps - 1)(finish)
    else:
        finish()


def loss_kernel(local, me_ref, all_ref, hot_ref, own_hot_ref, loss_ref, gq_ref, gp_ref, q_ref, p_ref):
    count = all_ref.shape[0]
    me = me_ref[0]
    wide = all_ref[...].astype(f32)
    q_ref[...] = wide[:, :PAD].reshape(count * PAD, WIDTH).astype(bf16)
    p_ref[...] = wide[:, PAD:].reshape(count * PAD, WIDTH).astype(bf16)
    own_q = all_ref[me][:PAD]
    own_p = all_ref[me][PAD:]
    logits = dot_nt(own_q, p_ref[...]) * score_scale
    column = lax.broadcasted_iota(jnp.int32, logits.shape, 1)
    logits = jnp.where(column % PAD < local, logits, masked_score)
    top = jnp.max(logits, axis=1, keepdims=True)
    total = top + jnp.log(jnp.sum(jnp.exp(logits - top), axis=1, keepdims=True))
    hot = (column == own_hot_ref[...]).astype(f32)
    loss_ref[...] = jnp.broadcast_to(total - jnp.sum(logits * hot, axis=1, keepdims=True), loss_ref.shape)
    grad = (jnp.exp(logits - total) - hot).astype(bf16)
    gq_ref[...] = dot(grad, p_ref[...]) * score_scale
    gp_ref[...] = jnp.zeros_like(gp_ref)
    block = 256 if count * PAD % 256 == 0 else count * PAD

    def part(index, carry):
        start = pl.multiple_of(index * block, block)
        queries = q_ref[pl.ds(start, block), :]
        scores = dot_nt(p_ref[...], queries) * score_scale
        row = lax.broadcasted_iota(jnp.int32, scores.shape, 0)
        scores = jnp.where(row % PAD < local, scores, masked_score)
        peak = jnp.max(scores, axis=0, keepdims=True)
        sums = peak + jnp.log(jnp.sum(jnp.exp(scores - peak), axis=0, keepdims=True))
        own = dot_nt(own_p, queries) * score_scale
        own_row = lax.broadcasted_iota(jnp.int32, own.shape, 0)
        own_lane = lax.broadcasted_iota(jnp.int32, own.shape, 1)
        own_hits = (own_row + me * PAD == hot_ref[:, pl.ds(start, block)]).astype(f32)
        own_grad = jnp.where(own_lane % PAD < local, jnp.exp(own - sums) - own_hits, 0.0)
        gp_ref[...] += dot(own_grad.astype(bf16), queries) * score_scale
        return carry

    lax.fori_loop(0, count * PAD // block, part, 0)


def combine_kernel(radix, digit_ref, *refs):
    total_ref = refs[-1]
    sends = refs[-1 - (radix - 1) : -1]
    keep_ref = refs[-1 - radix]
    pieces = refs[: -1 - radix]
    total = pieces[0][...].astype(f32)
    for piece in pieces[1:]:
        total = total + piece[...].astype(f32)
    total_ref[...] = total
    part = total_ref.shape[0] // radix
    digit = digit_ref[0]

    def section(which):
        return total_ref[pl.ds(pl.multiple_of(which * part, part), part), :].astype(bf16)

    keep_ref[...] = section(digit)
    for step, ref in enumerate(sends, start=1):
        ref[...] = section(digit ^ step)


VECTOR_OUTS = (QUERY_BIAS, VALUE_BIAS, PROJ_BIAS, ATTN_GAIN, ATTN_SHIFT, DOWN_BIAS, FFN_GAIN, FFN_SHIFT)


def unpack_kernel(bit_ref, q_own_ref, q_ref, p_own_ref, p_ref, qkv_ref, proj_ref, up_ref, down_ref, up_bias_ref, *refs):
    vector_refs, whole_ref = refs[:-1], refs[-1]
    own = pl.multiple_of(bit_ref[0] * HALF, HALF)
    other = pl.multiple_of((1 - bit_ref[0]) * HALF, HALF)
    tails = []
    for which, (own_ref, other_ref) in enumerate(((q_own_ref, q_ref), (p_own_ref, p_ref))):
        ref = whole_ref.at[which]
        ref[pl.ds(own, HALF), :] = own_ref[...]
        ref[pl.ds(other, HALF), :] = other_ref[...]
        for j in range(3):
            qkv_ref[which, :, j * WIDTH : (j + 1) * WIDTH] = ref[block_rows(QKV_BLOCK + j), :].astype(f32)
        proj_ref[which] = ref[block_rows(PROJ_BLOCK), :].astype(f32)
        for j in range(BLOCKS):
            up_ref[which, :, j * WIDTH : (j + 1) * WIDTH] = ref[block_rows(UP_BLOCK + j), :].astype(f32)
            down_ref[which, j * WIDTH : (j + 1) * WIDTH, :] = ref[block_rows(DOWN_BLOCK + j), :].astype(f32)
        tails.append(ref[VECTOR_START : VECTOR_START + VECTOR_ROWS, :].astype(f32))
    for row, ref in zip(VECTOR_OUTS, vector_refs):
        for which in range(2):
            ref[which : which + 1, :] = tails[which][row : row + 1]
    for j in range(BLOCKS):
        for which in range(2):
            up_bias_ref[which : which + 1, j * WIDTH : (j + 1) * WIDTH] = tails[which][UP_BIAS + j : UP_BIAS + j + 1]


def smem():
    return pl.BlockSpec(memory_space=pltpu.SMEM)


def whole(shape):
    return pl.BlockSpec(shape, lambda i: (0,) * len(shape))


def rows_of(rows, columns):
    return pl.BlockSpec((rows, columns), lambda i: (i, 0))


def part_of(which, shape):
    return pl.BlockSpec((None,) + shape, lambda i: (which, 0, 0))


def params():
    return pltpu.CompilerParams(vmem_limit_bytes=24 * 1024 * 1024)


def shape(dims, kind):
    return jax.ShapeDtypeStruct(dims, kind)


def cost(flops, moved):
    return pl.CostEstimate(flops=flops, bytes_accessed=moved, transcendentals=0)


def pair(columns):
    return whole((2, columns))


def in_hbm(values):
    return pltpu.with_memory_space_constraint(values, pltpu.HBM)


def first_call(count, local, len_questions, len_passages, x_q, x_p, weights):
    def matrix(rows, columns):
        return pl.BlockSpec((None, rows, columns), lambda i: (1 - i, 0, 0))

    specs = [
        matrix(WIDTH, 3 * WIDTH), pair(WIDTH), pair(WIDTH), matrix(WIDTH, WIDTH), pair(WIDTH), pair(WIDTH), pair(WIDTH),
        matrix(WIDTH, HIDDEN), pair(HIDDEN), matrix(HIDDEN, WIDTH), pair(WIDTH), pair(WIDTH), pair(WIDTH),
    ]
    return pl.pallas_call(
        functools.partial(first_kernel, local),
        out_shape=shape((count, 2 * PAD, WIDTH), bf16),
        grid=(2,),
        in_specs=[smem(), smem(), whole(x_q.shape), whole(x_p.shape)] + specs,
        out_specs=whole((count, 2 * PAD, WIDTH)),
        scratch_shapes=[pltpu.VMEM(x_p.shape, bf16), pltpu.VMEM(x_p.shape, bf16), pltpu.VMEM((PAD, WIDTH), f32)],
        compiler_params=params(),
        name="first",
    )(in_hbm(len_questions), in_hbm(len_passages), in_hbm(x_q), in_hbm(x_p), *[in_hbm(member) for member in weights])


def attend(which, steps, seqs, length, lengths, x, weights):
    wqkv, qb, vb, *_ = weights
    rows = seqs * length
    total = steps * rows
    stack = seqs * HEADS * length
    return pl.pallas_call(
        functools.partial(attend_kernel, which, seqs, length),
        out_shape=[
            pltpu.HBM((total, 3 * WIDTH), bf16), pltpu.HBM((steps * stack, length), f32), pltpu.HBM((total, WIDTH), bf16),
        ],
        grid=(steps,),
        in_specs=[smem(), rows_of(rows, WIDTH), part_of(which, (WIDTH, 3 * WIDTH)), pair(WIDTH), pair(WIDTH)],
        out_specs=[rows_of(rows, 3 * WIDTH), rows_of(stack, length), rows_of(rows, WIDTH)],
        scratch_shapes=[pltpu.VMEM((stack, length), f32), pltpu.VMEM((stack, length), bf16)],
        compiler_params=params(),
        cost_estimate=cost(total * 2 * 400000, total * 6000),
        name="attend",
    )(lengths, in_hbm(x), in_hbm(wqkv), in_hbm(qb), in_hbm(vb))


def layer(which, steps, seqs, length, bit, lengths, cls_grad, x, cot, attended, weights):
    rows = seqs * length
    total = steps * rows
    stack = seqs * HEADS * length
    wqkv, _, _, *rest = weights
    return pl.pallas_call(
        functools.partial(layer_kernel, which, steps, seqs, length),
        out_shape=[shape((total, WIDTH), bf16), shape((total, WIDTH), bf16), shape((HALF, WIDTH), bf16), shape((HALF, WIDTH), bf16)],
        grid=(steps,),
        in_specs=[
            smem(), smem(), whole((PAD, WIDTH)), rows_of(rows, WIDTH), rows_of(rows, WIDTH),
            rows_of(rows, 3 * WIDTH), rows_of(stack, length), rows_of(rows, WIDTH),
            part_of(which, (WIDTH, 3 * WIDTH)), part_of(which, (WIDTH, WIDTH)),
            pair(WIDTH), pair(WIDTH), pair(WIDTH), part_of(which, (WIDTH, HIDDEN)), pair(HIDDEN),
            part_of(which, (HIDDEN, WIDTH)), pair(WIDTH), pair(WIDTH), pair(WIDTH),
        ],
        out_specs=[rows_of(rows, WIDTH), rows_of(rows, WIDTH), whole((HALF, WIDTH)), whole((HALF, WIDTH))],
        scratch_shapes=[
            pltpu.VMEM((GROUP_ROWS, WIDTH), f32), pltpu.VMEM((VECTOR_ROWS, WIDTH), f32),
            pltpu.VMEM((rows, WIDTH), f32), pltpu.VMEM((rows, 1), f32), pltpu.VMEM((rows, WIDTH), bf16),
            pltpu.VMEM((rows, HIDDEN), f32), pltpu.VMEM((rows, HIDDEN), bf16), pltpu.VMEM((rows, WIDTH), f32),
            pltpu.VMEM((rows, 1), f32), pltpu.VMEM((rows, HIDDEN), f32), pltpu.VMEM((stack, length), f32),
            pltpu.VMEM((stack, length), bf16), pltpu.VMEM((rows, WIDTH), f32), pltpu.VMEM((rows, WIDTH), bf16),
            pltpu.VMEM((rows, HIDDEN), bf16), pltpu.VMEM((rows, WIDTH), f32), pltpu.VMEM((rows, WIDTH), bf16),
            pltpu.VMEM((rows, WIDTH), bf16), pltpu.VMEM((rows, 3 * WIDTH), bf16), pltpu.VMEM((stack, length), bf16),
        ],
        compiler_params=params(),
        cost_estimate=cost(total * 6 * 800000, total * 4000),
        name="layer",
    )(bit, lengths, cls_grad, in_hbm(x), in_hbm(cot), *[in_hbm(member) for member in attended], in_hbm(wqkv), *[in_hbm(member) for member in rest])


def stages(count):
    masks = []
    bit = 1
    while bit < count:
        masks.append(bit)
        bit = bit * 2
    groups = [masks[:1]]
    rest = masks[1:]
    while rest:
        groups.append(rest[:2])
        rest = rest[2:]
    return [group for group in groups if group]


def partner_send(values, mask, count):
    return lax.ppermute(values, "dp", [(i, i ^ mask) for i in range(count)])


def combos(group):
    return [index * group[0] for index in range(1, 2 ** len(group))]


def combine(pieces, group, me):
    radix = 2 ** len(group)
    digit = (me // group[0]) % radix
    rows = pieces[0].shape[0]
    part = rows // radix
    if part % 8 == 0:
        return pl.pallas_call(
            functools.partial(combine_kernel, radix),
            out_shape=[shape((part, WIDTH), bf16)] * radix,
            grid=(1,),
            in_specs=[smem()] + [whole((rows, WIDTH))] * len(pieces),
            out_specs=[whole((part, WIDTH))] * radix,
            scratch_shapes=[pltpu.VMEM((rows, WIDTH), f32)],
            compiler_params=params(),
            name="combine",
        )(digit.reshape(1), *pieces)
    total = pieces[0].astype(f32)
    for piece in pieces[1:]:
        total = total + piece.astype(f32)
    split = total.astype(bf16).reshape(radix, part, WIDTH)
    return [lax.dynamic_index_in_dim(split, digit ^ step, 0, keepdims=False) for step in range(radix)]


def send_parts(cut, group, count):
    own, *sends = cut
    return [own] + [partner_send(part, mask, count) for part, mask in zip(sends, combos(group))]


def send_whole(buffer, group, count):
    return [buffer] + [partner_send(buffer, mask, count) for mask in combos(group)]


def add_up(pieces):
    total = pieces[0].astype(f32)
    for piece in pieces[1:]:
        total = total + piece.astype(f32)
    return total.astype(bf16)


def join(pieces, group, me):
    radix = 2 ** len(group)
    digit = (me // group[0]) % radix
    joined = jnp.zeros((radix,) + pieces[0].shape, pieces[0].dtype)
    for step, piece in enumerate(pieces):
        joined = lax.dynamic_update_index_in_dim(joined, piece, digit ^ step, 0)
    return joined.reshape((radix * pieces[0].shape[0],) + pieces[0].shape[1:])


def prepare(pieces, done, following, me):
    reduce_done, group_done = done
    reduce_next, group_next = following
    if not reduce_done:
        return [join(pieces, group_done, me)]
    if reduce_next:
        return combine(pieces, group_next, me)
    return [add_up(pieces)]


def launch(operands, stage, count):
    reduce, group = stage
    return send_parts(operands, group, count) if reduce else send_whole(operands[0], group, count)


def after(values, *others):
    return list(lax.optimization_barrier((tuple(values), others))[0])


def body(questions, passages, cot_questions, cot_passages, len_questions, len_passages, positive, *weights):
    local = questions.shape[0]
    question_length = questions.shape[1]
    passage_length = passages.shape[1]
    count = positive.shape[0] // local
    me = lax.axis_index("dp")
    bit = (me % 2).reshape(1)
    x_q = questions.reshape(-1, WIDTH)
    x_p = passages.reshape(-1, WIDTH)
    own_cls = first_call(count, local, len_questions, len_passages, x_q, x_p, weights)
    own_cls, x_q, x_p = lax.optimization_barrier((own_cls, x_q, x_p))
    all_cls = lax.all_to_all(own_cls, "dp", 0, 0, tiled=True)
    attended_p = attend(1, local, 1, passage_length, len_passages, x_p, weights)
    attended_q = attend(0, 1, local, question_length, len_questions, x_q, weights)
    (all_cls,) = after([all_cls], attended_p[2], attended_q[2])
    slots = positive // local * PAD + positive % local
    slots = jnp.pad(slots.reshape(count, local), ((0, 0), (0, PAD - local)), constant_values=-1)
    own_slots = lax.dynamic_slice_in_dim(slots, me, 1, axis=0).reshape(PAD, 1)
    loss, grad_cls_q, grad_cls_p = pl.pallas_call(
        functools.partial(loss_kernel, local),
        out_shape=[shape((PAD, 128), f32), shape((PAD, WIDTH), f32), shape((PAD, WIDTH), f32)],
        grid=(1,),
        in_specs=[smem(), whole((count, 2 * PAD, WIDTH)), whole((1, count * PAD)), whole((PAD, 1))],
        out_specs=[whole((PAD, 128)), whole((PAD, WIDTH)), whole((PAD, WIDTH))],
        scratch_shapes=[pltpu.VMEM((count * PAD, WIDTH), bf16), pltpu.VMEM((count * PAD, WIDTH), bf16)],
        compiler_params=params(),
        name="loss",
    )(me.reshape(1), all_cls, slots.reshape(1, -1), own_slots)
    loss_rows = loss[:local, 0]
    out_q, grad_q, keep_q, send_q = layer(
        0, 1, local, question_length, bit, len_questions, grad_cls_q, x_q, cot_questions.reshape(-1, WIDTH),
        attended_q, weights,
    )
    groups = stages(count)
    steps = [(True, group) for group in groups] + [(False, group) for group in groups[::-1]]
    operands_q = prepare([keep_q, partner_send(send_q, groups[0][0], count)], steps[0], steps[1], me)
    (grad_cls_p,) = after([grad_cls_p], *operands_q)
    pieces_q = launch(operands_q, steps[1], count)
    out_p, grad_p, keep_p, send_p = layer(
        1, local, 1, passage_length, bit, len_passages, grad_cls_p, x_p, cot_passages.reshape(-1, WIDTH),
        attended_p, weights,
    )
    (send_p,) = after([send_p], *pieces_q)
    pieces_p = [keep_p, partner_send(send_p, groups[0][0], count)]
    for place in range(len(steps)):
        if place > 0:
            pieces_p = after(pieces_p, *operands_q)
            operands_p = prepare(pieces_p, steps[place - 1], steps[place], me)
            pieces_p = launch(operands_p, steps[place], count)
            pieces_q = after(pieces_q, *operands_p)
        if place + 2 < len(steps):
            operands_q = prepare(pieces_q, steps[place + 1], steps[place + 2], me)
            pieces_q = launch(operands_q, steps[place + 2], count)
    (own_q, other_q), (own_p, other_p) = pieces_q, pieces_p
    dims = [(2, WIDTH, 3 * WIDTH), (2, WIDTH, WIDTH), (2, WIDTH, HIDDEN), (2, HIDDEN, WIDTH), (2, HIDDEN)]
    dims += [(2, WIDTH)] * len(VECTOR_OUTS)
    d_qkv, d_proj, d_up, d_down, up_bias, query_bias, value_bias, proj_bias, gain_a, shift_a, down_bias, gain_f, shift_f = pl.pallas_call(
        unpack_kernel,
        out_shape=[shape(d, f32) for d in dims],
        grid=(1,),
        in_specs=[smem()] + [whole((HALF, WIDTH))] * 4,
        out_specs=[whole(d) for d in dims],
        scratch_shapes=[pltpu.VMEM((2, GROUP_ROWS, WIDTH), bf16)],
        compiler_params=params(),
        name="unpack",
    )(bit, own_q, other_q, own_p, other_p)
    return (
        loss_rows, out_q.reshape(questions.shape), out_p.reshape(passages.shape),
        grad_q.reshape(questions.shape), grad_p.reshape(passages.shape),
        d_qkv, query_bias, value_bias, d_proj, proj_bias, gain_a, shift_a, d_up, up_bias, d_down,
        down_bias, gain_f, shift_f,
    )


def solution(mesh):
    split = P("dp", None, None)
    return jax.shard_map(
        body,
        mesh=mesh,
        in_specs=(split, split, split, split, P("dp"), P("dp")) + (P(),) * 14,
        out_specs=(P("dp"), split, split, split, split) + (P(),) * 13,
        check_vma=False,
    )
```

```python
import functools

import jax
import jax.numpy as jnp
from jax import lax
from jax.experimental import pallas as pl
from jax.experimental.pallas import tpu as pltpu
from jax.sharding import PartitionSpec as P

HEAD_DIM = 64
WIDTH = 256
HEADS = WIDTH // HEAD_DIM
HIDDEN = 1024
BLOCKS = HIDDEN // WIDTH
PAD = 8
VECTOR_ROWS = 16
HALF = 6 * WIDTH + 128
GROUP_ROWS = 2 * HALF
SOFT = 128
NORM = 64
GELU = 32
ln_eps = 1e-06
score_scale = 0.125
masked_score = -1e30
f32 = jnp.float32
bf16 = jnp.bfloat16

QUERY_BIAS, VALUE_BIAS, PROJ_BIAS, ATTN_GAIN, ATTN_SHIFT, DOWN_BIAS, FFN_GAIN, FFN_SHIFT = range(8)
UP_BIAS = 8


def dot(a, b):
    return lax.dot_general(a, b, (((1,), (0,)), ((), ())), preferred_element_type=f32)


def dot_nt(a, b):
    return lax.dot_general(a, b, (((1,), (1,)), ((), ())), preferred_element_type=f32)


def dot_tn(a, b):
    return lax.dot_general(a, b, (((0,), (0,)), ((), ())), preferred_element_type=f32)


def row_loop(rows, chunk, step):
    def body(index, carry):
        step(pl.multiple_of(index * chunk, chunk))
        return carry

    lax.fori_loop(0, rows // chunk, body, 0, unroll=rows // chunk)


def vector(ref, which):
    return ref[...].astype(f32)[which : which + 1]


def lane_head(rows):
    return lax.broadcasted_iota(jnp.int32, (rows, WIDTH), 1) // HEAD_DIM


def stack_heads(values):
    head = lane_head(values.shape[0])
    wide = values.astype(f32)
    return jnp.concatenate(
        [jnp.where(head == h, wide, 0.0).astype(bf16) for h in range(HEADS)], axis=0
    )


def one_head(values, h):
    return jnp.where(lane_head(values.shape[0]) == h, values.astype(f32), 0.0).astype(bf16)


def pick_heads(stacked, rows):
    head = lane_head(rows)
    result = stacked[:rows]
    for h in range(1, HEADS):
        result = jnp.where(head == h, stacked[h * rows : (h + 1) * rows], result)
    return result


def block_rows(block):
    start = block * WIDTH if block < 6 else HALF + (block - 6) * WIDTH
    return slice(start, start + WIDTH)


VECTOR_START = 6 * WIDTH
QKV_BLOCK, PROJ_BLOCK, UP_BLOCK, DOWN_BLOCK = 0, 3, 4, 8


def normalize(value):
    centered = value - jnp.mean(value, axis=1, keepdims=True)
    inverse = lax.rsqrt(jnp.mean(centered * centered, axis=1, keepdims=True) + ln_eps)
    return centered * inverse, inverse


def masked_softmax(scores, size):
    part = scores * score_scale
    key = lax.broadcasted_iota(jnp.int32, part.shape, 1)
    part = jnp.where(key < size, part, masked_score)
    part = jnp.exp(part - jnp.max(part, axis=1, keepdims=True))
    return part * (1.0 / jnp.sum(part, axis=1, keepdims=True))


def gelu_parts(value):
    cumulative = 0.5 + 0.5 * lax.erf(value * 0.7071067811865476)
    density = jnp.exp(value * value * -0.5) * 0.3989422804014327
    return (value * cumulative).astype(bf16), cumulative + value * density


def first_kernel(
    seqs, lq_ref, lp_ref, xq_ref, xp_ref,
    wqkv_ref, qb_ref, vb_ref, wo_ref, ob_ref, g1_ref, b1_ref, w1_ref, hb_ref, w2_ref, fb_ref, g2_ref, b2_ref,
    cls_ref,
    kq_ref, vq_ref, kp_ref, vp_ref,
):
    sides = ((0, xq_ref, kq_ref, vq_ref, lq_ref), (1, xp_ref, kp_ref, vp_ref, lp_ref))
    filler = jnp.zeros((PAD - seqs, WIDTH), f32)
    inputs = []
    for which, x_ref, *_ in sides:
        length = x_ref.shape[0] // seqs
        firsts = [x_ref[s * length : s * length + 16, :].astype(f32)[:1] for s in range(seqs)]
        inputs.append(jnp.concatenate(firsts + [filler], axis=0))
    own_lanes = lane_head(PAD) == lax.broadcasted_iota(jnp.int32, (PAD, WIDTH), 0)
    queries = [
        (dot(inputs[which].astype(bf16), wqkv_ref[which, :, :WIDTH]) + vector(qb_ref, which)).astype(bf16).astype(f32)
        for which in range(2)
    ]
    for which, x_ref, k_ref, v_ref, _ in sides:
        x = x_ref[...]
        k_ref[...] = dot(x, wqkv_ref[which, :, WIDTH : 2 * WIDTH]).astype(bf16)
        v_ref[...] = (dot(x, wqkv_ref[which, :, 2 * WIDTH :]) + vector(vb_ref, which)).astype(bf16)
    context = []
    for which, x_ref, k_ref, v_ref, len_ref in sides:
        length = x_ref.shape[0] // seqs
        spans = [slice(s * length, (s + 1) * length) for s in range(seqs)]
        scores, sizes = [], []
        for s, span in enumerate(spans):
            heads = jnp.where(own_lanes, queries[which][s : s + 1], 0.0).astype(bf16)
            scores.append(dot_nt(heads, k_ref[span, :]))
            sizes.append(jnp.full((PAD, length), len_ref[s], jnp.int32))
        prob = masked_softmax(jnp.concatenate(scores, axis=0), jnp.concatenate(sizes, axis=0)).astype(f32)
        rows = []
        for s, span in enumerate(spans):
            mixed = dot(prob[s * PAD : (s + 1) * PAD].astype(bf16), v_ref[span, :])
            rows.append(jnp.sum(jnp.where(own_lanes, mixed, 0.0), axis=0, keepdims=True))
        context.append(jnp.concatenate(rows + [filler], axis=0).astype(bf16))
    normed = []
    for which in range(2):
        value = inputs[which] + (dot(context[which], wo_ref[which]) + vector(ob_ref, which))
        unit, _ = normalize(value)
        normed.append(unit * vector(g1_ref, which) + vector(b1_ref, which))
    active = []
    for which in range(2):
        active.append(gelu_parts(dot(normed[which].astype(bf16), w1_ref[which]) + vector(hb_ref, which))[0])
    results = []
    for which in range(2):
        value = normed[which] + (dot(active[which], w2_ref[which]) + vector(fb_ref, which))
        unit, _ = normalize(value)
        result = unit * vector(g2_ref, which) + vector(b2_ref, which)
        row = lax.broadcasted_iota(jnp.int32, result.shape, 0)
        results.append(jnp.where(row < seqs, result, 0.0))
    both = jnp.concatenate(results, axis=0).astype(bf16)

    def store(i, carry):
        cls_ref[i] = both
        return carry

    lax.fori_loop(0, cls_ref.shape[0], store, 0)


def attend_kernel(which, seqs, length, len_ref, x_ref, wqkv_ref, qb_ref, vb_ref, qkv_ref, p_ref, ctx_ref, score_ref, prob_ref):
    step = pl.program_id(0)
    x = x_ref[...]
    qkv_ref[:, :WIDTH] = (dot(x, wqkv_ref[:, :WIDTH]) + vector(qb_ref, which)).astype(bf16)
    qkv_ref[:, WIDTH : 2 * WIDTH] = dot(x, wqkv_ref[:, WIDTH : 2 * WIDTH]).astype(bf16)
    qkv_ref[:, 2 * WIDTH :] = (dot(x, wqkv_ref[:, 2 * WIDTH :]) + vector(vb_ref, which)).astype(bf16)
    stack_rows = HEADS * length
    for s in range(seqs):
        span = slice(s * length, (s + 1) * length)
        stack = slice(s * stack_rows, (s + 1) * stack_rows)
        size = len_ref[step * seqs + s]
        queries = qkv_ref[span, :WIDTH]
        for h in range(HEADS):
            start = s * stack_rows + h * length
            score_ref[start : start + length, :] = dot_nt(one_head(queries, h), qkv_ref[span, WIDTH : 2 * WIDTH])

            def softmax(row):
                here = pl.ds(start + row, min(SOFT, length))
                prob = masked_softmax(score_ref[here, :], size)
                p_ref[here, :] = prob
                prob_ref[here, :] = prob.astype(bf16)

            row_loop(length, min(SOFT, length), softmax)
        ctx_ref[span, :] = pick_heads(dot(prob_ref[stack, :], qkv_ref[span, 2 * WIDTH :]), length).astype(bf16)


def forward_phase(
    which, seqs, length, first,
    len_ref, x_ref, wo_ref, ob_ref, g1_ref, b1_ref, w1_ref, hb_ref, w2_ref, fb_ref, g2_ref, b2_ref,
    out_ref, ctx_ref, n1_ref, r1_ref, nb_ref, gp_ref, act_ref, n2_ref, r2_ref, wide_ref,
):
    rows = seqs * length
    n2_ref[...] = dot(ctx_ref[...], wo_ref[...])
    ob, g1, b1 = vector(ob_ref, which), vector(g1_ref, which), vector(b1_ref, which)

    def first_norm(row):
        here = pl.ds(row, NORM)
        unit, inverse = normalize(x_ref[here, :].astype(f32) + (n2_ref[here, :] + ob))
        n1_ref[here, :] = unit
        r1_ref[here, :] = inverse
        nb_ref[here, :] = (unit * g1 + b1).astype(bf16)

    row_loop(rows, NORM, first_norm)
    hb = vector(hb_ref, which)
    for j in range(BLOCKS):
        lanes = slice(j * WIDTH, (j + 1) * WIDTH)
        wide_ref[:, lanes] = dot(nb_ref[...], w1_ref[:, lanes])

        def gelu(row):
            here = pl.ds(row, GELU)
            active, slope = gelu_parts(wide_ref[here, lanes] + hb[:, lanes])
            act_ref[here, lanes] = active
            gp_ref[here, lanes] = slope

        row_loop(rows, GELU, gelu)
    n2_ref[...] = dot(act_ref[...], w2_ref[...])
    fb, g2, b2 = vector(fb_ref, which), vector(g2_ref, which), vector(b2_ref, which)
    for s in range(seqs):
        size = len_ref[first + s]

        def second_norm(row):
            here = pl.ds(s * length + row, NORM)
            unit, inverse = normalize((n1_ref[here, :] * g1 + b1) + (n2_ref[here, :] + fb))
            n2_ref[here, :] = unit
            r2_ref[here, :] = inverse
            position = row + lax.broadcasted_iota(jnp.int32, (NORM, WIDTH), 0)
            out_ref[here, :] = jnp.where(position < size, unit * g2 + b2, 0.0).astype(bf16)

        row_loop(length, NORM, second_norm)


def add_row(vec_ref, row, values):
    vec_ref[row : row + 1, :] = vec_ref[row : row + 1, :] + jnp.sum(values, axis=0, keepdims=True)


def ffn_phase(which, seqs, length, first, len_ref, cls_ref, cot_ref, n2_ref, r2_ref, gp_ref, w2_ref, g2_ref, two_ref, gffn_ref, gpre_ref, vec_ref, wide_ref):
    g2 = vector(g2_ref, which)
    for s in range(seqs):
        size = len_ref[first + s]
        cls_row = cls_ref[pl.ds(first + s, 1), :]

        def norm_back(row):
            here = pl.ds(s * length + row, NORM)
            position = row + lax.broadcasted_iota(jnp.int32, (NORM, WIDTH), 0)
            grad = cot_ref[here, :].astype(f32) + jnp.where(position == 0, cls_row, 0.0)
            grad = jnp.where(position < size, grad, 0.0)
            unit = n2_ref[here, :]
            scaled = grad * g2
            first_mean = jnp.mean(scaled, axis=1, keepdims=True)
            second_mean = jnp.mean(scaled * unit, axis=1, keepdims=True)
            two = r2_ref[here, :] * (scaled - first_mean - unit * second_mean)
            low = two.astype(bf16)
            two_ref[here, :] = two
            gffn_ref[here, :] = low
            add_row(vec_ref, FFN_GAIN, grad * unit)
            add_row(vec_ref, FFN_SHIFT, grad)
            add_row(vec_ref, DOWN_BIAS, low.astype(f32))

        row_loop(length, NORM, norm_back)
    for j in range(BLOCKS):
        lanes = slice(j * WIDTH, (j + 1) * WIDTH)
        wide_ref[:, lanes] = dot_nt(gffn_ref[...], w2_ref[lanes, :])

        def gelu_back(row):
            here = pl.ds(row, GELU)
            low = (wide_ref[here, lanes] * gp_ref[here, lanes]).astype(bf16)
            gpre_ref[here, lanes] = low
            add_row(vec_ref, UP_BIAS + j, low.astype(f32))

        row_loop(seqs * length, GELU, gelu_back)


def attn_norm_phase(which, rows, gpre_ref, w1_ref, two_ref, n1_ref, r1_ref, g1_ref, wo_ref, one_ref, gatt_ref, dctx_ref, vec_ref):
    one_ref[...] = dot_nt(gpre_ref[...], w1_ref[...])
    g1 = vector(g1_ref, which)

    def norm_back(row):
        here = pl.ds(row, NORM)
        grad = two_ref[here, :] + one_ref[here, :]
        unit = n1_ref[here, :]
        scaled = grad * g1
        first_mean = jnp.mean(scaled, axis=1, keepdims=True)
        second_mean = jnp.mean(scaled * unit, axis=1, keepdims=True)
        one = r1_ref[here, :] * (scaled - first_mean - unit * second_mean)
        low = one.astype(bf16)
        one_ref[here, :] = one
        gatt_ref[here, :] = low
        add_row(vec_ref, ATTN_GAIN, grad * unit)
        add_row(vec_ref, ATTN_SHIFT, grad)
        add_row(vec_ref, PROJ_BIAS, low.astype(f32))

    row_loop(rows, NORM, norm_back)
    dctx_ref[...] = dot_nt(gatt_ref[...], wo_ref[...]).astype(bf16)


def attn_core_phase(seqs, length, dctx_ref, qkv_ref, p_ref, gqkv_ref, vec_ref, dp_ref, ds_ref, pb_ref):
    stack_rows = HEADS * length
    for s in range(seqs):
        span = slice(s * length, (s + 1) * length)
        stack = slice(s * stack_rows, (s + 1) * stack_rows)
        contexts = [one_head(dctx_ref[span, :], h) for h in range(HEADS)]
        for h in range(HEADS):
            start = s * stack_rows + h * length
            dp_ref[start : start + length, :] = dot_nt(contexts[h], qkv_ref[span, 2 * WIDTH :])

            def softmax_back(row):
                here = pl.ds(start + row, min(SOFT, length))
                prob = p_ref[here, :]
                grad = dp_ref[here, :]
                inner = jnp.sum(prob * grad, axis=1, keepdims=True)
                ds_ref[here, :] = (prob * (grad - inner)).astype(bf16)
                pb_ref[here, :] = prob.astype(bf16)

            row_loop(length, min(SOFT, length), softmax_back)
        context = jnp.concatenate(contexts, axis=0)
        queries = stack_heads(qkv_ref[span, :WIDTH])
        grad_q = (pick_heads(dot(ds_ref[stack, :], qkv_ref[span, WIDTH : 2 * WIDTH]), length) * score_scale).astype(bf16)
        gqkv_ref[span, :WIDTH] = grad_q
        add_row(vec_ref, QUERY_BIAS, grad_q.astype(f32))
        gqkv_ref[span, WIDTH : 2 * WIDTH] = (dot_tn(ds_ref[stack, :], queries) * score_scale).astype(bf16)
        grad_v = dot_tn(pb_ref[stack, :], context).astype(bf16)
        gqkv_ref[span, 2 * WIDTH :] = grad_v
        add_row(vec_ref, VALUE_BIAS, grad_v.astype(f32))


def layer_kernel(
    which, steps, seqs, length,
    bit_ref, len_ref, cls_ref, x_ref, cot_ref, qkv_ref, p_ref, ctx_ref,
    wqkv_ref, wo_ref, ob_ref, g1_ref, b1_ref, w1_ref, hb_ref, w2_ref, fb_ref, g2_ref, b2_ref,
    out_ref, gx_ref, keep_ref, send_ref,
    acc_ref, vec_ref, n1_ref, r1_ref, nb_ref, gp_ref, act_ref, n2_ref, r2_ref,
    wide_ref, score_ref, prob_ref, two_ref, gffn_ref, gpre_ref, one_ref, gatt_ref, dctx_ref, gqkv_ref, ds_ref,
):
    rows = seqs * length
    step = pl.program_id(0)

    def start():
        vec_ref[...] = jnp.zeros_like(vec_ref)
        if steps > 1:
            acc_ref[...] = jnp.zeros_like(acc_ref)

    if steps > 1:
        pl.when(step == 0)(start)
    else:
        start()

    def add_block(block, value):
        if steps > 1:
            acc_ref[block_rows(block), :] += value
        else:
            acc_ref[block_rows(block), :] = value

    forward_phase(
        which, seqs, length, step * seqs,
        len_ref, x_ref, wo_ref, ob_ref, g1_ref, b1_ref, w1_ref, hb_ref, w2_ref, fb_ref, g2_ref, b2_ref,
        out_ref, ctx_ref, n1_ref, r1_ref, nb_ref, gp_ref, act_ref, n2_ref, r2_ref, wide_ref,
    )
    ffn_phase(which, seqs, length, step * seqs, len_ref, cls_ref, cot_ref, n2_ref, r2_ref, gp_ref, w2_ref, g2_ref, two_ref, gffn_ref, gpre_ref, vec_ref, wide_ref)
    for j in range(BLOCKS):
        lanes = slice(j * WIDTH, (j + 1) * WIDTH)
        add_block(DOWN_BLOCK + j, dot_tn(act_ref[:, lanes], gffn_ref[...]))
        add_block(UP_BLOCK + j, dot_tn(nb_ref[...], gpre_ref[:, lanes]))
    attn_norm_phase(which, rows, gpre_ref, w1_ref, two_ref, n1_ref, r1_ref, g1_ref, wo_ref, one_ref, gatt_ref, dctx_ref, vec_ref)
    add_block(PROJ_BLOCK, dot_tn(ctx_ref[...], gatt_ref[...]))
    attn_core_phase(seqs, length, dctx_ref, qkv_ref, p_ref, gqkv_ref, vec_ref, score_ref, ds_ref, prob_ref)
    for j in range(3):
        add_block(QKV_BLOCK + j, dot_tn(x_ref[...], gqkv_ref[:, j * WIDTH : (j + 1) * WIDTH]))
    gx_ref[...] = (one_ref[...] + dot_nt(gqkv_ref[...], wqkv_ref[...])).astype(bf16)

    def finish():
        acc_ref[VECTOR_START : VECTOR_START + VECTOR_ROWS, :] = vec_ref[...]
        if steps == 1:
            acc_ref[VECTOR_START + VECTOR_ROWS : HALF, :] = jnp.zeros((HALF - VECTOR_START - VECTOR_ROWS, WIDTH), f32)
            acc_ref[HALF + 6 * WIDTH :, :] = jnp.zeros((HALF - 6 * WIDTH, WIDTH), f32)
        keep = pl.multiple_of(bit_ref[0] * HALF, HALF)
        send = pl.multiple_of((1 - bit_ref[0]) * HALF, HALF)
        keep_ref[...] = acc_ref[pl.ds(keep, HALF), :].astype(bf16)
        send_ref[...] = acc_ref[pl.ds(send, HALF), :].astype(bf16)

    if steps > 1:
        pl.when(step == steps - 1)(finish)
    else:
        finish()


def loss_kernel(local, me_ref, all_ref, hot_ref, own_hot_ref, loss_ref, gq_ref, gp_ref, q_ref, p_ref):
    count = all_ref.shape[0]
    me = me_ref[0]
    wide = all_ref[...].astype(f32)
    q_ref[...] = wide[:, :PAD].reshape(count * PAD, WIDTH).astype(bf16)
    p_ref[...] = wide[:, PAD:].reshape(count * PAD, WIDTH).astype(bf16)
    own_q = all_ref[me][:PAD]
    own_p = all_ref[me][PAD:]
    logits = dot_nt(own_q, p_ref[...]) * score_scale
    column = lax.broadcasted_iota(jnp.int32, logits.shape, 1)
    logits = jnp.where(column % PAD < local, logits, masked_score)
    top = jnp.max(logits, axis=1, keepdims=True)
    total = top + jnp.log(jnp.sum(jnp.exp(logits - top), axis=1, keepdims=True))
    hot = (column == own_hot_ref[...]).astype(f32)
    loss_ref[...] = jnp.broadcast_to(total - jnp.sum(logits * hot, axis=1, keepdims=True), loss_ref.shape)
    grad = (jnp.exp(logits - total) - hot).astype(bf16)
    gq_ref[...] = dot(grad, p_ref[...]) * score_scale
    gp_ref[...] = jnp.zeros_like(gp_ref)
    block = 256 if count * PAD % 256 == 0 else count * PAD

    def part(index, carry):
        start = pl.multiple_of(index * block, block)
        queries = q_ref[pl.ds(start, block), :]
        scores = dot_nt(p_ref[...], queries) * score_scale
        row = lax.broadcasted_iota(jnp.int32, scores.shape, 0)
        scores = jnp.where(row % PAD < local, scores, masked_score)
        peak = jnp.max(scores, axis=0, keepdims=True)
        sums = peak + jnp.log(jnp.sum(jnp.exp(scores - peak), axis=0, keepdims=True))
        own = dot_nt(own_p, queries) * score_scale
        own_row = lax.broadcasted_iota(jnp.int32, own.shape, 0)
        own_lane = lax.broadcasted_iota(jnp.int32, own.shape, 1)
        own_hits = (own_row + me * PAD == hot_ref[:, pl.ds(start, block)]).astype(f32)
        own_grad = jnp.where(own_lane % PAD < local, jnp.exp(own - sums) - own_hits, 0.0)
        gp_ref[...] += dot(own_grad.astype(bf16), queries) * score_scale
        return carry

    lax.fori_loop(0, count * PAD // block, part, 0)


def combine_kernel(radix, digit_ref, *refs):
    total_ref = refs[-1]
    sends = refs[-1 - (radix - 1) : -1]
    keep_ref = refs[-1 - radix]
    pieces = refs[: -1 - radix]
    total = pieces[0][...].astype(f32)
    for piece in pieces[1:]:
        total = total + piece[...].astype(f32)
    total_ref[...] = total
    part = total_ref.shape[0] // radix
    digit = digit_ref[0]

    def section(which):
        return total_ref[pl.ds(pl.multiple_of(which * part, part), part), :].astype(bf16)

    keep_ref[...] = section(digit)
    for step, ref in enumerate(sends, start=1):
        ref[...] = section(digit ^ step)


VECTOR_OUTS = (QUERY_BIAS, VALUE_BIAS, PROJ_BIAS, ATTN_GAIN, ATTN_SHIFT, DOWN_BIAS, FFN_GAIN, FFN_SHIFT)


def spread(which, ref, qkv_ref, proj_ref, up_ref, down_ref):
    for j in range(3):
        qkv_ref[:, j * WIDTH : (j + 1) * WIDTH] = ref[block_rows(QKV_BLOCK + j), :].astype(f32)
    proj_ref[...] = ref[block_rows(PROJ_BLOCK), :].astype(f32)
    for j in range(BLOCKS):
        up_ref[:, j * WIDTH : (j + 1) * WIDTH] = ref[block_rows(UP_BLOCK + j), :].astype(f32)
        down_ref[j * WIDTH : (j + 1) * WIDTH, :] = ref[block_rows(DOWN_BLOCK + j), :].astype(f32)
    return ref[VECTOR_START : VECTOR_START + VECTOR_ROWS, :].astype(f32)


def question_unpack_kernel(bit_ref, own_ref, other_ref, qkv_ref, proj_ref, up_ref, down_ref, tail_ref, whole_ref):
    whole_ref[pl.ds(pl.multiple_of(bit_ref[0] * HALF, HALF), HALF), :] = own_ref[...]
    whole_ref[pl.ds(pl.multiple_of((1 - bit_ref[0]) * HALF, HALF), HALF), :] = other_ref[...]
    tail_ref[...] = spread(0, whole_ref, qkv_ref, proj_ref, up_ref, down_ref)


def passage_unpack_kernel(parts, bit_ref, digit_ref, *refs):
    own_refs, other_refs, (tail_ref, *_) = refs[:parts], refs[parts : 2 * parts], refs[2 * parts : 2 * parts + 5]
    qkv_ref, proj_ref, up_ref, down_ref, up_bias_ref, *vector_refs, whole_ref = refs[2 * parts + 5 :]
    size = HALF // parts
    for half, halves in ((bit_ref[0], own_refs), (1 - bit_ref[0], other_refs)):
        for step, ref in enumerate(halves):
            start = half * HALF + (digit_ref[0] ^ step) * size
            whole_ref[pl.ds(pl.multiple_of(start, 8), size), :] = ref[...]
    tails = (tail_ref[...], spread(1, whole_ref, qkv_ref, proj_ref, up_ref, down_ref))
    for row, ref in zip(VECTOR_OUTS, vector_refs):
        for which in range(2):
            ref[which : which + 1, :] = tails[which][row : row + 1]
    for j in range(BLOCKS):
        for which in range(2):
            up_bias_ref[which : which + 1, j * WIDTH : (j + 1) * WIDTH] = tails[which][UP_BIAS + j : UP_BIAS + j + 1]


def smem():
    return pl.BlockSpec(memory_space=pltpu.SMEM)


def whole(shape):
    return pl.BlockSpec(shape, lambda i: (0,) * len(shape))


def rows_of(rows, columns):
    return pl.BlockSpec((rows, columns), lambda i: (i, 0))


def part_of(which, shape):
    return pl.BlockSpec((None,) + shape, lambda i: (which, 0, 0))


def params():
    return pltpu.CompilerParams(vmem_limit_bytes=24 * 1024 * 1024)


def shape(dims, kind):
    return jax.ShapeDtypeStruct(dims, kind)


def cost(flops, moved):
    return pl.CostEstimate(flops=flops, bytes_accessed=moved, transcendentals=0)


def pair(columns):
    return whole((2, columns))


def in_hbm(values):
    return pltpu.with_memory_space_constraint(values, pltpu.HBM)


def first_call(count, local, len_questions, len_passages, x_q, x_p, weights):
    return pl.pallas_call(
        functools.partial(first_kernel, local),
        out_shape=shape((count, 2 * PAD, WIDTH), bf16),
        grid=(1,),
        in_specs=[smem(), smem(), whole(x_q.shape), whole(x_p.shape)] + [whole(member.shape) for member in weights],
        out_specs=whole((count, 2 * PAD, WIDTH)),
        scratch_shapes=[pltpu.VMEM(x_q.shape, bf16)] * 2 + [pltpu.VMEM(x_p.shape, bf16)] * 2,
        compiler_params=params(),
        name="first",
    )(in_hbm(len_questions), in_hbm(len_passages), in_hbm(x_q), in_hbm(x_p), *[in_hbm(member) for member in weights])


def attend(which, steps, seqs, length, lengths, x, weights):
    wqkv, qb, vb, *_ = weights
    rows = seqs * length
    total = steps * rows
    stack = seqs * HEADS * length
    return pl.pallas_call(
        functools.partial(attend_kernel, which, seqs, length),
        out_shape=[
            pltpu.HBM((total, 3 * WIDTH), bf16), pltpu.HBM((steps * stack, length), f32), pltpu.HBM((total, WIDTH), bf16),
        ],
        grid=(steps,),
        in_specs=[smem(), rows_of(rows, WIDTH), part_of(which, (WIDTH, 3 * WIDTH)), pair(WIDTH), pair(WIDTH)],
        out_specs=[rows_of(rows, 3 * WIDTH), rows_of(stack, length), rows_of(rows, WIDTH)],
        scratch_shapes=[pltpu.VMEM((stack, length), f32), pltpu.VMEM((stack, length), bf16)],
        compiler_params=params(),
        cost_estimate=cost(total * 2 * 400000, total * 6000),
        name="attend",
    )(lengths, in_hbm(x), in_hbm(wqkv), in_hbm(qb), in_hbm(vb))


def layer(which, steps, seqs, length, bit, lengths, cls_grad, x, cot, attended, weights):
    rows = seqs * length
    total = steps * rows
    stack = seqs * HEADS * length
    wqkv, _, _, *rest = weights
    return pl.pallas_call(
        functools.partial(layer_kernel, which, steps, seqs, length),
        out_shape=[shape((total, WIDTH), bf16), shape((total, WIDTH), bf16), shape((HALF, WIDTH), bf16), shape((HALF, WIDTH), bf16)],
        grid=(steps,),
        in_specs=[
            smem(), smem(), whole((PAD, WIDTH)), rows_of(rows, WIDTH), rows_of(rows, WIDTH),
            rows_of(rows, 3 * WIDTH), rows_of(stack, length), rows_of(rows, WIDTH),
            part_of(which, (WIDTH, 3 * WIDTH)), part_of(which, (WIDTH, WIDTH)),
            pair(WIDTH), pair(WIDTH), pair(WIDTH), part_of(which, (WIDTH, HIDDEN)), pair(HIDDEN),
            part_of(which, (HIDDEN, WIDTH)), pair(WIDTH), pair(WIDTH), pair(WIDTH),
        ],
        out_specs=[rows_of(rows, WIDTH), rows_of(rows, WIDTH), whole((HALF, WIDTH)), whole((HALF, WIDTH))],
        scratch_shapes=[
            pltpu.VMEM((GROUP_ROWS, WIDTH), f32), pltpu.VMEM((VECTOR_ROWS, WIDTH), f32),
            pltpu.VMEM((rows, WIDTH), f32), pltpu.VMEM((rows, 1), f32), pltpu.VMEM((rows, WIDTH), bf16),
            pltpu.VMEM((rows, HIDDEN), f32), pltpu.VMEM((rows, HIDDEN), bf16), pltpu.VMEM((rows, WIDTH), f32),
            pltpu.VMEM((rows, 1), f32), pltpu.VMEM((rows, HIDDEN), f32), pltpu.VMEM((stack, length), f32),
            pltpu.VMEM((stack, length), bf16), pltpu.VMEM((rows, WIDTH), f32), pltpu.VMEM((rows, WIDTH), bf16),
            pltpu.VMEM((rows, HIDDEN), bf16), pltpu.VMEM((rows, WIDTH), f32), pltpu.VMEM((rows, WIDTH), bf16),
            pltpu.VMEM((rows, WIDTH), bf16), pltpu.VMEM((rows, 3 * WIDTH), bf16), pltpu.VMEM((stack, length), bf16),
        ],
        compiler_params=params(),
        cost_estimate=cost(total * 6 * 800000, total * 4000),
        name="layer",
    )(bit, lengths, cls_grad, in_hbm(x), in_hbm(cot), *[in_hbm(member) for member in attended], in_hbm(wqkv), *[in_hbm(member) for member in rest])


def stages(count):
    masks = []
    bit = 1
    while bit < count:
        masks.append(bit)
        bit = bit * 2
    groups = [masks[:1]]
    rest = masks[1:]
    while rest:
        groups.append(rest[:2])
        rest = rest[2:]
    return [group for group in groups if group]


def partner_send(values, mask, count):
    return lax.ppermute(values, "dp", [(i, i ^ mask) for i in range(count)])


def combos(group):
    return [index * group[0] for index in range(1, 2 ** len(group))]


def combine(pieces, group, me):
    radix = 2 ** len(group)
    digit = (me // group[0]) % radix
    rows = pieces[0].shape[0]
    part = rows // radix
    if part % 8 == 0:
        return pl.pallas_call(
            functools.partial(combine_kernel, radix),
            out_shape=[shape((part, WIDTH), bf16)] * radix,
            grid=(1,),
            in_specs=[smem()] + [whole((rows, WIDTH))] * len(pieces),
            out_specs=[whole((part, WIDTH))] * radix,
            scratch_shapes=[pltpu.VMEM((rows, WIDTH), f32)],
            compiler_params=params(),
            name="combine",
        )(digit.reshape(1), *pieces)
    total = pieces[0].astype(f32)
    for piece in pieces[1:]:
        total = total + piece.astype(f32)
    split = total.astype(bf16).reshape(radix, part, WIDTH)
    return [lax.dynamic_index_in_dim(split, digit ^ step, 0, keepdims=False) for step in range(radix)]


def send_parts(cut, group, count):
    own, *sends = cut
    return [own] + [partner_send(part, mask, count) for part, mask in zip(sends, combos(group))]


def send_whole(buffer, group, count):
    return [buffer] + [partner_send(buffer, mask, count) for mask in combos(group)]


def add_up(pieces):
    total = pieces[0].astype(f32)
    for piece in pieces[1:]:
        total = total + piece.astype(f32)
    return total.astype(bf16)


def join(pieces, group, me):
    radix = 2 ** len(group)
    digit = (me // group[0]) % radix
    joined = jnp.zeros((radix,) + pieces[0].shape, pieces[0].dtype)
    for step, piece in enumerate(pieces):
        joined = lax.dynamic_update_index_in_dim(joined, piece, digit ^ step, 0)
    return joined.reshape((radix * pieces[0].shape[0],) + pieces[0].shape[1:])


def prepare(pieces, done, following, me):
    reduce_done, group_done = done
    reduce_next, group_next = following
    if not reduce_done:
        return [join(pieces, group_done, me)]
    if reduce_next:
        return combine(pieces, group_next, me)
    return [add_up(pieces)]


def launch(operands, stage, count):
    reduce, group = stage
    return send_parts(operands, group, count) if reduce else send_whole(operands[0], group, count)


def after(values, *others):
    return list(lax.optimization_barrier((tuple(values), others))[0])


def body(questions, passages, cot_questions, cot_passages, len_questions, len_passages, positive, *weights):
    local = questions.shape[0]
    question_length = questions.shape[1]
    passage_length = passages.shape[1]
    count = positive.shape[0] // local
    me = lax.axis_index("dp")
    bit = (me % 2).reshape(1)
    x_q = questions.reshape(-1, WIDTH)
    x_p = passages.reshape(-1, WIDTH)
    own_cls = first_call(count, local, len_questions, len_passages, x_q, x_p, weights)
    own_cls, x_q, x_p = lax.optimization_barrier((own_cls, x_q, x_p))
    all_cls = lax.all_to_all(own_cls, "dp", 0, 0, tiled=True)
    attended_p = attend(1, local, 1, passage_length, len_passages, x_p, weights)
    attended_q = attend(0, 1, local, question_length, len_questions, x_q, weights)
    (all_cls,) = after([all_cls], attended_p[2], attended_q[2])
    slots = positive // local * PAD + positive % local
    slots = jnp.pad(slots.reshape(count, local), ((0, 0), (0, PAD - local)), constant_values=-1)
    own_slots = lax.dynamic_slice_in_dim(slots, me, 1, axis=0).reshape(PAD, 1)
    loss, grad_cls_q, grad_cls_p = pl.pallas_call(
        functools.partial(loss_kernel, local),
        out_shape=[shape((PAD, 128), f32), shape((PAD, WIDTH), f32), shape((PAD, WIDTH), f32)],
        grid=(1,),
        in_specs=[smem(), whole((count, 2 * PAD, WIDTH)), whole((1, count * PAD)), whole((PAD, 1))],
        out_specs=[whole((PAD, 128)), whole((PAD, WIDTH)), whole((PAD, WIDTH))],
        scratch_shapes=[pltpu.VMEM((count * PAD, WIDTH), bf16), pltpu.VMEM((count * PAD, WIDTH), bf16)],
        compiler_params=params(),
        name="loss",
    )(me.reshape(1), all_cls, slots.reshape(1, -1), own_slots)
    loss_rows = loss[:local, 0]
    out_q, grad_q, keep_q, send_q = layer(
        0, 1, local, question_length, bit, len_questions, grad_cls_q, x_q, cot_questions.reshape(-1, WIDTH),
        attended_q, weights,
    )
    groups = stages(count)
    steps = [(True, group) for group in groups] + [(False, group) for group in groups[::-1]]
    operands_q = prepare([keep_q, partner_send(send_q, groups[0][0], count)], steps[0], steps[1], me)
    (grad_cls_p,) = after([grad_cls_p], *operands_q)
    pieces_q = launch(operands_q, steps[1], count)
    out_p, grad_p, keep_p, send_p = layer(
        1, local, 1, passage_length, bit, len_passages, grad_cls_p, x_p, cot_passages.reshape(-1, WIDTH),
        attended_p, weights,
    )
    (send_p,) = after([send_p], *pieces_q)
    pieces_p = [keep_p, partner_send(send_p, groups[0][0], count)]
    for place in range(len(steps)):
        if 0 < place < len(steps) - 1:
            pieces_p = after(pieces_p, *operands_q)
            operands_p = prepare(pieces_p, steps[place - 1], steps[place], me)
            pieces_p = launch(operands_p, steps[place], count)
            pieces_q = after(pieces_q, *operands_p)
        if place + 2 < len(steps):
            operands_q = prepare(pieces_q, steps[place + 1], steps[place + 2], me)
            pieces_q = launch(operands_q, steps[place + 2], count)
    own_q, other_q = pieces_q
    parts = len(pieces_p)
    digit = (me // groups[1][0] % parts).reshape(1)
    dims = [(WIDTH, 3 * WIDTH), (WIDTH, WIDTH), (WIDTH, HIDDEN), (HIDDEN, WIDTH)]
    matrices = [shape((2,) + d, f32) for d in dims]
    *halves, tail = pl.pallas_call(
        question_unpack_kernel,
        out_shape=matrices + [shape((VECTOR_ROWS, WIDTH), f32)],
        grid=(1,),
        in_specs=[smem()] + [whole((HALF, WIDTH))] * 2,
        out_specs=[part_of(0, d) for d in dims] + [whole((VECTOR_ROWS, WIDTH))],
        scratch_shapes=[pltpu.VMEM((GROUP_ROWS, WIDTH), bf16)],
        compiler_params=params(),
        name="unpack_q",
    )(bit, own_q, other_q)
    own_piece, *came = pieces_p
    came = after(came, tail, loss_rows)
    pieces_p = [own_piece] + came
    other_p = [partner_send(piece, groups[0][0], count) for piece in pieces_p]
    vectors = [(2, HIDDEN)] + [(2, WIDTH)] * len(VECTOR_OUTS)
    first_alias = 2 + 2 * parts + 1
    d_qkv, d_proj, d_up, d_down, up_bias, query_bias, value_bias, proj_bias, gain_a, shift_a, down_bias, gain_f, shift_f = pl.pallas_call(
        functools.partial(passage_unpack_kernel, parts),
        out_shape=matrices + [shape(d, f32) for d in vectors],
        grid=(1,),
        in_specs=[smem(), smem()] + [whole((HALF // parts, WIDTH))] * (2 * parts) + [whole((VECTOR_ROWS, WIDTH))]
        + [pl.BlockSpec(memory_space=pl.ANY)] * 4,
        out_specs=[part_of(1, d) for d in dims] + [whole(d) for d in vectors],
        scratch_shapes=[pltpu.VMEM((GROUP_ROWS, WIDTH), bf16)],
        input_output_aliases={first_alias + i: i for i in range(4)},
        compiler_params=params(),
        name="unpack_p",
    )(bit, digit, *pieces_p, *other_p, tail, *halves)
    return (
        loss_rows, out_q.reshape(questions.shape), out_p.reshape(passages.shape),
        grad_q.reshape(questions.shape), grad_p.reshape(passages.shape),
        d_qkv, query_bias, value_bias, d_proj, proj_bias, gain_a, shift_a, d_up, up_bias, d_down,
        down_bias, gain_f, shift_f,
    )


def solution(mesh):
    split = P("dp", None, None)
    return jax.shard_map(
        body,
        mesh=mesh,
        in_specs=(split, split, split, split, P("dp"), P("dp")) + (P(),) * 14,
        out_specs=(P("dp"), split, split, split, split) + (P(),) * 13,
        check_vma=False,
    )
```

```python
import functools

import jax
import jax.numpy as jnp
from jax import lax
from jax.experimental import pallas as pl
from jax.experimental.pallas import tpu as pltpu
from jax.sharding import PartitionSpec as P

HEAD_DIM = 64
WIDTH = 256
HEADS = WIDTH // HEAD_DIM
HIDDEN = 1024
BLOCKS = HIDDEN // WIDTH
PAD = 8
VECTOR_ROWS = 16
HALF = 6 * WIDTH + 128
GROUP_ROWS = 2 * HALF
LANES = 128
SOFT = 128
NORM = 32
GELU = 32
ln_eps = 1e-06
score_scale = 0.125
masked_score = -1e30
f32 = jnp.float32
bf16 = jnp.bfloat16

QUERY_BIAS, VALUE_BIAS, PROJ_BIAS, ATTN_GAIN, ATTN_SHIFT, DOWN_BIAS, FFN_GAIN, FFN_SHIFT = range(8)
UP_BIAS = 8


def dot(a, b):
    return lax.dot_general(a, b, (((1,), (0,)), ((), ())), preferred_element_type=f32)


def dot_nt(a, b):
    return lax.dot_general(a, b, (((1,), (1,)), ((), ())), preferred_element_type=f32)


def dot_tn(a, b):
    return lax.dot_general(a, b, (((0,), (0,)), ((), ())), preferred_element_type=f32)


def row_loop(rows, chunk, step):
    for row in range(0, rows, chunk):
        step(row)


def vector(ref, which):
    return ref[...].astype(f32)[which : which + 1]


def lane_head(rows):
    return lax.broadcasted_iota(jnp.int32, (rows, WIDTH), 1) // HEAD_DIM


def one_head(values, h, scale=1.0):
    return jnp.where(lane_head(values.shape[0]) == h, values.astype(f32) * scale, 0.0).astype(bf16)


def some_heads(values, first, last, scale=1.0):
    return jnp.concatenate([one_head(values, h, scale) for h in range(first, last)], axis=0)


def pick_heads(stacked, rows):
    head = lane_head(rows)
    result = stacked[:rows]
    for h in range(1, HEADS):
        result = jnp.where(head == h, stacked[h * rows : (h + 1) * rows], result)
    return result


def block_rows(block):
    start = block * WIDTH if block < 6 else HALF + (block - 6) * WIDTH
    return slice(start, start + WIDTH)


VECTOR_START = 6 * WIDTH
QKV_BLOCK, PROJ_BLOCK, UP_BLOCK, DOWN_BLOCK = 0, 3, 4, 8


def normalize(value):
    centered = value - jnp.mean(value, axis=1, keepdims=True)
    inverse = lax.rsqrt(jnp.mean(centered * centered, axis=1, keepdims=True) + ln_eps)
    return centered * inverse, inverse


def masked_softmax(scores, size, scale=score_scale):
    part = scores * scale if scale != 1.0 else scores
    key = lax.broadcasted_iota(jnp.int32, part.shape, 1)
    part = jnp.where(key < size, part, masked_score)
    part = jnp.exp(part - jnp.max(part, axis=1, keepdims=True))
    return part * (1.0 / jnp.sum(part, axis=1, keepdims=True))


def gelu_parts(value):
    cumulative = 0.5 + 0.5 * lax.erf(value * 0.7071067811865476)
    density = jnp.exp(value * value * -0.5) * 0.3989422804014327
    return (value * cumulative).astype(bf16), cumulative + value * density


def first_kernel(
    seqs, lq_ref, lp_ref, xq_ref, xp_ref,
    wqkv_ref, qb_ref, vb_ref, wo_ref, ob_ref, g1_ref, b1_ref, w1_ref, hb_ref, w2_ref, fb_ref, g2_ref, b2_ref,
    cls_ref,
    kq_ref, vq_ref, kp_ref, vp_ref,
):
    sides = ((0, xq_ref, kq_ref, vq_ref, lq_ref), (1, xp_ref, kp_ref, vp_ref, lp_ref))
    filler = jnp.zeros((PAD - seqs, WIDTH), f32)
    inputs = []
    for which, x_ref, *_ in sides:
        length = x_ref.shape[0] // seqs
        firsts = [x_ref[s * length : s * length + 16, :].astype(f32)[:1] for s in range(seqs)]
        inputs.append(jnp.concatenate(firsts + [filler], axis=0))
    own_lanes = lane_head(PAD) == lax.broadcasted_iota(jnp.int32, (PAD, WIDTH), 0)
    queries = [
        (dot(inputs[which].astype(bf16), wqkv_ref[which, :, :WIDTH]) + vector(qb_ref, which)).astype(bf16).astype(f32)
        for which in range(2)
    ]
    for which, x_ref, k_ref, v_ref, _ in sides:
        x = x_ref[...]
        k_ref[...] = dot(x, wqkv_ref[which, :, WIDTH : 2 * WIDTH]).astype(bf16)
        v_ref[...] = (dot(x, wqkv_ref[which, :, 2 * WIDTH :]) + vector(vb_ref, which)).astype(bf16)
    context = []
    for which, x_ref, k_ref, v_ref, len_ref in sides:
        length = x_ref.shape[0] // seqs
        spans = [slice(s * length, (s + 1) * length) for s in range(seqs)]
        scores, sizes = [], []
        for s, span in enumerate(spans):
            heads = jnp.where(own_lanes, queries[which][s : s + 1], 0.0).astype(bf16)
            scores.append(dot_nt(heads, k_ref[span, :]))
            sizes.append(jnp.full((PAD, length), len_ref[s], jnp.int32))
        prob = masked_softmax(jnp.concatenate(scores, axis=0), jnp.concatenate(sizes, axis=0)).astype(f32)
        rows = []
        for s, span in enumerate(spans):
            mixed = dot(prob[s * PAD : (s + 1) * PAD].astype(bf16), v_ref[span, :])
            rows.append(jnp.sum(jnp.where(own_lanes, mixed, 0.0), axis=0, keepdims=True))
        context.append(jnp.concatenate(rows + [filler], axis=0).astype(bf16))
    normed = []
    for which in range(2):
        value = inputs[which] + (dot(context[which], wo_ref[which]) + vector(ob_ref, which))
        unit, _ = normalize(value)
        normed.append(unit * vector(g1_ref, which) + vector(b1_ref, which))
    active = []
    for which in range(2):
        active.append(gelu_parts(dot(normed[which].astype(bf16), w1_ref[which]) + vector(hb_ref, which))[0])
    results = []
    for which in range(2):
        value = normed[which] + (dot(active[which], w2_ref[which]) + vector(fb_ref, which))
        unit, _ = normalize(value)
        result = unit * vector(g2_ref, which) + vector(b2_ref, which)
        row = lax.broadcasted_iota(jnp.int32, result.shape, 0)
        results.append(jnp.where(row < seqs, result, 0.0))
    both = jnp.concatenate(results, axis=0).astype(bf16)

    def store(i, carry):
        cls_ref[i] = both
        return carry

    lax.fori_loop(0, cls_ref.shape[0], store, 0)


def head_groups(length):
    together = max(1, WIDTH // length)
    return [(h, h + together, slice(h * length, (h + together) * length)) for h in range(0, HEADS, together)]


def attend_kernel(which, seqs, length, len_ref, x_ref, wqkv_ref, qb_ref, vb_ref, qkv_ref, p_ref, ctx_ref, score_ref, prob_ref):
    step = pl.program_id(0)
    x = x_ref[...]
    qkv_ref[:, :WIDTH] = (dot(x, wqkv_ref[:, :WIDTH]) + vector(qb_ref, which)).astype(bf16)
    qkv_ref[:, WIDTH : 2 * WIDTH] = dot(x, wqkv_ref[:, WIDTH : 2 * WIDTH]).astype(bf16)
    qkv_ref[:, 2 * WIDTH :] = (dot(x, wqkv_ref[:, 2 * WIDTH :]) + vector(vb_ref, which)).astype(bf16)
    for s in range(seqs):
        span = slice(s * length, (s + 1) * length)
        size = len_ref[step * seqs + s]
        keys = qkv_ref[span, WIDTH : 2 * WIDTH]
        for first, last, columns in head_groups(length):
            score_ref[span, columns] = dot_nt(keys, some_heads(qkv_ref[span, :WIDTH], first, last, score_scale))
            for lane in range(columns.start, columns.stop, LANES):
                here = slice(lane, lane + LANES)
                part = score_ref[span, here]
                key = lax.broadcasted_iota(jnp.int32, part.shape, 0)
                part = jnp.where(key < size, part, masked_score)
                part = jnp.exp(part - jnp.max(part, axis=0, keepdims=True))
                prob = part * (1.0 / jnp.sum(part, axis=0, keepdims=True))
                p_ref[span, here] = prob
                prob_ref[span, here] = prob.astype(bf16)
        ctx_ref[span, :] = pick_heads(dot_tn(prob_ref[span, :], qkv_ref[span, 2 * WIDTH :]), length).astype(bf16)


def attend_long_kernel(which, seqs, length, len_ref, x_ref, wqkv_ref, qb_ref, vb_ref, qkv_ref, p_ref, ctx_ref, score_ref, prob_ref):
    step = pl.program_id(0)
    x = x_ref[...]
    qkv_ref[:, :WIDTH] = (dot(x, wqkv_ref[:, :WIDTH]) + vector(qb_ref, which)).astype(bf16)
    qkv_ref[:, WIDTH : 2 * WIDTH] = dot(x, wqkv_ref[:, WIDTH : 2 * WIDTH]).astype(bf16)
    qkv_ref[:, 2 * WIDTH :] = (dot(x, wqkv_ref[:, 2 * WIDTH :]) + vector(vb_ref, which)).astype(bf16)
    stack_rows = HEADS * length
    for s in range(seqs):
        span = slice(s * length, (s + 1) * length)
        stack = slice(s * stack_rows, (s + 1) * stack_rows)
        size = len_ref[step * seqs + s]
        queries = qkv_ref[span, :WIDTH]
        for h in range(HEADS):
            start = s * stack_rows + h * length
            score_ref[start : start + length, :] = dot_nt(one_head(queries, h, score_scale), qkv_ref[span, WIDTH : 2 * WIDTH])

            def softmax(row):
                here = pl.ds(start + row, SOFT)
                prob = masked_softmax(score_ref[here, :], size, 1.0)
                p_ref[here, :] = prob
                prob_ref[here, :] = prob.astype(bf16)

            row_loop(length, SOFT, softmax)
        ctx_ref[span, :] = pick_heads(dot(prob_ref[stack, :], qkv_ref[span, 2 * WIDTH :]), length).astype(bf16)


def forward_phase(
    which, rows, x_ref, wo_ref, ob_ref, g1_ref, b1_ref, w1_ref, hb_ref, w2_ref,
    ctx_ref, n1_ref, r1_ref, nb_ref, gp_ref, act_ref, n2_ref, wide_ref,
):
    n2_ref[...] = dot(ctx_ref[...], wo_ref[...])
    ob, g1, b1 = vector(ob_ref, which), vector(g1_ref, which), vector(b1_ref, which)

    def first_norm(row):
        here = pl.ds(row, NORM)
        unit, inverse = normalize(x_ref[here, :].astype(f32) + (n2_ref[here, :] + ob))
        n1_ref[here, :] = unit
        r1_ref[here, :] = inverse
        nb_ref[here, :] = (unit * g1 + b1).astype(bf16)

    row_loop(rows, NORM, first_norm)
    hb = vector(hb_ref, which)
    for j in range(BLOCKS):
        lanes = slice(j * WIDTH, (j + 1) * WIDTH)
        wide_ref[:, lanes] = dot(nb_ref[...], w1_ref[:, lanes])

        def gelu(row):
            here = pl.ds(row, GELU)
            active, slope = gelu_parts(wide_ref[here, lanes] + hb[:, lanes])
            act_ref[here, lanes] = active
            gp_ref[here, lanes] = slope

        row_loop(rows, GELU, gelu)
    n2_ref[...] = dot(act_ref[...], w2_ref[...])


def add_row(vec_ref, row, values):
    here = slice(row * PAD, (row + 1) * PAD)
    vec_ref[here, :] = vec_ref[here, :] + jnp.sum(values.reshape(-1, PAD, WIDTH), axis=0)


def ffn_phase(which, seqs, length, first, len_ref, cls_ref, cot_ref, n1_ref, n2_ref, gp_ref, w2_ref, g1_ref, b1_ref, fb_ref, g2_ref, b2_ref, out_ref, two_ref, gffn_ref, gpre_ref, vec_ref, wide_ref):
    g1, g2, b2 = vector(g1_ref, which), vector(g2_ref, which), vector(b2_ref, which)
    shift = vector(b1_ref, which) + vector(fb_ref, which)
    for s in range(seqs):
        size = len_ref[first + s]
        cls_row = cls_ref[pl.ds(first + s, 1), :]

        def output_norm(row):
            here = pl.ds(s * length + row, NORM)
            inside = row + lax.broadcasted_iota(jnp.int32, (NORM, WIDTH), 0) < size
            unit, inverse = normalize(n1_ref[here, :] * g1 + (n2_ref[here, :] + shift))
            out_ref[here, :] = jnp.where(inside, unit * g2 + b2, 0.0).astype(bf16)
            grad = cot_ref[here, :].astype(f32)
            if row == 0:
                grad = grad + jnp.where(lax.broadcasted_iota(jnp.int32, (NORM, WIDTH), 0) == 0, cls_row, 0.0)
            grad = jnp.where(inside, grad, 0.0)
            scaled = grad * g2
            slope = scaled * unit
            first_mean = jnp.mean(scaled, axis=1, keepdims=True)
            second_mean = jnp.mean(slope, axis=1, keepdims=True)
            two = inverse * (scaled - first_mean - unit * second_mean)
            low = two.astype(bf16)
            two_ref[here, :] = two
            gffn_ref[here, :] = low
            add_row(vec_ref, FFN_GAIN, grad * unit)
            add_row(vec_ref, FFN_SHIFT, grad)
            add_row(vec_ref, DOWN_BIAS, low.astype(f32))

        row_loop(length, NORM, output_norm)
    for j in range(BLOCKS):
        lanes = slice(j * WIDTH, (j + 1) * WIDTH)
        wide_ref[:, lanes] = dot_nt(gffn_ref[...], w2_ref[lanes, :])

        def gelu_back(row):
            here = pl.ds(row, GELU)
            low = (wide_ref[here, lanes] * gp_ref[here, lanes]).astype(bf16)
            gpre_ref[here, lanes] = low
            add_row(vec_ref, UP_BIAS + j, low.astype(f32))

        row_loop(seqs * length, GELU, gelu_back)


def attn_norm_phase(which, rows, gpre_ref, w1_ref, two_ref, n1_ref, r1_ref, g1_ref, wo_ref, one_ref, gatt_ref, dctx_ref, vec_ref):
    one_ref[...] = dot_nt(gpre_ref[...], w1_ref[...])
    g1 = vector(g1_ref, which)

    def norm_back(row):
        here = pl.ds(row, NORM)
        grad = two_ref[here, :] + one_ref[here, :]
        unit = n1_ref[here, :]
        scaled = grad * g1
        first_mean = jnp.mean(scaled, axis=1, keepdims=True)
        second_mean = jnp.mean(scaled * unit, axis=1, keepdims=True)
        one = r1_ref[here, :] * (scaled - first_mean - unit * second_mean)
        low = one.astype(bf16)
        one_ref[here, :] = one
        gatt_ref[here, :] = low
        add_row(vec_ref, ATTN_GAIN, grad * unit)
        add_row(vec_ref, ATTN_SHIFT, grad)
        add_row(vec_ref, PROJ_BIAS, low.astype(f32))

    row_loop(rows, NORM, norm_back)
    dctx_ref[...] = dot_nt(gatt_ref[...], wo_ref[...]).astype(bf16)


def attn_core_phase(seqs, length, dctx_ref, qkv_ref, p_ref, gqkv_ref, vec_ref, dp_ref, ds_ref, pb_ref):
    for s in range(seqs):
        span = slice(s * length, (s + 1) * length)
        values = qkv_ref[span, 2 * WIDTH :]
        context = some_heads(dctx_ref[span, :], 0, HEADS)
        for first, last, columns in head_groups(length):
            dp_ref[span, columns] = dot_nt(values, context[columns])
            for lane in range(columns.start, columns.stop, LANES):
                here = slice(lane, lane + LANES)
                prob = p_ref[span, here]
                grad = dp_ref[span, here]
                inner = jnp.sum(prob * grad, axis=0, keepdims=True)
                ds_ref[span, here] = (prob * (grad - inner)).astype(bf16)
                pb_ref[span, here] = prob.astype(bf16)
        queries = some_heads(qkv_ref[span, :WIDTH], 0, HEADS, score_scale)
        gqkv_ref[span, WIDTH : 2 * WIDTH] = dot(ds_ref[span, :], queries).astype(bf16)
        grad_v = dot(pb_ref[span, :], context).astype(bf16)
        gqkv_ref[span, 2 * WIDTH :] = grad_v
        add_row(vec_ref, VALUE_BIAS, grad_v.astype(f32))
        grad_q = (pick_heads(dot_tn(ds_ref[span, :], qkv_ref[span, WIDTH : 2 * WIDTH]), length) * score_scale).astype(bf16)
        gqkv_ref[span, :WIDTH] = grad_q
        add_row(vec_ref, QUERY_BIAS, grad_q.astype(f32))


def attn_core_long(seqs, length, dctx_ref, qkv_ref, p_ref, gqkv_ref, vec_ref, dp_ref, ds_ref, pb_ref):
    stack_rows = HEADS * length
    for s in range(seqs):
        span = slice(s * length, (s + 1) * length)
        stack = slice(s * stack_rows, (s + 1) * stack_rows)
        contexts = [one_head(dctx_ref[span, :], h) for h in range(HEADS)]
        for h in range(HEADS):
            start = s * stack_rows + h * length
            dp_ref[start : start + length, :] = dot_nt(contexts[h], qkv_ref[span, 2 * WIDTH :])

            def softmax_back(row):
                here = pl.ds(start + row, SOFT)
                prob = p_ref[here, :]
                grad = dp_ref[here, :]
                inner = jnp.sum(prob * grad, axis=1, keepdims=True)
                ds_ref[here, :] = (prob * (grad - inner)).astype(bf16)
                pb_ref[here, :] = prob.astype(bf16)

            row_loop(length, SOFT, softmax_back)
        context = jnp.concatenate(contexts, axis=0)
        queries = some_heads(qkv_ref[span, :WIDTH], 0, HEADS, score_scale)
        grad_q = (pick_heads(dot(ds_ref[stack, :], qkv_ref[span, WIDTH : 2 * WIDTH]), length) * score_scale).astype(bf16)
        gqkv_ref[span, :WIDTH] = grad_q
        add_row(vec_ref, QUERY_BIAS, grad_q.astype(f32))
        gqkv_ref[span, WIDTH : 2 * WIDTH] = dot_tn(ds_ref[stack, :], queries).astype(bf16)
        grad_v = dot_tn(pb_ref[stack, :], context).astype(bf16)
        gqkv_ref[span, 2 * WIDTH :] = grad_v
        add_row(vec_ref, VALUE_BIAS, grad_v.astype(f32))


def layer_kernel(
    which, steps, seqs, length,
    bit_ref, len_ref, cls_ref, x_ref, cot_ref, qkv_ref, p_ref, ctx_ref,
    wqkv_ref, wo_ref, ob_ref, g1_ref, b1_ref, w1_ref, hb_ref, w2_ref, fb_ref, g2_ref, b2_ref,
    out_ref, gx_ref, keep_ref, send_ref,
    acc_ref, vec_ref, n1_ref, r1_ref, nb_ref, gp_ref, act_ref, n2_ref,
    wide_ref, score_ref, prob_ref, two_ref, gffn_ref, gpre_ref, one_ref, gatt_ref, dctx_ref, gqkv_ref, ds_ref,
):
    rows = seqs * length
    step = pl.program_id(0)

    def start():
        vec_ref[...] = jnp.zeros_like(vec_ref)
        if steps > 1:
            acc_ref[...] = jnp.zeros_like(acc_ref)

    if steps > 1:
        pl.when(step == 0)(start)
    else:
        start()

    def add_block(block, value):
        if steps > 1:
            acc_ref[block_rows(block), :] += value
        else:
            acc_ref[block_rows(block), :] = value

    forward_phase(
        which, rows, x_ref, wo_ref, ob_ref, g1_ref, b1_ref, w1_ref, hb_ref, w2_ref,
        ctx_ref, n1_ref, r1_ref, nb_ref, gp_ref, act_ref, n2_ref, wide_ref,
    )
    ffn_phase(which, seqs, length, step * seqs, len_ref, cls_ref, cot_ref, n1_ref, n2_ref, gp_ref, w2_ref, g1_ref, b1_ref, fb_ref, g2_ref, b2_ref, out_ref, two_ref, gffn_ref, gpre_ref, vec_ref, wide_ref)
    downs = dot_tn(act_ref[...], gffn_ref[...])
    ups = dot_tn(nb_ref[...], gpre_ref[...])
    for j in range(BLOCKS):
        lanes = slice(j * WIDTH, (j + 1) * WIDTH)
        add_block(DOWN_BLOCK + j, downs[lanes])
        add_block(UP_BLOCK + j, ups[:, lanes])
    attn_norm_phase(which, rows, gpre_ref, w1_ref, two_ref, n1_ref, r1_ref, g1_ref, wo_ref, one_ref, gatt_ref, dctx_ref, vec_ref)
    add_block(PROJ_BLOCK, dot_tn(ctx_ref[...], gatt_ref[...]))
    attn_core = attn_core_long if seqs == 1 else attn_core_phase
    attn_core(seqs, length, dctx_ref, qkv_ref, p_ref, gqkv_ref, vec_ref, score_ref, ds_ref, prob_ref)
    for j in range(3):
        add_block(QKV_BLOCK + j, dot_tn(x_ref[...], gqkv_ref[:, j * WIDTH : (j + 1) * WIDTH]))
    gx_ref[...] = (one_ref[...] + dot_nt(gqkv_ref[...], wqkv_ref[...])).astype(bf16)

    def finish():
        acc_ref[VECTOR_START : VECTOR_START + VECTOR_ROWS, :] = jnp.sum(vec_ref[...].reshape(VECTOR_ROWS, PAD, WIDTH), axis=1)
        if steps == 1:
            acc_ref[VECTOR_START + VECTOR_ROWS : HALF, :] = jnp.zeros((HALF - VECTOR_START - VECTOR_ROWS, WIDTH), f32)
            acc_ref[HALF + 6 * WIDTH :, :] = jnp.zeros((HALF - 6 * WIDTH, WIDTH), f32)
        keep = pl.multiple_of(bit_ref[0] * HALF, HALF)
        send = pl.multiple_of((1 - bit_ref[0]) * HALF, HALF)
        keep_ref[...] = acc_ref[pl.ds(keep, HALF), :].astype(bf16)
        send_ref[...] = acc_ref[pl.ds(send, HALF), :].astype(bf16)

    if steps > 1:
        pl.when(step == steps - 1)(finish)
    else:
        finish()


def loss_kernel(local, me_ref, all_ref, hot_ref, own_hot_ref, loss_ref, gq_ref, gp_ref, q_ref, p_ref):
    count = all_ref.shape[0]
    me = me_ref[0]
    wide = all_ref[...].astype(f32)
    q_ref[...] = wide[:, :PAD].reshape(count * PAD, WIDTH).astype(bf16)
    p_ref[...] = wide[:, PAD:].reshape(count * PAD, WIDTH).astype(bf16)
    own_q = all_ref[me][:PAD]
    own_p = all_ref[me][PAD:]
    logits = dot_nt(own_q, p_ref[...]) * score_scale
    column = lax.broadcasted_iota(jnp.int32, logits.shape, 1)
    logits = jnp.where(column % PAD < local, logits, masked_score)
    top = jnp.max(logits, axis=1, keepdims=True)
    total = top + jnp.log(jnp.sum(jnp.exp(logits - top), axis=1, keepdims=True))
    hot = (column == own_hot_ref[...]).astype(f32)
    loss_ref[...] = jnp.broadcast_to(total - jnp.sum(logits * hot, axis=1, keepdims=True), loss_ref.shape)
    grad = (jnp.exp(logits - total) - hot).astype(bf16)
    gq_ref[...] = dot(grad, p_ref[...]) * score_scale
    gp_ref[...] = jnp.zeros_like(gp_ref)
    block = 256 if count * PAD % 256 == 0 else count * PAD

    def part(index, carry):
        start = pl.multiple_of(index * block, block)
        queries = q_ref[pl.ds(start, block), :]
        scores = dot_nt(p_ref[...], queries) * score_scale
        row = lax.broadcasted_iota(jnp.int32, scores.shape, 0)
        scores = jnp.where(row % PAD < local, scores, masked_score)
        peak = jnp.max(scores, axis=0, keepdims=True)
        sums = peak + jnp.log(jnp.sum(jnp.exp(scores - peak), axis=0, keepdims=True))
        own = dot_nt(own_p, queries) * score_scale
        own_row = lax.broadcasted_iota(jnp.int32, own.shape, 0)
        own_lane = lax.broadcasted_iota(jnp.int32, own.shape, 1)
        own_hits = (own_row + me * PAD == hot_ref[:, pl.ds(start, block)]).astype(f32)
        own_grad = jnp.where(own_lane % PAD < local, jnp.exp(own - sums) - own_hits, 0.0)
        gp_ref[...] += dot(own_grad.astype(bf16), queries) * score_scale
        return carry

    lax.fori_loop(0, count * PAD // block, part, 0)


def combine_kernel(radix, digit_ref, *refs):
    total_ref = refs[-1]
    sends = refs[-1 - (radix - 1) : -1]
    keep_ref = refs[-1 - radix]
    pieces = refs[: -1 - radix]
    total = pieces[0][...].astype(f32)
    for piece in pieces[1:]:
        total = total + piece[...].astype(f32)
    total_ref[...] = total
    part = total_ref.shape[0] // radix
    digit = digit_ref[0]

    def section(which):
        return total_ref[pl.ds(pl.multiple_of(which * part, part), part), :].astype(bf16)

    keep_ref[...] = section(digit)
    for step, ref in enumerate(sends, start=1):
        ref[...] = section(digit ^ step)


VECTOR_OUTS = (QUERY_BIAS, VALUE_BIAS, PROJ_BIAS, ATTN_GAIN, ATTN_SHIFT, DOWN_BIAS, FFN_GAIN, FFN_SHIFT)


def spread(which, ref, qkv_ref, proj_ref, up_ref, down_ref):
    for j in range(3):
        qkv_ref[:, j * WIDTH : (j + 1) * WIDTH] = ref[block_rows(QKV_BLOCK + j), :].astype(f32)
    proj_ref[...] = ref[block_rows(PROJ_BLOCK), :].astype(f32)
    for j in range(BLOCKS):
        up_ref[:, j * WIDTH : (j + 1) * WIDTH] = ref[block_rows(UP_BLOCK + j), :].astype(f32)
        down_ref[j * WIDTH : (j + 1) * WIDTH, :] = ref[block_rows(DOWN_BLOCK + j), :].astype(f32)
    return ref[VECTOR_START : VECTOR_START + VECTOR_ROWS, :].astype(f32)


def question_unpack_kernel(bit_ref, own_ref, other_ref, qkv_ref, proj_ref, up_ref, down_ref, tail_ref, whole_ref):
    whole_ref[pl.ds(pl.multiple_of(bit_ref[0] * HALF, HALF), HALF), :] = own_ref[...]
    whole_ref[pl.ds(pl.multiple_of((1 - bit_ref[0]) * HALF, HALF), HALF), :] = other_ref[...]
    tail_ref[...] = spread(0, whole_ref, qkv_ref, proj_ref, up_ref, down_ref)


def passage_unpack_kernel(parts, bit_ref, digit_ref, *refs):
    own_refs, other_refs, (tail_ref, *_) = refs[:parts], refs[parts : 2 * parts], refs[2 * parts : 2 * parts + 5]
    qkv_ref, proj_ref, up_ref, down_ref, up_bias_ref, *vector_refs, whole_ref = refs[2 * parts + 5 :]
    size = HALF // parts
    for half, halves in ((bit_ref[0], own_refs), (1 - bit_ref[0], other_refs)):
        for step, ref in enumerate(halves):
            start = half * HALF + (digit_ref[0] ^ step) * size
            whole_ref[pl.ds(pl.multiple_of(start, 8), size), :] = ref[...]
    tails = (tail_ref[...], spread(1, whole_ref, qkv_ref, proj_ref, up_ref, down_ref))
    for row, ref in zip(VECTOR_OUTS, vector_refs):
        for which in range(2):
            ref[which : which + 1, :] = tails[which][row : row + 1]
    for j in range(BLOCKS):
        for which in range(2):
            up_bias_ref[which : which + 1, j * WIDTH : (j + 1) * WIDTH] = tails[which][UP_BIAS + j : UP_BIAS + j + 1]


def smem():
    return pl.BlockSpec(memory_space=pltpu.SMEM)


def whole(shape):
    return pl.BlockSpec(shape, lambda i: (0,) * len(shape))


def rows_of(rows, columns):
    return pl.BlockSpec((rows, columns), lambda i: (i, 0))


def part_of(which, shape):
    return pl.BlockSpec((None,) + shape, lambda i: (which, 0, 0))


def params():
    return pltpu.CompilerParams(vmem_limit_bytes=24 * 1024 * 1024)


def shape(dims, kind):
    return jax.ShapeDtypeStruct(dims, kind)


def cost(flops, moved):
    return pl.CostEstimate(flops=flops, bytes_accessed=moved, transcendentals=0)


def pair(columns):
    return whole((2, columns))


def in_hbm(values):
    return pltpu.with_memory_space_constraint(values, pltpu.HBM)


def first_call(count, local, len_questions, len_passages, x_q, x_p, weights):
    return pl.pallas_call(
        functools.partial(first_kernel, local),
        out_shape=shape((count, 2 * PAD, WIDTH), bf16),
        grid=(1,),
        in_specs=[smem(), smem(), whole(x_q.shape), whole(x_p.shape)] + [whole(member.shape) for member in weights],
        out_specs=whole((count, 2 * PAD, WIDTH)),
        scratch_shapes=[pltpu.VMEM(x_q.shape, bf16)] * 2 + [pltpu.VMEM(x_p.shape, bf16)] * 2,
        compiler_params=params(),
        name="first",
    )(in_hbm(len_questions), in_hbm(len_passages), in_hbm(x_q), in_hbm(x_p), *[in_hbm(member) for member in weights])


def attend(which, steps, seqs, length, lengths, x, weights):
    wqkv, qb, vb, *_ = weights
    rows = seqs * length
    total = steps * rows
    block = (HEADS * length, length) if seqs == 1 else (rows, HEADS * length)
    return pl.pallas_call(
        functools.partial(attend_long_kernel if seqs == 1 else attend_kernel, which, seqs, length),
        out_shape=[
            pltpu.HBM((total, 3 * WIDTH), bf16), pltpu.HBM((steps * block[0], block[1]), f32), pltpu.HBM((total, WIDTH), bf16),
        ],
        grid=(steps,),
        in_specs=[smem(), rows_of(rows, WIDTH), part_of(which, (WIDTH, 3 * WIDTH)), pair(WIDTH), pair(WIDTH)],
        out_specs=[rows_of(rows, 3 * WIDTH), rows_of(*block), rows_of(rows, WIDTH)],
        scratch_shapes=[pltpu.VMEM(block, f32), pltpu.VMEM(block, bf16)],
        compiler_params=params(),
        cost_estimate=cost(total * 2 * 400000, total * 6000),
        name="attend",
    )(lengths, in_hbm(x), in_hbm(wqkv), in_hbm(qb), in_hbm(vb))


def layer(which, steps, seqs, length, bit, lengths, cls_grad, x, cot, attended, weights):
    rows = seqs * length
    total = steps * rows
    block = (HEADS * length, length) if seqs == 1 else (rows, HEADS * length)
    wqkv, _, _, *rest = weights
    return pl.pallas_call(
        functools.partial(layer_kernel, which, steps, seqs, length),
        out_shape=[shape((total, WIDTH), bf16), shape((total, WIDTH), bf16), shape((HALF, WIDTH), bf16), shape((HALF, WIDTH), bf16)],
        grid=(steps,),
        in_specs=[
            smem(), smem(), whole((PAD, WIDTH)), rows_of(rows, WIDTH), rows_of(rows, WIDTH),
            rows_of(rows, 3 * WIDTH), rows_of(*block), rows_of(rows, WIDTH),
            part_of(which, (WIDTH, 3 * WIDTH)), part_of(which, (WIDTH, WIDTH)),
            pair(WIDTH), pair(WIDTH), pair(WIDTH), part_of(which, (WIDTH, HIDDEN)), pair(HIDDEN),
            part_of(which, (HIDDEN, WIDTH)), pair(WIDTH), pair(WIDTH), pair(WIDTH),
        ],
        out_specs=[rows_of(rows, WIDTH), rows_of(rows, WIDTH), whole((HALF, WIDTH)), whole((HALF, WIDTH))],
        scratch_shapes=[
            pltpu.VMEM((GROUP_ROWS, WIDTH), f32), pltpu.VMEM((VECTOR_ROWS * PAD, WIDTH), f32),
            pltpu.VMEM((rows, WIDTH), f32), pltpu.VMEM((rows, 1), f32), pltpu.VMEM((rows, WIDTH), bf16),
            pltpu.VMEM((rows, HIDDEN), f32), pltpu.VMEM((rows, HIDDEN), bf16), pltpu.VMEM((rows, WIDTH), f32),
            pltpu.VMEM((rows, HIDDEN), f32), pltpu.VMEM(block, f32),
            pltpu.VMEM(block, bf16), pltpu.VMEM((rows, WIDTH), f32), pltpu.VMEM((rows, WIDTH), bf16),
            pltpu.VMEM((rows, HIDDEN), bf16), pltpu.VMEM((rows, WIDTH), f32), pltpu.VMEM((rows, WIDTH), bf16),
            pltpu.VMEM((rows, WIDTH), bf16), pltpu.VMEM((rows, 3 * WIDTH), bf16), pltpu.VMEM(block, bf16),
        ],
        compiler_params=params(),
        cost_estimate=cost(total * 6 * 800000, total * 4000),
        name="layer",
    )(bit, lengths, cls_grad, in_hbm(x), in_hbm(cot), *[in_hbm(member) for member in attended], in_hbm(wqkv), *[in_hbm(member) for member in rest])


def stages(count):
    masks = []
    bit = 1
    while bit < count:
        masks.append(bit)
        bit = bit * 2
    groups = [masks[:1]]
    rest = masks[1:]
    while rest:
        groups.append(rest[:2])
        rest = rest[2:]
    return [group for group in groups if group]


def partner_send(values, mask, count):
    return lax.ppermute(values, "dp", [(i, i ^ mask) for i in range(count)])


def combos(group):
    return [index * group[0] for index in range(1, 2 ** len(group))]


def combine(pieces, group, me):
    radix = 2 ** len(group)
    digit = (me // group[0]) % radix
    rows = pieces[0].shape[0]
    part = rows // radix
    if part % 8 == 0:
        return pl.pallas_call(
            functools.partial(combine_kernel, radix),
            out_shape=[shape((part, WIDTH), bf16)] * radix,
            grid=(1,),
            in_specs=[smem()] + [whole((rows, WIDTH))] * len(pieces),
            out_specs=[whole((part, WIDTH))] * radix,
            scratch_shapes=[pltpu.VMEM((rows, WIDTH), f32)],
            compiler_params=params(),
            name="combine",
        )(digit.reshape(1), *pieces)
    total = pieces[0].astype(f32)
    for piece in pieces[1:]:
        total = total + piece.astype(f32)
    split = total.astype(bf16).reshape(radix, part, WIDTH)
    return [lax.dynamic_index_in_dim(split, digit ^ step, 0, keepdims=False) for step in range(radix)]


def send_parts(cut, group, count):
    own, *sends = cut
    return [own] + [partner_send(part, mask, count) for part, mask in zip(sends, combos(group))]


def send_whole(buffer, group, count):
    return [buffer] + [partner_send(buffer, mask, count) for mask in combos(group)]


def add_up(pieces):
    total = pieces[0].astype(f32)
    for piece in pieces[1:]:
        total = total + piece.astype(f32)
    return total.astype(bf16)


def join(pieces, group, me):
    radix = 2 ** len(group)
    digit = (me // group[0]) % radix
    joined = jnp.zeros((radix,) + pieces[0].shape, pieces[0].dtype)
    for step, piece in enumerate(pieces):
        joined = lax.dynamic_update_index_in_dim(joined, piece, digit ^ step, 0)
    return joined.reshape((radix * pieces[0].shape[0],) + pieces[0].shape[1:])


def prepare(pieces, done, following, me):
    reduce_done, group_done = done
    reduce_next, group_next = following
    if not reduce_done:
        return [join(pieces, group_done, me)]
    if reduce_next:
        return combine(pieces, group_next, me)
    return [add_up(pieces)]


def launch(operands, stage, count):
    reduce, group = stage
    return send_parts(operands, group, count) if reduce else send_whole(operands[0], group, count)


def after(values, *others):
    return list(lax.optimization_barrier((tuple(values), others))[0])


def body(questions, passages, cot_questions, cot_passages, len_questions, len_passages, positive, *weights):
    local = questions.shape[0]
    question_length = questions.shape[1]
    passage_length = passages.shape[1]
    count = positive.shape[0] // local
    me = lax.axis_index("dp")
    bit = (me % 2).reshape(1)
    x_q = questions.reshape(-1, WIDTH)
    x_p = passages.reshape(-1, WIDTH)
    own_cls = first_call(count, local, len_questions, len_passages, x_q, x_p, weights)
    own_cls, x_q, x_p = lax.optimization_barrier((own_cls, x_q, x_p))
    all_cls = lax.all_to_all(own_cls, "dp", 0, 0, tiled=True)
    attended_p = attend(1, local, 1, passage_length, len_passages, x_p, weights)
    attended_q = attend(0, 1, local, question_length, len_questions, x_q, weights)
    (all_cls,) = after([all_cls], attended_p[2], attended_q[2])
    slots = positive // local * PAD + positive % local
    slots = jnp.pad(slots.reshape(count, local), ((0, 0), (0, PAD - local)), constant_values=-1)
    own_slots = lax.dynamic_slice_in_dim(slots, me, 1, axis=0).reshape(PAD, 1)
    loss, grad_cls_q, grad_cls_p = pl.pallas_call(
        functools.partial(loss_kernel, local),
        out_shape=[shape((PAD, 128), f32), shape((PAD, WIDTH), f32), shape((PAD, WIDTH), f32)],
        grid=(1,),
        in_specs=[smem(), whole((count, 2 * PAD, WIDTH)), whole((1, count * PAD)), whole((PAD, 1))],
        out_specs=[whole((PAD, 128)), whole((PAD, WIDTH)), whole((PAD, WIDTH))],
        scratch_shapes=[pltpu.VMEM((count * PAD, WIDTH), bf16), pltpu.VMEM((count * PAD, WIDTH), bf16)],
        compiler_params=params(),
        name="loss",
    )(me.reshape(1), all_cls, slots.reshape(1, -1), own_slots)
    loss_rows = loss[:local, 0]
    out_q, grad_q, keep_q, send_q = layer(
        0, 1, local, question_length, bit, len_questions, grad_cls_q, x_q, cot_questions.reshape(-1, WIDTH),
        attended_q, weights,
    )
    groups = stages(count)
    steps = [(True, group) for group in groups] + [(False, group) for group in groups[::-1]]
    operands_q = prepare([keep_q, partner_send(send_q, groups[0][0], count)], steps[0], steps[1], me)
    (grad_cls_p,) = after([grad_cls_p], *operands_q)
    pieces_q = launch(operands_q, steps[1], count)
    out_p, grad_p, keep_p, send_p = layer(
        1, local, 1, passage_length, bit, len_passages, grad_cls_p, x_p, cot_passages.reshape(-1, WIDTH),
        attended_p, weights,
    )
    (send_p,) = after([send_p], *pieces_q)
    pieces_p = [keep_p, partner_send(send_p, groups[0][0], count)]
    for place in range(len(steps)):
        if 0 < place < len(steps) - 1:
            pieces_p = after(pieces_p, *operands_q)
            operands_p = prepare(pieces_p, steps[place - 1], steps[place], me)
            pieces_p = launch(operands_p, steps[place], count)
            pieces_q = after(pieces_q, *operands_p)
        if place + 2 < len(steps):
            operands_q = prepare(pieces_q, steps[place + 1], steps[place + 2], me)
            pieces_q = launch(operands_q, steps[place + 2], count)
    own_q, other_q = pieces_q
    parts = len(pieces_p)
    digit = (me // groups[1][0] % parts).reshape(1)
    dims = [(WIDTH, 3 * WIDTH), (WIDTH, WIDTH), (WIDTH, HIDDEN), (HIDDEN, WIDTH)]
    matrices = [shape((2,) + d, f32) for d in dims]
    *halves, tail = pl.pallas_call(
        question_unpack_kernel,
        out_shape=matrices + [shape((VECTOR_ROWS, WIDTH), f32)],
        grid=(1,),
        in_specs=[smem()] + [whole((HALF, WIDTH))] * 2,
        out_specs=[part_of(0, d) for d in dims] + [whole((VECTOR_ROWS, WIDTH))],
        scratch_shapes=[pltpu.VMEM((GROUP_ROWS, WIDTH), bf16)],
        compiler_params=params(),
        name="unpack_q",
    )(bit, own_q, other_q)
    own_piece, *came = pieces_p
    came = after(came, tail, loss_rows)
    pieces_p = [own_piece] + came
    other_p = [partner_send(piece, groups[0][0], count) for piece in pieces_p]
    vectors = [(2, HIDDEN)] + [(2, WIDTH)] * len(VECTOR_OUTS)
    first_alias = 2 + 2 * parts + 1
    d_qkv, d_proj, d_up, d_down, up_bias, query_bias, value_bias, proj_bias, gain_a, shift_a, down_bias, gain_f, shift_f = pl.pallas_call(
        functools.partial(passage_unpack_kernel, parts),
        out_shape=matrices + [shape(d, f32) for d in vectors],
        grid=(1,),
        in_specs=[smem(), smem()] + [whole((HALF // parts, WIDTH))] * (2 * parts) + [whole((VECTOR_ROWS, WIDTH))]
        + [pl.BlockSpec(memory_space=pl.ANY)] * 4,
        out_specs=[part_of(1, d) for d in dims] + [whole(d) for d in vectors],
        scratch_shapes=[pltpu.VMEM((GROUP_ROWS, WIDTH), bf16)],
        input_output_aliases={first_alias + i: i for i in range(4)},
        compiler_params=params(),
        name="unpack_p",
    )(bit, digit, *pieces_p, *other_p, tail, *halves)
    return (
        loss_rows, out_q.reshape(questions.shape), out_p.reshape(passages.shape),
        grad_q.reshape(questions.shape), grad_p.reshape(passages.shape),
        d_qkv, query_bias, value_bias, d_proj, proj_bias, gain_a, shift_a, d_up, up_bias, d_down,
        down_bias, gain_f, shift_f,
    )


def solution(mesh):
    split = P("dp", None, None)
    return jax.shard_map(
        body,
        mesh=mesh,
        in_specs=(split, split, split, split, P("dp"), P("dp")) + (P(),) * 14,
        out_specs=(P("dp"), split, split, split, split) + (P(),) * 13,
        check_vma=False,
    )
```

```python
import functools

import jax
import jax.numpy as jnp
from jax import lax
from jax.experimental import pallas as pl
from jax.experimental.pallas import tpu as pltpu
from jax.sharding import PartitionSpec as P

HEAD_DIM = 64
WIDTH = 256
HEADS = WIDTH // HEAD_DIM
HIDDEN = 1024
BLOCKS = HIDDEN // WIDTH
PAD = 8
VECTOR_ROWS = 16
HALF = 6 * WIDTH + 128
GROUP_ROWS = 2 * HALF
LANES = 128
SOFT = 128
NORM = 32
GELU = 32
ln_eps = 1e-06
score_scale = 0.125
masked_score = -1e30
f32 = jnp.float32
bf16 = jnp.bfloat16

QUERY_BIAS, VALUE_BIAS, PROJ_BIAS, ATTN_GAIN, ATTN_SHIFT, DOWN_BIAS, FFN_GAIN, FFN_SHIFT = range(8)
UP_BIAS = 8


def dot(a, b):
    return lax.dot_general(a, b, (((1,), (0,)), ((), ())), preferred_element_type=f32)


def dot_nt(a, b):
    return lax.dot_general(a, b, (((1,), (1,)), ((), ())), preferred_element_type=f32)


def dot_tn(a, b):
    return lax.dot_general(a, b, (((0,), (0,)), ((), ())), preferred_element_type=f32)


def row_loop(rows, chunk, step):
    for row in range(0, rows, chunk):
        step(row)


def vector(ref, which):
    return ref[...].astype(f32)[which : which + 1]


def lane_head(rows):
    return lax.broadcasted_iota(jnp.int32, (rows, WIDTH), 1) // HEAD_DIM


def one_head(values, h, scale=1.0):
    return jnp.where(lane_head(values.shape[0]) == h, values.astype(f32) * scale, 0.0).astype(bf16)


def some_heads(values, first, last, scale=1.0):
    return jnp.concatenate([one_head(values, h, scale) for h in range(first, last)], axis=0)


def pick_heads(stacked, rows):
    head = lane_head(rows)
    result = stacked[:rows]
    for h in range(1, HEADS):
        result = jnp.where(head == h, stacked[h * rows : (h + 1) * rows], result)
    return result


def block_rows(block):
    start = block * WIDTH if block < 6 else HALF + (block - 6) * WIDTH
    return slice(start, start + WIDTH)


VECTOR_START = 6 * WIDTH
QKV_BLOCK, PROJ_BLOCK, UP_BLOCK, DOWN_BLOCK = 0, 3, 4, 8


def normalize(value):
    centered = value - jnp.mean(value, axis=1, keepdims=True)
    inverse = lax.rsqrt(jnp.mean(centered * centered, axis=1, keepdims=True) + ln_eps)
    return centered * inverse, inverse


def masked_softmax(scores, size, scale=score_scale):
    part = scores * scale if scale != 1.0 else scores
    key = lax.broadcasted_iota(jnp.int32, part.shape, 1)
    part = jnp.where(key < size, part, masked_score)
    part = jnp.exp(part - jnp.max(part, axis=1, keepdims=True))
    return part * (1.0 / jnp.sum(part, axis=1, keepdims=True))


def gelu_parts(value):
    cumulative = 0.5 + 0.5 * lax.erf(value * 0.7071067811865476)
    density = jnp.exp(value * value * -0.5) * 0.3989422804014327
    return (value * cumulative).astype(bf16), cumulative + value * density


def first_kernel(
    seqs, lq_ref, lp_ref, xq_ref, xp_ref,
    wqkv_ref, qb_ref, vb_ref, wo_ref, ob_ref, g1_ref, b1_ref, w1_ref, hb_ref, w2_ref, fb_ref, g2_ref, b2_ref,
    cls_ref,
    kq_ref, vq_ref, kp_ref, vp_ref,
):
    sides = ((0, xq_ref, kq_ref, vq_ref, lq_ref), (1, xp_ref, kp_ref, vp_ref, lp_ref))
    filler = jnp.zeros((PAD - seqs, WIDTH), f32)
    inputs = []
    for which, x_ref, *_ in sides:
        length = x_ref.shape[0] // seqs
        firsts = [x_ref[s * length : s * length + 16, :].astype(f32)[:1] for s in range(seqs)]
        inputs.append(jnp.concatenate(firsts + [filler], axis=0))
    own_lanes = lane_head(PAD) == lax.broadcasted_iota(jnp.int32, (PAD, WIDTH), 0)
    queries = [
        (dot(inputs[which].astype(bf16), wqkv_ref[which, :, :WIDTH]) + vector(qb_ref, which)).astype(bf16).astype(f32)
        for which in range(2)
    ]
    for which, x_ref, k_ref, v_ref, _ in sides:
        x = x_ref[...]
        k_ref[...] = dot(x, wqkv_ref[which, :, WIDTH : 2 * WIDTH]).astype(bf16)
        v_ref[...] = (dot(x, wqkv_ref[which, :, 2 * WIDTH :]) + vector(vb_ref, which)).astype(bf16)
    context = []
    for which, x_ref, k_ref, v_ref, len_ref in sides:
        length = x_ref.shape[0] // seqs
        spans = [slice(s * length, (s + 1) * length) for s in range(seqs)]
        scores, sizes = [], []
        for s, span in enumerate(spans):
            heads = jnp.where(own_lanes, queries[which][s : s + 1], 0.0).astype(bf16)
            scores.append(dot_nt(heads, k_ref[span, :]))
            sizes.append(jnp.full((PAD, length), len_ref[s], jnp.int32))
        prob = masked_softmax(jnp.concatenate(scores, axis=0), jnp.concatenate(sizes, axis=0)).astype(f32)
        rows = []
        for s, span in enumerate(spans):
            mixed = dot(prob[s * PAD : (s + 1) * PAD].astype(bf16), v_ref[span, :])
            rows.append(jnp.sum(jnp.where(own_lanes, mixed, 0.0), axis=0, keepdims=True))
        context.append(jnp.concatenate(rows + [filler], axis=0).astype(bf16))
    normed = []
    for which in range(2):
        value = inputs[which] + (dot(context[which], wo_ref[which]) + vector(ob_ref, which))
        unit, _ = normalize(value)
        normed.append(unit * vector(g1_ref, which) + vector(b1_ref, which))
    active = []
    for which in range(2):
        active.append(gelu_parts(dot(normed[which].astype(bf16), w1_ref[which]) + vector(hb_ref, which))[0])
    results = []
    for which in range(2):
        value = normed[which] + (dot(active[which], w2_ref[which]) + vector(fb_ref, which))
        unit, _ = normalize(value)
        result = unit * vector(g2_ref, which) + vector(b2_ref, which)
        row = lax.broadcasted_iota(jnp.int32, result.shape, 0)
        results.append(jnp.where(row < seqs, result, 0.0))
    both = jnp.concatenate(results, axis=0).astype(bf16)

    def store(i, carry):
        cls_ref[i] = both
        return carry

    lax.fori_loop(0, cls_ref.shape[0], store, 0)


def head_groups(length):
    together = max(1, WIDTH // length)
    return [(h, h + together, slice(h * length, (h + together) * length)) for h in range(0, HEADS, together)]


def attend_kernel(which, seqs, length, len_ref, x_ref, wqkv_ref, qb_ref, vb_ref, qkv_ref, p_ref, ctx_ref, score_ref, prob_ref):
    step = pl.program_id(0)
    x = x_ref[...]
    qkv_ref[:, :WIDTH] = (dot(x, wqkv_ref[:, :WIDTH]) + vector(qb_ref, which)).astype(bf16)
    qkv_ref[:, WIDTH : 2 * WIDTH] = dot(x, wqkv_ref[:, WIDTH : 2 * WIDTH]).astype(bf16)
    qkv_ref[:, 2 * WIDTH :] = (dot(x, wqkv_ref[:, 2 * WIDTH :]) + vector(vb_ref, which)).astype(bf16)
    for s in range(seqs):
        span = slice(s * length, (s + 1) * length)
        size = len_ref[step * seqs + s]
        keys = qkv_ref[span, WIDTH : 2 * WIDTH]
        for first, last, columns in head_groups(length):
            score_ref[span, columns] = dot_nt(keys, some_heads(qkv_ref[span, :WIDTH], first, last, score_scale))
            for lane in range(columns.start, columns.stop, LANES):
                here = slice(lane, lane + LANES)
                part = score_ref[span, here]
                key = lax.broadcasted_iota(jnp.int32, part.shape, 0)
                part = jnp.where(key < size, part, masked_score)
                part = jnp.exp(part - jnp.max(part, axis=0, keepdims=True))
                prob = part * (1.0 / jnp.sum(part, axis=0, keepdims=True))
                p_ref[span, here] = prob
                prob_ref[span, here] = prob.astype(bf16)
        ctx_ref[span, :] = pick_heads(dot_tn(prob_ref[span, :], qkv_ref[span, 2 * WIDTH :]), length).astype(bf16)


def attend_long_kernel(which, seqs, length, len_ref, x_ref, wqkv_ref, qb_ref, vb_ref, qkv_ref, p_ref, ctx_ref, score_ref, prob_ref):
    step = pl.program_id(0)
    x = x_ref[...]
    qkv_ref[:, :WIDTH] = (dot(x, wqkv_ref[:, :WIDTH]) + vector(qb_ref, which)).astype(bf16)
    qkv_ref[:, WIDTH : 2 * WIDTH] = dot(x, wqkv_ref[:, WIDTH : 2 * WIDTH]).astype(bf16)
    qkv_ref[:, 2 * WIDTH :] = (dot(x, wqkv_ref[:, 2 * WIDTH :]) + vector(vb_ref, which)).astype(bf16)
    stack_rows = HEADS * length
    for s in range(seqs):
        span = slice(s * length, (s + 1) * length)
        stack = slice(s * stack_rows, (s + 1) * stack_rows)
        size = len_ref[step * seqs + s]
        queries = qkv_ref[span, :WIDTH]
        for h in range(HEADS):
            start = s * stack_rows + h * length
            score_ref[start : start + length, :] = dot_nt(one_head(queries, h, score_scale), qkv_ref[span, WIDTH : 2 * WIDTH])

            def softmax(row):
                here = pl.ds(start + row, SOFT)
                prob = masked_softmax(score_ref[here, :], size, 1.0)
                p_ref[here, :] = prob
                prob_ref[here, :] = prob.astype(bf16)

            row_loop(length, SOFT, softmax)
        ctx_ref[span, :] = pick_heads(dot(prob_ref[stack, :], qkv_ref[span, 2 * WIDTH :]), length).astype(bf16)


def forward_phase(
    which, rows, x_ref, wo_ref, ob_ref, g1_ref, b1_ref, w1_ref, hb_ref, w2_ref,
    ctx_ref, n1_ref, r1_ref, nb_ref, gp_ref, act_ref, n2_ref, wide_ref,
):
    n2_ref[...] = dot(ctx_ref[...], wo_ref[...])
    ob, g1, b1 = vector(ob_ref, which), vector(g1_ref, which), vector(b1_ref, which)

    def first_norm(row):
        here = pl.ds(row, NORM)
        unit, inverse = normalize(x_ref[here, :].astype(f32) + (n2_ref[here, :] + ob))
        n1_ref[here, :] = unit
        r1_ref[here, :] = inverse
        nb_ref[here, :] = (unit * g1 + b1).astype(bf16)

    row_loop(rows, NORM, first_norm)
    hb = vector(hb_ref, which)
    for j in range(BLOCKS):
        lanes = slice(j * WIDTH, (j + 1) * WIDTH)
        wide_ref[:, lanes] = dot(nb_ref[...], w1_ref[:, lanes])

        def gelu(row):
            here = pl.ds(row, GELU)
            active, slope = gelu_parts(wide_ref[here, lanes] + hb[:, lanes])
            act_ref[here, lanes] = active
            gp_ref[here, lanes] = slope

        row_loop(rows, GELU, gelu)
    n2_ref[...] = dot(act_ref[...], w2_ref[...])


def add_row(vec_ref, row, values):
    here = slice(row * PAD, (row + 1) * PAD)
    vec_ref[here, :] = vec_ref[here, :] + jnp.sum(values.reshape(-1, PAD, WIDTH), axis=0)


def ffn_phase(which, seqs, length, first, len_ref, cls_ref, cot_ref, n1_ref, n2_ref, gp_ref, w2_ref, g1_ref, b1_ref, fb_ref, g2_ref, b2_ref, out_ref, two_ref, gffn_ref, gpre_ref, vec_ref, wide_ref):
    g1, g2, b2 = vector(g1_ref, which), vector(g2_ref, which), vector(b2_ref, which)
    shift = vector(b1_ref, which) + vector(fb_ref, which)
    for s in range(seqs):
        size = len_ref[first + s]
        cls_row = cls_ref[pl.ds(first + s, 1), :]

        def output_norm(row):
            here = pl.ds(s * length + row, NORM)
            inside = row + lax.broadcasted_iota(jnp.int32, (NORM, WIDTH), 0) < size
            unit, inverse = normalize(n1_ref[here, :] * g1 + (n2_ref[here, :] + shift))
            out_ref[here, :] = jnp.where(inside, unit * g2 + b2, 0.0).astype(bf16)
            grad = cot_ref[here, :].astype(f32)
            if row == 0:
                grad = grad + jnp.where(lax.broadcasted_iota(jnp.int32, (NORM, WIDTH), 0) == 0, cls_row, 0.0)
            grad = jnp.where(inside, grad, 0.0)
            scaled = grad * g2
            slope = scaled * unit
            first_mean = jnp.mean(scaled, axis=1, keepdims=True)
            second_mean = jnp.mean(slope, axis=1, keepdims=True)
            two = inverse * (scaled - first_mean - unit * second_mean)
            low = two.astype(bf16)
            two_ref[here, :] = two
            gffn_ref[here, :] = low
            add_row(vec_ref, FFN_GAIN, grad * unit)
            add_row(vec_ref, FFN_SHIFT, grad)
            add_row(vec_ref, DOWN_BIAS, low.astype(f32))

        row_loop(length, NORM, output_norm)
    for j in range(BLOCKS):
        lanes = slice(j * WIDTH, (j + 1) * WIDTH)
        wide_ref[:, lanes] = dot_nt(gffn_ref[...], w2_ref[lanes, :])

        def gelu_back(row):
            here = pl.ds(row, GELU)
            low = (wide_ref[here, lanes] * gp_ref[here, lanes]).astype(bf16)
            gpre_ref[here, lanes] = low
            add_row(vec_ref, UP_BIAS + j, low.astype(f32))

        row_loop(seqs * length, GELU, gelu_back)


def attn_norm_phase(which, rows, gpre_ref, w1_ref, two_ref, n1_ref, r1_ref, g1_ref, wo_ref, one_ref, gatt_ref, dctx_ref, vec_ref):
    one_ref[...] = dot_nt(gpre_ref[...], w1_ref[...])
    g1 = vector(g1_ref, which)

    def norm_back(row):
        here = pl.ds(row, NORM)
        grad = two_ref[here, :] + one_ref[here, :]
        unit = n1_ref[here, :]
        scaled = grad * g1
        first_mean = jnp.mean(scaled, axis=1, keepdims=True)
        second_mean = jnp.mean(scaled * unit, axis=1, keepdims=True)
        one = r1_ref[here, :] * (scaled - first_mean - unit * second_mean)
        low = one.astype(bf16)
        one_ref[here, :] = one
        gatt_ref[here, :] = low
        add_row(vec_ref, ATTN_GAIN, grad * unit)
        add_row(vec_ref, ATTN_SHIFT, grad)
        add_row(vec_ref, PROJ_BIAS, low.astype(f32))

    row_loop(rows, NORM, norm_back)
    dctx_ref[...] = dot_nt(gatt_ref[...], wo_ref[...]).astype(bf16)


def attn_core_phase(seqs, length, dctx_ref, qkv_ref, p_ref, gqkv_ref, vec_ref, dp_ref, ds_ref, pb_ref):
    for s in range(seqs):
        span = slice(s * length, (s + 1) * length)
        values = qkv_ref[span, 2 * WIDTH :]
        context = some_heads(dctx_ref[span, :], 0, HEADS)
        for first, last, columns in head_groups(length):
            dp_ref[span, columns] = dot_nt(values, context[columns])
            for lane in range(columns.start, columns.stop, LANES):
                here = slice(lane, lane + LANES)
                prob = p_ref[span, here]
                grad = dp_ref[span, here]
                inner = jnp.sum(prob * grad, axis=0, keepdims=True)
                ds_ref[span, here] = (prob * (grad - inner)).astype(bf16)
                pb_ref[span, here] = prob.astype(bf16)
        queries = some_heads(qkv_ref[span, :WIDTH], 0, HEADS, score_scale)
        gqkv_ref[span, WIDTH : 2 * WIDTH] = dot(ds_ref[span, :], queries).astype(bf16)
        grad_v = dot(pb_ref[span, :], context).astype(bf16)
        gqkv_ref[span, 2 * WIDTH :] = grad_v
        add_row(vec_ref, VALUE_BIAS, grad_v.astype(f32))
        grad_q = (pick_heads(dot_tn(ds_ref[span, :], qkv_ref[span, WIDTH : 2 * WIDTH]), length) * score_scale).astype(bf16)
        gqkv_ref[span, :WIDTH] = grad_q
        add_row(vec_ref, QUERY_BIAS, grad_q.astype(f32))


def attn_core_long(seqs, length, dctx_ref, qkv_ref, p_ref, gqkv_ref, vec_ref, dp_ref, ds_ref, pb_ref):
    stack_rows = HEADS * length
    for s in range(seqs):
        span = slice(s * length, (s + 1) * length)
        stack = slice(s * stack_rows, (s + 1) * stack_rows)
        contexts = [one_head(dctx_ref[span, :], h) for h in range(HEADS)]
        for h in range(HEADS):
            start = s * stack_rows + h * length
            dp_ref[start : start + length, :] = dot_nt(contexts[h], qkv_ref[span, 2 * WIDTH :])

            def softmax_back(row):
                here = pl.ds(start + row, SOFT)
                prob = p_ref[here, :]
                grad = dp_ref[here, :]
                inner = jnp.sum(prob * grad, axis=1, keepdims=True)
                ds_ref[here, :] = (prob * (grad - inner)).astype(bf16)
                pb_ref[here, :] = prob.astype(bf16)

            row_loop(length, SOFT, softmax_back)
        context = jnp.concatenate(contexts, axis=0)
        queries = some_heads(qkv_ref[span, :WIDTH], 0, HEADS, score_scale)
        grad_q = (pick_heads(dot(ds_ref[stack, :], qkv_ref[span, WIDTH : 2 * WIDTH]), length) * score_scale).astype(bf16)
        gqkv_ref[span, :WIDTH] = grad_q
        add_row(vec_ref, QUERY_BIAS, grad_q.astype(f32))
        gqkv_ref[span, WIDTH : 2 * WIDTH] = dot_tn(ds_ref[stack, :], queries).astype(bf16)
        grad_v = dot_tn(pb_ref[stack, :], context).astype(bf16)
        gqkv_ref[span, 2 * WIDTH :] = grad_v
        add_row(vec_ref, VALUE_BIAS, grad_v.astype(f32))


def layer_kernel(
    which, steps, seqs, length,
    bit_ref, len_ref, cls_ref, x_ref, cot_ref, qkv_ref, p_ref, ctx_ref,
    wo_ref, ob_ref, g1_ref, b1_ref, w1_ref, hb_ref, w2_ref, fb_ref, g2_ref, b2_ref,
    out_ref, one_ref, gqkv_ref, keep_ref, send_ref,
    acc_ref, vec_ref, n1_ref, r1_ref, nb_ref, gp_ref, act_ref, n2_ref,
    wide_ref, score_ref, prob_ref, two_ref, gffn_ref, gpre_ref, gatt_ref, dctx_ref, ds_ref,
):
    rows = seqs * length
    step = pl.program_id(0)

    def start():
        vec_ref[...] = jnp.zeros_like(vec_ref)
        if steps > 1:
            acc_ref[...] = jnp.zeros_like(acc_ref)

    if steps > 1:
        pl.when(step == 0)(start)
    else:
        start()

    def add_block(block, value):
        if steps > 1:
            acc_ref[block_rows(block), :] += value
        else:
            acc_ref[block_rows(block), :] = value

    forward_phase(
        which, rows, x_ref, wo_ref, ob_ref, g1_ref, b1_ref, w1_ref, hb_ref, w2_ref,
        ctx_ref, n1_ref, r1_ref, nb_ref, gp_ref, act_ref, n2_ref, wide_ref,
    )
    ffn_phase(which, seqs, length, step * seqs, len_ref, cls_ref, cot_ref, n1_ref, n2_ref, gp_ref, w2_ref, g1_ref, b1_ref, fb_ref, g2_ref, b2_ref, out_ref, two_ref, gffn_ref, gpre_ref, vec_ref, wide_ref)
    downs = dot_tn(act_ref[...], gffn_ref[...])
    ups = dot_tn(nb_ref[...], gpre_ref[...])
    for j in range(BLOCKS):
        lanes = slice(j * WIDTH, (j + 1) * WIDTH)
        add_block(DOWN_BLOCK + j, downs[lanes])
        add_block(UP_BLOCK + j, ups[:, lanes])
    attn_norm_phase(which, rows, gpre_ref, w1_ref, two_ref, n1_ref, r1_ref, g1_ref, wo_ref, one_ref, gatt_ref, dctx_ref, vec_ref)
    add_block(PROJ_BLOCK, dot_tn(ctx_ref[...], gatt_ref[...]))
    attn_core = attn_core_long if seqs == 1 else attn_core_phase
    attn_core(seqs, length, dctx_ref, qkv_ref, p_ref, gqkv_ref, vec_ref, score_ref, ds_ref, prob_ref)
    for j in range(3):
        add_block(QKV_BLOCK + j, dot_tn(x_ref[...], gqkv_ref[:, j * WIDTH : (j + 1) * WIDTH]))

    def finish():
        acc_ref[VECTOR_START : VECTOR_START + VECTOR_ROWS, :] = jnp.sum(vec_ref[...].reshape(VECTOR_ROWS, PAD, WIDTH), axis=1)
        if steps == 1:
            acc_ref[VECTOR_START + VECTOR_ROWS : HALF, :] = jnp.zeros((HALF - VECTOR_START - VECTOR_ROWS, WIDTH), f32)
            acc_ref[HALF + 6 * WIDTH :, :] = jnp.zeros((HALF - 6 * WIDTH, WIDTH), f32)
        keep = pl.multiple_of(bit_ref[0] * HALF, HALF)
        send = pl.multiple_of((1 - bit_ref[0]) * HALF, HALF)
        keep_ref[...] = acc_ref[pl.ds(keep, HALF), :].astype(bf16)
        send_ref[...] = acc_ref[pl.ds(send, HALF), :].astype(bf16)

    if steps > 1:
        pl.when(step == steps - 1)(finish)
    else:
        finish()


def loss_phase(local, me_ref, all_ref, hot_ref, own_hot_ref, loss_ref, gq_ref, gp_ref, q_ref, p_ref):
    count = all_ref.shape[0]
    me = me_ref[0]
    wide = all_ref[...].astype(f32)
    q_ref[...] = wide[:, :PAD].reshape(count * PAD, WIDTH).astype(bf16)
    p_ref[...] = wide[:, PAD:].reshape(count * PAD, WIDTH).astype(bf16)
    own_q = all_ref[me][:PAD]
    own_p = all_ref[me][PAD:]
    logits = dot_nt(own_q, p_ref[...]) * score_scale
    column = lax.broadcasted_iota(jnp.int32, logits.shape, 1)
    logits = jnp.where(column % PAD < local, logits, masked_score)
    top = jnp.max(logits, axis=1, keepdims=True)
    total = top + jnp.log(jnp.sum(jnp.exp(logits - top), axis=1, keepdims=True))
    hot = (column == own_hot_ref[...]).astype(f32)
    loss_ref[...] = jnp.broadcast_to(total - jnp.sum(logits * hot, axis=1, keepdims=True), loss_ref.shape)
    grad = (jnp.exp(logits - total) - hot).astype(bf16)
    gq_ref[...] = dot(grad, p_ref[...]) * score_scale
    gp_ref[...] = jnp.zeros_like(gp_ref)
    block = 256 if count * PAD % 256 == 0 else count * PAD

    def part(index, carry):
        start = index * block if isinstance(index, int) else pl.multiple_of(index * block, block)
        queries = q_ref[pl.ds(start, block), :]
        scores = dot_nt(p_ref[...], queries) * score_scale
        row = lax.broadcasted_iota(jnp.int32, scores.shape, 0)
        scores = jnp.where(row % PAD < local, scores, masked_score)
        peak = jnp.max(scores, axis=0, keepdims=True)
        sums = peak + jnp.log(jnp.sum(jnp.exp(scores - peak), axis=0, keepdims=True))
        own = dot_nt(own_p, queries) * score_scale
        own_row = lax.broadcasted_iota(jnp.int32, own.shape, 0)
        own_lane = lax.broadcasted_iota(jnp.int32, own.shape, 1)
        own_hits = (own_row + me * PAD == hot_ref[:, pl.ds(start, block)]).astype(f32)
        own_grad = jnp.where(own_lane % PAD < local, jnp.exp(own - sums) - own_hits, 0.0)
        gp_ref[...] += dot(own_grad.astype(bf16), queries) * score_scale
        return carry

    if count * PAD == block:
        part(0, 0)
    else:
        lax.fori_loop(0, count * PAD // block, part, 0)


def question_kernel(local, seqs, length, me_ref, all_ref, hot_ref, own_hot_ref, bit_ref, len_ref, *refs):
    inputs, outputs, scratch = refs[:15], refs[15:22], refs[22:]
    loss_ref, gp_ref = outputs[5:]
    gq_ref, q_ref, p_ref = scratch[:3]
    loss_phase(local, me_ref, all_ref, hot_ref, own_hot_ref, loss_ref, gq_ref, gp_ref, q_ref, p_ref)
    layer_kernel(0, 1, seqs, length, bit_ref, len_ref, gq_ref, *inputs, *outputs[:5], *scratch[3:])


def combine_kernel(radix, digit_ref, *refs):
    total_ref = refs[-1]
    sends = refs[-1 - (radix - 1) : -1]
    keep_ref = refs[-1 - radix]
    pieces = refs[: -1 - radix]
    total = pieces[0][...].astype(f32)
    for piece in pieces[1:]:
        total = total + piece[...].astype(f32)
    total_ref[...] = total
    part = total_ref.shape[0] // radix
    digit = digit_ref[0]

    def section(which):
        return total_ref[pl.ds(pl.multiple_of(which * part, part), part), :].astype(bf16)

    keep_ref[...] = section(digit)
    for step, ref in enumerate(sends, start=1):
        ref[...] = section(digit ^ step)


VECTOR_OUTS = (QUERY_BIAS, VALUE_BIAS, PROJ_BIAS, ATTN_GAIN, ATTN_SHIFT, DOWN_BIAS, FFN_GAIN, FFN_SHIFT)


def spread(which, ref, qkv_ref, proj_ref, up_ref, down_ref):
    for j in range(3):
        qkv_ref[:, j * WIDTH : (j + 1) * WIDTH] = ref[block_rows(QKV_BLOCK + j), :].astype(f32)
    proj_ref[...] = ref[block_rows(PROJ_BLOCK), :].astype(f32)
    for j in range(BLOCKS):
        up_ref[:, j * WIDTH : (j + 1) * WIDTH] = ref[block_rows(UP_BLOCK + j), :].astype(f32)
        down_ref[j * WIDTH : (j + 1) * WIDTH, :] = ref[block_rows(DOWN_BLOCK + j), :].astype(f32)
    return ref[VECTOR_START : VECTOR_START + VECTOR_ROWS, :].astype(f32)


def question_unpack_kernel(bit_ref, own_ref, other_ref, qkv_ref, proj_ref, up_ref, down_ref, tail_ref, whole_ref):
    whole_ref[pl.ds(pl.multiple_of(bit_ref[0] * HALF, HALF), HALF), :] = own_ref[...]
    whole_ref[pl.ds(pl.multiple_of((1 - bit_ref[0]) * HALF, HALF), HALF), :] = other_ref[...]
    tail_ref[...] = spread(0, whole_ref, qkv_ref, proj_ref, up_ref, down_ref)


def passage_unpack_kernel(parts, bit_ref, digit_ref, *refs):
    own_refs, other_refs, (tail_ref, *_) = refs[:parts], refs[parts : 2 * parts], refs[2 * parts : 2 * parts + 5]
    qkv_ref, proj_ref, up_ref, down_ref, up_bias_ref, *vector_refs, whole_ref = refs[2 * parts + 5 :]
    size = HALF // parts
    for half, halves in ((bit_ref[0], own_refs), (1 - bit_ref[0], other_refs)):
        for step, ref in enumerate(halves):
            start = half * HALF + (digit_ref[0] ^ step) * size
            whole_ref[pl.ds(pl.multiple_of(start, 8), size), :] = ref[...]
    tails = (tail_ref[...], spread(1, whole_ref, qkv_ref, proj_ref, up_ref, down_ref))
    for row, ref in zip(VECTOR_OUTS, vector_refs):
        for which in range(2):
            ref[which : which + 1, :] = tails[which][row : row + 1]
    for j in range(BLOCKS):
        for which in range(2):
            up_bias_ref[which : which + 1, j * WIDTH : (j + 1) * WIDTH] = tails[which][UP_BIAS + j : UP_BIAS + j + 1]


def smem():
    return pl.BlockSpec(memory_space=pltpu.SMEM)


def whole(shape):
    return pl.BlockSpec(shape, lambda i: (0,) * len(shape))


def rows_of(rows, columns):
    return pl.BlockSpec((rows, columns), lambda i: (i, 0))


def part_of(which, shape):
    return pl.BlockSpec((None,) + shape, lambda i: (which, 0, 0))


def params():
    return pltpu.CompilerParams(vmem_limit_bytes=24 * 1024 * 1024)


def shape(dims, kind):
    return jax.ShapeDtypeStruct(dims, kind)


def cost(flops, moved):
    return pl.CostEstimate(flops=flops, bytes_accessed=moved, transcendentals=0)


def pair(columns):
    return whole((2, columns))


def in_hbm(values):
    return pltpu.with_memory_space_constraint(values, pltpu.HBM)


def first_call(count, local, len_questions, len_passages, x_q, x_p, weights):
    return pl.pallas_call(
        functools.partial(first_kernel, local),
        out_shape=shape((count, 2 * PAD, WIDTH), bf16),
        grid=(1,),
        in_specs=[smem(), smem(), whole(x_q.shape), whole(x_p.shape)] + [whole(member.shape) for member in weights],
        out_specs=whole((count, 2 * PAD, WIDTH)),
        scratch_shapes=[pltpu.VMEM(x_q.shape, bf16)] * 2 + [pltpu.VMEM(x_p.shape, bf16)] * 2,
        compiler_params=params(),
        name="first",
    )(in_hbm(len_questions), in_hbm(len_passages), in_hbm(x_q), in_hbm(x_p), *[in_hbm(member) for member in weights])


def attend(which, steps, seqs, length, lengths, x, weights):
    wqkv, qb, vb, *_ = weights
    rows = seqs * length
    total = steps * rows
    block = (HEADS * length, length) if seqs == 1 else (rows, HEADS * length)
    return pl.pallas_call(
        functools.partial(attend_long_kernel if seqs == 1 else attend_kernel, which, seqs, length),
        out_shape=[
            pltpu.HBM((total, 3 * WIDTH), bf16), pltpu.HBM((steps * block[0], block[1]), f32), pltpu.HBM((total, WIDTH), bf16),
        ],
        grid=(steps,),
        in_specs=[smem(), rows_of(rows, WIDTH), part_of(which, (WIDTH, 3 * WIDTH)), pair(WIDTH), pair(WIDTH)],
        out_specs=[rows_of(rows, 3 * WIDTH), rows_of(*block), rows_of(rows, WIDTH)],
        scratch_shapes=[pltpu.VMEM(block, f32), pltpu.VMEM(block, bf16)],
        compiler_params=params(),
        cost_estimate=cost(total * 2 * 400000, total * 6000),
        name="attend",
    )(lengths, in_hbm(x), in_hbm(wqkv), in_hbm(qb), in_hbm(vb))


def layer(which, steps, seqs, length, bit, lengths, cls_grad, x, cot, attended, weights, exchange=None):
    rows = seqs * length
    total = steps * rows
    block = (HEADS * length, length) if seqs == 1 else (rows, HEADS * length)
    _, _, _, *rest = weights
    kernel = functools.partial(layer_kernel, which, steps, seqs, length)
    extra_shape, extra_spec, extra_scratch = [], [], []
    leading, cls_spec = (bit, lengths, cls_grad), [smem(), smem(), whole((PAD, WIDTH))]
    if exchange:
        kernel = functools.partial(question_kernel, seqs, seqs, length)
        count = exchange[1].shape[0]
        leading = (*exchange, bit, lengths)
        cls_spec = [smem(), whole(exchange[1].shape), whole((1, count * PAD)), whole((PAD, 1)), smem(), smem()]
        extra_shape = [shape((PAD, 128), f32), shape((PAD, WIDTH), f32)]
        extra_spec = [whole((PAD, 128)), whole((PAD, WIDTH))]
        extra_scratch = [pltpu.VMEM((PAD, WIDTH), f32)] + [pltpu.VMEM((count * PAD, WIDTH), bf16)] * 2
    return pl.pallas_call(
        kernel,
        out_shape=[shape((total, WIDTH), bf16), pltpu.HBM((total, WIDTH), f32), pltpu.HBM((total, 3 * WIDTH), bf16), shape((HALF, WIDTH), bf16), shape((HALF, WIDTH), bf16)] + extra_shape,
        grid=(steps,),
        in_specs=[
            *cls_spec, rows_of(rows, WIDTH), rows_of(rows, WIDTH),
            rows_of(rows, 3 * WIDTH), rows_of(*block), rows_of(rows, WIDTH),
            part_of(which, (WIDTH, WIDTH)),
            pair(WIDTH), pair(WIDTH), pair(WIDTH), part_of(which, (WIDTH, HIDDEN)), pair(HIDDEN),
            part_of(which, (HIDDEN, WIDTH)), pair(WIDTH), pair(WIDTH), pair(WIDTH),
        ],
        out_specs=[rows_of(rows, WIDTH), rows_of(rows, WIDTH), rows_of(rows, 3 * WIDTH), whole((HALF, WIDTH)), whole((HALF, WIDTH))] + extra_spec,
        scratch_shapes=extra_scratch + [
            pltpu.VMEM((GROUP_ROWS, WIDTH), f32), pltpu.VMEM((VECTOR_ROWS * PAD, WIDTH), f32),
            pltpu.VMEM((rows, WIDTH), f32), pltpu.VMEM((rows, 1), f32), pltpu.VMEM((rows, WIDTH), bf16),
            pltpu.VMEM((rows, HIDDEN), f32), pltpu.VMEM((rows, HIDDEN), bf16), pltpu.VMEM((rows, WIDTH), f32),
            pltpu.VMEM((rows, HIDDEN), f32), pltpu.VMEM(block, f32),
            pltpu.VMEM(block, bf16), pltpu.VMEM((rows, WIDTH), f32), pltpu.VMEM((rows, WIDTH), bf16),
            pltpu.VMEM((rows, HIDDEN), bf16), pltpu.VMEM((rows, WIDTH), bf16), pltpu.VMEM((rows, WIDTH), bf16),
            pltpu.VMEM(block, bf16),
        ],
        compiler_params=params(),
        cost_estimate=cost(total * 6 * 800000, total * 4000),
        name="layer",
    )(*leading, in_hbm(x), in_hbm(cot), *[in_hbm(member) for member in attended], *[in_hbm(member) for member in rest])


def input_grad_kernel(one_ref, gqkv_ref, wqkv_ref, gx_ref):
    gx_ref[...] = (one_ref[...] + dot_nt(gqkv_ref[...], wqkv_ref[...])).astype(bf16)


def input_grad(which, steps, one, gqkv, weights):
    total = one.shape[0]
    rows = total // steps
    return pl.pallas_call(
        input_grad_kernel,
        out_shape=shape((total, WIDTH), bf16),
        grid=(steps,),
        in_specs=[rows_of(rows, WIDTH), rows_of(rows, 3 * WIDTH), part_of(which, (WIDTH, 3 * WIDTH))],
        out_specs=rows_of(rows, WIDTH),
        compiler_params=params(),
        cost_estimate=cost(total * 2 * 200000, total * 3000),
        name="input_grad",
    )(in_hbm(one), in_hbm(gqkv), in_hbm(weights[0]))


def stages(count):
    masks = []
    bit = 1
    while bit < count:
        masks.append(bit)
        bit = bit * 2
    groups = [masks[:1]]
    rest = masks[1:]
    while rest:
        groups.append(rest[:2])
        rest = rest[2:]
    return [group for group in groups if group]


def partner_send(values, mask, count):
    return lax.ppermute(values, "dp", [(i, i ^ mask) for i in range(count)])


def combos(group):
    return [index * group[0] for index in range(1, 2 ** len(group))]


def combine(pieces, group, me):
    radix = 2 ** len(group)
    digit = (me // group[0]) % radix
    rows = pieces[0].shape[0]
    part = rows // radix
    if part % 8 == 0:
        return pl.pallas_call(
            functools.partial(combine_kernel, radix),
            out_shape=[shape((part, WIDTH), bf16)] * radix,
            grid=(1,),
            in_specs=[smem()] + [whole((rows, WIDTH))] * len(pieces),
            out_specs=[whole((part, WIDTH))] * radix,
            scratch_shapes=[pltpu.VMEM((rows, WIDTH), f32)],
            compiler_params=params(),
            name="combine",
        )(digit.reshape(1), *pieces)
    total = pieces[0].astype(f32)
    for piece in pieces[1:]:
        total = total + piece.astype(f32)
    split = total.astype(bf16).reshape(radix, part, WIDTH)
    return [lax.dynamic_index_in_dim(split, digit ^ step, 0, keepdims=False) for step in range(radix)]


def send_parts(cut, group, count):
    own, *sends = cut
    return [own] + [partner_send(part, mask, count) for part, mask in zip(sends, combos(group))]


def send_whole(buffer, group, count):
    return [buffer] + [partner_send(buffer, mask, count) for mask in combos(group)]


def add_up(pieces):
    total = pieces[0].astype(f32)
    for piece in pieces[1:]:
        total = total + piece.astype(f32)
    return total.astype(bf16)


def join(pieces, group, me):
    radix = 2 ** len(group)
    digit = (me // group[0]) % radix
    joined = jnp.zeros((radix,) + pieces[0].shape, pieces[0].dtype)
    for step, piece in enumerate(pieces):
        joined = lax.dynamic_update_index_in_dim(joined, piece, digit ^ step, 0)
    return joined.reshape((radix * pieces[0].shape[0],) + pieces[0].shape[1:])


def prepare(pieces, done, following, me):
    reduce_done, group_done = done
    reduce_next, group_next = following
    if not reduce_done:
        return [join(pieces, group_done, me)]
    if reduce_next:
        return combine(pieces, group_next, me)
    return [add_up(pieces)]


def launch(operands, stage, count):
    reduce, group = stage
    return send_parts(operands, group, count) if reduce else send_whole(operands[0], group, count)


def after(values, *others):
    return list(lax.optimization_barrier((tuple(values), others))[0])


def body(questions, passages, cot_questions, cot_passages, len_questions, len_passages, positive, *weights):
    local = questions.shape[0]
    question_length = questions.shape[1]
    passage_length = passages.shape[1]
    count = positive.shape[0] // local
    me = lax.axis_index("dp")
    bit = (me % 2).reshape(1)
    x_q = questions.reshape(-1, WIDTH)
    x_p = passages.reshape(-1, WIDTH)
    own_cls = first_call(count, local, len_questions, len_passages, x_q, x_p, weights)
    own_cls, x_q, x_p = lax.optimization_barrier((own_cls, x_q, x_p))
    all_cls = lax.all_to_all(own_cls, "dp", 0, 0, tiled=True)
    attended_p = attend(1, local, 1, passage_length, len_passages, x_p, weights)
    attended_q = attend(0, 1, local, question_length, len_questions, x_q, weights)
    (all_cls,) = after([all_cls], attended_p[2], attended_q[2])
    slots = positive // local * PAD + positive % local
    slots = jnp.pad(slots.reshape(count, local), ((0, 0), (0, PAD - local)), constant_values=-1)
    own_slots = lax.dynamic_slice_in_dim(slots, me, 1, axis=0).reshape(PAD, 1)
    out_q, one_q, gqkv_q, keep_q, send_q, loss, grad_cls_p = layer(
        0, 1, local, question_length, bit, len_questions, None, x_q, cot_questions.reshape(-1, WIDTH),
        attended_q, weights, (me.reshape(1), all_cls, slots.reshape(1, -1), own_slots),
    )
    loss_rows = loss[:local, 0]
    groups = stages(count)
    steps = [(True, group) for group in groups] + [(False, group) for group in groups[::-1]]
    pieces_q = [keep_q, partner_send(send_q, groups[0][0], count)]
    grad_q = input_grad(0, 1, one_q, gqkv_q, weights)
    operands_q = prepare(after(pieces_q, grad_q), steps[0], steps[1], me)
    (grad_cls_p,) = after([grad_cls_p], *operands_q)
    pieces_q = launch(operands_q, steps[1], count)
    out_p, one_p, gqkv_p, keep_p, send_p = layer(
        1, local, 1, passage_length, bit, len_passages, grad_cls_p, x_p, cot_passages.reshape(-1, WIDTH),
        attended_p, weights,
    )
    (send_p,) = after([send_p], *pieces_q)
    pieces_p = [keep_p, partner_send(send_p, groups[0][0], count)]
    for place in range(len(steps)):
        if 0 < place < len(steps) - 1:
            pieces_p = after(pieces_p, *operands_q)
            operands_p = prepare(pieces_p, steps[place - 1], steps[place], me)
            pieces_p = launch(operands_p, steps[place], count)
            pieces_q = after(pieces_q, *operands_p)
        if place + 2 < len(steps):
            operands_q = prepare(pieces_q, steps[place + 1], steps[place + 2], me)
            pieces_q = launch(operands_q, steps[place + 2], count)
    own_q, other_q = pieces_q
    parts = len(pieces_p)
    digit = (me // groups[1][0] % parts).reshape(1)
    dims = [(WIDTH, 3 * WIDTH), (WIDTH, WIDTH), (WIDTH, HIDDEN), (HIDDEN, WIDTH)]
    matrices = [shape((2,) + d, f32) for d in dims]
    *halves, tail = pl.pallas_call(
        question_unpack_kernel,
        out_shape=matrices + [shape((VECTOR_ROWS, WIDTH), f32)],
        grid=(1,),
        in_specs=[smem()] + [whole((HALF, WIDTH))] * 2,
        out_specs=[part_of(0, d) for d in dims] + [whole((VECTOR_ROWS, WIDTH))],
        scratch_shapes=[pltpu.VMEM((GROUP_ROWS, WIDTH), bf16)],
        compiler_params=params(),
        name="unpack_q",
    )(bit, own_q, other_q)
    own_piece, *came = pieces_p
    grad_p = input_grad(1, 1, one_p, gqkv_p, weights)
    came = after(came, tail, loss_rows, grad_p)
    pieces_p = [own_piece] + came
    other_p = [partner_send(piece, groups[0][0], count) for piece in pieces_p]
    vectors = [(2, HIDDEN)] + [(2, WIDTH)] * len(VECTOR_OUTS)
    first_alias = 2 + 2 * parts + 1
    d_qkv, d_proj, d_up, d_down, up_bias, query_bias, value_bias, proj_bias, gain_a, shift_a, down_bias, gain_f, shift_f = pl.pallas_call(
        functools.partial(passage_unpack_kernel, parts),
        out_shape=matrices + [shape(d, f32) for d in vectors],
        grid=(1,),
        in_specs=[smem(), smem()] + [whole((HALF // parts, WIDTH))] * (2 * parts) + [whole((VECTOR_ROWS, WIDTH))]
        + [pl.BlockSpec(memory_space=pl.ANY)] * 4,
        out_specs=[part_of(1, d) for d in dims] + [whole(d) for d in vectors],
        scratch_shapes=[pltpu.VMEM((GROUP_ROWS, WIDTH), bf16)],
        input_output_aliases={first_alias + i: i for i in range(4)},
        compiler_params=params(),
        name="unpack_p",
    )(bit, digit, *pieces_p, *other_p, tail, *halves)
    return (
        loss_rows, out_q.reshape(questions.shape), out_p.reshape(passages.shape),
        grad_q.reshape(questions.shape), grad_p.reshape(passages.shape),
        d_qkv, query_bias, value_bias, d_proj, proj_bias, gain_a, shift_a, d_up, up_bias, d_down,
        down_bias, gain_f, shift_f,
    )


def solution(mesh):
    split = P("dp", None, None)
    return jax.shard_map(
        body,
        mesh=mesh,
        in_specs=(split, split, split, split, P("dp"), P("dp")) + (P(),) * 14,
        out_specs=(P("dp"), split, split, split, split) + (P(),) * 13,
        check_vma=False,
    )
```

```python
import functools

import jax
import jax.numpy as jnp
from jax import lax
from jax.experimental import pallas as pl
from jax.experimental.pallas import tpu as pltpu
from jax.sharding import PartitionSpec as P

HEAD_DIM = 64
WIDTH = 256
HEADS = WIDTH // HEAD_DIM
HIDDEN = 1024
BLOCKS = HIDDEN // WIDTH
PAD = 8
VECTOR_ROWS = 16
HALF = 6 * WIDTH + 128
GROUP_ROWS = 2 * HALF
LANES = 128
SOFT = 128
NORM = 32
GELU = 32
ln_eps = 1e-06
score_scale = 0.125
masked_score = -1e30
f32 = jnp.float32
bf16 = jnp.bfloat16

QUERY_BIAS, VALUE_BIAS, PROJ_BIAS, ATTN_GAIN, ATTN_SHIFT, DOWN_BIAS, FFN_GAIN, FFN_SHIFT = range(8)
UP_BIAS = 8


def dot(a, b):
    return lax.dot_general(a, b, (((1,), (0,)), ((), ())), preferred_element_type=f32)


def dot_nt(a, b):
    return lax.dot_general(a, b, (((1,), (1,)), ((), ())), preferred_element_type=f32)


def dot_tn(a, b):
    return lax.dot_general(a, b, (((0,), (0,)), ((), ())), preferred_element_type=f32)


def row_loop(rows, chunk, step):
    for row in range(0, rows, chunk):
        step(row)


def vector(ref, which):
    return ref[...].astype(f32)[which : which + 1]


def lane_head(rows):
    return lax.broadcasted_iota(jnp.int32, (rows, WIDTH), 1) // HEAD_DIM


def one_head(values, h, scale=1.0):
    return jnp.where(lane_head(values.shape[0]) == h, values.astype(f32) * scale, 0.0).astype(bf16)


def some_heads(values, first, last, scale=1.0):
    return jnp.concatenate([one_head(values, h, scale) for h in range(first, last)], axis=0)


def pick_heads(stacked, rows):
    head = lane_head(rows)
    result = stacked[:rows]
    for h in range(1, HEADS):
        result = jnp.where(head == h, stacked[h * rows : (h + 1) * rows], result)
    return result


def block_rows(block):
    start = block * WIDTH if block < 6 else HALF + (block - 6) * WIDTH
    return slice(start, start + WIDTH)


VECTOR_START = 6 * WIDTH
QKV_BLOCK, PROJ_BLOCK, UP_BLOCK, DOWN_BLOCK = 0, 3, 4, 8


def normalize(value):
    centered = value - jnp.mean(value, axis=1, keepdims=True)
    inverse = lax.rsqrt(jnp.mean(centered * centered, axis=1, keepdims=True) + ln_eps)
    return centered * inverse, inverse


def masked_softmax(scores, size, scale=score_scale):
    part = scores * scale if scale != 1.0 else scores
    key = lax.broadcasted_iota(jnp.int32, part.shape, 1)
    part = jnp.where(key < size, part, masked_score)
    part = jnp.exp(part - jnp.max(part, axis=1, keepdims=True))
    return part * (1.0 / jnp.sum(part, axis=1, keepdims=True))


def gelu_parts(value):
    cumulative = 0.5 + 0.5 * lax.erf(value * 0.7071067811865476)
    density = jnp.exp(value * value * -0.5) * 0.3989422804014327
    return (value * cumulative).astype(bf16), cumulative + value * density


def first_kernel(
    seqs, lq_ref, lp_ref, xq_ref, xp_ref,
    wqkv_ref, qb_ref, vb_ref, wo_ref, ob_ref, g1_ref, b1_ref, w1_ref, hb_ref, w2_ref, fb_ref, g2_ref, b2_ref,
    cls_ref,
    kq_ref, vq_ref, kp_ref, vp_ref,
):
    sides = ((0, xq_ref, kq_ref, vq_ref, lq_ref), (1, xp_ref, kp_ref, vp_ref, lp_ref))
    filler = jnp.zeros((PAD - seqs, WIDTH), f32)
    inputs = []
    for which, x_ref, *_ in sides:
        length = x_ref.shape[0] // seqs
        firsts = [x_ref[s * length : s * length + 16, :].astype(f32)[:1] for s in range(seqs)]
        inputs.append(jnp.concatenate(firsts + [filler], axis=0))
    own_lanes = lane_head(PAD) == lax.broadcasted_iota(jnp.int32, (PAD, WIDTH), 0)
    queries = [
        (dot(inputs[which].astype(bf16), wqkv_ref[which, :, :WIDTH]) + vector(qb_ref, which)).astype(bf16).astype(f32)
        for which in range(2)
    ]
    for which, x_ref, k_ref, v_ref, _ in sides:
        x = x_ref[...]
        k_ref[...] = dot(x, wqkv_ref[which, :, WIDTH : 2 * WIDTH]).astype(bf16)
        v_ref[...] = (dot(x, wqkv_ref[which, :, 2 * WIDTH :]) + vector(vb_ref, which)).astype(bf16)
    context = []
    for which, x_ref, k_ref, v_ref, len_ref in sides:
        length = x_ref.shape[0] // seqs
        spans = [slice(s * length, (s + 1) * length) for s in range(seqs)]
        scores, sizes = [], []
        for s, span in enumerate(spans):
            heads = jnp.where(own_lanes, queries[which][s : s + 1], 0.0).astype(bf16)
            scores.append(dot_nt(heads, k_ref[span, :]))
            sizes.append(jnp.full((PAD, length), len_ref[s], jnp.int32))
        prob = masked_softmax(jnp.concatenate(scores, axis=0), jnp.concatenate(sizes, axis=0)).astype(f32)
        rows = []
        for s, span in enumerate(spans):
            mixed = dot(prob[s * PAD : (s + 1) * PAD].astype(bf16), v_ref[span, :])
            rows.append(jnp.sum(jnp.where(own_lanes, mixed, 0.0), axis=0, keepdims=True))
        context.append(jnp.concatenate(rows + [filler], axis=0).astype(bf16))
    normed = []
    for which in range(2):
        value = inputs[which] + (dot(context[which], wo_ref[which]) + vector(ob_ref, which))
        unit, _ = normalize(value)
        normed.append(unit * vector(g1_ref, which) + vector(b1_ref, which))
    active = []
    for which in range(2):
        active.append(gelu_parts(dot(normed[which].astype(bf16), w1_ref[which]) + vector(hb_ref, which))[0])
    results = []
    for which in range(2):
        value = normed[which] + (dot(active[which], w2_ref[which]) + vector(fb_ref, which))
        unit, _ = normalize(value)
        result = unit * vector(g2_ref, which) + vector(b2_ref, which)
        row = lax.broadcasted_iota(jnp.int32, result.shape, 0)
        results.append(jnp.where(row < seqs, result, 0.0))
    both = jnp.concatenate(results, axis=0).astype(bf16)

    def store(i, carry):
        cls_ref[i] = both
        return carry

    lax.fori_loop(0, cls_ref.shape[0], store, 0)


def head_groups(length):
    together = max(1, WIDTH // length)
    return [(h, h + together, slice(h * length, (h + together) * length)) for h in range(0, HEADS, together)]


def attend_kernel(which, seqs, length, len_ref, x_ref, wqkv_ref, qb_ref, vb_ref, qkv_ref, p_ref, ctx_ref, score_ref, prob_ref):
    step = pl.program_id(0)
    x = x_ref[...]
    qkv_ref[:, :WIDTH] = (dot(x, wqkv_ref[:, :WIDTH]) + vector(qb_ref, which)).astype(bf16)
    qkv_ref[:, WIDTH : 2 * WIDTH] = dot(x, wqkv_ref[:, WIDTH : 2 * WIDTH]).astype(bf16)
    qkv_ref[:, 2 * WIDTH :] = (dot(x, wqkv_ref[:, 2 * WIDTH :]) + vector(vb_ref, which)).astype(bf16)
    for s in range(seqs):
        span = slice(s * length, (s + 1) * length)
        size = len_ref[step * seqs + s]
        keys = qkv_ref[span, WIDTH : 2 * WIDTH]
        for first, last, columns in head_groups(length):
            score_ref[span, columns] = dot_nt(keys, some_heads(qkv_ref[span, :WIDTH], first, last, score_scale))
            for lane in range(columns.start, columns.stop, LANES):
                here = slice(lane, lane + LANES)
                part = score_ref[span, here]
                key = lax.broadcasted_iota(jnp.int32, part.shape, 0)
                part = jnp.where(key < size, part, masked_score)
                part = jnp.exp(part - jnp.max(part, axis=0, keepdims=True))
                prob = part * (1.0 / jnp.sum(part, axis=0, keepdims=True))
                p_ref[span, here] = prob
                prob_ref[span, here] = prob.astype(bf16)
        ctx_ref[span, :] = pick_heads(dot_tn(prob_ref[span, :], qkv_ref[span, 2 * WIDTH :]), length).astype(bf16)


def attend_long_kernel(which, seqs, length, len_ref, x_ref, wqkv_ref, qb_ref, vb_ref, qkv_ref, p_ref, ctx_ref, score_ref, prob_ref):
    step = pl.program_id(0)
    x = x_ref[...]
    qkv_ref[:, :WIDTH] = (dot(x, wqkv_ref[:, :WIDTH]) + vector(qb_ref, which)).astype(bf16)
    qkv_ref[:, WIDTH : 2 * WIDTH] = dot(x, wqkv_ref[:, WIDTH : 2 * WIDTH]).astype(bf16)
    qkv_ref[:, 2 * WIDTH :] = (dot(x, wqkv_ref[:, 2 * WIDTH :]) + vector(vb_ref, which)).astype(bf16)
    stack_rows = HEADS * length
    for s in range(seqs):
        span = slice(s * length, (s + 1) * length)
        stack = slice(s * stack_rows, (s + 1) * stack_rows)
        size = len_ref[step * seqs + s]
        queries = qkv_ref[span, :WIDTH]
        for h in range(HEADS):
            start = s * stack_rows + h * length
            score_ref[start : start + length, :] = dot_nt(one_head(queries, h, score_scale), qkv_ref[span, WIDTH : 2 * WIDTH])

            def softmax(row):
                here = pl.ds(start + row, SOFT)
                prob = masked_softmax(score_ref[here, :], size, 1.0)
                p_ref[here, :] = prob
                prob_ref[here, :] = prob.astype(bf16)

            row_loop(length, SOFT, softmax)
        ctx_ref[span, :] = pick_heads(dot(prob_ref[stack, :], qkv_ref[span, 2 * WIDTH :]), length).astype(bf16)


def forward_phase(
    which, rows, x_ref, wo_ref, ob_ref, g1_ref, b1_ref, w1_ref, hb_ref, w2_ref,
    ctx_ref, n1_ref, r1_ref, nb_ref, gp_ref, act_ref, n2_ref, wide_ref,
):
    n2_ref[...] = dot(ctx_ref[...], wo_ref[...])
    ob, g1, b1 = vector(ob_ref, which), vector(g1_ref, which), vector(b1_ref, which)

    def first_norm(row):
        here = pl.ds(row, NORM)
        unit, inverse = normalize(x_ref[here, :].astype(f32) + (n2_ref[here, :] + ob))
        n1_ref[here, :] = unit
        r1_ref[here, :] = inverse
        nb_ref[here, :] = (unit * g1 + b1).astype(bf16)

    row_loop(rows, NORM, first_norm)
    hb = vector(hb_ref, which)
    for j in range(BLOCKS):
        lanes = slice(j * WIDTH, (j + 1) * WIDTH)
        wide_ref[:, lanes] = dot(nb_ref[...], w1_ref[:, lanes])

        def gelu(row):
            here = pl.ds(row, GELU)
            active, slope = gelu_parts(wide_ref[here, lanes] + hb[:, lanes])
            act_ref[here, lanes] = active
            gp_ref[here, lanes] = slope

        row_loop(rows, GELU, gelu)
    n2_ref[...] = dot(act_ref[...], w2_ref[...])


def add_row(vec_ref, row, values):
    here = slice(row * PAD, (row + 1) * PAD)
    vec_ref[here, :] = vec_ref[here, :] + jnp.sum(values.reshape(-1, PAD, WIDTH), axis=0)


def ffn_phase(which, seqs, length, first, len_ref, cls_ref, cot_ref, n1_ref, n2_ref, gp_ref, w2_ref, g1_ref, b1_ref, fb_ref, g2_ref, b2_ref, out_ref, two_ref, gffn_ref, gpre_ref, vec_ref, wide_ref):
    g1, g2, b2 = vector(g1_ref, which), vector(g2_ref, which), vector(b2_ref, which)
    shift = vector(b1_ref, which) + vector(fb_ref, which)
    for s in range(seqs):
        size = len_ref[first + s]
        cls_row = cls_ref[pl.ds(first + s, 1), :]

        def output_norm(row):
            here = pl.ds(s * length + row, NORM)
            inside = row + lax.broadcasted_iota(jnp.int32, (NORM, WIDTH), 0) < size
            unit, inverse = normalize(n1_ref[here, :] * g1 + (n2_ref[here, :] + shift))
            out_ref[here, :] = jnp.where(inside, unit * g2 + b2, 0.0).astype(bf16)
            grad = cot_ref[here, :].astype(f32)
            if row == 0:
                grad = grad + jnp.where(lax.broadcasted_iota(jnp.int32, (NORM, WIDTH), 0) == 0, cls_row, 0.0)
            grad = jnp.where(inside, grad, 0.0)
            scaled = grad * g2
            slope = scaled * unit
            first_mean = jnp.mean(scaled, axis=1, keepdims=True)
            second_mean = jnp.mean(slope, axis=1, keepdims=True)
            two = inverse * (scaled - first_mean - unit * second_mean)
            low = two.astype(bf16)
            two_ref[here, :] = two
            gffn_ref[here, :] = low
            add_row(vec_ref, FFN_GAIN, grad * unit)
            add_row(vec_ref, FFN_SHIFT, grad)
            add_row(vec_ref, DOWN_BIAS, low.astype(f32))

        row_loop(length, NORM, output_norm)
    for j in range(BLOCKS):
        lanes = slice(j * WIDTH, (j + 1) * WIDTH)
        wide_ref[:, lanes] = dot_nt(gffn_ref[...], w2_ref[lanes, :])

        def gelu_back(row):
            here = pl.ds(row, GELU)
            low = (wide_ref[here, lanes] * gp_ref[here, lanes]).astype(bf16)
            gpre_ref[here, lanes] = low
            add_row(vec_ref, UP_BIAS + j, low.astype(f32))

        row_loop(seqs * length, GELU, gelu_back)


def attn_norm_phase(which, rows, gpre_ref, w1_ref, two_ref, n1_ref, r1_ref, g1_ref, wo_ref, one_ref, gatt_ref, dctx_ref, vec_ref):
    one_ref[...] = dot_nt(gpre_ref[...], w1_ref[...])
    g1 = vector(g1_ref, which)

    def norm_back(row):
        here = pl.ds(row, NORM)
        grad = two_ref[here, :] + one_ref[here, :]
        unit = n1_ref[here, :]
        scaled = grad * g1
        first_mean = jnp.mean(scaled, axis=1, keepdims=True)
        second_mean = jnp.mean(scaled * unit, axis=1, keepdims=True)
        one = r1_ref[here, :] * (scaled - first_mean - unit * second_mean)
        low = one.astype(bf16)
        one_ref[here, :] = one
        gatt_ref[here, :] = low
        add_row(vec_ref, ATTN_GAIN, grad * unit)
        add_row(vec_ref, ATTN_SHIFT, grad)
        add_row(vec_ref, PROJ_BIAS, low.astype(f32))

    row_loop(rows, NORM, norm_back)
    dctx_ref[...] = dot_nt(gatt_ref[...], wo_ref[...]).astype(bf16)


def attn_core_phase(seqs, length, dctx_ref, qkv_ref, p_ref, gqkv_ref, vec_ref, dp_ref, ds_ref, pb_ref):
    for s in range(seqs):
        span = slice(s * length, (s + 1) * length)
        values = qkv_ref[span, 2 * WIDTH :]
        context = some_heads(dctx_ref[span, :], 0, HEADS)
        for first, last, columns in head_groups(length):
            dp_ref[span, columns] = dot_nt(values, context[columns])
            for lane in range(columns.start, columns.stop, LANES):
                here = slice(lane, lane + LANES)
                prob = p_ref[span, here]
                grad = dp_ref[span, here]
                inner = jnp.sum(prob * grad, axis=0, keepdims=True)
                ds_ref[span, here] = (prob * (grad - inner)).astype(bf16)
                pb_ref[span, here] = prob.astype(bf16)
        queries = some_heads(qkv_ref[span, :WIDTH], 0, HEADS, score_scale)
        gqkv_ref[span, WIDTH : 2 * WIDTH] = dot(ds_ref[span, :], queries).astype(bf16)
        grad_v = dot(pb_ref[span, :], context).astype(bf16)
        gqkv_ref[span, 2 * WIDTH :] = grad_v
        add_row(vec_ref, VALUE_BIAS, grad_v.astype(f32))
        grad_q = (pick_heads(dot_tn(ds_ref[span, :], qkv_ref[span, WIDTH : 2 * WIDTH]), length) * score_scale).astype(bf16)
        gqkv_ref[span, :WIDTH] = grad_q
        add_row(vec_ref, QUERY_BIAS, grad_q.astype(f32))


def attn_core_long(seqs, length, dctx_ref, qkv_ref, p_ref, gqkv_ref, vec_ref, dp_ref, ds_ref, pb_ref):
    stack_rows = HEADS * length
    for s in range(seqs):
        span = slice(s * length, (s + 1) * length)
        stack = slice(s * stack_rows, (s + 1) * stack_rows)
        contexts = [one_head(dctx_ref[span, :], h) for h in range(HEADS)]
        for h in range(HEADS):
            start = s * stack_rows + h * length
            dp_ref[start : start + length, :] = dot_nt(contexts[h], qkv_ref[span, 2 * WIDTH :])

            def softmax_back(row):
                here = pl.ds(start + row, SOFT)
                prob = p_ref[here, :]
                grad = dp_ref[here, :]
                inner = jnp.sum(prob * grad, axis=1, keepdims=True)
                ds_ref[here, :] = (prob * (grad - inner)).astype(bf16)
                pb_ref[here, :] = prob.astype(bf16)

            row_loop(length, SOFT, softmax_back)
        context = jnp.concatenate(contexts, axis=0)
        queries = some_heads(qkv_ref[span, :WIDTH], 0, HEADS, score_scale)
        grad_q = (pick_heads(dot(ds_ref[stack, :], qkv_ref[span, WIDTH : 2 * WIDTH]), length) * score_scale).astype(bf16)
        gqkv_ref[span, :WIDTH] = grad_q
        add_row(vec_ref, QUERY_BIAS, grad_q.astype(f32))
        gqkv_ref[span, WIDTH : 2 * WIDTH] = dot_tn(ds_ref[stack, :], queries).astype(bf16)
        grad_v = dot_tn(pb_ref[stack, :], context).astype(bf16)
        gqkv_ref[span, 2 * WIDTH :] = grad_v
        add_row(vec_ref, VALUE_BIAS, grad_v.astype(f32))


def layer_kernel(
    which, steps, seqs, length,
    bit_ref, len_ref, cls_ref, x_ref, cot_ref, qkv_ref, p_ref, ctx_ref,
    wo_ref, ob_ref, g1_ref, b1_ref, w1_ref, hb_ref, w2_ref, fb_ref, g2_ref, b2_ref,
    out_ref, one_ref, gqkv_ref, keep_ref, send_ref,
    acc_ref, vec_ref, n1_ref, r1_ref, nb_ref, gp_ref, act_ref, n2_ref,
    wide_ref, score_ref, prob_ref, two_ref, gffn_ref, gpre_ref, gatt_ref, dctx_ref, ds_ref,
):
    rows = seqs * length
    step = pl.program_id(0)

    def start():
        vec_ref[...] = jnp.zeros_like(vec_ref)
        if steps > 1:
            acc_ref[...] = jnp.zeros_like(acc_ref)

    if steps > 1:
        pl.when(step == 0)(start)
    else:
        start()

    def add_block(block, value):
        if steps > 1:
            acc_ref[block_rows(block), :] += value
        else:
            acc_ref[block_rows(block), :] = value

    forward_phase(
        which, rows, x_ref, wo_ref, ob_ref, g1_ref, b1_ref, w1_ref, hb_ref, w2_ref,
        ctx_ref, n1_ref, r1_ref, nb_ref, gp_ref, act_ref, n2_ref, wide_ref,
    )
    ffn_phase(which, seqs, length, step * seqs, len_ref, cls_ref, cot_ref, n1_ref, n2_ref, gp_ref, w2_ref, g1_ref, b1_ref, fb_ref, g2_ref, b2_ref, out_ref, two_ref, gffn_ref, gpre_ref, vec_ref, wide_ref)
    downs = dot_tn(act_ref[...], gffn_ref[...])
    ups = dot_tn(nb_ref[...], gpre_ref[...])
    for j in range(BLOCKS):
        lanes = slice(j * WIDTH, (j + 1) * WIDTH)
        add_block(DOWN_BLOCK + j, downs[lanes])
        add_block(UP_BLOCK + j, ups[:, lanes])
    attn_norm_phase(which, rows, gpre_ref, w1_ref, two_ref, n1_ref, r1_ref, g1_ref, wo_ref, one_ref, gatt_ref, dctx_ref, vec_ref)
    add_block(PROJ_BLOCK, dot_tn(ctx_ref[...], gatt_ref[...]))
    attn_core = attn_core_long if seqs == 1 else attn_core_phase
    attn_core(seqs, length, dctx_ref, qkv_ref, p_ref, gqkv_ref, vec_ref, score_ref, ds_ref, prob_ref)
    for j in range(3):
        add_block(QKV_BLOCK + j, dot_tn(x_ref[...], gqkv_ref[:, j * WIDTH : (j + 1) * WIDTH]))

    def finish():
        acc_ref[VECTOR_START : VECTOR_START + VECTOR_ROWS, :] = jnp.sum(vec_ref[...].reshape(VECTOR_ROWS, PAD, WIDTH), axis=1)
        if steps == 1:
            acc_ref[VECTOR_START + VECTOR_ROWS : HALF, :] = jnp.zeros((HALF - VECTOR_START - VECTOR_ROWS, WIDTH), f32)
            acc_ref[HALF + 6 * WIDTH :, :] = jnp.zeros((HALF - 6 * WIDTH, WIDTH), f32)
        keep = pl.multiple_of(bit_ref[0] * HALF, HALF)
        send = pl.multiple_of((1 - bit_ref[0]) * HALF, HALF)
        keep_ref[...] = acc_ref[pl.ds(keep, HALF), :].astype(bf16)
        send_ref[...] = acc_ref[pl.ds(send, HALF), :].astype(bf16)

    if steps > 1:
        pl.when(step == steps - 1)(finish)
    else:
        finish()


def loss_phase(local, me_ref, all_ref, hot_ref, own_hot_ref, loss_ref, gq_ref, gp_ref, q_ref, p_ref):
    count = all_ref.shape[0]
    me = me_ref[0]
    wide = all_ref[...].astype(f32)
    q_ref[...] = wide[:, :PAD].reshape(count * PAD, WIDTH).astype(bf16)
    p_ref[...] = wide[:, PAD:].reshape(count * PAD, WIDTH).astype(bf16)
    own_q = all_ref[me][:PAD]
    own_p = all_ref[me][PAD:]
    logits = dot_nt(own_q, p_ref[...]) * score_scale
    column = lax.broadcasted_iota(jnp.int32, logits.shape, 1)
    logits = jnp.where(column % PAD < local, logits, masked_score)
    top = jnp.max(logits, axis=1, keepdims=True)
    total = top + jnp.log(jnp.sum(jnp.exp(logits - top), axis=1, keepdims=True))
    hot = (column == own_hot_ref[...]).astype(f32)
    loss_ref[...] = jnp.broadcast_to(total - jnp.sum(logits * hot, axis=1, keepdims=True), loss_ref.shape)
    grad = (jnp.exp(logits - total) - hot).astype(bf16)
    gq_ref[...] = dot(grad, p_ref[...]) * score_scale
    gp_ref[...] = jnp.zeros_like(gp_ref)
    block = 256 if count * PAD % 256 == 0 else count * PAD

    def part(index, carry):
        start = index * block if isinstance(index, int) else pl.multiple_of(index * block, block)
        queries = q_ref[pl.ds(start, block), :]
        scores = dot_nt(p_ref[...], queries) * score_scale
        row = lax.broadcasted_iota(jnp.int32, scores.shape, 0)
        scores = jnp.where(row % PAD < local, scores, masked_score)
        peak = jnp.max(scores, axis=0, keepdims=True)
        sums = peak + jnp.log(jnp.sum(jnp.exp(scores - peak), axis=0, keepdims=True))
        own = dot_nt(own_p, queries) * score_scale
        own_row = lax.broadcasted_iota(jnp.int32, own.shape, 0)
        own_lane = lax.broadcasted_iota(jnp.int32, own.shape, 1)
        own_hits = (own_row + me * PAD == hot_ref[:, pl.ds(start, block)]).astype(f32)
        own_grad = jnp.where(own_lane % PAD < local, jnp.exp(own - sums) - own_hits, 0.0)
        gp_ref[...] += dot(own_grad.astype(bf16), queries) * score_scale
        return carry

    if count * PAD == block:
        part(0, 0)
    else:
        lax.fori_loop(0, count * PAD // block, part, 0)


def question_kernel(local, seqs, length, me_ref, all_ref, hot_ref, own_hot_ref, bit_ref, len_ref, *refs):
    inputs, outputs, scratch = refs[:15], refs[15:22], refs[22:]
    loss_ref, gp_ref = outputs[5:]
    gq_ref, q_ref, p_ref = scratch[:3]
    loss_phase(local, me_ref, all_ref, hot_ref, own_hot_ref, loss_ref, gq_ref, gp_ref, q_ref, p_ref)
    layer_kernel(0, 1, seqs, length, bit_ref, len_ref, gq_ref, *inputs, *outputs[:5], *scratch[3:])


def combine_kernel(distances, digit_ref, *refs):
    radix = len(distances) + 1
    total_ref = refs[-1]
    sends = refs[-1 - (radix - 1) : -1]
    keep_ref = refs[-1 - radix]
    pieces = refs[: -1 - radix]
    total = pieces[0][...].astype(f32)
    for piece in pieces[1:]:
        total = total + piece[...].astype(f32)
    total_ref[...] = total
    part = total_ref.shape[0] // radix
    digit = digit_ref[0]

    def section(which):
        return total_ref[pl.ds(pl.multiple_of(which * part, part), part), :].astype(bf16)

    keep_ref[...] = section(digit)
    for distance, ref in zip(distances, sends):
        ref[...] = section(digit ^ distance)


VECTOR_OUTS = (QUERY_BIAS, VALUE_BIAS, PROJ_BIAS, ATTN_GAIN, ATTN_SHIFT, DOWN_BIAS, FFN_GAIN, FFN_SHIFT)


def spread(which, ref, qkv_ref, proj_ref, up_ref, down_ref):
    for j in range(3):
        qkv_ref[:, j * WIDTH : (j + 1) * WIDTH] = ref[block_rows(QKV_BLOCK + j), :].astype(f32)
    proj_ref[...] = ref[block_rows(PROJ_BLOCK), :].astype(f32)
    for j in range(BLOCKS):
        up_ref[:, j * WIDTH : (j + 1) * WIDTH] = ref[block_rows(UP_BLOCK + j), :].astype(f32)
        down_ref[j * WIDTH : (j + 1) * WIDTH, :] = ref[block_rows(DOWN_BLOCK + j), :].astype(f32)
    return ref[VECTOR_START : VECTOR_START + VECTOR_ROWS, :].astype(f32)


def question_unpack_kernel(bit_ref, own_ref, other_ref, qkv_ref, proj_ref, up_ref, down_ref, tail_ref, whole_ref):
    whole_ref[pl.ds(pl.multiple_of(bit_ref[0] * HALF, HALF), HALF), :] = own_ref[...]
    whole_ref[pl.ds(pl.multiple_of((1 - bit_ref[0]) * HALF, HALF), HALF), :] = other_ref[...]
    tail_ref[...] = spread(0, whole_ref, qkv_ref, proj_ref, up_ref, down_ref)


def passage_unpack_kernel(parts, bit_ref, digit_ref, *refs):
    own_refs, other_refs, (tail_ref, *_) = refs[:parts], refs[parts : 2 * parts], refs[2 * parts : 2 * parts + 5]
    qkv_ref, proj_ref, up_ref, down_ref, up_bias_ref, *vector_refs, whole_ref = refs[2 * parts + 5 :]
    size = HALF // parts
    for half, halves in ((bit_ref[0], own_refs), (1 - bit_ref[0], other_refs)):
        for step, ref in enumerate(halves):
            start = half * HALF + (digit_ref[0] ^ step) * size
            whole_ref[pl.ds(pl.multiple_of(start, 8), size), :] = ref[...]
    tails = (tail_ref[...], spread(1, whole_ref, qkv_ref, proj_ref, up_ref, down_ref))
    for row, ref in zip(VECTOR_OUTS, vector_refs):
        for which in range(2):
            ref[which : which + 1, :] = tails[which][row : row + 1]
    for j in range(BLOCKS):
        for which in range(2):
            up_bias_ref[which : which + 1, j * WIDTH : (j + 1) * WIDTH] = tails[which][UP_BIAS + j : UP_BIAS + j + 1]


def smem():
    return pl.BlockSpec(memory_space=pltpu.SMEM)


def whole(shape):
    return pl.BlockSpec(shape, lambda i: (0,) * len(shape))


def rows_of(rows, columns):
    return pl.BlockSpec((rows, columns), lambda i: (i, 0))


def part_of(which, shape):
    return pl.BlockSpec((None,) + shape, lambda i: (which, 0, 0))


def params():
    return pltpu.CompilerParams(vmem_limit_bytes=24 * 1024 * 1024)


def shape(dims, kind):
    return jax.ShapeDtypeStruct(dims, kind)


def cost(flops, moved):
    return pl.CostEstimate(flops=flops, bytes_accessed=moved, transcendentals=0)


def pair(columns):
    return whole((2, columns))


def in_hbm(values):
    return pltpu.with_memory_space_constraint(values, pltpu.HBM)


def first_call(count, local, len_questions, len_passages, x_q, x_p, weights):
    return pl.pallas_call(
        functools.partial(first_kernel, local),
        out_shape=shape((count, 2 * PAD, WIDTH), bf16),
        grid=(1,),
        in_specs=[smem(), smem(), whole(x_q.shape), whole(x_p.shape)] + [whole(member.shape) for member in weights],
        out_specs=whole((count, 2 * PAD, WIDTH)),
        scratch_shapes=[pltpu.VMEM(x_q.shape, bf16)] * 2 + [pltpu.VMEM(x_p.shape, bf16)] * 2,
        compiler_params=params(),
        name="first",
    )(in_hbm(len_questions), in_hbm(len_passages), in_hbm(x_q), in_hbm(x_p), *[in_hbm(member) for member in weights])


def attend(which, steps, seqs, length, lengths, x, weights):
    wqkv, qb, vb, *_ = weights
    rows = seqs * length
    total = steps * rows
    block = (HEADS * length, length) if seqs == 1 else (rows, HEADS * length)
    return pl.pallas_call(
        functools.partial(attend_long_kernel if seqs == 1 else attend_kernel, which, seqs, length),
        out_shape=[
            pltpu.HBM((total, 3 * WIDTH), bf16), pltpu.HBM((steps * block[0], block[1]), f32), pltpu.HBM((total, WIDTH), bf16),
        ],
        grid=(steps,),
        in_specs=[smem(), rows_of(rows, WIDTH), part_of(which, (WIDTH, 3 * WIDTH)), pair(WIDTH), pair(WIDTH)],
        out_specs=[rows_of(rows, 3 * WIDTH), rows_of(*block), rows_of(rows, WIDTH)],
        scratch_shapes=[pltpu.VMEM(block, f32), pltpu.VMEM(block, bf16)],
        compiler_params=params(),
        cost_estimate=cost(total * 2 * 400000, total * 6000),
        name="attend",
    )(lengths, in_hbm(x), in_hbm(wqkv), in_hbm(qb), in_hbm(vb))


def layer(which, steps, seqs, length, bit, lengths, cls_grad, x, cot, attended, weights, exchange=None):
    rows = seqs * length
    total = steps * rows
    block = (HEADS * length, length) if seqs == 1 else (rows, HEADS * length)
    _, _, _, *rest = weights
    kernel = functools.partial(layer_kernel, which, steps, seqs, length)
    extra_shape, extra_spec, extra_scratch = [], [], []
    leading, cls_spec = (bit, lengths, cls_grad), [smem(), smem(), whole((PAD, WIDTH))]
    if exchange:
        kernel = functools.partial(question_kernel, seqs, seqs, length)
        count = exchange[1].shape[0]
        leading = (*exchange, bit, lengths)
        cls_spec = [smem(), whole(exchange[1].shape), whole((1, count * PAD)), whole((PAD, 1)), smem(), smem()]
        extra_shape = [shape((PAD, 128), f32), shape((PAD, WIDTH), f32)]
        extra_spec = [whole((PAD, 128)), whole((PAD, WIDTH))]
        extra_scratch = [pltpu.VMEM((PAD, WIDTH), f32)] + [pltpu.VMEM((count * PAD, WIDTH), bf16)] * 2
    return pl.pallas_call(
        kernel,
        out_shape=[shape((total, WIDTH), bf16), pltpu.HBM((total, WIDTH), f32), pltpu.HBM((total, 3 * WIDTH), bf16), shape((HALF, WIDTH), bf16), shape((HALF, WIDTH), bf16)] + extra_shape,
        grid=(steps,),
        in_specs=[
            *cls_spec, rows_of(rows, WIDTH), rows_of(rows, WIDTH),
            rows_of(rows, 3 * WIDTH), rows_of(*block), rows_of(rows, WIDTH),
            part_of(which, (WIDTH, WIDTH)),
            pair(WIDTH), pair(WIDTH), pair(WIDTH), part_of(which, (WIDTH, HIDDEN)), pair(HIDDEN),
            part_of(which, (HIDDEN, WIDTH)), pair(WIDTH), pair(WIDTH), pair(WIDTH),
        ],
        out_specs=[rows_of(rows, WIDTH), rows_of(rows, WIDTH), rows_of(rows, 3 * WIDTH), whole((HALF, WIDTH)), whole((HALF, WIDTH))] + extra_spec,
        scratch_shapes=extra_scratch + [
            pltpu.VMEM((GROUP_ROWS, WIDTH), f32), pltpu.VMEM((VECTOR_ROWS * PAD, WIDTH), f32),
            pltpu.VMEM((rows, WIDTH), f32), pltpu.VMEM((rows, 1), f32), pltpu.VMEM((rows, WIDTH), bf16),
            pltpu.VMEM((rows, HIDDEN), f32), pltpu.VMEM((rows, HIDDEN), bf16), pltpu.VMEM((rows, WIDTH), f32),
            pltpu.VMEM((rows, HIDDEN), f32), pltpu.VMEM(block, f32),
            pltpu.VMEM(block, bf16), pltpu.VMEM((rows, WIDTH), f32), pltpu.VMEM((rows, WIDTH), bf16),
            pltpu.VMEM((rows, HIDDEN), bf16), pltpu.VMEM((rows, WIDTH), bf16), pltpu.VMEM((rows, WIDTH), bf16),
            pltpu.VMEM(block, bf16),
        ],
        compiler_params=params(),
        cost_estimate=cost(total * 6 * 800000, total * 4000),
        name="layer",
    )(*leading, in_hbm(x), in_hbm(cot), *[in_hbm(member) for member in attended], *[in_hbm(member) for member in rest])


def input_grad_kernel(one_ref, gqkv_ref, wqkv_ref, gx_ref):
    gx_ref[...] = (one_ref[...] + dot_nt(gqkv_ref[...], wqkv_ref[...])).astype(bf16)


def input_grad(which, steps, one, gqkv, weights):
    total = one.shape[0]
    rows = total // steps
    return pl.pallas_call(
        input_grad_kernel,
        out_shape=shape((total, WIDTH), bf16),
        grid=(steps,),
        in_specs=[rows_of(rows, WIDTH), rows_of(rows, 3 * WIDTH), part_of(which, (WIDTH, 3 * WIDTH))],
        out_specs=rows_of(rows, WIDTH),
        compiler_params=params(),
        cost_estimate=cost(total * 2 * 200000, total * 3000),
        name="input_grad",
    )(in_hbm(one), in_hbm(gqkv), in_hbm(weights[0]))


def stages(count):
    masks = []
    bit = 1
    while bit < count:
        masks.append(bit)
        bit = bit * 2
    groups = [masks[:1]]
    rest = masks[1:]
    while rest:
        groups.append(rest[:2])
        rest = rest[2:]
    return [group for group in groups if group]


def partner_send(values, mask, count):
    return lax.ppermute(values, "dp", [(i, i ^ mask) for i in range(count)])


def visits(group):
    distances = list(range(1, 2 ** len(group)))
    return distances[::-1] if group[0] >= 8 else distances


def combos(group):
    return [distance * group[0] for distance in visits(group)]


def combine(pieces, group, me):
    radix = 2 ** len(group)
    digit = (me // group[0]) % radix
    rows = pieces[0].shape[0]
    part = rows // radix
    if part % 8 == 0:
        return pl.pallas_call(
            functools.partial(combine_kernel, tuple(visits(group))),
            out_shape=[shape((part, WIDTH), bf16)] * radix,
            grid=(1,),
            in_specs=[smem()] + [whole((rows, WIDTH))] * len(pieces),
            out_specs=[whole((part, WIDTH))] * radix,
            scratch_shapes=[pltpu.VMEM((rows, WIDTH), f32)],
            compiler_params=params(),
            name="combine",
        )(digit.reshape(1), *pieces)
    total = pieces[0].astype(f32)
    for piece in pieces[1:]:
        total = total + piece.astype(f32)
    split = total.astype(bf16).reshape(radix, part, WIDTH)
    return [lax.dynamic_index_in_dim(split, digit ^ distance, 0, keepdims=False) for distance in [0] + visits(group)]


def send_parts(cut, group, count):
    own, *sends = cut
    return [own] + [partner_send(part, mask, count) for part, mask in zip(sends, combos(group))]


def send_whole(buffer, group, count):
    return [buffer] + [partner_send(buffer, mask, count) for mask in combos(group)]


def add_up(pieces):
    total = pieces[0].astype(f32)
    for piece in pieces[1:]:
        total = total + piece.astype(f32)
    return total.astype(bf16)


def join(pieces, group, me):
    radix = 2 ** len(group)
    digit = (me // group[0]) % radix
    joined = jnp.zeros((radix,) + pieces[0].shape, pieces[0].dtype)
    for distance, piece in zip([0] + visits(group), pieces):
        joined = lax.dynamic_update_index_in_dim(joined, piece, digit ^ distance, 0)
    return joined.reshape((radix * pieces[0].shape[0],) + pieces[0].shape[1:])


def prepare(pieces, done, following, me):
    reduce_done, group_done = done
    reduce_next, group_next = following
    if not reduce_done:
        return [join(pieces, group_done, me)]
    if reduce_next:
        return combine(pieces, group_next, me)
    return [add_up(pieces)]


def launch(operands, stage, count):
    reduce, group = stage
    return send_parts(operands, group, count) if reduce else send_whole(operands[0], group, count)


def after(values, *others):
    return list(lax.optimization_barrier((tuple(values), others))[0])


def body(questions, passages, cot_questions, cot_passages, len_questions, len_passages, positive, *weights):
    local = questions.shape[0]
    question_length = questions.shape[1]
    passage_length = passages.shape[1]
    count = positive.shape[0] // local
    me = lax.axis_index("dp")
    bit = (me % 2).reshape(1)
    x_q = questions.reshape(-1, WIDTH)
    x_p = passages.reshape(-1, WIDTH)
    own_cls = first_call(count, local, len_questions, len_passages, x_q, x_p, weights)
    own_cls, x_q, x_p = lax.optimization_barrier((own_cls, x_q, x_p))
    all_cls = lax.all_to_all(own_cls, "dp", 0, 0, tiled=True)
    attended_p = attend(1, local, 1, passage_length, len_passages, x_p, weights)
    attended_q = attend(0, 1, local, question_length, len_questions, x_q, weights)
    (all_cls,) = after([all_cls], attended_p[2], attended_q[2])
    slots = positive // local * PAD + positive % local
    slots = jnp.pad(slots.reshape(count, local), ((0, 0), (0, PAD - local)), constant_values=-1)
    own_slots = lax.dynamic_slice_in_dim(slots, me, 1, axis=0).reshape(PAD, 1)
    out_q, one_q, gqkv_q, keep_q, send_q, loss, grad_cls_p = layer(
        0, 1, local, question_length, bit, len_questions, None, x_q, cot_questions.reshape(-1, WIDTH),
        attended_q, weights, (me.reshape(1), all_cls, slots.reshape(1, -1), own_slots),
    )
    loss_rows = loss[:local, 0]
    groups = stages(count)
    steps = [(True, group) for group in groups] + [(False, group) for group in groups[::-1]]
    pieces_q = [keep_q, partner_send(send_q, groups[0][0], count)]
    grad_q = input_grad(0, 1, one_q, gqkv_q, weights)
    operands_q = prepare(after(pieces_q, grad_q), steps[0], steps[1], me)
    (grad_cls_p,) = after([grad_cls_p], *operands_q)
    pieces_q = launch(operands_q, steps[1], count)
    out_p, one_p, gqkv_p, keep_p, send_p = layer(
        1, local, 1, passage_length, bit, len_passages, grad_cls_p, x_p, cot_passages.reshape(-1, WIDTH),
        attended_p, weights,
    )
    (send_p,) = after([send_p], *pieces_q)
    pieces_p = [keep_p, partner_send(send_p, groups[0][0], count)]
    for place in range(len(steps)):
        if 0 < place < len(steps) - 1:
            pieces_p = after(pieces_p, *operands_q)
            operands_p = prepare(pieces_p, steps[place - 1], steps[place], me)
            pieces_p = launch(operands_p, steps[place], count)
            pieces_q = after(pieces_q, *operands_p)
        if place + 2 < len(steps):
            operands_q = prepare(pieces_q, steps[place + 1], steps[place + 2], me)
            pieces_q = launch(operands_q, steps[place + 2], count)
    own_q, other_q = pieces_q
    parts = len(pieces_p)
    digit = (me // groups[1][0] % parts).reshape(1)
    dims = [(WIDTH, 3 * WIDTH), (WIDTH, WIDTH), (WIDTH, HIDDEN), (HIDDEN, WIDTH)]
    matrices = [shape((2,) + d, f32) for d in dims]
    *halves, tail = pl.pallas_call(
        question_unpack_kernel,
        out_shape=matrices + [shape((VECTOR_ROWS, WIDTH), f32)],
        grid=(1,),
        in_specs=[smem()] + [whole((HALF, WIDTH))] * 2,
        out_specs=[part_of(0, d) for d in dims] + [whole((VECTOR_ROWS, WIDTH))],
        scratch_shapes=[pltpu.VMEM((GROUP_ROWS, WIDTH), bf16)],
        compiler_params=params(),
        name="unpack_q",
    )(bit, own_q, other_q)
    own_piece, *came = pieces_p
    grad_p = input_grad(1, 1, one_p, gqkv_p, weights)
    came = after(came, tail, loss_rows, grad_p)
    pieces_p = [own_piece] + came
    other_p = [partner_send(piece, groups[0][0], count) for piece in pieces_p]
    vectors = [(2, HIDDEN)] + [(2, WIDTH)] * len(VECTOR_OUTS)
    first_alias = 2 + 2 * parts + 1
    d_qkv, d_proj, d_up, d_down, up_bias, query_bias, value_bias, proj_bias, gain_a, shift_a, down_bias, gain_f, shift_f = pl.pallas_call(
        functools.partial(passage_unpack_kernel, parts),
        out_shape=matrices + [shape(d, f32) for d in vectors],
        grid=(1,),
        in_specs=[smem(), smem()] + [whole((HALF // parts, WIDTH))] * (2 * parts) + [whole((VECTOR_ROWS, WIDTH))]
        + [pl.BlockSpec(memory_space=pl.ANY)] * 4,
        out_specs=[part_of(1, d) for d in dims] + [whole(d) for d in vectors],
        scratch_shapes=[pltpu.VMEM((GROUP_ROWS, WIDTH), bf16)],
        input_output_aliases={first_alias + i: i for i in range(4)},
        compiler_params=params(),
        name="unpack_p",
    )(bit, digit, *pieces_p, *other_p, tail, *halves)
    return (
        loss_rows, out_q.reshape(questions.shape), out_p.reshape(passages.shape),
        grad_q.reshape(questions.shape), grad_p.reshape(passages.shape),
        d_qkv, query_bias, value_bias, d_proj, proj_bias, gain_a, shift_a, d_up, up_bias, d_down,
        down_bias, gain_f, shift_f,
    )


def solution(mesh):
    split = P("dp", None, None)
    return jax.shard_map(
        body,
        mesh=mesh,
        in_specs=(split, split, split, split, P("dp"), P("dp")) + (P(),) * 14,
        out_specs=(P("dp"), split, split, split, split) + (P(),) * 13,
        check_vma=False,
    )
```

```python
import functools

import jax
import jax.numpy as jnp
from jax import lax
from jax.experimental import pallas as pl
from jax.experimental.pallas import tpu as pltpu
from jax.sharding import PartitionSpec as P

HEAD_DIM = 64
WIDTH = 256
HEADS = WIDTH // HEAD_DIM
HIDDEN = 1024
BLOCKS = HIDDEN // WIDTH
PAD = 8
VECTOR_ROWS = 16
HALF = 6 * WIDTH + 128
GROUP_ROWS = 2 * HALF
LANES = 256
SOFT = 256
NORM = 32
GELU = 16
ln_eps = 1e-06
score_scale = 0.125
masked_score = -1e30
f32 = jnp.float32
bf16 = jnp.bfloat16

QUERY_BIAS, VALUE_BIAS, PROJ_BIAS, ATTN_GAIN, ATTN_SHIFT, DOWN_BIAS, FFN_GAIN, FFN_SHIFT = range(8)
UP_BIAS = 8


def dot(a, b):
    return lax.dot_general(a, b, (((1,), (0,)), ((), ())), preferred_element_type=f32)


def dot_nt(a, b):
    return lax.dot_general(a, b, (((1,), (1,)), ((), ())), preferred_element_type=f32)


def dot_tn(a, b):
    return lax.dot_general(a, b, (((0,), (0,)), ((), ())), preferred_element_type=f32)


def row_loop(rows, chunk, step):
    for row in range(0, rows, chunk):
        step(row)


def vector(ref, which):
    return ref[...].astype(f32)[which : which + 1]


def lane_head(rows):
    return lax.broadcasted_iota(jnp.int32, (rows, WIDTH), 1) // HEAD_DIM


def one_head(values, h, scale=1.0):
    return jnp.where(lane_head(values.shape[0]) == h, values.astype(f32) * scale, 0.0).astype(bf16)


def some_heads(values, first, last, scale=1.0):
    return jnp.concatenate([one_head(values, h, scale) for h in range(first, last)], axis=0)


def pick_heads(stacked, rows):
    head = lane_head(rows)
    result = stacked[:rows]
    for h in range(1, HEADS):
        result = jnp.where(head == h, stacked[h * rows : (h + 1) * rows], result)
    return result


def block_rows(block):
    start = block * WIDTH if block < 6 else HALF + (block - 6) * WIDTH
    return slice(start, start + WIDTH)


VECTOR_START = 6 * WIDTH
QKV_BLOCK, PROJ_BLOCK, UP_BLOCK, DOWN_BLOCK = 0, 3, 4, 8


def normalize(value):
    centered = value - jnp.mean(value, axis=1, keepdims=True)
    inverse = lax.rsqrt(jnp.mean(centered * centered, axis=1, keepdims=True) + ln_eps)
    return centered * inverse, inverse


def masked_softmax(scores, size, scale=score_scale):
    part = scores * scale if scale != 1.0 else scores
    key = lax.broadcasted_iota(jnp.int32, part.shape, 1)
    part = jnp.where(key < size, part, masked_score)
    part = jnp.exp(part - jnp.max(part, axis=1, keepdims=True))
    return part * (1.0 / jnp.sum(part, axis=1, keepdims=True))


def gelu_parts(value):
    cumulative = 0.5 + 0.5 * lax.erf(value * 0.7071067811865476)
    density = jnp.exp(value * value * -0.5) * 0.3989422804014327
    return (value * cumulative).astype(bf16), cumulative + value * density


def first_kernel(
    seqs, lq_ref, lp_ref, xq_ref, xp_ref,
    wqkv_ref, qb_ref, vb_ref, wo_ref, ob_ref, g1_ref, b1_ref, w1_ref, hb_ref, w2_ref, fb_ref, g2_ref, b2_ref,
    cls_ref,
    kq_ref, vq_ref, kp_ref, vp_ref,
):
    sides = ((0, xq_ref, kq_ref, vq_ref, lq_ref), (1, xp_ref, kp_ref, vp_ref, lp_ref))
    filler = jnp.zeros((PAD - seqs, WIDTH), f32)
    inputs = []
    for which, x_ref, *_ in sides:
        length = x_ref.shape[0] // seqs
        firsts = [x_ref[s * length : s * length + 16, :].astype(f32)[:1] for s in range(seqs)]
        inputs.append(jnp.concatenate(firsts + [filler], axis=0))
    own_lanes = lane_head(PAD) == lax.broadcasted_iota(jnp.int32, (PAD, WIDTH), 0)
    queries = [
        (dot(inputs[which].astype(bf16), wqkv_ref[which, :, :WIDTH]) + vector(qb_ref, which)).astype(bf16).astype(f32)
        for which in range(2)
    ]
    for which, x_ref, k_ref, v_ref, _ in sides:
        x = x_ref[...]
        k_ref[...] = dot(x, wqkv_ref[which, :, WIDTH : 2 * WIDTH]).astype(bf16)
        v_ref[...] = (dot(x, wqkv_ref[which, :, 2 * WIDTH :]) + vector(vb_ref, which)).astype(bf16)
    context = []
    for which, x_ref, k_ref, v_ref, len_ref in sides:
        length = x_ref.shape[0] // seqs
        spans = [slice(s * length, (s + 1) * length) for s in range(seqs)]
        scores, sizes = [], []
        for s, span in enumerate(spans):
            heads = jnp.where(own_lanes, queries[which][s : s + 1], 0.0).astype(bf16)
            scores.append(dot_nt(heads, k_ref[span, :]))
            sizes.append(jnp.full((PAD, length), len_ref[s], jnp.int32))
        prob = masked_softmax(jnp.concatenate(scores, axis=0), jnp.concatenate(sizes, axis=0)).astype(f32)
        rows = []
        for s, span in enumerate(spans):
            mixed = dot(prob[s * PAD : (s + 1) * PAD].astype(bf16), v_ref[span, :])
            rows.append(jnp.sum(jnp.where(own_lanes, mixed, 0.0), axis=0, keepdims=True))
        context.append(jnp.concatenate(rows + [filler], axis=0).astype(bf16))
    normed = []
    for which in range(2):
        value = inputs[which] + (dot(context[which], wo_ref[which]) + vector(ob_ref, which))
        unit, _ = normalize(value)
        normed.append(unit * vector(g1_ref, which) + vector(b1_ref, which))
    active = []
    for which in range(2):
        active.append(gelu_parts(dot(normed[which].astype(bf16), w1_ref[which]) + vector(hb_ref, which))[0])
    results = []
    for which in range(2):
        value = normed[which] + (dot(active[which], w2_ref[which]) + vector(fb_ref, which))
        unit, _ = normalize(value)
        result = unit * vector(g2_ref, which) + vector(b2_ref, which)
        row = lax.broadcasted_iota(jnp.int32, result.shape, 0)
        results.append(jnp.where(row < seqs, result, 0.0))
    both = jnp.concatenate(results, axis=0).astype(bf16)

    def store(i, carry):
        cls_ref[i] = both
        return carry

    lax.fori_loop(0, cls_ref.shape[0], store, 0)


def head_groups(length):
    together = max(1, WIDTH // length)
    return [(h, h + together, slice(h * length, (h + together) * length)) for h in range(0, HEADS, together)]


def attend_kernel(which, seqs, length, len_ref, x_ref, wqkv_ref, qb_ref, vb_ref, qkv_ref, p_ref, ctx_ref, score_ref, prob_ref):
    step = pl.program_id(0)
    x = x_ref[...]
    qkv_ref[:, :WIDTH] = (dot(x, wqkv_ref[:, :WIDTH]) + vector(qb_ref, which)).astype(bf16)
    qkv_ref[:, WIDTH : 2 * WIDTH] = dot(x, wqkv_ref[:, WIDTH : 2 * WIDTH]).astype(bf16)
    qkv_ref[:, 2 * WIDTH :] = (dot(x, wqkv_ref[:, 2 * WIDTH :]) + vector(vb_ref, which)).astype(bf16)
    for s in range(seqs):
        span = slice(s * length, (s + 1) * length)
        size = len_ref[step * seqs + s]
        keys = qkv_ref[span, WIDTH : 2 * WIDTH]
        for first, last, columns in head_groups(length):
            score_ref[span, columns] = dot_nt(keys, some_heads(qkv_ref[span, :WIDTH], first, last, score_scale))
            for lane in range(columns.start, columns.stop, LANES):
                here = slice(lane, lane + LANES)
                part = score_ref[span, here]
                key = lax.broadcasted_iota(jnp.int32, part.shape, 0)
                part = jnp.where(key < size, part, masked_score)
                part = jnp.exp(part - jnp.max(part, axis=0, keepdims=True))
                prob = part * (1.0 / jnp.sum(part, axis=0, keepdims=True))
                p_ref[span, here] = prob
                prob_ref[span, here] = prob.astype(bf16)
        ctx_ref[span, :] = pick_heads(dot_tn(prob_ref[span, :], qkv_ref[span, 2 * WIDTH :]), length).astype(bf16)


def attend_long_kernel(which, seqs, length, len_ref, x_ref, wqkv_ref, qb_ref, vb_ref, qkv_ref, p_ref, ctx_ref, score_ref, prob_ref):
    step = pl.program_id(0)
    x = x_ref[...]
    qkv_ref[:, :WIDTH] = (dot(x, wqkv_ref[:, :WIDTH]) + vector(qb_ref, which)).astype(bf16)
    qkv_ref[:, WIDTH : 2 * WIDTH] = dot(x, wqkv_ref[:, WIDTH : 2 * WIDTH]).astype(bf16)
    qkv_ref[:, 2 * WIDTH :] = (dot(x, wqkv_ref[:, 2 * WIDTH :]) + vector(vb_ref, which)).astype(bf16)
    stack_rows = HEADS * length
    for s in range(seqs):
        span = slice(s * length, (s + 1) * length)
        stack = slice(s * stack_rows, (s + 1) * stack_rows)
        size = len_ref[step * seqs + s]
        queries = qkv_ref[span, :WIDTH]
        for h in range(HEADS):
            start = s * stack_rows + h * length
            score_ref[start : start + length, :] = dot_nt(one_head(queries, h, score_scale), qkv_ref[span, WIDTH : 2 * WIDTH])

            def softmax(row):
                here = pl.ds(start + row, SOFT)
                prob = masked_softmax(score_ref[here, :], size, 1.0)
                p_ref[here, :] = prob
                prob_ref[here, :] = prob.astype(bf16)

            row_loop(length, SOFT, softmax)
        ctx_ref[span, :] = pick_heads(dot(prob_ref[stack, :], qkv_ref[span, 2 * WIDTH :]), length).astype(bf16)


def forward_phase(
    which, rows, x_ref, wo_ref, ob_ref, g1_ref, b1_ref, w1_ref, hb_ref, w2_ref,
    ctx_ref, n1_ref, r1_ref, nb_ref, gp_ref, act_ref, n2_ref, wide_ref,
):
    n2_ref[...] = dot(ctx_ref[...], wo_ref[...])
    ob, g1, b1 = vector(ob_ref, which), vector(g1_ref, which), vector(b1_ref, which)

    def first_norm(row):
        here = pl.ds(row, NORM)
        unit, inverse = normalize(x_ref[here, :].astype(f32) + (n2_ref[here, :] + ob))
        n1_ref[here, :] = unit
        r1_ref[here, :] = inverse
        nb_ref[here, :] = (unit * g1 + b1).astype(bf16)

    row_loop(rows, NORM, first_norm)
    hb = vector(hb_ref, which)
    for j in range(BLOCKS):
        lanes = slice(j * WIDTH, (j + 1) * WIDTH)
        wide_ref[:, lanes] = dot(nb_ref[...], w1_ref[:, lanes])

        def gelu(row):
            here = pl.ds(row, GELU)
            active, slope = gelu_parts(wide_ref[here, lanes] + hb[:, lanes])
            act_ref[here, lanes] = active
            gp_ref[here, lanes] = slope

        row_loop(rows, GELU, gelu)
    n2_ref[...] = dot(act_ref[...], w2_ref[...])


def add_row(vec_ref, row, values):
    here = slice(row * PAD, (row + 1) * PAD)
    vec_ref[here, :] = vec_ref[here, :] + jnp.sum(values.reshape(-1, PAD, WIDTH), axis=0)


def ffn_phase(which, seqs, length, first, len_ref, cls_ref, cot_ref, n1_ref, n2_ref, gp_ref, w2_ref, g1_ref, b1_ref, fb_ref, g2_ref, b2_ref, out_ref, two_ref, gffn_ref, gpre_ref, vec_ref, wide_ref):
    g1, g2, b2 = vector(g1_ref, which), vector(g2_ref, which), vector(b2_ref, which)
    shift = vector(b1_ref, which) + vector(fb_ref, which)
    for s in range(seqs):
        size = len_ref[first + s]
        cls_row = cls_ref[pl.ds(first + s, 1), :]

        def output_norm(row):
            here = pl.ds(s * length + row, NORM)
            inside = row + lax.broadcasted_iota(jnp.int32, (NORM, WIDTH), 0) < size
            unit, inverse = normalize(n1_ref[here, :] * g1 + (n2_ref[here, :] + shift))
            out_ref[here, :] = jnp.where(inside, unit * g2 + b2, 0.0).astype(bf16)
            grad = cot_ref[here, :].astype(f32)
            if row == 0:
                grad = grad + jnp.where(lax.broadcasted_iota(jnp.int32, (NORM, WIDTH), 0) == 0, cls_row, 0.0)
            grad = jnp.where(inside, grad, 0.0)
            scaled = grad * g2
            slope = scaled * unit
            first_mean = jnp.mean(scaled, axis=1, keepdims=True)
            second_mean = jnp.mean(slope, axis=1, keepdims=True)
            two = inverse * (scaled - first_mean - unit * second_mean)
            low = two.astype(bf16)
            two_ref[here, :] = two
            gffn_ref[here, :] = low
            add_row(vec_ref, FFN_GAIN, grad * unit)
            add_row(vec_ref, FFN_SHIFT, grad)
            add_row(vec_ref, DOWN_BIAS, low.astype(f32))

        row_loop(length, NORM, output_norm)
    for j in range(BLOCKS):
        lanes = slice(j * WIDTH, (j + 1) * WIDTH)
        wide_ref[:, lanes] = dot_nt(gffn_ref[...], w2_ref[lanes, :])

        def gelu_back(row):
            here = pl.ds(row, GELU)
            low = (wide_ref[here, lanes] * gp_ref[here, lanes]).astype(bf16)
            gpre_ref[here, lanes] = low
            add_row(vec_ref, UP_BIAS + j, low.astype(f32))

        row_loop(seqs * length, GELU, gelu_back)


def attn_norm_phase(which, rows, gpre_ref, w1_ref, two_ref, n1_ref, r1_ref, g1_ref, wo_ref, one_ref, gatt_ref, dctx_ref, vec_ref):
    one_ref[...] = dot_nt(gpre_ref[...], w1_ref[...])
    g1 = vector(g1_ref, which)

    def norm_back(row):
        here = pl.ds(row, NORM)
        grad = two_ref[here, :] + one_ref[here, :]
        unit = n1_ref[here, :]
        scaled = grad * g1
        first_mean = jnp.mean(scaled, axis=1, keepdims=True)
        second_mean = jnp.mean(scaled * unit, axis=1, keepdims=True)
        one = r1_ref[here, :] * (scaled - first_mean - unit * second_mean)
        low = one.astype(bf16)
        one_ref[here, :] = one
        gatt_ref[here, :] = low
        add_row(vec_ref, ATTN_GAIN, grad * unit)
        add_row(vec_ref, ATTN_SHIFT, grad)
        add_row(vec_ref, PROJ_BIAS, low.astype(f32))

    row_loop(rows, NORM, norm_back)
    dctx_ref[...] = dot_nt(gatt_ref[...], wo_ref[...]).astype(bf16)


def attn_core_phase(seqs, length, dctx_ref, qkv_ref, p_ref, gqkv_ref, vec_ref, dp_ref, ds_ref, pb_ref):
    for s in range(seqs):
        span = slice(s * length, (s + 1) * length)
        values = qkv_ref[span, 2 * WIDTH :]
        context = some_heads(dctx_ref[span, :], 0, HEADS)
        for first, last, columns in head_groups(length):
            dp_ref[span, columns] = dot_nt(values, context[columns])
            for lane in range(columns.start, columns.stop, LANES):
                here = slice(lane, lane + LANES)
                prob = p_ref[span, here]
                grad = dp_ref[span, here]
                inner = jnp.sum(prob * grad, axis=0, keepdims=True)
                ds_ref[span, here] = (prob * (grad - inner)).astype(bf16)
                pb_ref[span, here] = prob.astype(bf16)
        queries = some_heads(qkv_ref[span, :WIDTH], 0, HEADS, score_scale)
        gqkv_ref[span, WIDTH : 2 * WIDTH] = dot(ds_ref[span, :], queries).astype(bf16)
        grad_v = dot(pb_ref[span, :], context).astype(bf16)
        gqkv_ref[span, 2 * WIDTH :] = grad_v
        add_row(vec_ref, VALUE_BIAS, grad_v.astype(f32))
        grad_q = (pick_heads(dot_tn(ds_ref[span, :], qkv_ref[span, WIDTH : 2 * WIDTH]), length) * score_scale).astype(bf16)
        gqkv_ref[span, :WIDTH] = grad_q
        add_row(vec_ref, QUERY_BIAS, grad_q.astype(f32))


def attn_core_long(seqs, length, dctx_ref, qkv_ref, p_ref, gqkv_ref, vec_ref, dp_ref, ds_ref, pb_ref):
    stack_rows = HEADS * length
    for s in range(seqs):
        span = slice(s * length, (s + 1) * length)
        stack = slice(s * stack_rows, (s + 1) * stack_rows)
        contexts = [one_head(dctx_ref[span, :], h) for h in range(HEADS)]
        for h in range(HEADS):
            start = s * stack_rows + h * length
            dp_ref[start : start + length, :] = dot_nt(contexts[h], qkv_ref[span, 2 * WIDTH :])

            def softmax_back(row):
                here = pl.ds(start + row, SOFT)
                prob = p_ref[here, :]
                grad = dp_ref[here, :]
                inner = jnp.sum(prob * grad, axis=1, keepdims=True)
                ds_ref[here, :] = (prob * (grad - inner)).astype(bf16)
                pb_ref[here, :] = prob.astype(bf16)

            row_loop(length, SOFT, softmax_back)
        context = jnp.concatenate(contexts, axis=0)
        queries = some_heads(qkv_ref[span, :WIDTH], 0, HEADS, score_scale)
        grad_q = (pick_heads(dot(ds_ref[stack, :], qkv_ref[span, WIDTH : 2 * WIDTH]), length) * score_scale).astype(bf16)
        gqkv_ref[span, :WIDTH] = grad_q
        add_row(vec_ref, QUERY_BIAS, grad_q.astype(f32))
        gqkv_ref[span, WIDTH : 2 * WIDTH] = dot_tn(ds_ref[stack, :], queries).astype(bf16)
        grad_v = dot_tn(pb_ref[stack, :], context).astype(bf16)
        gqkv_ref[span, 2 * WIDTH :] = grad_v
        add_row(vec_ref, VALUE_BIAS, grad_v.astype(f32))


def layer_kernel(
    which, steps, seqs, length,
    bit_ref, len_ref, cls_ref, x_ref, cot_ref, qkv_ref, p_ref, ctx_ref,
    wo_ref, ob_ref, g1_ref, b1_ref, w1_ref, hb_ref, w2_ref, fb_ref, g2_ref, b2_ref,
    out_ref, one_ref, gqkv_ref, keep_ref, send_ref,
    acc_ref, vec_ref, n1_ref, r1_ref, nb_ref, gp_ref, act_ref, n2_ref,
    wide_ref, score_ref, prob_ref, two_ref, gffn_ref, gpre_ref, gatt_ref, dctx_ref, ds_ref,
):
    rows = seqs * length
    step = pl.program_id(0)

    def start():
        vec_ref[...] = jnp.zeros_like(vec_ref)
        if steps > 1:
            acc_ref[...] = jnp.zeros_like(acc_ref)

    if steps > 1:
        pl.when(step == 0)(start)
    else:
        start()

    def add_block(block, value):
        if steps > 1:
            acc_ref[block_rows(block), :] += value
        else:
            acc_ref[block_rows(block), :] = value

    forward_phase(
        which, rows, x_ref, wo_ref, ob_ref, g1_ref, b1_ref, w1_ref, hb_ref, w2_ref,
        ctx_ref, n1_ref, r1_ref, nb_ref, gp_ref, act_ref, n2_ref, wide_ref,
    )
    ffn_phase(which, seqs, length, step * seqs, len_ref, cls_ref, cot_ref, n1_ref, n2_ref, gp_ref, w2_ref, g1_ref, b1_ref, fb_ref, g2_ref, b2_ref, out_ref, two_ref, gffn_ref, gpre_ref, vec_ref, wide_ref)
    downs = dot_tn(act_ref[...], gffn_ref[...])
    ups = dot_tn(nb_ref[...], gpre_ref[...])
    for j in range(BLOCKS):
        lanes = slice(j * WIDTH, (j + 1) * WIDTH)
        add_block(DOWN_BLOCK + j, downs[lanes])
        add_block(UP_BLOCK + j, ups[:, lanes])
    attn_norm_phase(which, rows, gpre_ref, w1_ref, two_ref, n1_ref, r1_ref, g1_ref, wo_ref, one_ref, gatt_ref, dctx_ref, vec_ref)
    add_block(PROJ_BLOCK, dot_tn(ctx_ref[...], gatt_ref[...]))
    attn_core = attn_core_long if seqs == 1 else attn_core_phase
    attn_core(seqs, length, dctx_ref, qkv_ref, p_ref, gqkv_ref, vec_ref, score_ref, ds_ref, prob_ref)
    for j in range(3):
        add_block(QKV_BLOCK + j, dot_tn(x_ref[...], gqkv_ref[:, j * WIDTH : (j + 1) * WIDTH]))

    def finish():
        acc_ref[VECTOR_START : VECTOR_START + VECTOR_ROWS, :] = jnp.sum(vec_ref[...].reshape(VECTOR_ROWS, PAD, WIDTH), axis=1)
        if steps == 1:
            acc_ref[VECTOR_START + VECTOR_ROWS : HALF, :] = jnp.zeros((HALF - VECTOR_START - VECTOR_ROWS, WIDTH), f32)
            acc_ref[HALF + 6 * WIDTH :, :] = jnp.zeros((HALF - 6 * WIDTH, WIDTH), f32)
        keep = pl.multiple_of(bit_ref[0] * HALF, HALF)
        send = pl.multiple_of((1 - bit_ref[0]) * HALF, HALF)
        keep_ref[...] = acc_ref[pl.ds(keep, HALF), :].astype(bf16)
        send_ref[...] = acc_ref[pl.ds(send, HALF), :].astype(bf16)

    if steps > 1:
        pl.when(step == steps - 1)(finish)
    else:
        finish()


def loss_phase(local, me_ref, all_ref, hot_ref, own_hot_ref, loss_ref, gq_ref, gp_ref, q_ref, p_ref):
    count = all_ref.shape[0]
    me = me_ref[0]
    wide = all_ref[...].astype(f32)
    q_ref[...] = wide[:, :PAD].reshape(count * PAD, WIDTH).astype(bf16)
    p_ref[...] = wide[:, PAD:].reshape(count * PAD, WIDTH).astype(bf16)
    own_q = all_ref[me][:PAD]
    own_p = all_ref[me][PAD:]
    logits = dot_nt(own_q, p_ref[...]) * score_scale
    column = lax.broadcasted_iota(jnp.int32, logits.shape, 1)
    logits = jnp.where(column % PAD < local, logits, masked_score)
    top = jnp.max(logits, axis=1, keepdims=True)
    total = top + jnp.log(jnp.sum(jnp.exp(logits - top), axis=1, keepdims=True))
    hot = (column == own_hot_ref[...]).astype(f32)
    loss_ref[...] = jnp.broadcast_to(total - jnp.sum(logits * hot, axis=1, keepdims=True), loss_ref.shape)
    grad = (jnp.exp(logits - total) - hot).astype(bf16)
    gq_ref[...] = dot(grad, p_ref[...]) * score_scale
    gp_ref[...] = jnp.zeros_like(gp_ref)
    block = 256 if count * PAD % 256 == 0 else count * PAD

    def part(index, carry):
        start = index * block if isinstance(index, int) else pl.multiple_of(index * block, block)
        queries = q_ref[pl.ds(start, block), :]
        scores = dot_nt(p_ref[...], queries) * score_scale
        row = lax.broadcasted_iota(jnp.int32, scores.shape, 0)
        scores = jnp.where(row % PAD < local, scores, masked_score)
        peak = jnp.max(scores, axis=0, keepdims=True)
        sums = peak + jnp.log(jnp.sum(jnp.exp(scores - peak), axis=0, keepdims=True))
        own = dot_nt(own_p, queries) * score_scale
        own_row = lax.broadcasted_iota(jnp.int32, own.shape, 0)
        own_lane = lax.broadcasted_iota(jnp.int32, own.shape, 1)
        own_hits = (own_row + me * PAD == hot_ref[:, pl.ds(start, block)]).astype(f32)
        own_grad = jnp.where(own_lane % PAD < local, jnp.exp(own - sums) - own_hits, 0.0)
        gp_ref[...] += dot(own_grad.astype(bf16), queries) * score_scale
        return carry

    if count * PAD == block:
        part(0, 0)
    else:
        lax.fori_loop(0, count * PAD // block, part, 0)


def question_kernel(local, seqs, length, me_ref, all_ref, hot_ref, own_hot_ref, bit_ref, len_ref, *refs):
    inputs, outputs, scratch = refs[:15], refs[15:22], refs[22:]
    loss_ref, gp_ref = outputs[5:]
    gq_ref, q_ref, p_ref = scratch[:3]
    loss_phase(local, me_ref, all_ref, hot_ref, own_hot_ref, loss_ref, gq_ref, gp_ref, q_ref, p_ref)
    layer_kernel(0, 1, seqs, length, bit_ref, len_ref, gq_ref, *inputs, *outputs[:5], *scratch[3:])


def combine_kernel(distances, digit_ref, *refs):
    radix = len(distances) + 1
    total_ref = refs[-1]
    sends = refs[-1 - (radix - 1) : -1]
    keep_ref = refs[-1 - radix]
    pieces = refs[: -1 - radix]
    total = pieces[0][...].astype(f32)
    for piece in pieces[1:]:
        total = total + piece[...].astype(f32)
    total_ref[...] = total
    part = total_ref.shape[0] // radix
    digit = digit_ref[0]

    def section(which):
        return total_ref[pl.ds(pl.multiple_of(which * part, part), part), :].astype(bf16)

    keep_ref[...] = section(digit)
    for distance, ref in zip(distances, sends):
        ref[...] = section(digit ^ distance)


VECTOR_OUTS = (QUERY_BIAS, VALUE_BIAS, PROJ_BIAS, ATTN_GAIN, ATTN_SHIFT, DOWN_BIAS, FFN_GAIN, FFN_SHIFT)


def spread(which, ref, qkv_ref, proj_ref, up_ref, down_ref):
    for j in range(3):
        qkv_ref[:, j * WIDTH : (j + 1) * WIDTH] = ref[block_rows(QKV_BLOCK + j), :].astype(f32)
    proj_ref[...] = ref[block_rows(PROJ_BLOCK), :].astype(f32)
    for j in range(BLOCKS):
        up_ref[:, j * WIDTH : (j + 1) * WIDTH] = ref[block_rows(UP_BLOCK + j), :].astype(f32)
        down_ref[j * WIDTH : (j + 1) * WIDTH, :] = ref[block_rows(DOWN_BLOCK + j), :].astype(f32)
    return ref[VECTOR_START : VECTOR_START + VECTOR_ROWS, :].astype(f32)


def question_unpack_kernel(bit_ref, own_ref, other_ref, qkv_ref, proj_ref, up_ref, down_ref, tail_ref, whole_ref):
    whole_ref[pl.ds(pl.multiple_of(bit_ref[0] * HALF, HALF), HALF), :] = own_ref[...]
    whole_ref[pl.ds(pl.multiple_of((1 - bit_ref[0]) * HALF, HALF), HALF), :] = other_ref[...]
    tail_ref[...] = spread(0, whole_ref, qkv_ref, proj_ref, up_ref, down_ref)


def passage_unpack_kernel(parts, bit_ref, digit_ref, *refs):
    own_refs, other_refs, (tail_ref, *_) = refs[:parts], refs[parts : 2 * parts], refs[2 * parts : 2 * parts + 5]
    qkv_ref, proj_ref, up_ref, down_ref, up_bias_ref, *vector_refs, whole_ref = refs[2 * parts + 5 :]
    size = HALF // parts
    for half, halves in ((bit_ref[0], own_refs), (1 - bit_ref[0], other_refs)):
        for step, ref in enumerate(halves):
            start = half * HALF + (digit_ref[0] ^ step) * size
            whole_ref[pl.ds(pl.multiple_of(start, 8), size), :] = ref[...]
    tails = (tail_ref[...], spread(1, whole_ref, qkv_ref, proj_ref, up_ref, down_ref))
    for row, ref in zip(VECTOR_OUTS, vector_refs):
        for which in range(2):
            ref[which : which + 1, :] = tails[which][row : row + 1]
    for j in range(BLOCKS):
        for which in range(2):
            up_bias_ref[which : which + 1, j * WIDTH : (j + 1) * WIDTH] = tails[which][UP_BIAS + j : UP_BIAS + j + 1]


def smem():
    return pl.BlockSpec(memory_space=pltpu.SMEM)


def whole(shape):
    return pl.BlockSpec(shape, lambda i: (0,) * len(shape))


def rows_of(rows, columns):
    return pl.BlockSpec((rows, columns), lambda i: (i, 0))


def part_of(which, shape):
    return pl.BlockSpec((None,) + shape, lambda i: (which, 0, 0))


def params():
    return pltpu.CompilerParams(vmem_limit_bytes=24 * 1024 * 1024)


def shape(dims, kind):
    return jax.ShapeDtypeStruct(dims, kind)


def cost(flops, moved):
    return pl.CostEstimate(flops=flops, bytes_accessed=moved, transcendentals=0)


def pair(columns):
    return whole((2, columns))


def in_hbm(values):
    return pltpu.with_memory_space_constraint(values, pltpu.HBM)


def first_call(count, local, len_questions, len_passages, x_q, x_p, weights):
    return pl.pallas_call(
        functools.partial(first_kernel, local),
        out_shape=shape((count, 2 * PAD, WIDTH), bf16),
        grid=(1,),
        in_specs=[smem(), smem(), whole(x_q.shape), whole(x_p.shape)] + [whole(member.shape) for member in weights],
        out_specs=whole((count, 2 * PAD, WIDTH)),
        scratch_shapes=[pltpu.VMEM(x_q.shape, bf16)] * 2 + [pltpu.VMEM(x_p.shape, bf16)] * 2,
        compiler_params=params(),
        name="first",
    )(in_hbm(len_questions), in_hbm(len_passages), in_hbm(x_q), in_hbm(x_p), *[in_hbm(member) for member in weights])


def attend(which, steps, seqs, length, lengths, x, weights):
    wqkv, qb, vb, *_ = weights
    rows = seqs * length
    total = steps * rows
    block = (HEADS * length, length) if seqs == 1 else (rows, HEADS * length)
    return pl.pallas_call(
        functools.partial(attend_long_kernel if seqs == 1 else attend_kernel, which, seqs, length),
        out_shape=[
            pltpu.HBM((total, 3 * WIDTH), bf16), pltpu.HBM((steps * block[0], block[1]), f32), pltpu.HBM((total, WIDTH), bf16),
        ],
        grid=(steps,),
        in_specs=[smem(), rows_of(rows, WIDTH), part_of(which, (WIDTH, 3 * WIDTH)), pair(WIDTH), pair(WIDTH)],
        out_specs=[rows_of(rows, 3 * WIDTH), rows_of(*block), rows_of(rows, WIDTH)],
        scratch_shapes=[pltpu.VMEM(block, f32), pltpu.VMEM(block, bf16)],
        compiler_params=params(),
        cost_estimate=cost(total * 2 * 400000, total * 6000),
        name="attend",
    )(lengths, in_hbm(x), in_hbm(wqkv), in_hbm(qb), in_hbm(vb))


def layer(which, steps, seqs, length, bit, lengths, cls_grad, x, cot, attended, weights, exchange=None):
    rows = seqs * length
    total = steps * rows
    block = (HEADS * length, length) if seqs == 1 else (rows, HEADS * length)
    _, _, _, *rest = weights
    kernel = functools.partial(layer_kernel, which, steps, seqs, length)
    extra_shape, extra_spec, extra_scratch = [], [], []
    leading, cls_spec = (bit, lengths, cls_grad), [smem(), smem(), whole((PAD, WIDTH))]
    if exchange:
        kernel = functools.partial(question_kernel, seqs, seqs, length)
        count = exchange[1].shape[0]
        leading = (*exchange, bit, lengths)
        cls_spec = [smem(), whole(exchange[1].shape), whole((1, count * PAD)), whole((PAD, 1)), smem(), smem()]
        extra_shape = [shape((PAD, 128), f32), shape((PAD, WIDTH), f32)]
        extra_spec = [whole((PAD, 128)), whole((PAD, WIDTH))]
        extra_scratch = [pltpu.VMEM((PAD, WIDTH), f32)] + [pltpu.VMEM((count * PAD, WIDTH), bf16)] * 2
    return pl.pallas_call(
        kernel,
        out_shape=[shape((total, WIDTH), bf16), pltpu.HBM((total, WIDTH), f32), pltpu.HBM((total, 3 * WIDTH), bf16), shape((HALF, WIDTH), bf16), shape((HALF, WIDTH), bf16)] + extra_shape,
        grid=(steps,),
        in_specs=[
            *cls_spec, rows_of(rows, WIDTH), rows_of(rows, WIDTH),
            rows_of(rows, 3 * WIDTH), rows_of(*block), rows_of(rows, WIDTH),
            part_of(which, (WIDTH, WIDTH)),
            pair(WIDTH), pair(WIDTH), pair(WIDTH), part_of(which, (WIDTH, HIDDEN)), pair(HIDDEN),
            part_of(which, (HIDDEN, WIDTH)), pair(WIDTH), pair(WIDTH), pair(WIDTH),
        ],
        out_specs=[rows_of(rows, WIDTH), rows_of(rows, WIDTH), rows_of(rows, 3 * WIDTH), whole((HALF, WIDTH)), whole((HALF, WIDTH))] + extra_spec,
        scratch_shapes=extra_scratch + [
            pltpu.VMEM((GROUP_ROWS, WIDTH), f32), pltpu.VMEM((VECTOR_ROWS * PAD, WIDTH), f32),
            pltpu.VMEM((rows, WIDTH), f32), pltpu.VMEM((rows, 1), f32), pltpu.VMEM((rows, WIDTH), bf16),
            pltpu.VMEM((rows, HIDDEN), f32), pltpu.VMEM((rows, HIDDEN), bf16), pltpu.VMEM((rows, WIDTH), f32),
            pltpu.VMEM((rows, HIDDEN), f32), pltpu.VMEM(block, f32),
            pltpu.VMEM(block, bf16), pltpu.VMEM((rows, WIDTH), f32), pltpu.VMEM((rows, WIDTH), bf16),
            pltpu.VMEM((rows, HIDDEN), bf16), pltpu.VMEM((rows, WIDTH), bf16), pltpu.VMEM((rows, WIDTH), bf16),
            pltpu.VMEM(block, bf16),
        ],
        compiler_params=params(),
        cost_estimate=cost(total * 6 * 800000, total * 4000),
        name="layer",
    )(*leading, in_hbm(x), in_hbm(cot), *[in_hbm(member) for member in attended], *[in_hbm(member) for member in rest])


def input_grad_kernel(one_ref, gqkv_ref, wqkv_ref, gx_ref):
    gx_ref[...] = (one_ref[...] + dot_nt(gqkv_ref[...], wqkv_ref[...])).astype(bf16)


def input_grad(which, steps, one, gqkv, weights):
    total = one.shape[0]
    rows = total // steps
    return pl.pallas_call(
        input_grad_kernel,
        out_shape=shape((total, WIDTH), bf16),
        grid=(steps,),
        in_specs=[rows_of(rows, WIDTH), rows_of(rows, 3 * WIDTH), part_of(which, (WIDTH, 3 * WIDTH))],
        out_specs=rows_of(rows, WIDTH),
        compiler_params=params(),
        cost_estimate=cost(total * 2 * 200000, total * 3000),
        name="input_grad",
    )(in_hbm(one), in_hbm(gqkv), in_hbm(weights[0]))


def stages(count):
    masks = []
    bit = 1
    while bit < count:
        masks.append(bit)
        bit = bit * 2
    groups = [masks[:1]]
    rest = masks[1:]
    while rest:
        groups.append(rest[:2])
        rest = rest[2:]
    return [group for group in groups if group]


def partner_send(values, mask, count):
    return lax.ppermute(values, "dp", [(i, i ^ mask) for i in range(count)])


def visits(group):
    distances = list(range(1, 2 ** len(group)))
    return distances[::-1] if group[0] >= 8 else distances


def combos(group):
    return [distance * group[0] for distance in visits(group)]


def combine(pieces, group, me):
    radix = 2 ** len(group)
    digit = (me // group[0]) % radix
    rows = pieces[0].shape[0]
    part = rows // radix
    if part % 8 == 0:
        return pl.pallas_call(
            functools.partial(combine_kernel, tuple(visits(group))),
            out_shape=[shape((part, WIDTH), bf16)] * radix,
            grid=(1,),
            in_specs=[smem()] + [whole((rows, WIDTH))] * len(pieces),
            out_specs=[whole((part, WIDTH))] * radix,
            scratch_shapes=[pltpu.VMEM((rows, WIDTH), f32)],
            compiler_params=params(),
            name="combine",
        )(digit.reshape(1), *pieces)
    total = pieces[0].astype(f32)
    for piece in pieces[1:]:
        total = total + piece.astype(f32)
    split = total.astype(bf16).reshape(radix, part, WIDTH)
    return [lax.dynamic_index_in_dim(split, digit ^ distance, 0, keepdims=False) for distance in [0] + visits(group)]


def send_parts(cut, group, count):
    own, *sends = cut
    return [own] + [partner_send(part, mask, count) for part, mask in zip(sends, combos(group))]


def send_whole(buffer, group, count):
    return [buffer] + [partner_send(buffer, mask, count) for mask in combos(group)]


def add_up(pieces):
    total = pieces[0].astype(f32)
    for piece in pieces[1:]:
        total = total + piece.astype(f32)
    return total.astype(bf16)


def join(pieces, group, me):
    radix = 2 ** len(group)
    digit = (me // group[0]) % radix
    joined = jnp.zeros((radix,) + pieces[0].shape, pieces[0].dtype)
    for distance, piece in zip([0] + visits(group), pieces):
        joined = lax.dynamic_update_index_in_dim(joined, piece, digit ^ distance, 0)
    return joined.reshape((radix * pieces[0].shape[0],) + pieces[0].shape[1:])


def prepare(pieces, done, following, me):
    reduce_done, group_done = done
    reduce_next, group_next = following
    if not reduce_done:
        return [join(pieces, group_done, me)]
    if reduce_next:
        return combine(pieces, group_next, me)
    return [add_up(pieces)]


def launch(operands, stage, count):
    reduce, group = stage
    return send_parts(operands, group, count) if reduce else send_whole(operands[0], group, count)


def after(values, *others):
    return list(lax.optimization_barrier((tuple(values), others))[0])


def body(questions, passages, cot_questions, cot_passages, len_questions, len_passages, positive, *weights):
    local = questions.shape[0]
    question_length = questions.shape[1]
    passage_length = passages.shape[1]
    count = positive.shape[0] // local
    me = lax.axis_index("dp")
    bit = (me % 2).reshape(1)
    x_q = questions.reshape(-1, WIDTH)
    x_p = passages.reshape(-1, WIDTH)
    own_cls = first_call(count, local, len_questions, len_passages, x_q, x_p, weights)
    own_cls, x_q, x_p = lax.optimization_barrier((own_cls, x_q, x_p))
    all_cls = lax.all_to_all(own_cls, "dp", 0, 0, tiled=True)
    attended_p = attend(1, local, 1, passage_length, len_passages, x_p, weights)
    attended_q = attend(0, 1, local, question_length, len_questions, x_q, weights)
    (all_cls,) = after([all_cls], attended_p[2], attended_q[2])
    slots = positive // local * PAD + positive % local
    slots = jnp.pad(slots.reshape(count, local), ((0, 0), (0, PAD - local)), constant_values=-1)
    own_slots = lax.dynamic_slice_in_dim(slots, me, 1, axis=0).reshape(PAD, 1)
    out_q, one_q, gqkv_q, keep_q, send_q, loss, grad_cls_p = layer(
        0, 1, local, question_length, bit, len_questions, None, x_q, cot_questions.reshape(-1, WIDTH),
        attended_q, weights, (me.reshape(1), all_cls, slots.reshape(1, -1), own_slots),
    )
    loss_rows = loss[:local, 0]
    groups = stages(count)
    steps = [(True, group) for group in groups] + [(False, group) for group in groups[::-1]]
    pieces_q = [keep_q, partner_send(send_q, groups[0][0], count)]
    grad_q = input_grad(0, 1, one_q, gqkv_q, weights)
    operands_q = prepare(after(pieces_q, grad_q), steps[0], steps[1], me)
    (grad_cls_p,) = after([grad_cls_p], *operands_q)
    pieces_q = launch(operands_q, steps[1], count)
    out_p, one_p, gqkv_p, keep_p, send_p = layer(
        1, local, 1, passage_length, bit, len_passages, grad_cls_p, x_p, cot_passages.reshape(-1, WIDTH),
        attended_p, weights,
    )
    (send_p,) = after([send_p], *pieces_q)
    pieces_p = [keep_p, partner_send(send_p, groups[0][0], count)]
    for place in range(len(steps)):
        if 0 < place < len(steps) - 1:
            pieces_p = after(pieces_p, *operands_q)
            operands_p = prepare(pieces_p, steps[place - 1], steps[place], me)
            pieces_p = launch(operands_p, steps[place], count)
            pieces_q = after(pieces_q, *operands_p)
        if place + 2 < len(steps):
            operands_q = prepare(pieces_q, steps[place + 1], steps[place + 2], me)
            pieces_q = launch(operands_q, steps[place + 2], count)
    own_q, other_q = pieces_q
    parts = len(pieces_p)
    digit = (me // groups[1][0] % parts).reshape(1)
    dims = [(WIDTH, 3 * WIDTH), (WIDTH, WIDTH), (WIDTH, HIDDEN), (HIDDEN, WIDTH)]
    matrices = [shape((2,) + d, f32) for d in dims]
    *halves, tail = pl.pallas_call(
        question_unpack_kernel,
        out_shape=matrices + [shape((VECTOR_ROWS, WIDTH), f32)],
        grid=(1,),
        in_specs=[smem()] + [whole((HALF, WIDTH))] * 2,
        out_specs=[part_of(0, d) for d in dims] + [whole((VECTOR_ROWS, WIDTH))],
        scratch_shapes=[pltpu.VMEM((GROUP_ROWS, WIDTH), bf16)],
        compiler_params=params(),
        name="unpack_q",
    )(bit, own_q, other_q)
    own_piece, *came = pieces_p
    grad_p = input_grad(1, 1, one_p, gqkv_p, weights)
    came = after(came, tail, loss_rows, grad_p)
    pieces_p = [own_piece] + came
    other_p = [partner_send(piece, groups[0][0], count) for piece in pieces_p]
    vectors = [(2, HIDDEN)] + [(2, WIDTH)] * len(VECTOR_OUTS)
    first_alias = 2 + 2 * parts + 1
    d_qkv, d_proj, d_up, d_down, up_bias, query_bias, value_bias, proj_bias, gain_a, shift_a, down_bias, gain_f, shift_f = pl.pallas_call(
        functools.partial(passage_unpack_kernel, parts),
        out_shape=matrices + [shape(d, f32) for d in vectors],
        grid=(1,),
        in_specs=[smem(), smem()] + [whole((HALF // parts, WIDTH))] * (2 * parts) + [whole((VECTOR_ROWS, WIDTH))]
        + [pl.BlockSpec(memory_space=pl.ANY)] * 4,
        out_specs=[part_of(1, d) for d in dims] + [whole(d) for d in vectors],
        scratch_shapes=[pltpu.VMEM((GROUP_ROWS, WIDTH), bf16)],
        input_output_aliases={first_alias + i: i for i in range(4)},
        compiler_params=params(),
        name="unpack_p",
    )(bit, digit, *pieces_p, *other_p, tail, *halves)
    return (
        loss_rows, out_q.reshape(questions.shape), out_p.reshape(passages.shape),
        grad_q.reshape(questions.shape), grad_p.reshape(passages.shape),
        d_qkv, query_bias, value_bias, d_proj, proj_bias, gain_a, shift_a, d_up, up_bias, d_down,
        down_bias, gain_f, shift_f,
    )


def solution(mesh):
    split = P("dp", None, None)
    return jax.shard_map(
        body,
        mesh=mesh,
        in_specs=(split, split, split, split, P("dp"), P("dp")) + (P(),) * 14,
        out_specs=(P("dp"), split, split, split, split) + (P(),) * 13,
        check_vma=False,
    )
```
